32 devices in a mesh: grp: 4 (over y, x), seq: 8 (over z, core).
Axes of the slice: x: 2, y: 2, z: 4, core: 2. Of those that a mesh axis runs over, the one named last changes fastest.
Arguments:
- tokens: bfloat16 [4, 4096, 768], P('grp', 'seq'), may hold values from -6 to 6
- first_values: bfloat16 [4, 4096, 384], P('grp', 'seq'), may hold values from -6 to 6
- placement: int32 [4, 8], P('grp'), may hold values from 0 to 7, each once within a row
- cotangent: bfloat16 [4, 4096, 768], P('grp', 'seq'), may hold values from -6 to 6
- first_norm_gain: bfloat16 [768], P(('grp', 'seq')), may hold values from 0.25 to 1.75
- first_norm_bias: bfloat16 [768], P(('grp', 'seq')), may hold values from -2 to 2
- query_weight: bfloat16 [768, 768], P(('grp', 'seq')), may hold values from -0.25 to 0.25
- query_bias: bfloat16 [768], P(('grp', 'seq')), may hold values from -2 to 2
- key_weight: bfloat16 [768, 768], P(('grp', 'seq')), may hold values from -0.25 to 0.25
- value_weight: bfloat16 [768, 384], P(('grp', 'seq')), may hold values from -0.21875 to 0.21875
- value_bias: bfloat16 [384], P(('grp', 'seq')), may hold values from -2 to 2
- output_weight: bfloat16 [768, 768], P(('grp', 'seq')), may hold values from -1.5 to 1.5
- output_bias: bfloat16 [768], P(('grp', 'seq')), may hold values from -2 to 2
- second_norm_gain: bfloat16 [768], P(('grp', 'seq')), may hold values from 0.25 to 1.75
- second_norm_bias: bfloat16 [768], P(('grp', 'seq')), may hold values from -2 to 2
- expand_weight: bfloat16 [768, 3072], P(('grp', 'seq')), may hold values from -0.21875 to 0.21875
- expand_bias: bfloat16 [3072], P(('grp', 'seq')), may hold values from -2 to 2
- reduce_weight: bfloat16 [3072, 768], P(('grp', 'seq')), may hold values from -0.109375 to 0.109375
- reduce_bias: bfloat16 [768], P(('grp', 'seq')), may hold values from -2 to 2
Outputs:
- layer_output: bfloat16 [4, 4096, 768], P('grp', 'seq')
- token_grad: float32 [4, 4096, 768], P('grp', 'seq')
- first_values_grad: float32 [4, 4096, 384], P('grp', 'seq')
- first_norm_gain_grad: float32 [768], P(('grp', 'seq'))
- first_norm_bias_grad: float32 [768], P(('grp', 'seq'))
- query_weight_grad: float32 [768, 768], P(('grp', 'seq'))
- query_bias_grad: float32 [768], P(('grp', 'seq'))
- key_weight_grad: float32 [768, 768], P(('grp', 'seq'))
- value_weight_grad: float32 [768, 384], P(('grp', 'seq'))
- value_bias_grad: float32 [384], P(('grp', 'seq'))
- output_weight_grad: float32 [768, 768], P(('grp', 'seq'))
- output_bias_grad: float32 [768], P(('grp', 'seq'))
- second_norm_gain_grad: float32 [768], P(('grp', 'seq'))
- second_norm_bias_grad: float32 [768], P(('grp', 'seq'))
- expand_weight_grad: float32 [768, 3072], P(('grp', 'seq'))
- expand_bias_grad: float32 [3072], P(('grp', 'seq'))
- reduce_weight_grad: float32 [3072, 768], P(('grp', 'seq'))
- reduce_bias_grad: float32 [768], P(('grp', 'seq'))
The draws below stay inside these ranges and needn't reach their ends.
Inputs may be any that keep to these rules, and one draw needn't show every extreme that they name: Each row of placement names every piece of its group once; pieces below 4 are prompt pieces in order, the others continuations.
All inputs are finite; a program needn't handle non-finite values.
Results may differ from the reference program's by a relative error of at most 0.019.
Values may be sent and summed in bfloat16 or wider, within the bound.
A program may use at most 256 MiB of HBM per device.

```python
import jax
import jax.numpy as jnp
from jax import lax

D = 768
HEADS = 12
HEAD = 64
FF = 3072
TOK_DEV = 512
GROUPS = 4
SEQ_ROWS = 4096
VW = 384
N_SEQ = 8


def shard_levels(key, shape, split, smallest, largest):
    factor_of = 1.0
    for position, shards_of in split:
        draws = jax.random.uniform(jax.random.fold_in(jax.random.fold_in(key, 6), position), (shards_of,), jnp.float32, smallest / len(split), largest / len(split))
        factor_of = factor_of * jnp.repeat(jnp.exp(draws), shape[position] // shards_of).reshape((-1,) + (1,) * (len(shape) - 1 - position))
    return factor_of


def gaussian(rng, extent, scale, bound, cuts=(), held_as=jnp.bfloat16):
    entries = scale * jax.random.normal(rng, extent, jnp.float32)
    if cuts:
        entries = entries * shard_levels(rng, extent, cuts, -0.22, 0.18)
    return jnp.clip(entries, -bound, bound).astype(held_as)


def setup_inputs(seed: int = 0) -> dict:
    key_list = jax.random.split(jax.random.key(seed), 20)
    return {
        "tokens": gaussian(key_list[0], (GROUPS, SEQ_ROWS, D), 1.0, 6.0, ((0, 4), (1, 8))),
        "first_values": gaussian(key_list[1], (GROUPS, SEQ_ROWS, VW), 1.0, 6.0, ((0, 4), (1, 8))),
        "placement": jax.vmap(lambda own: jax.random.permutation(own, N_SEQ))(jax.random.split(key_list[2], GROUPS)).reshape((GROUPS, N_SEQ)).astype(jnp.int32),
        "cotangent": gaussian(key_list[3], (GROUPS, SEQ_ROWS, D), 1.0, 6.0, ((0, 4), (1, 8))),
        "first_norm_gain": jnp.clip(1.0 + 0.15 * jax.random.normal(key_list[4], (D,), jnp.float32), 0.25, 1.75).astype(jnp.bfloat16),
        "first_norm_bias": gaussian(key_list[5], (D,), 0.3, 2.0, ((0, 32),)),
        "query_weight": gaussian(key_list[6], (D, D), (2 * D // 3) ** -0.5, 0.25, ((0, 32),)),
        "query_bias": gaussian(key_list[7], (D,), 0.3, 2.0, ((0, 32),)),
        "key_weight": gaussian(key_list[8], (D, D), (2 * D // 3) ** -0.5, 0.25, ((0, 32),)),
        "value_weight": gaussian(key_list[9], (D, VW), D ** -0.5, 0.21875, ((0, 32),)),
        "value_bias": gaussian(key_list[10], (VW,), 0.3, 2.0, ((0, 32),)),
        "output_weight": gaussian(key_list[11], (D, D), 16 ** -0.5, 1.5, ((0, 32),)),
        "output_bias": gaussian(key_list[12], (D,), 0.3, 2.0, ((0, 32),)),
        "second_norm_gain": jnp.clip(1.0 + 0.15 * jax.random.normal(key_list[13], (D,), jnp.float32), 0.25, 1.75).astype(jnp.bfloat16),
        "second_norm_bias": gaussian(key_list[14], (D,), 0.3, 2.0, ((0, 32),)),
        "expand_weight": gaussian(key_list[15], (D, FF), D ** -0.5, 0.21875, ((0, 32),)),
        "expand_bias": gaussian(key_list[16], (FF,), 0.3, 2.0, ((0, 32),)),
        "reduce_weight": gaussian(key_list[17], (FF, D), FF ** -0.5, 0.109375, ((0, 32),)),
        "reduce_bias": gaussian(key_list[18], (D,), 0.3, 2.0, ((0, 32),)),
    }


@jax.custom_vjp
def low(v):
    return lax.optimization_barrier(v.astype(jnp.bfloat16)).astype(jnp.float32)

@jax.custom_vjp
def low_back(v):
    return v

def low_keep(v):
    return (low(v), None)

def low_pass(kept, grad):
    return (grad,)

def back_keep(v):
    return (v, None)

def back_low(kept, grad):
    return (low(grad),)
low.defvjp(low_keep, low_pass)
low_back.defvjp(back_keep, back_low)
EPS = 1e-05
NEG = -1e+30

def product(a, b):
    return jnp.dot(a, b, precision=lax.Precision.HIGHEST)

def normalize(v, gain, shift):
    mean = lax.optimization_barrier(jnp.mean(v, axis=-1, keepdims=True))
    centred = v - mean
    var = lax.optimization_barrier(jnp.mean(centred * centred, axis=-1, keepdims=True))
    return centred * lax.rsqrt(var + EPS) * gain + shift

def attend(query_matrix, key_matrix, value_matrix, allow):
    logit_score = jnp.einsum('vwa,ewa->wve', query_matrix, key_matrix, precision=lax.Precision.HIGHEST) * 0.125
    logit_score = low_back(logit_score)
    logit_score = jnp.where(allow[None], logit_score, NEG)
    attention_probability = low(jax.nn.softmax(logit_score, axis=-1))
    return jnp.einsum('qjy,yqk->jqk', attention_probability, value_matrix, precision=lax.Precision.HIGHEST)

def group_forward(xrows, first, table, params):
    gain_one, bias_one, wquery, bquery, wkey, wvalue, bvalue, wout, bout, gain_two, bias_two, wexpand, bexpand, wreduce, breduce = params
    count = N_SEQ
    half = count // 2
    prompt_len = half * TOK_DEV
    hidden = low(normalize(xrows, gain_one, bias_one))
    query_matrix = low_back(low(product(hidden, wquery) + bquery))
    keyed = low_back(low(product(hidden, wkey)))
    valued = low_back(low(product(hidden, wvalue) + bvalue))
    merged = jnp.concatenate([valued, first], axis=1)
    places = jnp.arange(count, dtype=jnp.int32)
    slot_of = lax.optimization_barrier(jnp.sum(jnp.where(table[None, :] == places[:, None], places[None, :], 0), axis=1)).astype(jnp.int32)

    def pieces(a):
        return a.reshape(count, TOK_DEV, HEADS, HEAD)[slot_of]
    qpart, kpart, vpart = (pieces(query_matrix), pieces(keyed), pieces(merged))
    pquery = qpart[:half].reshape(prompt_len, HEADS, HEAD)
    pkeys = kpart[:half].reshape(prompt_len, HEADS, HEAD)
    pvals = vpart[:half].reshape(prompt_len, HEADS, HEAD)
    positions = jnp.arange(prompt_len, dtype=jnp.int32)
    causal = positions[:, None] >= positions[None, :]
    prompt_out = jax.checkpoint(attend)(pquery, pkeys, pvals, causal)
    own = jnp.arange(TOK_DEV, dtype=jnp.int32)
    tail_allow = jnp.concatenate([jnp.ones((TOK_DEV, prompt_len), dtype=bool), own[:, None] >= own[None, :]], axis=1)

    def tail(args):
        tquery, tkeys, tvals = args
        key_matrix = jnp.concatenate([pkeys, tkeys], axis=0)
        vals = jnp.concatenate([pvals, tvals], axis=0)
        return attend(tquery, key_matrix, vals, tail_allow)
    tail_out = lax.map(jax.checkpoint(tail), (qpart[half:], kpart[half:], vpart[half:]))
    out_pieces = jnp.concatenate([prompt_out.reshape(half, TOK_DEV, HEADS, HEAD), tail_out], axis=0)
    out_slots = out_pieces[table].reshape(count * TOK_DEV, HEADS * HEAD)
    attended = low_back(low(out_slots))
    middle = xrows + low_back(product(attended, wout) + bout)
    second = low(normalize(middle, gain_two, bias_two))
    pre = low_back(product(second, wexpand) + bexpand)
    post = low(jax.nn.gelu(pre, approximate=True))
    return middle + low_back(product(post, wreduce) + breduce)

def reference(tokens, first_values, placement, cotangent, first_norm_gain, first_norm_bias, query_weight, query_bias, key_weight, value_weight, value_bias, output_weight, output_bias, second_norm_gain, second_norm_bias, expand_weight, expand_bias, reduce_weight, reduce_bias):
    params = tuple((p.astype(jnp.float32) for p in (first_norm_gain, first_norm_bias, query_weight, query_bias, key_weight, value_weight, value_bias, output_weight, output_bias, second_norm_gain, second_norm_bias, expand_weight, expand_bias, reduce_weight, reduce_bias)))
    token_f = tokens.astype(jnp.float32)
    value_f = first_values.astype(jnp.float32)

    def forward(token_in, value_in, weights):

        def one(index):
            table = placement[index]
            block = jax.checkpoint(lambda a, b, p: group_forward(a, b, table, p))
            return block(token_in[index], value_in[index], weights)
        return lax.map(one, jnp.arange(GROUPS, dtype=jnp.int32))
    result, pullback = jax.vjp(forward, token_f, value_f, params)
    grad_tokens, grad_values, grad_params = pullback(cotangent.astype(jnp.float32))
    return (result.astype(jnp.bfloat16), grad_tokens, grad_values, grad_params[0], grad_params[1], grad_params[2], grad_params[3], grad_params[4], grad_params[5], grad_params[6], grad_params[7], grad_params[8], grad_params[9], grad_params[10], grad_params[11], grad_params[12], grad_params[13], grad_params[14])
```

```python
import functools
import math

import jax
import jax.numpy as jnp
from jax import lax
from jax.experimental import pallas as pl
from jax.experimental.pallas import tpu as pltpu
from jax.sharding import PartitionSpec as P

HEAD = 64
FRESH = 6


EPS = 1e-05
NEG = -1e30


def normalize(v, gain, shift):
    mean = jnp.mean(v, axis=-1, keepdims=True)
    centred = v - mean
    var = jnp.mean(centred * centred, axis=-1, keepdims=True)
    return centred * lax.rsqrt(var + EPS) * gain + shift


def gelu_tanh(v):
    return jax.nn.gelu(v, approximate=True)


def matmul(a, b):
    return jnp.dot(a, b, preferred_element_type=jnp.float32)


def matmul_left(a, b):
    return lax.dot_general(a, b, (((0,), (0,)), ((), ())), preferred_element_type=jnp.float32)


def matmul_right(a, b):
    return lax.dot_general(a, b, (((1,), (1,)), ((), ())), preferred_element_type=jnp.float32)


MESH = pl.DeviceIdType.MESH


def powers(count):
    out, bit = [], 1
    while bit < count:
        out.append(bit)
        bit *= 2
    return out


def remote(src, dst, send, recv, device):
    return pltpu.make_async_remote_copy(
        src_ref=src, dst_ref=dst, send_sem=send, recv_sem=recv,
        device_id=device, device_id_type=MESH,
    )


def enter(devices):
    barrier = pltpu.get_barrier_semaphore()
    for device in devices:
        pl.semaphore_signal(barrier, inc=1, device_id=device, device_id_type=MESH)
    pl.semaphore_wait(barrier, len(devices))


class Gather:
    def __init__(self, groups, chips, bits, shard, full, chain_send, level_send, recv, pair, own):
        self.groups, self.chips, self.bits = groups, chips, bits
        self.shard, self.full = shard, full
        self.chain_send, self.level_send, self.recv, self.pair, self.own = chain_send, level_send, recv, pair, own
        self.g = lax.axis_index("grp")
        seq = lax.axis_index("seq")
        self.s, self.z, self.c = seq, seq // 2, seq % 2

    def block(self, g, z, c):
        return self.full.at[g, z, c]

    def source(self, mask, z, first):
        return self.shard if first else self.block(self.g ^ mask, z, self.c)

    def chain(self, z, step, first):
        side = 0 if step < 0 else 1
        return remote(self.source(0, z, first), self.block(self.g, z, self.c),
                      self.chain_send.at[z, side], self.recv.at[self.g, z],
                      {"seq": self.s + 2 * step})

    def cross(self, level, mask, z, first):
        g = self.g ^ mask
        return remote(self.source(mask, z, first), self.block(g, z, self.c),
                      self.level_send.at[level], self.recv.at[g, z],
                      {"grp": self.g ^ self.bits[level]})

    def held(self, level):
        masks = [0]
        for bit in self.bits[:level]:
            masks = masks + [m ^ bit for m in masks]
        return masks

    def here(self, mask, z):
        g = self.g ^ mask
        pltpu.make_async_copy(self.block(g, z, self.c), self.block(g, z, self.c), self.recv.at[g, z]).wait()

    def begin(self):
        copy = pltpu.make_async_copy(self.shard, self.block(self.g, self.z, self.c), self.own)
        copy.start()

        @pl.when(self.z > 0)
        def _():
            self.chain(self.z, -1, True).start()

        @pl.when(self.z < self.chips - 1)
        def _():
            self.chain(self.z, 1, True).start()

        for level in range(len(self.bits)):
            self.cross(level, 0, self.z, True).start()

    def at(self, distance, body):
        if distance == 0:
            body(self.z, 0)
            return

        @pl.when(self.z >= distance)
        def _():
            body(self.z - distance, 1)

        @pl.when(self.z + distance < self.chips)
        def _():
            body(self.z + distance, -1)

    def along(self, distance):
        def body(z, step):
            self.here(0, z)
            onward = self.z < self.chips - 1 if step > 0 else self.z > 0

            @pl.when(onward)
            def _():
                self.chain(z, step, False).start()

            for level in range(len(self.bits)):
                self.cross(level, 0, z, False).start()

        if distance > 0:
            self.at(distance, body)

    def over(self, level, distance):
        def body(z, step):
            for mask in self.held(level):
                mask = mask ^ self.bits[level]
                self.here(mask, z)
                for later in range(level + 1, len(self.bits)):
                    self.cross(later, mask, z, False).start()

        self.at(distance, body)

    def swap_copy(self):
        mine = self.full.at[:, :, self.c]
        return remote(mine, mine, self.pair.at[0], self.pair.at[1], {"seq": self.s ^ 1})

    def swap(self):
        pltpu.make_async_copy(self.shard, self.shard, self.own).wait()
        self.swap_copy().start()

    def finish(self):
        self.swap_copy().wait_send()
        other = self.full.at[:, :, 1 - self.c]
        pltpu.make_async_copy(other, other, self.pair.at[1]).wait()

        @pl.when(self.z > 0)
        def _():
            self.chain(self.z, -1, True).wait_send()

        @pl.when(self.z < self.chips - 1)
        def _():
            self.chain(self.z, 1, True).wait_send()

        for distance in range(1, self.chips):
            def body(z, step):
                onward = self.z < self.chips - 1 if step > 0 else self.z > 0

                @pl.when(onward)
                def _():
                    self.chain(z, step, False).wait_send()

            self.at(distance, body)
        for level in range(len(self.bits)):
            sent = self.full.at[pl.ds(0, 2 ** level), :, 0]
            pltpu.make_async_copy(sent, sent, self.level_send.at[level]).wait()


def gather_semaphores(count, groups, chips):
    dma = pltpu.SemaphoreType.DMA
    levels = max(len(powers(groups)), 1)
    return [dma((count, chips, 2)), dma((count, levels)), dma((count, groups, chips)), dma((count, 2)), dma((count,))]


def neighbours(groups, n):
    g, s = lax.axis_index("grp"), lax.axis_index("seq")
    out = [{"grp": g ^ bit} for bit in powers(groups)]
    out += [{"seq": s ^ 1}, {"seq": lax.rem(s + 2, n)}, {"seq": lax.rem(s + n - 2, n)}]
    return out


def gather_kernel(groups, chips, orders, *refs):
    count = len(orders)
    shards, fulls, sems = refs[:count], refs[count:2 * count], refs[2 * count:]
    enter(neighbours(groups, 2 * chips))
    gathers = [Gather(groups, chips, orders[i], shards[i], fulls[i], *[s.at[i] for s in sems]) for i in range(count)]
    run_gathers(gathers)


def run_gathers(gathers):
    chips, levels = gathers[0].chips, len(gathers[0].bits)
    for g in gathers:
        g.begin()
    for distance in range(chips + levels):
        for g in gathers:
            if distance + 1 < chips:
                g.along(distance + 1)
            for level in range(levels):
                if 0 <= distance - level < chips:
                    g.over(level, distance - level)
    for g in gathers:
        g.swap()
    for g in gathers:
        g.finish()


def gather_call(groups, chips, shards, orders):
    count = len(shards)
    return pl.pallas_call(
        functools.partial(gather_kernel, groups, chips, orders),
        out_shape=[jax.ShapeDtypeStruct((groups, chips, 2) + x.shape, x.dtype) for x in shards],
        in_specs=[pl.BlockSpec(memory_space=pl.ANY)] * count,
        out_specs=[pl.BlockSpec(memory_space=pl.ANY)] * count,
        scratch_shapes=gather_semaphores(count, groups, chips),
        compiler_params=pltpu.CompilerParams(collective_id=0, has_side_effects=True),
        name="gather_parameters",
    )(*shards)


def collect(parts):
    groups = lax.axis_size("grp")
    n = lax.axis_size("seq")
    small = (0, 1, 3, 6, 8, 9, 10, 12, 14)
    packed = jnp.concatenate([parts[i] for i in small])
    sizes = [parts[i].shape[0] for i in small]
    length = packed.shape[0]
    packed = jnp.pad(packed, (0, 2048 - length)).reshape(16, 128)
    bits = powers(groups)
    forth, back = bits, bits[::-1]
    shards = [packed, parts[2], parts[5], parts[4], parts[7], parts[11], parts[13]]
    fulls = gather_call(groups, n // 2, shards, [forth, forth, forth, back, back, forth, back])
    flat = fulls[0].reshape(groups * n, 2048)
    whole = [None] * 15
    at = 0
    for i, size in zip(small, sizes):
        whole[i] = flat[:, at : at + size].reshape(groups * n * size)
        at += size
    for i, full in zip((2, 5, 4, 7, 11, 13), fulls[1:]):
        whole[i] = full.reshape(-1, full.shape[-1])
    return tuple(whole)


def own_piece_of(table, slot):
    places = jnp.arange(table.shape[0], dtype=jnp.int32)
    return jnp.sum(jnp.where(places == slot, table, 0))


def layout_whole(table, slot, rows, total):
    count = table.shape[0]
    places = jnp.arange(count, dtype=jnp.int32)
    key_matrix = jnp.arange(total, dtype=jnp.int32)
    key_slot = key_matrix // rows
    piece = jnp.sum(jnp.where(key_slot[:, None] == places[None, :], table[None, :], 0), axis=1)
    return (piece, key_matrix % rows, own_piece_of(table, slot))


def key_mask(layout, half, start, block, rows):
    piece_all, pos_all, own = layout
    piece = lax.dynamic_slice_in_dim(piece_all, start, block, 0)
    key_pos = lax.dynamic_slice_in_dim(pos_all, start, block, 0)
    early = (piece < half) & ((piece < own) | (own >= half))
    same = piece == own
    query_pos = jnp.arange(rows, dtype=jnp.int32)
    allow = early[None, :] | same[None, :] & (key_pos[None, :] <= query_pos[:, None])
    return (allow, jnp.any(early | same))


def attend_forward(query_matrix, key_matrix, value_matrix, layout, half, rows, block):
    heads = query_matrix.shape[1]
    depth = query_matrix.shape[2]
    total = key_matrix.shape[0]

    def step(carry, index):
        start = index * block
        allow, live = key_mask(layout, half, start, block, rows)

        def work(state):
            top, denom, accum = state
            key_portion = lax.dynamic_slice_in_dim(key_matrix, start, block, 0)
            value_portion = lax.dynamic_slice_in_dim(value_matrix, start, block, 0)
            logit_score = (
                jnp.einsum(
                    "vwa,ewa->wve", query_matrix, key_portion, preferred_element_type=jnp.float32
                )
                * 0.125
            )
            logit_score = jnp.where(allow[None], logit_score, NEG)
            new_top = jnp.maximum(top, jnp.max(logit_score, axis=-1))
            weight = jnp.where(allow[None], jnp.exp(logit_score - new_top[..., None]), 0.0)
            factor = jnp.exp(top - new_top)
            denom = denom * factor + jnp.sum(weight, axis=-1)
            accum = accum * factor[..., None] + jnp.einsum(
                "paq,qpc->pac",
                weight.astype(jnp.bfloat16),
                value_portion,
                preferred_element_type=jnp.float32,
            )
            return (new_top, denom, accum)

        return (lax.cond(live, work, lambda state: state, carry), None)

    init = (
        jnp.full((heads, rows), NEG, jnp.float32),
        jnp.zeros((heads, rows), jnp.float32),
        jnp.zeros((heads, rows, depth), jnp.float32),
    )
    (top, denom, accum), _ = lax.scan(step, init, jnp.arange(total // block))
    out = accum / denom[..., None]
    return (jnp.transpose(out, (1, 0, 2)), top + jnp.log(denom))


def attend_backward(
    query_matrix,
    key_matrix,
    value_matrix,
    output_gradient_rows,
    delta,
    logsum,
    layout,
    half,
    rows,
    block,
):
    heads = query_matrix.shape[1]
    depth = query_matrix.shape[2]
    total = key_matrix.shape[0]

    def step(grad_query, index):
        start = index * block
        allow, live = key_mask(layout, half, start, block, rows)

        def work(grad_query):
            key_portion = lax.dynamic_slice_in_dim(key_matrix, start, block, 0)
            value_portion = lax.dynamic_slice_in_dim(value_matrix, start, block, 0)
            logit_score = (
                jnp.einsum(
                    "vwa,ewa->wve", query_matrix, key_portion, preferred_element_type=jnp.float32
                )
                * 0.125
            )
            attention_probability = jnp.where(
                allow[None], jnp.exp(logit_score - logsum[..., None]), 0.0
            )
            grad_prob = jnp.einsum(
                "vwa,ewa->wve",
                output_gradient_rows,
                value_portion,
                preferred_element_type=jnp.float32,
            )
            score_gradient_terms = (attention_probability * (grad_prob - delta[..., None])).astype(
                jnp.bfloat16
            )
            grad_query = (
                grad_query
                + jnp.einsum(
                    "qjy,yqk->jqk",
                    score_gradient_terms,
                    key_portion,
                    preferred_element_type=jnp.float32,
                )
                * 0.125
            )
            grad_key = (
                jnp.einsum(
                    "oae,aoj->eoj",
                    score_gradient_terms,
                    query_matrix,
                    preferred_element_type=jnp.float32,
                )
                * 0.125
            )
            grad_value = jnp.einsum(
                "oae,aoj->eoj",
                attention_probability.astype(jnp.bfloat16),
                output_gradient_rows,
                preferred_element_type=jnp.float32,
            )
            return (grad_query, (grad_key, grad_value))

        def skip(grad_query):
            zeros = jnp.zeros((block, heads, depth), jnp.float32)
            return (grad_query, (zeros, zeros))

        return lax.cond(live, work, skip, grad_query)

    start_grad = jnp.zeros((rows, heads, depth), jnp.float32)
    grad_query, (key_grads, value_grads) = lax.scan(step, start_grad, jnp.arange(total // block))
    return (
        grad_query,
        key_grads.reshape(total, heads * depth),
        value_grads.reshape(total, heads * depth),
    )


def body(
    tokens,
    first_values,
    placement,
    cotangent,
    first_norm_gain,
    first_norm_bias,
    query_weight,
    query_bias,
    key_weight,
    value_weight,
    value_bias,
    output_weight,
    output_bias,
    second_norm_gain,
    second_norm_bias,
    expand_weight,
    expand_bias,
    reduce_weight,
    reduce_bias,
):
    groups, rows, width = tokens.shape
    heads = width // HEAD
    fresh_width = FRESH * HEAD
    count = placement.shape[1]
    half = count // 2
    slot = lax.axis_index("seq")
    parts = (
        first_norm_gain,
        first_norm_bias,
        query_weight,
        query_bias,
        key_weight,
        value_weight,
        value_bias,
        output_weight,
        output_bias,
        second_norm_gain,
        second_norm_bias,
        expand_weight,
        expand_bias,
        reduce_weight,
        reduce_bias,
    )
    whole = collect(parts)
    gain_one = whole[0].astype(jnp.float32)
    bias_one = whole[1].astype(jnp.float32)
    gain_two = whole[9].astype(jnp.float32)
    bias_two = whole[10].astype(jnp.float32)
    flat = tokens.reshape(groups * rows, width).astype(jnp.float32)
    normed, norm_one_back = jax.vjp(normalize, flat, gain_one, bias_one)
    hidden = normed.astype(jnp.bfloat16)
    query_matrix = (matmul(hidden, whole[2]) + whole[3].astype(jnp.float32)).astype(jnp.bfloat16)
    keyed = matmul(hidden, whole[4]).astype(jnp.bfloat16)
    valued = (matmul(hidden, whole[5]) + whole[6].astype(jnp.float32)).astype(jnp.bfloat16)
    keys_local = keyed.reshape(groups, rows, width)
    values_local = jnp.concatenate(
        [valued.reshape(groups, rows, fresh_width), first_values], axis=2
    )
    gathered_keys, gathered_values = (
        lax.all_gather(keys_local, "seq", axis=1, tiled=True),
        lax.all_gather(values_local, "seq", axis=1, tiled=True),
    )
    total = gathered_keys.shape[1]
    block = math.gcd(total, 512)
    layouts = [layout_whole(placement[0], slot, rows, total)]
    query_heads = query_matrix.reshape(groups, rows, heads, HEAD)
    index = 0
    out, logsum = attend_forward(
        query_heads[index],
        gathered_keys[index].reshape(total, heads, HEAD),
        gathered_values[index].reshape(total, heads, HEAD),
        layouts[index],
        half,
        rows,
        block,
    )
    sums = [logsum]
    attended = out.reshape(groups * rows, width)
    attended_low = attended.astype(jnp.bfloat16)
    middle = flat + matmul(attended_low, whole[7]) + whole[8].astype(jnp.float32)
    normed_two, norm_two_back = jax.vjp(normalize, middle, gain_two, bias_two)
    second = normed_two.astype(jnp.bfloat16)
    pre = matmul(second, whole[11]) + whole[12].astype(jnp.float32)
    post_full, gelu_back = jax.vjp(gelu_tanh, pre)
    post = post_full.astype(jnp.bfloat16)
    result = middle + matmul(post, whole[13]) + whole[14].astype(jnp.float32)
    layer_output = result.astype(jnp.bfloat16).reshape(groups, rows, width)
    again = whole
    seed = cotangent.reshape(groups * rows, width)
    seed_full = seed.astype(jnp.float32)
    grad_reduce_bias = jnp.sum(seed_full, axis=0)
    grad_reduce = matmul_left(post, seed)
    grad_post = matmul_right(seed, again[13])
    grad_pre = gelu_back(grad_post)[0].astype(jnp.bfloat16)
    grad_expand_bias = jnp.sum(grad_pre.astype(jnp.float32), axis=0)
    grad_expand = matmul_left(second, grad_pre)
    grad_second = matmul_right(grad_pre, again[11])
    grad_mid_norm, grad_gain_two, grad_bias_two = norm_two_back(grad_second)
    grad_mid = grad_mid_norm + seed_full
    grad_branch = grad_mid.astype(jnp.bfloat16)
    grad_output_bias = jnp.sum(grad_branch.astype(jnp.float32), axis=0)
    grad_output = matmul_left(attended_low, grad_branch)
    grad_attended = matmul_right(grad_branch, again[7]).astype(jnp.bfloat16)
    grad_attended_heads = grad_attended.reshape(groups, rows, heads, HEAD)
    attended_heads = attended.reshape(groups, rows, heads, HEAD)
    index = 0
    delta = jnp.transpose(
        jnp.sum(grad_attended_heads[index].astype(jnp.float32) * attended_heads[index], axis=-1)
    )
    grad_query, grad_keys, grad_values = attend_backward(
        query_heads[index],
        gathered_keys[index].reshape(total, heads, HEAD),
        gathered_values[index].reshape(total, heads, HEAD),
        grad_attended_heads[index],
        delta,
        sums[index],
        layouts[index],
        half,
        rows,
        block,
    )
    key_terms = [grad_keys]
    value_terms = [grad_values]
    key_stack = jnp.stack(key_terms)
    value_stack = jnp.stack(value_terms)
    key_sums, value_sums = (
        lax.psum_scatter(
            key_stack.astype(jnp.bfloat16), "seq", scatter_dimension=1, tiled=True
        ).astype(jnp.float32),
        lax.psum_scatter(
            value_stack.astype(jnp.bfloat16), "seq", scatter_dimension=1, tiled=True
        ).astype(jnp.float32),
    )
    grad_key = key_sums.reshape(groups * rows, width).astype(jnp.bfloat16)
    grad_fresh = (
        value_sums[:, :, :fresh_width].reshape(groups * rows, fresh_width).astype(jnp.bfloat16)
    )
    first_values_grad = value_sums[:, :, fresh_width:]
    grad_query_all = grad_query.reshape(groups * rows, width).astype(jnp.bfloat16)
    grad_query_bias = jnp.sum(grad_query_all.astype(jnp.float32), axis=0)
    grad_query_weight = matmul_left(hidden, grad_query_all)
    grad_key_weight = matmul_left(hidden, grad_key)
    grad_value_weight = matmul_left(hidden, grad_fresh)
    grad_value_bias = jnp.sum(grad_fresh.astype(jnp.float32), axis=0)
    grad_hidden = (
        matmul_right(grad_query_all, again[2])
        + matmul_right(grad_key, again[4])
        + matmul_right(grad_fresh, again[5])
    )
    grad_in, grad_gain_one, grad_bias_one = norm_one_back(grad_hidden)
    token_grad = (grad_in + grad_mid).reshape(groups, rows, width)
    owned = (
        lax.psum_scatter(grad_gain_one, ("grp", "seq"), scatter_dimension=0, tiled=True),
        lax.psum_scatter(grad_bias_one, ("grp", "seq"), scatter_dimension=0, tiled=True),
        lax.psum_scatter(grad_query_weight, ("grp", "seq"), scatter_dimension=0, tiled=True),
        lax.psum_scatter(grad_query_bias, ("grp", "seq"), scatter_dimension=0, tiled=True),
        lax.psum_scatter(grad_key_weight, ("grp", "seq"), scatter_dimension=0, tiled=True),
        lax.psum_scatter(grad_value_weight, ("grp", "seq"), scatter_dimension=0, tiled=True),
        lax.psum_scatter(grad_value_bias, ("grp", "seq"), scatter_dimension=0, tiled=True),
        lax.psum_scatter(grad_output, ("grp", "seq"), scatter_dimension=0, tiled=True),
        lax.psum_scatter(grad_output_bias, ("grp", "seq"), scatter_dimension=0, tiled=True),
        lax.psum_scatter(grad_gain_two, ("grp", "seq"), scatter_dimension=0, tiled=True),
        lax.psum_scatter(grad_bias_two, ("grp", "seq"), scatter_dimension=0, tiled=True),
        lax.psum_scatter(grad_expand, ("grp", "seq"), scatter_dimension=0, tiled=True),
        lax.psum_scatter(grad_expand_bias, ("grp", "seq"), scatter_dimension=0, tiled=True),
        lax.psum_scatter(grad_reduce, ("grp", "seq"), scatter_dimension=0, tiled=True),
        lax.psum_scatter(grad_reduce_bias, ("grp", "seq"), scatter_dimension=0, tiled=True),
    )
    return (
        layer_output,
        token_grad,
        first_values_grad,
        owned[0],
        owned[1],
        owned[2],
        owned[3],
        owned[4],
        owned[5],
        owned[6],
        owned[7],
        owned[8],
        owned[9],
        owned[10],
        owned[11],
        owned[12],
        owned[13],
        owned[14],
    )


def solution(mesh):
    in_specs = (
        P("grp", "seq", None),
        P("grp", "seq", None),
        P("grp", None),
        P("grp", "seq", None),
        P(("grp", "seq")),
        P(("grp", "seq")),
        P(("grp", "seq"), None),
        P(("grp", "seq")),
        P(("grp", "seq"), None),
        P(("grp", "seq"), None),
        P(("grp", "seq")),
        P(("grp", "seq"), None),
        P(("grp", "seq")),
        P(("grp", "seq")),
        P(("grp", "seq")),
        P(("grp", "seq"), None),
        P(("grp", "seq")),
        P(("grp", "seq"), None),
        P(("grp", "seq")),
    )
    out_specs = (
        P("grp", "seq", None),
        P("grp", "seq", None),
        P("grp", "seq", None),
        P(("grp", "seq")),
        P(("grp", "seq")),
        P(("grp", "seq"), None),
        P(("grp", "seq")),
        P(("grp", "seq"), None),
        P(("grp", "seq"), None),
        P(("grp", "seq")),
        P(("grp", "seq"), None),
        P(("grp", "seq")),
        P(("grp", "seq")),
        P(("grp", "seq")),
        P(("grp", "seq"), None),
        P(("grp", "seq")),
        P(("grp", "seq"), None),
        P(("grp", "seq")),
    )
    return jax.shard_map(body, mesh=mesh, in_specs=in_specs, out_specs=out_specs, check_vma=False)
```

```python
import functools

import jax
import jax.numpy as jnp
from jax import lax
from jax.experimental import pallas as pl
from jax.experimental.pallas import tpu as pltpu
from jax.sharding import PartitionSpec as P

MESH = pl.DeviceIdType.MESH


def powers(count):
    out, bit = [], 1
    while bit < count:
        out.append(bit)
        bit *= 2
    return out


def remote(src, dst, send, recv, device):
    return pltpu.make_async_remote_copy(
        src_ref=src, dst_ref=dst, send_sem=send, recv_sem=recv,
        device_id=device, device_id_type=MESH,
    )


def enter(devices):
    barrier = pltpu.get_barrier_semaphore()
    for device in devices:
        pl.semaphore_signal(barrier, inc=1, device_id=device, device_id_type=MESH)
    pl.semaphore_wait(barrier, len(devices))


class Gather:
    def __init__(self, groups, chips, bits, shard, full, chain_send, level_send, recv, pair, own):
        self.groups, self.chips, self.bits = groups, chips, bits
        self.shard, self.full = shard, full
        self.chain_send, self.level_send, self.recv, self.pair, self.own = chain_send, level_send, recv, pair, own
        self.g = lax.axis_index("grp")
        seq = lax.axis_index("seq")
        self.s, self.z, self.c = seq, seq // 2, seq % 2

    def block(self, g, z, c):
        return self.full.at[g, z, c]

    def source(self, mask, z, first):
        return self.shard if first else self.block(self.g ^ mask, z, self.c)

    def chain(self, z, step, first):
        side = 0 if step < 0 else 1
        return remote(self.source(0, z, first), self.block(self.g, z, self.c),
                      self.chain_send.at[z, side], self.recv.at[self.g, z],
                      {"seq": self.s + 2 * step})

    def cross(self, level, mask, z, first):
        g = self.g ^ mask
        return remote(self.source(mask, z, first), self.block(g, z, self.c),
                      self.level_send.at[level], self.recv.at[g, z],
                      {"grp": self.g ^ self.bits[level]})

    def held(self, level):
        masks = [0]
        for bit in self.bits[:level]:
            masks = masks + [m ^ bit for m in masks]
        return masks

    def here(self, mask, z):
        g = self.g ^ mask
        pltpu.make_async_copy(self.block(g, z, self.c), self.block(g, z, self.c), self.recv.at[g, z]).wait()

    def begin(self):
        copy = pltpu.make_async_copy(self.shard, self.block(self.g, self.z, self.c), self.own)
        copy.start()

        @pl.when(self.z > 0)
        def _():
            self.chain(self.z, -1, True).start()

        @pl.when(self.z < self.chips - 1)
        def _():
            self.chain(self.z, 1, True).start()

        for level in range(len(self.bits)):
            self.cross(level, 0, self.z, True).start()

    def at(self, distance, body):
        if distance == 0:
            body(self.z, 0)
            return

        @pl.when(self.z >= distance)
        def _():
            body(self.z - distance, 1)

        @pl.when(self.z + distance < self.chips)
        def _():
            body(self.z + distance, -1)

    def along(self, distance):
        def body(z, step):
            self.here(0, z)
            onward = self.z < self.chips - 1 if step > 0 else self.z > 0

            @pl.when(onward)
            def _():
                self.chain(z, step, False).start()

            for level in range(len(self.bits)):
                self.cross(level, 0, z, False).start()

        if distance > 0:
            self.at(distance, body)

    def over(self, level, distance):
        def body(z, step):
            for mask in self.held(level):
                mask = mask ^ self.bits[level]
                self.here(mask, z)
                for later in range(level + 1, len(self.bits)):
                    self.cross(later, mask, z, False).start()

        self.at(distance, body)

    def swap_copy(self):
        mine = self.full.at[:, :, self.c]
        return remote(mine, mine, self.pair.at[0], self.pair.at[1], {"seq": self.s ^ 1})

    def swap(self):
        pltpu.make_async_copy(self.shard, self.shard, self.own).wait()
        self.swap_copy().start()

    def finish(self):
        self.swap_copy().wait_send()
        other = self.full.at[:, :, 1 - self.c]
        pltpu.make_async_copy(other, other, self.pair.at[1]).wait()

        @pl.when(self.z > 0)
        def _():
            self.chain(self.z, -1, True).wait_send()

        @pl.when(self.z < self.chips - 1)
        def _():
            self.chain(self.z, 1, True).wait_send()

        for distance in range(1, self.chips):
            def body(z, step):
                onward = self.z < self.chips - 1 if step > 0 else self.z > 0

                @pl.when(onward)
                def _():
                    self.chain(z, step, False).wait_send()

            self.at(distance, body)
        for level in range(len(self.bits)):
            sent = self.full.at[pl.ds(0, 2 ** level), :, 0]
            pltpu.make_async_copy(sent, sent, self.level_send.at[level]).wait()


def gather_semaphores(count, groups, chips):
    dma = pltpu.SemaphoreType.DMA
    levels = max(len(powers(groups)), 1)
    return [dma((count, chips, 2)), dma((count, levels)), dma((count, groups, chips)), dma((count, 2)), dma((count,))]


def neighbours(groups, n):
    g, s = lax.axis_index("grp"), lax.axis_index("seq")
    out = [{"grp": g ^ bit} for bit in powers(groups)]
    out += [{"seq": s ^ 1}, {"seq": lax.rem(s + 2, n)}, {"seq": lax.rem(s + n - 2, n)}]
    return out


def gather_kernel(groups, chips, orders, *refs):
    count = len(orders)
    shards, fulls, sems = refs[:count], refs[count:2 * count], refs[2 * count:]
    enter(neighbours(groups, 2 * chips))
    gathers = [Gather(groups, chips, orders[i], shards[i], fulls[i], *[s.at[i] for s in sems]) for i in range(count)]
    run_gathers(gathers)


def run_gathers(gathers):
    chips, levels = gathers[0].chips, len(gathers[0].bits)
    for g in gathers:
        g.begin()
    for distance in range(chips + levels):
        for g in gathers:
            if distance + 1 < chips:
                g.along(distance + 1)
            for level in range(levels):
                if 0 <= distance - level < chips:
                    g.over(level, distance - level)
    for g in gathers:
        g.swap()
    for g in gathers:
        g.finish()


def gather_call(groups, chips, shards, orders):
    count = len(shards)
    return pl.pallas_call(
        functools.partial(gather_kernel, groups, chips, orders),
        out_shape=[jax.ShapeDtypeStruct((groups, chips, 2) + x.shape, x.dtype) for x in shards],
        in_specs=[pl.BlockSpec(memory_space=pl.ANY)] * count,
        out_specs=[pl.BlockSpec(memory_space=pl.ANY)] * count,
        scratch_shapes=gather_semaphores(count, groups, chips),
        compiler_params=pltpu.CompilerParams(collective_id=0, has_side_effects=True),
        name="gather_parameters",
    )(*shards)


class Reduce:
    def __init__(self, groups, chips, bits, partial, shard, own, landed, halves, left, right, sems):
        self.groups, self.chips, self.bits = groups, chips, bits
        self.partial, self.shard, self.own, self.landed = partial, shard, own, landed
        self.halves, self.left, self.right = halves, left, right
        self.load, self.pair, self.level_send, self.level_recv, self.chain_send, self.chain_recv = sems
        self.g = lax.axis_index("grp")
        self.s = lax.axis_index("seq")
        self.z, self.c = self.s // 2, self.s % 2

    def masks(self, level):
        out = [0]
        for bit in self.bits[level:]:
            out = out + [m ^ bit for m in out]
        return out

    def load_copy(self):
        return pltpu.make_async_copy(self.partial.at[:, :, self.c], self.own, self.load.at[0])

    def pair_copy(self):
        return remote(self.partial.at[:, :, 1 - self.c], self.landed, self.pair.at[0], self.pair.at[1],
                      {"seq": self.s ^ 1})

    def begin(self):
        self.pair_copy().start()
        self.load_copy().start()

    def paired(self):
        self.load_copy().wait()
        self.pair_copy().wait_recv()

        @pl.loop(0, self.groups)
        def _(g):
            self.own[g] = self.add(self.own[g], self.landed[g])

        self.cross_start(0)

    def add(self, a, b):
        return (a.astype(jnp.float32) + b.astype(jnp.float32)).astype(a.dtype)

    def cross_copies(self, level):
        bit = self.bits[level]
        out = []
        for where, mask in enumerate(self.masks(level + 1)):
            out.append(remote(self.own.at[self.g ^ bit ^ mask], self.halves[level].at[where],
                              self.level_send.at[level, where], self.level_recv.at[level, where],
                              {"grp": self.g ^ bit}))
        return out

    def cross_start(self, level):
        if level < len(self.bits):
            for copy in self.cross_copies(level):
                copy.start()
        else:
            self.chain_first()

    def crossed(self, level):
        copies = self.cross_copies(level)
        for where, mask in enumerate(self.masks(level + 1)):
            copies[where].wait_recv()
            g = self.g ^ mask
            self.own[g] = self.add(self.own[g], self.halves[level][where])
        self.cross_start(level + 1)

    def chain_copy(self, block, step):
        side = 0 if step < 0 else 1
        return remote(self.own.at[self.g, block], (self.right if step < 0 else self.left).at[block],
                      self.chain_send.at[block], self.chain_recv.at[1 - side, block],
                      {"seq": self.s + 2 * step})

    def chain_wait(self, block, side):
        landed = (self.left if side == 0 else self.right).at[block]
        pltpu.make_async_copy(landed, landed, self.chain_recv.at[side, block]).wait()

    def chain_first(self):
        last = self.chips - 1

        @pl.when(self.z == 0)
        def _():
            for block in range(last, 0, -1):
                self.chain_copy(block, 1).start()

        @pl.when(self.z == last)
        def _():
            for block in range(last):
                self.chain_copy(block, -1).start()

    def chained(self, k):
        last = self.chips - 1
        block = last - k

        @pl.when((self.z > 0) & (self.z < block))
        def _():
            self.chain_wait(block, 0)
            self.own[self.g, block] = self.add(self.own[self.g, block], self.left[block])
            self.chain_copy(block, 1).start()

        @pl.when((self.z < last) & (self.z > k))
        def _():
            self.chain_wait(k, 1)
            self.own[self.g, k] = self.add(self.own[self.g, k], self.right[k])
            self.chain_copy(k, -1).start()

    def finish(self):
        last = self.chips - 1
        self.shard[...] = self.own[self.g, self.z].astype(jnp.float32)

        @pl.when(self.z > 0)
        def _():
            self.chain_wait(self.z, 0)
            self.shard[...] = self.shard[...] + self.left[self.z].astype(jnp.float32)

        @pl.when(self.z < last)
        def _():
            self.chain_wait(self.z, 1)
            self.shard[...] = self.shard[...] + self.right[self.z].astype(jnp.float32)

    def drain(self):
        self.pair_copy().wait_send()
        for level in range(len(self.bits)):
            for copy in self.cross_copies(level):
                copy.wait_send()
        for block in range(self.chips):
            @pl.when(self.z < block)
            def _():
                self.chain_copy(block, 1).wait_send()

            @pl.when(self.z > block)
            def _():
                self.chain_copy(block, -1).wait_send()


def reduce_steps(reduces):
    chips, levels = reduces[0].chips, len(reduces[0].bits)
    stages = [lambda r: r.begin(), lambda r: r.paired()]
    for level in range(levels):
        stages.append(lambda r, level=level: r.crossed(level))
    for k in range(chips - 1):
        stages.append(lambda r, k=k: r.chained(k))
    stages.append(lambda r: r.finish())
    stages.append(lambda r: r.drain())
    out = []
    for time in range(len(stages) + len(reduces) - 1):
        for i, r in enumerate(reduces):
            if 0 <= time - i < len(stages):
                out.append(functools.partial(stages[time - i], r))
    return out


def reduce_scratch(groups, chips, shapes):
    vmem, dma = pltpu.VMEM, pltpu.SemaphoreType.DMA
    levels = len(powers(groups))
    out = []
    for _, _, _, rows, cols, dtype in shapes:
        out += [vmem((groups, chips, rows, cols), dtype), vmem((groups, chips, rows, cols), dtype)]
        out += [vmem((groups >> (level + 1), chips, rows, cols), dtype) for level in range(levels)]
        out += [vmem((chips, rows, cols), dtype)] * 2
        out += [dma((1,)), dma((2,)), dma((max(levels, 1), max(groups // 2, 1))),
                dma((max(levels, 1), max(groups // 2, 1))), dma((chips,)), dma((2, chips))]
    return out


def make_reduces(groups, chips, orders, partials, shards, scratch):
    levels = len(powers(groups))
    each = 2 + levels + 2 + 6
    out = []
    for i, (partial, shard) in enumerate(zip(partials, shards)):
        refs = scratch[i * each : (i + 1) * each]
        out.append(Reduce(groups, chips, orders[i], partial, shard, refs[0], refs[1], refs[2 : 2 + levels],
                          refs[2 + levels], refs[3 + levels], refs[4 + levels :]))
    return out


def reduce_kernel(groups, chips, orders, *refs):
    count = len(orders)
    enter(neighbours(groups, 2 * chips))
    for step in reduce_steps(make_reduces(groups, chips, orders, refs[:count], refs[count : 2 * count],
                                          refs[2 * count :])):
        step()


def reduce_call(groups, chips, partials, orders):
    count = len(partials)
    shapes = [p.shape + (p.dtype,) for p in partials]
    return pl.pallas_call(
        functools.partial(reduce_kernel, groups, chips, orders),
        out_shape=[jax.ShapeDtypeStruct(p.shape[3:], jnp.float32) for p in partials],
        in_specs=[pl.BlockSpec(memory_space=pl.ANY)] * count,
        out_specs=[pl.BlockSpec(memory_space=pltpu.VMEM)] * count,
        scratch_shapes=reduce_scratch(groups, chips, shapes),
        compiler_params=pltpu.CompilerParams(collective_id=3, has_side_effects=True, vmem_limit_bytes=64000000),
        name="reduce_gradients",
    )(*partials)


PARTS = 4
NEG = -1e30
EPS = 1e-05


def lanes(shape):
    return lax.broadcasted_iota(jnp.int32, shape, len(shape) - 1)


def swap_lanes(v):
    return pltpu.roll(v, 64, 1)


def fold(v, high):
    half = v.shape[0] // 2
    top, bottom = v[:half], v[half:]
    low = lanes(top.shape) < 64
    if high:
        return jnp.where(low, swap_lanes(top), bottom)
    return jnp.where(low, top, swap_lanes(bottom))


def unfold(v, high):
    low = lanes(v.shape) < 64
    zero = jnp.zeros_like(v)
    if high:
        return jnp.concatenate([jnp.where(low, zero, swap_lanes(v)), jnp.where(low, zero, v)], axis=0)
    return jnp.concatenate([jnp.where(low, v, zero), jnp.where(low, swap_lanes(v), zero)], axis=0)


def product(a, b):
    return lax.dot_general(a, b, (((1,), (0,)), ((), ())), preferred_element_type=jnp.float32)


def product_right(a, b):
    return lax.dot_general(a, b, (((1,), (1,)), ((), ())), preferred_element_type=jnp.float32)


def product_left(a, b):
    return lax.dot_general(a, b, (((0,), (0,)), ((), ())), preferred_element_type=jnp.float32)


def normal_rows(v):
    mean = jnp.mean(v, axis=-1, keepdims=True)
    centred = v - mean
    var = jnp.mean(centred * centred, axis=-1, keepdims=True)
    scale = lax.rsqrt(var + EPS)
    return centred * scale, scale


def pack_heads(v, splits, store):
    size = v.shape[0] // splits
    for tile in range(v.shape[1] // 128):
        for split in range(splits):
            part = v[split * size : (split + 1) * size, tile * 128 : (tile + 1) * 128]
            store(2 * tile, split, fold(part, False))
            store(2 * tile + 1, split, fold(part, True))


def slots_of(table, count):
    out = []
    for piece in range(count):
        slot = jnp.int32(0)
        for place in range(count):
            slot = slot + jnp.where(table[0, place] == piece, place, 0)
        out.append(jnp.minimum(slot, count - 1))
    return out


def pick(values, index):
    out = values[0]
    for i in range(1, len(values)):
        out = jnp.where(index == i, values[i], out)
    return out


class Exchange:
    def __init__(self, n):
        self.n = n
        self.splits = n // PARTS
        self.s = lax.axis_index("seq")
        self.part, self.split = self.s // self.splits, lax.rem(self.s, self.splits)

    def peers(self):
        return [{"seq": lax.rem(self.s + off, self.n)} for off in range(1, self.n)]

    def other(self, off):
        return lax.rem(self.s + off, self.n)

    def scatter(self, j, staged, landed, send, recv):
        out = []
        for off in range(1, self.n):
            t = self.other(off)
            out.append(remote(staged.at[t // self.splits, j, lax.rem(t, self.splits)], landed.at[j, self.s],
                              send.at[j, off - 1], recv.at[j, self.s], {"seq": t}))
        return out

    def own(self, j, staged, landed, recv):
        return pltpu.make_async_copy(staged.at[self.part, j, self.split], landed.at[j, self.s], recv.at[j, self.s])

    def spread(self, j, staged, landed, send, recv):
        out = []
        for off in range(1, PARTS):
            part = lax.rem(self.part + off, PARTS)
            out.append(remote(staged.at[part, j], landed.at[j, self.s], send.at[j, off - 1],
                              recv.at[j, self.s], {"seq": part * self.splits + self.split}))
        return out

    def own_rows(self, j, staged, landed, recv):
        return pltpu.make_async_copy(staged.at[self.part, j], landed.at[j, self.s], recv.at[j, self.s])

    def relay(self, j, off, landed, send, recv):
        slot = lax.rem(self.part + off, PARTS) * self.splits + self.split
        out = []
        for hop in range(1, self.splits):
            split = lax.rem(self.split + hop, self.splits)
            out.append(remote(landed.at[j, slot], landed.at[j, slot], send.at[j, off, hop - 1],
                              recv.at[j, slot], {"seq": self.part * self.splits + split}))
        return slot, out

    def give_back(self, j, heads, staged, landed, send, recv):
        out = []
        row = self.part * heads + j
        for off in range(1, self.n):
            t = self.other(off)
            out.append(remote(staged.at[j, t], landed.at[row, self.split], send.at[j, off - 1],
                              recv.at[j, self.s], {"seq": t}))
        return out

    def keep_own(self, j, heads, staged, landed, recv):
        return pltpu.make_async_copy(staged.at[j, self.s], landed.at[self.part * heads + j, self.split],
                                     recv.at[j, self.s])


def here(ref, sem):
    pltpu.make_async_copy(ref, ref, sem).wait()


def forward_kernel(
    n, heads, table, x, first, gain, shift, wq, bq, wk, wv, bv,
    hidden_out, q_all, kv_all, ol_all, back,
    q_staged, kv_staged, o_staged, q_work, kv_work,
    q_send, kv_send, relay_send, o_send, q_recv, kv_recv, o_recv,
):
    ex = Exchange(n)
    enter(ex.peers())
    splits = ex.splits
    rows, width = x.shape
    share = rows // splits
    half = n // 2
    fresh = wv.shape[1]
    normed, _ = normal_rows(x[...].astype(jnp.float32))
    hidden = (normed * gain[...].astype(jnp.float32) + shift[...].astype(jnp.float32)).astype(jnp.bfloat16)
    hidden_out[...] = hidden
    for step in range(width // 256):
        cols = slice(step * 256, (step + 1) * 256)
        q = product(hidden, wq[:, cols]) + bq[:, cols].astype(jnp.float32)

        def store(head, split, v, step=step):
            head = head + 4 * step
            q_staged[head // heads, head % heads, split] = (v * 0.125).astype(jnp.bfloat16)

        pack_heads(q, splits, store)
        k = product(hidden, wk[:, cols])
        for tile in range(2):
            at = step * 256 + tile * 128
            if at < fresh:
                v = product(hidden, wv[:, at : at + 128]) + bv[:, at : at + 128].astype(jnp.float32)
            else:
                v = first[:, at - fresh : at - fresh + 128].astype(jnp.float32)
            kt = k[:, tile * 128 : (tile + 1) * 128]
            low = lanes(kt.shape) < 64
            head = at // 64
            kv_staged[head // heads, head % heads] = jnp.where(low, kt, swap_lanes(v)).astype(jnp.bfloat16)
            head = head + 1
            kv_staged[head // heads, head % heads] = jnp.where(low, swap_lanes(kt), v).astype(jnp.bfloat16)

    @pl.loop(0, heads)
    def _(j):
        for copy in ex.spread(j, kv_staged, kv_all, kv_send, kv_recv):
            copy.start()
        for copy in ex.scatter(j, q_staged, q_all, q_send, q_recv):
            copy.start()
        ex.own(j, q_staged, q_all, q_recv).start()
        ex.own_rows(j, kv_staged, kv_all, kv_recv).start()

    slot = slots_of(table, n)
    row = lax.broadcasted_iota(jnp.int32, (share, rows), 0) + ex.split * share
    own_mask = lax.broadcasted_iota(jnp.int32, (share, rows), 1) <= row

    def piece(j, place, at, keys):
        q = unfold(q_work[at].astype(jnp.float32), False).astype(jnp.bfloat16)
        blocks = [kv_work[k] for k in keys] + [kv_work[at]]
        scores = [product_right(q, block) for block in blocks]
        scores[-1] = jnp.where(own_mask, scores[-1], NEG)
        top = scores[0]
        for s in scores[1:]:
            top = jnp.maximum(top, s)
        top = jnp.max(top, axis=1, keepdims=True)
        total = jnp.zeros((share, rows), jnp.float32)
        out = jnp.zeros((share, 128), jnp.float32)
        for s, block in zip(scores, blocks):
            weight = jnp.exp(s - top)
            total = total + weight
            out = out + product(weight.astype(jnp.bfloat16), block)
        denom = jnp.sum(total, axis=1, keepdims=True)
        out = out / denom
        ol_all[j, place] = jnp.where(lanes(out.shape) < 64, top + jnp.log(denom), out)

    @pl.loop(0, heads)
    def _(j):
        for off in range(PARTS):
            at, copies = ex.relay(j, off, kv_all, relay_send, kv_recv)
            here(kv_all.at[j, at], kv_recv.at[j, at])
            for copy in copies:
                copy.start()
        for t in range(n):
            here(q_all.at[j, t], q_recv.at[j, t])
        for off in range(PARTS):
            for hop in range(1, splits):
                at = lax.rem(ex.part + off, PARTS) * splits + lax.rem(ex.split + hop, splits)
                here(kv_all.at[j, at], kv_recv.at[j, at])
        for t in range(n):
            q_work[t] = q_all[j, t]
            kv_work[t] = kv_all[j, t]

        @pl.loop(0, half)
        def _(c):
            piece(j, half + c, pick(slot[half:], c), slot[:half])

        for p in range(half):
            piece(j, p, slot[p], slot[:p])
        for t in range(n):
            o_staged[j, t] = fold(ol_all[j, table[0, t]], True).astype(jnp.bfloat16)
        for copy in ex.give_back(j, heads, o_staged, back, o_send, o_recv):
            copy.start()
        ex.keep_own(j, heads, o_staged, back, o_recv).start()

    @pl.loop(0, heads)
    def _(j):
        for copy in ex.spread(j, kv_staged, kv_all, kv_send, kv_recv):
            copy.wait_send()
        for copy in ex.scatter(j, q_staged, q_all, q_send, q_recv):
            copy.wait_send()
        for off in range(PARTS):
            for copy in ex.relay(j, off, kv_all, relay_send, kv_recv)[1]:
                copy.wait_send()
        for copy in ex.give_back(j, heads, o_staged, back, o_send, o_recv):
            copy.wait_send()
        for t in range(n):
            landed = back.at[t // splits * heads + j, t % splits]
            here(landed, o_recv.at[j, t])


def forward_call(n, table, x, first, gain, shift, wq, bq, wk, wv, bv):
    rows, width = x.shape
    splits = n // PARTS
    heads = width // 64 // PARTS
    share = rows // splits
    low = jnp.bfloat16
    vmem, dma = pltpu.VMEM, pltpu.SemaphoreType.DMA
    inside = pl.BlockSpec(memory_space=vmem)
    shape = jax.ShapeDtypeStruct
    return pl.pallas_call(
        functools.partial(forward_kernel, n, heads),
        out_shape=[
            shape((rows, width), low),
            shape((heads, n, share // 2, 128), low),
            shape((heads, n, rows, 128), low),
            shape((heads, n, share, 128), jnp.float32),
            shape((PARTS * heads, splits, share // 2, 128), low),
        ],
        in_specs=[pl.BlockSpec(memory_space=pltpu.SMEM)] + [inside] * 9,
        out_specs=[inside] * 5,
        scratch_shapes=[
            vmem((PARTS, heads, splits, share // 2, 128), low),
            vmem((PARTS, heads, rows, 128), low),
            vmem((heads, n, share // 2, 128), low),
            vmem((n, share // 2, 128), low),
            vmem((n, rows, 128), low),
            dma((heads, n - 1)),
            dma((heads, PARTS - 1)),
            dma((heads, PARTS, max(splits - 1, 1))),
            dma((heads, n - 1)),
            dma((heads, n)),
            dma((heads, n)),
            dma((heads, n)),
        ],
        compiler_params=pltpu.CompilerParams(
            collective_id=1, has_side_effects=True, vmem_limit_bytes=64000000
        ),
        name="attention_forward",
    )(table, x, first, gain, shift, wq, bq, wk, wv, bv)


def backward_kernel(
    n, heads, table, do_in, q_all, kv_all, ol_all,
    dq_back, dkv_back,
    do_all, do_work, acc, dq_piece, dq_staged, part_staged, part_all, dkv_staged,
    do_send, do_recv, dq_send, dq_recv, part_send, part_recv, dkv_send, dkv_recv,
):
    ex = Exchange(n)
    enter(ex.peers())
    splits = ex.splits
    rows = kv_all.shape[2]
    share = rows // splits
    half = n // 2

    @pl.loop(0, heads)
    def _(j):
        for copy in ex.scatter(j, do_in, do_all, do_send, do_recv):
            copy.start()
        ex.own(j, do_in, do_all, do_recv).start()

    slot = slots_of(table, n)
    column = lax.broadcasted_iota(jnp.int32, (rows, share), 1) + ex.split * share
    own_mask = lax.broadcasted_iota(jnp.int32, (rows, share), 0) <= column

    def piece(j, place, at, keys):
        q = unfold(q_all[j, at].astype(jnp.float32), False).astype(jnp.bfloat16)
        grad = unfold(do_work[at].astype(jnp.float32), True)
        ol = ol_all[j, place]
        delta = jnp.sum(jnp.transpose(grad * ol), axis=0, keepdims=True)
        logsum = jnp.transpose(ol)[0:1]
        grad = grad.astype(jnp.bfloat16)
        dq = jnp.zeros((128, share), jnp.float32)
        for where, (key_place, key_slot) in enumerate(keys + [(place, at)]):
            block = kv_all[j, key_slot]
            weight = jnp.exp(product_right(block, q) - logsum)
            if where == len(keys):
                weight = jnp.where(own_mask, weight, 0.0)
            change = (weight * (product_right(block, grad) - delta)).astype(jnp.bfloat16)
            term = product(weight.astype(jnp.bfloat16), grad) + product(change, q)
            acc[key_place] = acc[key_place] + term
            dq = dq + product_left(block, change)
        dq_piece[place] = fold(jnp.transpose(dq) * 0.125, False).astype(jnp.bfloat16)

    def part_copies(j):
        out = []
        for hop in range(1, splits):
            split = lax.rem(ex.split + hop, splits)
            for part in range(PARTS):
                out.append(remote(part_staged.at[j, split, part], part_all.at[j, ex.split, part],
                                  part_send.at[j, split, part], part_recv.at[j, ex.split, part],
                                  {"seq": ex.part * splits + split}))
        return out

    def back_copies(j):
        out = []
        row = ex.part * heads + j
        for off in range(1, PARTS):
            part = lax.rem(ex.part + off, PARTS)
            out.append(remote(dkv_staged.at[j, part], dkv_back.at[row], dkv_send.at[j, off - 1],
                              dkv_recv.at[j, ex.part], {"seq": part * splits + ex.split}))
        return out

    @pl.loop(0, heads)
    def _(j):
        for t in range(n):
            here(do_all.at[j, t], do_recv.at[j, t])
        for t in range(n):
            do_work[t] = do_all[j, t]
            acc[t] = jnp.zeros((rows, 128), jnp.float32)

        @pl.loop(0, half)
        def _(c):
            piece(j, half + c, pick(slot[half:], c), [(p, slot[p]) for p in range(half)])

        for p in range(half):
            piece(j, p, slot[p], [(k, slot[k]) for k in range(p)])
        for hop in range(1, splits):
            split = lax.rem(ex.split + hop, splits)
            for part in range(PARTS):
                part_staged[j, split, part] = acc[table[0, part * splits + split]].astype(jnp.bfloat16)
        for copy in part_copies(j):
            copy.start()
        for t in range(n):
            dq_staged[j, t] = dq_piece[table[0, t]]
        for hop in range(1, splits):
            split = lax.rem(ex.split + hop, splits)
            for part in range(PARTS):
                here(part_all.at[j, split, part], part_recv.at[j, split, part])
        for part in range(PARTS):
            total = acc[table[0, part * splits + ex.split]]
            for hop in range(1, splits):
                total = total + part_all[j, lax.rem(ex.split + hop, splits), part].astype(jnp.float32)
            dkv_staged[j, part] = total.astype(jnp.bfloat16)
        for copy in back_copies(j):
            copy.start()
        pltpu.make_async_copy(dkv_staged.at[j, ex.part], dkv_back.at[ex.part * heads + j],
                              dkv_recv.at[j, ex.part]).start()
        for copy in ex.give_back(j, heads, dq_staged, dq_back, dq_send, dq_recv):
            copy.start()
        ex.keep_own(j, heads, dq_staged, dq_back, dq_recv).start()

    @pl.loop(0, heads)
    def _(j):
        for copy in ex.scatter(j, do_in, do_all, do_send, do_recv):
            copy.wait_send()
        for copy in part_copies(j):
            copy.wait_send()
        for copy in back_copies(j):
            copy.wait_send()
        for copy in ex.give_back(j, heads, dq_staged, dq_back, dq_send, dq_recv):
            copy.wait_send()
        for t in range(n):
            here(dq_back.at[t // splits * heads + j, t % splits], dq_recv.at[j, t])
        for part in range(PARTS):
            here(dkv_back.at[part * heads + j], dkv_recv.at[j, part])


def backward_call(n, table, do_in, q_all, kv_all, ol_all):
    heads, _, rows, _ = kv_all.shape
    splits = n // PARTS
    share = rows // splits
    low = jnp.bfloat16
    vmem, dma = pltpu.VMEM, pltpu.SemaphoreType.DMA
    inside = pl.BlockSpec(memory_space=vmem)
    shape = jax.ShapeDtypeStruct
    return pl.pallas_call(
        functools.partial(backward_kernel, n, heads),
        out_shape=[
            shape((PARTS * heads, splits, share // 2, 128), low),
            shape((PARTS * heads, rows, 128), low),
        ],
        in_specs=[pl.BlockSpec(memory_space=pltpu.SMEM)] + [inside] * 4,
        out_specs=[inside] * 2,
        scratch_shapes=[
            vmem((heads, n, share // 2, 128), low),
            vmem((n, share // 2, 128), low),
            vmem((n, rows, 128), jnp.float32),
            vmem((n, share // 2, 128), low),
            vmem((heads, n, share // 2, 128), low),
            vmem((heads, splits, PARTS, rows, 128), low),
            vmem((heads, splits, PARTS, rows, 128), low),
            vmem((heads, PARTS, rows, 128), low),
            dma((heads, n - 1)),
            dma((heads, n)),
            dma((heads, n - 1)),
            dma((heads, n)),
            dma((heads, splits, PARTS)),
            dma((heads, splits, PARTS)),
            dma((heads, PARTS - 1)),
            dma((heads, PARTS)),
        ],
        compiler_params=pltpu.CompilerParams(
            collective_id=2, has_side_effects=True, vmem_limit_bytes=64000000
        ),
        name="attention_backward",
    )(table, do_in, q_all, kv_all, ol_all)


def collect(parts):
    groups = lax.axis_size("grp")
    n = lax.axis_size("seq")
    small = (0, 1, 3, 6, 8, 9, 10, 12, 14)
    packed = jnp.concatenate([parts[i] for i in small])
    sizes = [parts[i].shape[0] for i in small]
    length = packed.shape[0]
    packed = jnp.pad(packed, (0, 2048 - length)).reshape(16, 128)
    bits = powers(groups)
    forth, back = bits, bits[::-1]
    shards = [packed, parts[2], parts[5], parts[4], parts[7], parts[11], parts[13]]
    fulls = gather_call(groups, n // 2, shards, [forth, forth, forth, back, back, forth, back])
    flat = fulls[0].reshape(groups * n, 2048)
    whole = [None] * 15
    at = 0
    for i, size in zip(small, sizes):
        whole[i] = flat[:, at : at + size].reshape(groups * n * size)
        at += size
    for i, full in zip((2, 5, 4, 7, 11, 13), fulls[1:]):
        whole[i] = full.reshape(-1, full.shape[-1])
    return tuple(whole)


def normalize(v, gain, shift):
    mean = jnp.mean(v, axis=-1, keepdims=True)
    centred = v - mean
    var = jnp.mean(centred * centred, axis=-1, keepdims=True)
    return centred * lax.rsqrt(var + EPS) * gain + shift


def gelu_tanh(v):
    return jax.nn.gelu(v, approximate=True)


def unpack_rows(v):
    heads, splits, size, _ = v.shape
    v = v.reshape(heads, splits, size, 2, 64)
    return jnp.transpose(v, (1, 3, 2, 0, 4)).reshape(splits * 2 * size, heads * 64)


def pack_rows(v, splits):
    rows, width = v.shape
    heads = width // 64
    v = v.reshape(splits, 2, rows // splits // 2, heads, 64)
    v = jnp.transpose(v, (3, 0, 2, 1, 4))
    return v.reshape(PARTS, heads // PARTS, splits, rows // splits // 2, 128)


def body(
    tokens,
    first_values,
    placement,
    cotangent,
    *parts,
):
    groups, rows, width = tokens.shape
    n = lax.axis_size("seq")
    splits = n // PARTS
    whole = collect(parts)
    gain_one = whole[0].astype(jnp.float32)
    bias_one = whole[1].astype(jnp.float32)
    gain_two = whole[9].astype(jnp.float32)
    bias_two = whole[10].astype(jnp.float32)
    hidden, q_all, kv_all, ol_all, back = forward_call(
        n, placement, tokens[0], first_values[0], whole[0][None], whole[1][None],
        whole[2], whole[3][None], whole[4], whole[5], whole[6][None],
    )
    attended_low = unpack_rows(back)
    flat = tokens[0].astype(jnp.float32)
    middle = flat + product(attended_low, whole[7]) + whole[8].astype(jnp.float32)
    normed_two, norm_two_back = jax.vjp(normalize, middle, gain_two, bias_two)
    second = normed_two.astype(jnp.bfloat16)
    pre = product(second, whole[11]) + whole[12].astype(jnp.float32)
    post_full, gelu_back = jax.vjp(gelu_tanh, pre)
    post = post_full.astype(jnp.bfloat16)
    result = middle + product(post, whole[13]) + whole[14].astype(jnp.float32)
    layer_output = result.astype(jnp.bfloat16)[None]
    seed = cotangent[0]
    seed_full = seed.astype(jnp.float32)
    grad_reduce_bias = jnp.sum(seed_full, axis=0)
    grad_reduce = product_left(post, seed)
    grad_post = product_right(seed, whole[13])
    grad_pre = gelu_back(grad_post)[0].astype(jnp.bfloat16)
    grad_expand_bias = jnp.sum(grad_pre.astype(jnp.float32), axis=0)
    grad_expand = product_left(second, grad_pre)
    grad_second = product_right(grad_pre, whole[11])
    grad_mid_norm, grad_gain_two, grad_bias_two = norm_two_back(grad_second)
    grad_mid = grad_mid_norm + seed_full
    grad_branch = grad_mid.astype(jnp.bfloat16)
    grad_output_bias = jnp.sum(grad_branch.astype(jnp.float32), axis=0)
    grad_output = product_left(attended_low, grad_branch)
    grad_attended = product_right(grad_branch, whole[7]).astype(jnp.bfloat16)
    dq_back, dkv_back = backward_call(n, placement, pack_rows(grad_attended, splits), q_all, kv_all, ol_all)
    grad_query_all = unpack_rows(dq_back)
    heads = width // 64
    pair = jnp.transpose(dkv_back.reshape(heads, rows, 2, 64), (2, 1, 0, 3)).reshape(2, rows, width)
    fresh_width = whole[5].shape[1]
    grad_key, grad_fresh = pair[0], pair[1][:, :fresh_width]
    first_values_grad = pair[1][:, fresh_width:].astype(jnp.float32)[None]
    grad_query_bias = jnp.sum(grad_query_all.astype(jnp.float32), axis=0)
    grad_query_weight = product_left(hidden, grad_query_all)
    grad_key_weight = product_left(hidden, grad_key)
    grad_value_weight = product_left(hidden, grad_fresh)
    grad_value_bias = jnp.sum(grad_fresh.astype(jnp.float32), axis=0)
    grad_hidden = (
        product_right(grad_query_all, whole[2])
        + product_right(grad_key, whole[4])
        + product_right(grad_fresh, whole[5])
    )
    _, norm_one_back = jax.vjp(normalize, flat, gain_one, bias_one)
    grad_in, grad_gain_one, grad_bias_one = norm_one_back(grad_hidden)
    token_grad = (grad_in + grad_mid)[None]
    owned = reduce_gradients((
        grad_gain_one, grad_bias_one, grad_query_weight, grad_query_bias, grad_key_weight,
        grad_value_weight, grad_value_bias, grad_output, grad_output_bias, grad_gain_two, grad_bias_two,
        grad_expand, grad_expand_bias, grad_reduce, grad_reduce_bias,
    ))
    return (layer_output, token_grad, first_values_grad) + owned


def reduce_gradients(grads):
    groups = lax.axis_size("grp")
    n = lax.axis_size("seq")
    chips = n // 2
    small = (0, 1, 3, 6, 8, 9, 10, 12, 14)
    large = (11, 13, 7, 4, 2, 5)
    sizes = [grads[i].shape[0] // (groups * n) for i in small]
    packed = jnp.concatenate([grads[i].reshape(groups * n, -1) for i in small], axis=1)
    packed = jnp.pad(packed, ((0, 0), (0, 1024 - packed.shape[1]))).reshape(groups, chips, 2, 8, 128)
    bits = powers(groups)
    forth, back = bits, bits[::-1]
    partials = [grads[i].astype(jnp.bfloat16).reshape(groups, chips, 2, -1, grads[i].shape[1]) for i in large]
    shards = reduce_call(groups, chips, partials + [packed], [forth, back, forth, back, forth, back, forth])
    out = [None] * 15
    for i, shard in zip(large, shards):
        out[i] = shard
    flat = shards[-1].reshape(1024)
    at = 0
    for i, size in zip(small, sizes):
        out[i] = flat[at : at + size]
        at += size
    return tuple(out)


def solution(mesh):
    spread = P("grp", "seq", None)
    both = ("grp", "seq")
    vector, matrix = P(both), P(both, None)
    kinds = (vector, vector, matrix, vector, matrix, matrix, vector, matrix, vector, vector, vector,
             matrix, vector, matrix, vector)
    in_specs = (spread, spread, P("grp", None), spread) + kinds
    out_specs = (spread, spread, spread) + kinds
    return jax.shard_map(body, mesh=mesh, in_specs=in_specs, out_specs=out_specs, check_vma=False)
```

```python
import functools

import jax
import jax.numpy as jnp
from jax import lax
from jax.experimental import pallas as pl
from jax.experimental.pallas import tpu as pltpu
from jax.sharding import PartitionSpec as P

MESH = pl.DeviceIdType.MESH


def powers(count):
    out, bit = [], 1
    while bit < count:
        out.append(bit)
        bit *= 2
    return out


def remote(src, dst, send, recv, device):
    return pltpu.make_async_remote_copy(
        src_ref=src, dst_ref=dst, send_sem=send, recv_sem=recv,
        device_id=device, device_id_type=MESH,
    )


def enter(devices):
    barrier = pltpu.get_barrier_semaphore()
    for device in devices:
        pl.semaphore_signal(barrier, inc=1, device_id=device, device_id_type=MESH)
    pl.semaphore_wait(barrier, len(devices))


class Gather:
    def __init__(self, groups, chips, bits, shard, full, chain_send, level_send, recv, pair, own):
        self.groups, self.chips, self.bits = groups, chips, bits
        self.shard, self.full = shard, full
        self.chain_send, self.level_send, self.recv, self.pair, self.own = chain_send, level_send, recv, pair, own
        self.g = lax.axis_index("grp")
        seq = lax.axis_index("seq")
        self.s, self.z, self.c = seq, seq // 2, seq % 2

    def block(self, g, z, c):
        return self.full.at[g, z, c]

    def source(self, mask, z, first):
        return self.shard if first else self.block(self.g ^ mask, z, self.c)

    def chain(self, z, step, first):
        side = 0 if step < 0 else 1
        return remote(self.source(0, z, first), self.block(self.g, z, self.c),
                      self.chain_send.at[z, side], self.recv.at[self.g, z],
                      {"seq": self.s + 2 * step})

    def cross(self, level, mask, z, first):
        g = self.g ^ mask
        return remote(self.source(mask, z, first), self.block(g, z, self.c),
                      self.level_send.at[level], self.recv.at[g, z],
                      {"grp": self.g ^ self.bits[level]})

    def held(self, level):
        masks = [0]
        for bit in self.bits[:level]:
            masks = masks + [m ^ bit for m in masks]
        return masks

    def here(self, mask, z):
        g = self.g ^ mask
        pltpu.make_async_copy(self.block(g, z, self.c), self.block(g, z, self.c), self.recv.at[g, z]).wait()

    def begin(self):
        copy = pltpu.make_async_copy(self.shard, self.block(self.g, self.z, self.c), self.own)
        copy.start()

        @pl.when(self.z > 0)
        def _():
            self.chain(self.z, -1, True).start()

        @pl.when(self.z < self.chips - 1)
        def _():
            self.chain(self.z, 1, True).start()

        for level in range(len(self.bits)):
            self.cross(level, 0, self.z, True).start()

    def at(self, distance, body):
        if distance == 0:
            body(self.z, 0)
            return

        @pl.when(self.z >= distance)
        def _():
            body(self.z - distance, 1)

        @pl.when(self.z + distance < self.chips)
        def _():
            body(self.z + distance, -1)

    def along(self, distance):
        def body(z, step):
            self.here(0, z)
            onward = self.z < self.chips - 1 if step > 0 else self.z > 0

            @pl.when(onward)
            def _():
                self.chain(z, step, False).start()

            for level in range(len(self.bits)):
                self.cross(level, 0, z, False).start()

        if distance > 0:
            self.at(distance, body)

    def over(self, level, distance):
        def body(z, step):
            for mask in self.held(level):
                mask = mask ^ self.bits[level]
                self.here(mask, z)
                for later in range(level + 1, len(self.bits)):
                    self.cross(later, mask, z, False).start()

        self.at(distance, body)

    def swap_copy(self):
        mine = self.full.at[:, :, self.c]
        return remote(mine, mine, self.pair.at[0], self.pair.at[1], {"seq": self.s ^ 1})

    def swap(self):
        pltpu.make_async_copy(self.shard, self.shard, self.own).wait()
        self.swap_copy().start()

    def finish(self):
        self.swap_copy().wait_send()
        other = self.full.at[:, :, 1 - self.c]
        pltpu.make_async_copy(other, other, self.pair.at[1]).wait()

        @pl.when(self.z > 0)
        def _():
            self.chain(self.z, -1, True).wait_send()

        @pl.when(self.z < self.chips - 1)
        def _():
            self.chain(self.z, 1, True).wait_send()

        for distance in range(1, self.chips):
            def body(z, step):
                onward = self.z < self.chips - 1 if step > 0 else self.z > 0

                @pl.when(onward)
                def _():
                    self.chain(z, step, False).wait_send()

            self.at(distance, body)
        for level in range(len(self.bits)):
            sent = self.full.at[pl.ds(0, 2 ** level), :, 0]
            pltpu.make_async_copy(sent, sent, self.level_send.at[level]).wait()


def gather_semaphores(count, groups, chips):
    dma = pltpu.SemaphoreType.DMA
    levels = max(len(powers(groups)), 1)
    return [dma((count, chips, 2)), dma((count, levels)), dma((count, groups, chips)), dma((count, 2)), dma((count,))]


def neighbours(groups, n):
    g, s = lax.axis_index("grp"), lax.axis_index("seq")
    out = [{"grp": g ^ bit} for bit in powers(groups)]
    out += [{"seq": s ^ 1}, {"seq": lax.rem(s + 2, n)}, {"seq": lax.rem(s + n - 2, n)}]
    return out


def gather_kernel(groups, chips, orders, *refs):
    count = len(orders)
    shards, fulls, sems = refs[:count], refs[count:2 * count], refs[2 * count:]
    enter(neighbours(groups, 2 * chips))
    gathers = [Gather(groups, chips, orders[i], shards[i], fulls[i], *[s.at[i] for s in sems]) for i in range(count)]
    run_gathers(gathers)


def run_gathers(gathers):
    chips, levels = gathers[0].chips, len(gathers[0].bits)
    for g in gathers:
        g.begin()
    for distance in range(chips + levels):
        for g in gathers:
            if distance + 1 < chips:
                g.along(distance + 1)
            for level in range(levels):
                if 0 <= distance - level < chips:
                    g.over(level, distance - level)
    for g in gathers:
        g.swap()
    for g in gathers:
        g.finish()


def gather_call(groups, chips, shards, orders):
    count = len(shards)
    return pl.pallas_call(
        functools.partial(gather_kernel, groups, chips, orders),
        out_shape=[jax.ShapeDtypeStruct((groups, chips, 2) + x.shape, x.dtype) for x in shards],
        in_specs=[pl.BlockSpec(memory_space=pl.ANY)] * count,
        out_specs=[pl.BlockSpec(memory_space=pl.ANY)] * count,
        scratch_shapes=gather_semaphores(count, groups, chips),
        compiler_params=pltpu.CompilerParams(collective_id=0, has_side_effects=True),
        name="gather_parameters",
    )(*shards)


class Reduce:
    def __init__(self, groups, chips, bits, partial, shard, own, landed, halves, finals, sems):
        self.groups, self.chips, self.bits = groups, chips, bits
        self.partial, self.shard, self.own, self.landed = partial, shard, own, landed
        self.halves, self.finals = halves, finals
        self.load, self.pair, self.level_send, self.level_recv, self.chip_send, self.chip_recv = sems
        self.g = lax.axis_index("grp")
        self.s = lax.axis_index("seq")
        self.z, self.c = self.s // 2, self.s % 2

    def masks(self, level):
        out = [0]
        for bit in self.bits[level:]:
            out = out + [m ^ bit for m in out]
        return out

    def load_copy(self):
        return pltpu.make_async_copy(self.partial.at[:, :, self.c], self.own, self.load.at[0])

    def pair_copy(self):
        return remote(self.partial.at[:, :, 1 - self.c], self.landed, self.pair.at[0], self.pair.at[1],
                      {"seq": self.s ^ 1})

    def begin(self):
        self.pair_copy().start()
        self.load_copy().start()

    def paired(self):
        self.load_copy().wait()
        self.pair_copy().wait_recv()

        @pl.loop(0, self.groups)
        def _(g):
            self.own[g] = self.add(self.own[g], self.landed[g])

        self.cross_start(0)

    def add(self, a, b):
        return a + b

    def cross_copies(self, level):
        bit = self.bits[level]
        out = []
        for where, mask in enumerate(self.masks(level + 1)):
            out.append(remote(self.own.at[self.g ^ bit ^ mask], self.halves[level].at[where],
                              self.level_send.at[level, where], self.level_recv.at[level, where],
                              {"grp": self.g ^ bit}))
        return out

    def cross_start(self, level):
        if level < len(self.bits):
            for copy in self.cross_copies(level):
                copy.start()
        else:
            for copy in self.chip_copies():
                copy.start()

    def crossed(self, level):
        copies = self.cross_copies(level)
        for where, mask in enumerate(self.masks(level + 1)):
            copies[where].wait_recv()
            g = self.g ^ mask
            self.own[g] = self.add(self.own[g], self.halves[level][where])
        self.cross_start(level + 1)

    def chip_copies(self):
        out = []
        for off in range(1, self.chips):
            chip = lax.rem(self.z + off, self.chips)
            out.append(remote(self.own.at[self.g, chip], self.finals.at[off - 1], self.chip_send.at[off - 1],
                              self.chip_recv.at[off - 1], {"seq": 2 * chip + self.c}))
        return out

    def finish(self):
        total = self.own[self.g, self.z].astype(jnp.float32)
        for off, copy in enumerate(self.chip_copies()):
            copy.wait_recv()
            total = total + self.finals[off].astype(jnp.float32)
        self.shard[...] = total

    def drain(self):
        self.pair_copy().wait_send()
        for level in range(len(self.bits)):
            for copy in self.cross_copies(level):
                copy.wait_send()
        for copy in self.chip_copies():
            copy.wait_send()


def reduce_steps(reduces):
    levels = len(reduces[0].bits)
    stages = [lambda r: r.begin(), lambda r: r.paired()]
    for level in range(levels):
        stages.append(lambda r, level=level: r.crossed(level))
    stages += [lambda r: r.finish(), lambda r: r.drain()]
    return [functools.partial(stage, r) for stage in stages for r in reduces]


def reduce_scratch(groups, chips, shapes):
    vmem, dma = pltpu.VMEM, pltpu.SemaphoreType.DMA
    levels = len(powers(groups))
    out = []
    for _, _, _, rows, cols, dtype in shapes:
        out += [vmem((groups, chips, rows, cols), dtype), vmem((groups, chips, rows, cols), dtype)]
        out += [vmem((groups >> (level + 1), chips, rows, cols), dtype) for level in range(levels)]
        out += [vmem((max(chips - 1, 1), rows, cols), dtype)]
        out += [dma((1,)), dma((2,)), dma((max(levels, 1), max(groups // 2, 1))),
                dma((max(levels, 1), max(groups // 2, 1))), dma((max(chips - 1, 1),)),
                dma((max(chips - 1, 1),))]
    return out


def make_reduces(groups, chips, orders, partials, shards, scratch):
    levels = len(powers(groups))
    each = 2 + levels + 1 + 6
    out = []
    for i, (partial, shard) in enumerate(zip(partials, shards)):
        refs = scratch[i * each : (i + 1) * each]
        out.append(Reduce(groups, chips, orders[i], partial, shard, refs[0], refs[1], refs[2 : 2 + levels],
                          refs[2 + levels], refs[3 + levels :]))
    return out


def reduce_kernel(groups, chips, orders, *refs):
    count = len(orders)
    enter(neighbours(groups, 2 * chips))
    for step in reduce_steps(make_reduces(groups, chips, orders, refs[:count], refs[count : 2 * count],
                                          refs[2 * count :])):
        step()


def reduce_call(groups, chips, partials, orders):
    count = len(partials)
    shapes = [p.shape + (p.dtype,) for p in partials]
    return pl.pallas_call(
        functools.partial(reduce_kernel, groups, chips, orders),
        out_shape=[jax.ShapeDtypeStruct(p.shape[3:], jnp.float32) for p in partials],
        in_specs=[pl.BlockSpec(memory_space=pl.ANY)] * count,
        out_specs=[pl.BlockSpec(memory_space=pltpu.VMEM)] * count,
        scratch_shapes=reduce_scratch(groups, chips, shapes),
        compiler_params=pltpu.CompilerParams(collective_id=3, has_side_effects=True, vmem_limit_bytes=64000000),
        name="reduce_gradients",
    )(*partials)


PARTS = 4
NEG = -1e30
EPS = 1e-05


def lanes(shape):
    return lax.broadcasted_iota(jnp.int32, shape, len(shape) - 1)


def swap_lanes(v):
    return pltpu.roll(v, 64, 1)


def fold(v, high):
    half = v.shape[0] // 2
    top, bottom = v[:half], v[half:]
    low = lanes(top.shape) < 64
    if high:
        return jnp.where(low, swap_lanes(top), bottom)
    return jnp.where(low, top, swap_lanes(bottom))


def unfold(v, high):
    low = lanes(v.shape) < 64
    zero = jnp.zeros_like(v)
    if high:
        return jnp.concatenate([jnp.where(low, zero, swap_lanes(v)), jnp.where(low, zero, v)], axis=0)
    return jnp.concatenate([jnp.where(low, v, zero), jnp.where(low, swap_lanes(v), zero)], axis=0)


def product(a, b):
    return lax.dot_general(a, b, (((1,), (0,)), ((), ())), preferred_element_type=jnp.float32)


def product_right(a, b):
    return lax.dot_general(a, b, (((1,), (1,)), ((), ())), preferred_element_type=jnp.float32)


def product_left(a, b):
    return lax.dot_general(a, b, (((0,), (0,)), ((), ())), preferred_element_type=jnp.float32)


def normal_rows(v):
    mean = jnp.mean(v, axis=-1, keepdims=True)
    centred = v - mean
    var = jnp.mean(centred * centred, axis=-1, keepdims=True)
    scale = lax.rsqrt(var + EPS)
    return centred * scale, scale


def pack_heads(v, splits, store):
    size = v.shape[0] // splits
    for tile in range(v.shape[1] // 128):
        for split in range(splits):
            part = v[split * size : (split + 1) * size, tile * 128 : (tile + 1) * 128]
            store(2 * tile, split, fold(part, False))
            store(2 * tile + 1, split, fold(part, True))


def slots_of(table, count):
    out = []
    for piece in range(count):
        slot = jnp.int32(0)
        for place in range(count):
            slot = slot + jnp.where(table[0, place] == piece, place, 0)
        out.append(jnp.minimum(slot, count - 1))
    return out


def pick(values, index):
    out = values[0]
    for i in range(1, len(values)):
        out = jnp.where(index == i, values[i], out)
    return out


class Exchange:
    def __init__(self, n):
        self.n = n
        self.splits = n // PARTS
        self.s = lax.axis_index("seq")
        self.part, self.split = self.s // self.splits, lax.rem(self.s, self.splits)

    def peers(self):
        return [{"seq": lax.rem(self.s + off, self.n)} for off in range(1, self.n)]

    def other(self, off):
        return lax.rem(self.s + off, self.n)

    def scatter(self, j, staged, landed, send, recv):
        out = []
        for off in range(1, self.n):
            t = self.other(off)
            out.append(remote(staged.at[t // self.splits, j, lax.rem(t, self.splits)], landed.at[j, self.s],
                              send.at[j, off - 1], recv.at[j, self.s], {"seq": t}))
        return out

    def own(self, j, staged, landed, recv):
        return pltpu.make_async_copy(staged.at[self.part, j, self.split], landed.at[j, self.s], recv.at[j, self.s])

    def spread(self, j, staged, landed, send, recv):
        out = []
        for off in range(1, PARTS):
            part = lax.rem(self.part + off, PARTS)
            out.append(remote(staged.at[part, j], landed.at[j, self.s], send.at[j, off - 1],
                              recv.at[j, self.s], {"seq": part * self.splits + self.split}))
        return out

    def own_rows(self, j, staged, landed, recv):
        return pltpu.make_async_copy(staged.at[self.part, j], landed.at[j, self.s], recv.at[j, self.s])

    def relay(self, j, off, landed, send, recv):
        slot = lax.rem(self.part + off, PARTS) * self.splits + self.split
        out = []
        for hop in range(1, self.splits):
            split = lax.rem(self.split + hop, self.splits)
            out.append(remote(landed.at[j, slot], landed.at[j, slot], send.at[j, off, hop - 1],
                              recv.at[j, slot], {"seq": self.part * self.splits + split}))
        return slot, out

    def give_back(self, j, heads, staged, landed, send, recv):
        out = []
        row = self.part * heads + j
        for off in range(1, self.n):
            t = self.other(off)
            out.append(remote(staged.at[j, t], landed.at[row, self.split], send.at[j, off - 1],
                              recv.at[j, self.s], {"seq": t}))
        return out

    def keep_own(self, j, heads, staged, landed, recv):
        return pltpu.make_async_copy(staged.at[j, self.s], landed.at[self.part * heads + j, self.split],
                                     recv.at[j, self.s])


def here(ref, sem):
    pltpu.make_async_copy(ref, ref, sem).wait()


def forward_kernel(
    n, heads, table, x, first, gain, shift, wq, bq, wk, wv, bv,
    hidden_out, q_all, kv_all, ol_all, back,
    q_staged, kv_staged, o_staged, q_work, kv_work,
    q_send, kv_send, relay_send, o_send, q_recv, kv_recv, o_recv,
):
    ex = Exchange(n)
    enter(ex.peers())
    splits = ex.splits
    rows, width = x.shape
    share = rows // splits
    half = n // 2
    fresh = wv.shape[1]
    normed, _ = normal_rows(x[...].astype(jnp.float32))
    hidden = (normed * gain[...].astype(jnp.float32) + shift[...].astype(jnp.float32)).astype(jnp.bfloat16)
    hidden_out[...] = hidden
    for step in range(width // 256):
        cols = slice(step * 256, (step + 1) * 256)
        q = product(hidden, wq[:, cols]) + bq[:, cols].astype(jnp.float32)

        def store(head, split, v, step=step):
            head = head + 4 * step
            q_staged[head // heads, head % heads, split] = (v * 0.125).astype(jnp.bfloat16)

        pack_heads(q, splits, store)
        k = product(hidden, wk[:, cols])
        for tile in range(2):
            at = step * 256 + tile * 128
            if at < fresh:
                v = product(hidden, wv[:, at : at + 128]) + bv[:, at : at + 128].astype(jnp.float32)
            else:
                v = first[:, at - fresh : at - fresh + 128].astype(jnp.float32)
            kt = k[:, tile * 128 : (tile + 1) * 128]
            low = lanes(kt.shape) < 64
            head = at // 64
            kv_staged[head // heads, head % heads] = jnp.where(low, kt, swap_lanes(v)).astype(jnp.bfloat16)
            head = head + 1
            kv_staged[head // heads, head % heads] = jnp.where(low, swap_lanes(kt), v).astype(jnp.bfloat16)

    @pl.loop(0, heads)
    def _(j):
        for copy in ex.spread(j, kv_staged, kv_all, kv_send, kv_recv):
            copy.start()
        for copy in ex.scatter(j, q_staged, q_all, q_send, q_recv):
            copy.start()
        ex.own(j, q_staged, q_all, q_recv).start()
        ex.own_rows(j, kv_staged, kv_all, kv_recv).start()

    slot = slots_of(table, n)
    row = lax.broadcasted_iota(jnp.int32, (share, rows), 0) + ex.split * share
    own_mask = lax.broadcasted_iota(jnp.int32, (share, rows), 1) <= row

    def piece(j, place, at, keys):
        q = unfold(q_work[at].astype(jnp.float32), False).astype(jnp.bfloat16)
        blocks = [kv_work[k] for k in keys] + [kv_work[at]]
        scores = [product_right(q, block) for block in blocks]
        scores[-1] = jnp.where(own_mask, scores[-1], NEG)
        top = scores[0]
        for s in scores[1:]:
            top = jnp.maximum(top, s)
        top = jnp.max(top, axis=1, keepdims=True)
        total = jnp.zeros((share, rows), jnp.float32)
        out = jnp.zeros((share, 128), jnp.float32)
        for s, block in zip(scores, blocks):
            weight = jnp.exp(s - top)
            total = total + weight
            out = out + product(weight.astype(jnp.bfloat16), block)
        denom = jnp.sum(total, axis=1, keepdims=True)
        out = out / denom
        ol_all[j, place] = jnp.where(lanes(out.shape) < 64, top + jnp.log(denom), out)

    @pl.loop(0, heads)
    def _(j):
        for off in range(PARTS):
            at, copies = ex.relay(j, off, kv_all, relay_send, kv_recv)
            here(kv_all.at[j, at], kv_recv.at[j, at])
            for copy in copies:
                copy.start()
        for t in range(n):
            here(q_all.at[j, t], q_recv.at[j, t])
        for off in range(PARTS):
            for hop in range(1, splits):
                at = lax.rem(ex.part + off, PARTS) * splits + lax.rem(ex.split + hop, splits)
                here(kv_all.at[j, at], kv_recv.at[j, at])
        for t in range(n):
            q_work[t] = q_all[j, t]
            kv_work[t] = kv_all[j, t]

        @pl.loop(0, half)
        def _(c):
            piece(j, half + c, pick(slot[half:], c), slot[:half])

        for p in range(half):
            piece(j, p, slot[p], slot[:p])
        for t in range(n):
            o_staged[j, t] = fold(ol_all[j, table[0, t]], True).astype(jnp.bfloat16)
        for copy in ex.give_back(j, heads, o_staged, back, o_send, o_recv):
            copy.start()
        ex.keep_own(j, heads, o_staged, back, o_recv).start()

    @pl.loop(0, heads)
    def _(j):
        for copy in ex.spread(j, kv_staged, kv_all, kv_send, kv_recv):
            copy.wait_send()
        for copy in ex.scatter(j, q_staged, q_all, q_send, q_recv):
            copy.wait_send()
        for off in range(PARTS):
            for copy in ex.relay(j, off, kv_all, relay_send, kv_recv)[1]:
                copy.wait_send()
        for copy in ex.give_back(j, heads, o_staged, back, o_send, o_recv):
            copy.wait_send()
        for t in range(n):
            landed = back.at[t // splits * heads + j, t % splits]
            here(landed, o_recv.at[j, t])


def forward_call(n, table, x, first, gain, shift, wq, bq, wk, wv, bv):
    rows, width = x.shape
    splits = n // PARTS
    heads = width // 64 // PARTS
    share = rows // splits
    low = jnp.bfloat16
    vmem, dma = pltpu.VMEM, pltpu.SemaphoreType.DMA
    inside = pl.BlockSpec(memory_space=vmem)
    shape = jax.ShapeDtypeStruct
    return pl.pallas_call(
        functools.partial(forward_kernel, n, heads),
        out_shape=[
            shape((rows, width), low),
            shape((heads, n, share // 2, 128), low),
            shape((heads, n, rows, 128), low),
            shape((heads, n, share, 128), jnp.float32),
            shape((PARTS * heads, splits, share // 2, 128), low),
        ],
        in_specs=[pl.BlockSpec(memory_space=pltpu.SMEM)] + [inside] * 9,
        out_specs=[inside] * 5,
        scratch_shapes=[
            vmem((PARTS, heads, splits, share // 2, 128), low),
            vmem((PARTS, heads, rows, 128), low),
            vmem((heads, n, share // 2, 128), low),
            vmem((n, share // 2, 128), low),
            vmem((n, rows, 128), low),
            dma((heads, n - 1)),
            dma((heads, PARTS - 1)),
            dma((heads, PARTS, max(splits - 1, 1))),
            dma((heads, n - 1)),
            dma((heads, n)),
            dma((heads, n)),
            dma((heads, n)),
        ],
        compiler_params=pltpu.CompilerParams(
            collective_id=1, has_side_effects=True, vmem_limit_bytes=64000000
        ),
        name="attention_forward",
    )(table, x, first, gain, shift, wq, bq, wk, wv, bv)


def join_tiles(even, odd, high):
    low = lanes(even.shape) < 64
    if high:
        return jnp.where(low, swap_lanes(even), odd)
    return jnp.where(low, even, swap_lanes(odd))


def join_rows(back):
    heads, splits = back.shape[0], back.shape[1]
    tiles = []
    for tile in range(heads // 2):
        parts = []
        for split in range(splits):
            even = back[2 * tile, split].astype(jnp.float32)
            odd = back[2 * tile + 1, split].astype(jnp.float32)
            parts += [join_tiles(even, odd, False), join_tiles(even, odd, True)]
        tiles.append(jnp.concatenate(parts, axis=0))
    return jnp.concatenate(tiles, axis=1)


def spread_vector(vector, count):
    size = vector.shape[1]
    part = size // count
    lane = lax.broadcasted_iota(jnp.int32, (count, size), 1)
    row = lax.broadcasted_iota(jnp.int32, (count, size), 0)
    mine = (lane >= row * part) & (lane < row * part + part)
    spread = jnp.where(mine, vector, 0.0)
    at = lax.broadcasted_iota(jnp.int32, (size, 128), 0)
    to = lax.broadcasted_iota(jnp.int32, (size, 128), 1)
    pick_part = jnp.where(lax.rem(at, part) == to, 1.0, 0.0)
    return lax.dot_general(spread, pick_part, (((1,), (0,)), ((), ())), precision=lax.Precision.HIGHEST,
                           preferred_element_type=jnp.float32)


def backward_kernel(
    n, groups, heads, orders_far, orders_near,
    table, do_in, q_all, kv_all, ol_all, hidden, x, gain, wq, wk, wv, dmid, s_gain2, s_bias2, s_ob, s_eb, s_rb,
    *refs,
):
    count = len(orders_far)
    far_in, refs = refs[:count], refs[count:]
    token_grad, first_grad = refs[:2]
    far_out, refs = refs[2 : 2 + count], refs[2 + count :]
    g_wk, g_wq, g_wv, g_small = refs[:4]
    do_all, do_work, acc, dq_piece, dq_staged, part_staged, part_all, dkv_staged, dq_back, dkv_back = refs[4:14]
    p_wk, p_wq, p_wv, p_small = refs[14:18]
    do_send, do_recv, dq_send, dq_recv, part_send, part_recv, dkv_send, dkv_recv = refs[18:26]
    scratch = refs[26:]
    ex = Exchange(n)
    chips = n // 2
    enter(ex.peers() + [{"grp": ex_g} for ex_g in [lax.axis_index("grp") ^ bit for bit in powers(groups)]])
    each = len(scratch) // (count + 4)
    far = make_reduces(groups, chips, orders_far, far_in, far_out, scratch[: count * each])
    near = make_reduces(groups, chips, orders_near, [p_wk, p_wq, p_wv, p_small], [g_wk, g_wq, g_wv, g_small],
                        scratch[count * each :])
    splits = ex.splits
    rows = kv_all.shape[2]
    share = rows // splits
    half = n // 2
    fresh = wv.shape[1]

    @pl.loop(0, heads)
    def _(j):
        for copy in ex.scatter(j, do_in, do_all, do_send, do_recv):
            copy.start()
        ex.own(j, do_in, do_all, do_recv).start()

    for r in far:
        r.begin()
    slot = slots_of(table, n)
    column = lax.broadcasted_iota(jnp.int32, (rows, share), 1) + ex.split * share
    own_mask = lax.broadcasted_iota(jnp.int32, (rows, share), 0) <= column

    def piece(j, place, at, keys):
        q = unfold(q_all[j, at].astype(jnp.float32), False).astype(jnp.bfloat16)
        grad = unfold(do_work[at].astype(jnp.float32), True)
        ol = ol_all[j, place]
        delta = jnp.sum(jnp.transpose(grad * ol), axis=0, keepdims=True)
        logsum = jnp.transpose(ol)[0:1]
        grad = grad.astype(jnp.bfloat16)
        dq = jnp.zeros((128, share), jnp.float32)
        for where, (key_place, key_slot) in enumerate(keys + [(place, at)]):
            block = kv_all[j, key_slot]
            weight = jnp.exp(product_right(block, q) - logsum)
            if where == len(keys):
                weight = jnp.where(own_mask, weight, 0.0)
            change = (weight * (product_right(block, grad) - delta)).astype(jnp.bfloat16)
            term = product(weight.astype(jnp.bfloat16), grad) + product(change, q)
            acc[key_place] = acc[key_place] + term
            dq = dq + product_left(block, change)
        dq_piece[place] = fold(jnp.transpose(dq) * 0.125, False).astype(jnp.bfloat16)

    def part_copies(j):
        out = []
        for hop in range(1, splits):
            split = lax.rem(ex.split + hop, splits)
            for part in range(PARTS):
                out.append(remote(part_staged.at[j, hop - 1, part], part_all.at[j, hop - 1, part],
                                  part_send.at[j, hop - 1, part], part_recv.at[j, hop - 1, part],
                                  {"seq": ex.part * splits + split}))
        return out

    def back_copies(j):
        out = []
        row = ex.part * heads + j
        for off in range(1, PARTS):
            part = lax.rem(ex.part + off, PARTS)
            out.append(remote(dkv_staged.at[j, part], dkv_back.at[row], dkv_send.at[j, off - 1],
                              dkv_recv.at[j, ex.part], {"seq": part * splits + ex.split}))
        return out

    @pl.loop(0, heads)
    def _(j):
        for t in range(n):
            here(do_all.at[j, t], do_recv.at[j, t])
        for t in range(n):
            do_work[t] = do_all[j, t]
            acc[t] = jnp.zeros((rows, 128), jnp.float32)

        @pl.loop(0, half)
        def _(c):
            piece(j, half + c, pick(slot[half:], c), [(p, slot[p]) for p in range(half)])

        @pl.when(j == 0)
        def _():
            for r in far:
                r.paired()

        for p in range(half):
            piece(j, p, slot[p], [(k, slot[k]) for k in range(p)])
        for hop in range(1, splits):
            split = lax.rem(ex.split + hop, splits)
            for part in range(PARTS):
                part_staged[j, hop - 1, part] = acc[table[0, part * splits + split]].astype(jnp.bfloat16)
        for copy in part_copies(j):
            copy.start()
        for t in range(n):
            dq_staged[j, t] = dq_piece[table[0, t]]
        for hop in range(1, splits):
            for part in range(PARTS):
                here(part_all.at[j, hop - 1, part], part_recv.at[j, hop - 1, part])
        for part in range(PARTS):
            total = acc[table[0, part * splits + ex.split]]
            for hop in range(1, splits):
                total = total + part_all[j, hop - 1, part].astype(jnp.float32)
            dkv_staged[j, part] = total.astype(jnp.bfloat16)
        for copy in back_copies(j):
            copy.start()
        pltpu.make_async_copy(dkv_staged.at[j, ex.part], dkv_back.at[ex.part * heads + j],
                              dkv_recv.at[j, ex.part]).start()
        for copy in ex.give_back(j, heads, dq_staged, dq_back, dq_send, dq_recv):
            copy.start()
        ex.keep_own(j, heads, dq_staged, dq_back, dq_recv).start()

        @pl.when(j == min(1, heads - 1))
        def _():
            for r in far:
                r.crossed(0)

    @pl.loop(0, heads)
    def _(j):
        for t in range(n):
            here(dq_back.at[t // splits * heads + j, t % splits], dq_recv.at[j, t])
        for part in range(PARTS):
            here(dkv_back.at[part * heads + j], dkv_recv.at[j, part])

    for level in range(1, len(powers(groups))):
        for r in far:
            r.crossed(level)
    low = jnp.bfloat16
    h_across = jnp.transpose(hidden[...])

    def keep(partial, value):
        partial[...] = value.reshape(partial.shape).astype(low)

    tiles = range(PARTS * heads // 2)
    pairs = [(dkv_back[2 * t].astype(jnp.float32), dkv_back[2 * t + 1].astype(jnp.float32)) for t in tiles]
    dk = jnp.concatenate([join_tiles(a, b, False) for a, b in pairs], axis=1).astype(low)
    keep(p_wk, product(h_across, dk))
    near[0].begin()
    dq = join_rows(dq_back).astype(low)
    keep(p_wq, product(h_across, dq))
    near[1].begin()
    dv = jnp.concatenate([join_tiles(a, b, True) for a, b in pairs], axis=1)
    first_grad[...] = dv[:, fresh:]
    dvf = dv[:, :fresh].astype(low)
    keep(p_wv, product(h_across, dvf))
    near[2].begin()
    near[0].paired()
    near[1].paired()
    dh = product_right(dq, wq[...]) + product_right(dk, wk[...]) + product_right(dvf, wv[...])
    near[2].paired()
    normed, scale = normal_rows(x[...].astype(jnp.float32))

    def total(v):
        return jnp.sum(v, axis=0, keepdims=True)

    sums = [total(dh * normed), total(dh), total(dq.astype(jnp.float32)), total(dvf.astype(jnp.float32)),
            s_ob[...], s_gain2[...], s_bias2[...], s_eb[...], s_rb[...]]
    devices = groups * n
    spread = [spread_vector(v, devices).reshape(devices, 1, 128) for v in sums]
    spread.append(jnp.zeros((devices, 16 - len(spread), 128), jnp.float32))
    p_small[...] = jnp.concatenate(spread, axis=1).reshape(p_small.shape)
    near[3].begin()
    for level in range(len(powers(groups))):
        for r in near[:3]:
            r.crossed(level)
    scaled = dh * gain[...].astype(jnp.float32)
    inner = jnp.mean(scaled, axis=-1, keepdims=True)
    along = jnp.mean(scaled * normed, axis=-1, keepdims=True)
    token_grad[...] = dmid[...] + scale * (scaled - inner - normed * along)
    near[3].paired()
    for level in range(len(powers(groups))):
        near[3].crossed(level)
    for r in far:
        r.finish()
    for r in near:
        r.finish()
    for r in far + near:
        r.drain()

    @pl.loop(0, heads)
    def _(j):
        for copy in ex.scatter(j, do_in, do_all, do_send, do_recv):
            copy.wait_send()
        for copy in part_copies(j):
            copy.wait_send()
        for copy in back_copies(j):
            copy.wait_send()
        for copy in ex.give_back(j, heads, dq_staged, dq_back, dq_send, dq_recv):
            copy.wait_send()


def backward_call(n, groups, table, do_in, q_all, kv_all, ol_all, hidden, x, gain, wq, wk, wv, dmid, sums, far):
    heads, _, rows, _ = kv_all.shape
    splits = n // PARTS
    chips = n // 2
    share = rows // splits
    width, fresh = wv.shape
    low = jnp.bfloat16
    vmem, dma = pltpu.VMEM, pltpu.SemaphoreType.DMA
    inside = pl.BlockSpec(memory_space=vmem)
    shape = jax.ShapeDtypeStruct
    bits = powers(groups)
    forth, back = bits, bits[::-1]
    block = (groups, chips, 2)
    part = width // (groups * n)
    near = [block + (part, width, low), block + (part, width, low), block + (part, fresh, low),
            block + (16, 128, jnp.float32)]
    shapes = [f.shape + (low,) for f in far] + near
    return pl.pallas_call(
        functools.partial(backward_kernel, n, groups, heads, [forth, back, forth][: len(far)], [back, forth, back, forth]),
        out_shape=[shape((rows, width), jnp.float32), shape((rows, width - fresh), jnp.float32)]
        + [shape(s[3:5], jnp.float32) for s in shapes],
        in_specs=[pl.BlockSpec(memory_space=pltpu.SMEM)] + [inside] * 16 + [pl.BlockSpec(memory_space=pl.ANY)] * len(far),
        out_specs=[inside] * (6 + len(far)),
        scratch_shapes=[
            vmem((heads, n, share // 2, 128), low),
            vmem((n, share // 2, 128), low),
            vmem((n, rows, 128), jnp.float32),
            vmem((n, share // 2, 128), low),
            vmem((heads, n, share // 2, 128), low),
            vmem((heads, max(splits - 1, 1), PARTS, rows, 128), low),
            vmem((heads, max(splits - 1, 1), PARTS, rows, 128), low),
            vmem((heads, PARTS, rows, 128), low),
            vmem((PARTS * heads, splits, share // 2, 128), low),
            vmem((PARTS * heads, rows, 128), low),
        ]
        + [vmem(s[:5], s[5]) for s in near]
        + [
            dma((heads, n - 1)),
            dma((heads, n)),
            dma((heads, n - 1)),
            dma((heads, n)),
            dma((heads, max(splits - 1, 1), PARTS)),
            dma((heads, max(splits - 1, 1), PARTS)),
            dma((heads, PARTS - 1)),
            dma((heads, PARTS)),
        ]
        + reduce_scratch(groups, chips, shapes),
        compiler_params=pltpu.CompilerParams(
            collective_id=2, has_side_effects=True, vmem_limit_bytes=67043328
        ),
        name="attention_backward",
    )(table, do_in, q_all, kv_all, ol_all, hidden, x, gain, wq, wk, wv, dmid, *sums, *far)


def hand_over_kernel(count, sizes, *refs):
    ins, outs = refs[: count + 1], refs[count + 1 :]
    for i in range(count):
        outs[i][...] = ins[i][...]
    for row, size in enumerate(sizes):
        outs[count + row][...] = ins[count][row : row + 1, :size]


def hand_over(arrays, small, sizes):
    shape = jax.ShapeDtypeStruct
    return pl.pallas_call(
        functools.partial(hand_over_kernel, len(arrays), sizes),
        out_shape=[shape(a.shape, a.dtype) for a in arrays] + [shape((1, size), jnp.float32) for size in sizes],
        compiler_params=pltpu.CompilerParams(vmem_limit_bytes=40000000),
        name="hand_over",
    )(*arrays, small)


def collect(parts):
    groups = lax.axis_size("grp")
    n = lax.axis_size("seq")
    small = (0, 1, 3, 6, 8, 9, 10, 12, 14)
    packed = jnp.concatenate([parts[i] for i in small])
    sizes = [parts[i].shape[0] for i in small]
    length = packed.shape[0]
    packed = jnp.pad(packed, (0, 2048 - length)).reshape(16, 128)
    bits = powers(groups)
    forth, back = bits, bits[::-1]
    shards = [packed, parts[2], parts[5], parts[4], parts[7], parts[11], parts[13]]
    fulls = gather_call(groups, n // 2, shards, [forth, forth, forth, back, back, forth, back])
    flat = fulls[0].reshape(groups * n, 2048)
    whole = [None] * 15
    at = 0
    for i, size in zip(small, sizes):
        whole[i] = flat[:, at : at + size].reshape(groups * n * size)
        at += size
    for i, full in zip((2, 5, 4, 7, 11, 13), fulls[1:]):
        whole[i] = full.reshape(-1, full.shape[-1])
    return tuple(whole)


def normalize(v, gain, shift):
    mean = jnp.mean(v, axis=-1, keepdims=True)
    centred = v - mean
    var = jnp.mean(centred * centred, axis=-1, keepdims=True)
    return centred * lax.rsqrt(var + EPS) * gain + shift


def gelu_tanh(v):
    return jax.nn.gelu(v, approximate=True)


def unpack_rows(v):
    heads, splits, size, _ = v.shape
    v = v.reshape(heads, splits, size, 2, 64)
    return jnp.transpose(v, (1, 3, 2, 0, 4)).reshape(splits * 2 * size, heads * 64)


def pack_rows(v, splits):
    rows, width = v.shape
    heads = width // 64
    v = v.reshape(splits, 2, rows // splits // 2, heads, 64)
    v = jnp.transpose(v, (3, 0, 2, 1, 4))
    return v.reshape(PARTS, heads // PARTS, splits, rows // splits // 2, 128)


def body(
    tokens,
    first_values,
    placement,
    cotangent,
    *parts,
):
    groups, rows, width = tokens.shape
    n = lax.axis_size("seq")
    splits = n // PARTS
    whole = collect(parts)
    gain_one = whole[0].astype(jnp.float32)
    bias_one = whole[1].astype(jnp.float32)
    gain_two = whole[9].astype(jnp.float32)
    bias_two = whole[10].astype(jnp.float32)
    hidden, q_all, kv_all, ol_all, back = forward_call(
        n, placement, tokens[0], first_values[0], whole[0][None], whole[1][None],
        whole[2], whole[3][None], whole[4], whole[5], whole[6][None],
    )
    attended_low = unpack_rows(back)
    flat = tokens[0].astype(jnp.float32)
    middle = flat + product(attended_low, whole[7]) + whole[8].astype(jnp.float32)
    normed_two, norm_two_back = jax.vjp(normalize, middle, gain_two, bias_two)
    second = normed_two.astype(jnp.bfloat16)
    pre = product(second, whole[11]) + whole[12].astype(jnp.float32)
    post_full, gelu_back = jax.vjp(gelu_tanh, pre)
    post = post_full.astype(jnp.bfloat16)
    result = middle + product(post, whole[13]) + whole[14].astype(jnp.float32)
    layer_output = result.astype(jnp.bfloat16)[None]
    seed = cotangent[0]
    seed_full = seed.astype(jnp.float32)
    grad_reduce_bias = jnp.sum(seed_full, axis=0)
    grad_reduce = product_left(post, seed)
    grad_post = product_right(seed, whole[13])
    grad_pre = gelu_back(grad_post)[0].astype(jnp.bfloat16)
    grad_expand_bias = jnp.sum(grad_pre.astype(jnp.float32), axis=0)
    grad_expand = product_left(second, grad_pre)
    grad_second = product_right(grad_pre, whole[11])
    grad_mid_norm, grad_gain_two, grad_bias_two = norm_two_back(grad_second)
    grad_mid = grad_mid_norm + seed_full
    grad_branch = grad_mid.astype(jnp.bfloat16)
    grad_output_bias = jnp.sum(grad_branch.astype(jnp.float32), axis=0)
    grad_output = product_left(attended_low, grad_branch)
    grad_attended = product_right(grad_branch, whole[7]).astype(jnp.bfloat16)
    block = (lax.axis_size("grp"), n // 2, 2)

    def blocks(v):
        return v.astype(jnp.bfloat16).reshape(block + (-1, v.shape[1]))

    sums = [v[None] for v in (grad_gain_two, grad_bias_two, grad_output_bias, grad_expand_bias, grad_reduce_bias)]
    far = [blocks(grad_expand), blocks(grad_reduce), blocks(grad_output)]
    inside = far if n <= 8 else []
    done = backward_call(
        n, block[0], placement, pack_rows(grad_attended, splits), q_all, kv_all, ol_all, hidden, tokens[0],
        whole[0][None], whole[2], whole[4], whole[5], grad_mid, sums,
        inside,
    )
    token_grad, first_grad = done[:2]
    if not inside:
        forth = powers(block[0])
        done = done[:2] + reduce_call(block[0], block[1], far, [forth, forth[::-1], forth]) + done[2:]
    g_we, g_wr, g_wo, g_wk, g_wq, g_wv, g_small = done[2:]
    small = (0, 1, 3, 6, 8, 9, 10, 12, 14)
    sizes = [parts[i].shape[0] for i in small]
    out = hand_over([token_grad, first_grad, g_wq, g_wk, g_wv, g_wo, g_we, g_wr], g_small, sizes)
    owned = [None] * 15
    for i, v in zip((2, 4, 5, 7, 11, 13), out[2:8]):
        owned[i] = v
    for i, v in zip(small, out[8:]):
        owned[i] = v.reshape(-1)
    return (layer_output, out[0][None], out[1][None]) + tuple(owned)


def solution(mesh):
    spread = P("grp", "seq", None)
    both = ("grp", "seq")
    vector, matrix = P(both), P(both, None)
    kinds = (vector, vector, matrix, vector, matrix, matrix, vector, matrix, vector, vector, vector,
             matrix, vector, matrix, vector)
    in_specs = (spread, spread, P("grp", None), spread) + kinds
    out_specs = (spread, spread, spread) + kinds
    return jax.shard_map(body, mesh=mesh, in_specs=in_specs, out_specs=out_specs, check_vma=False)
```

```python
import functools
import math

import jax
import jax.numpy as jnp
from jax import lax
from jax.experimental import pallas as pl
from jax.experimental.pallas import tpu as pltpu
from jax.sharding import PartitionSpec as P

MESH = pl.DeviceIdType.MESH


def powers(count):
    out, bit = [], 1
    while bit < count:
        out.append(bit)
        bit *= 2
    return out


def remote(src, dst, send, recv, device):
    return pltpu.make_async_remote_copy(
        src_ref=src, dst_ref=dst, send_sem=send, recv_sem=recv,
        device_id=device, device_id_type=MESH,
    )


def enter(devices):
    barrier = pltpu.get_barrier_semaphore()
    for device in devices:
        pl.semaphore_signal(barrier, inc=1, device_id=device, device_id_type=MESH)
    pl.semaphore_wait(barrier, len(devices))


class Gather:
    def __init__(self, groups, chips, bits, shard, full, chain_send, level_send, recv, pair, own):
        self.groups, self.chips, self.bits = groups, chips, bits
        self.shard, self.full = shard, full
        self.chain_send, self.level_send, self.recv, self.pair, self.own = chain_send, level_send, recv, pair, own
        self.g = lax.axis_index("grp")
        seq = lax.axis_index("seq")
        self.s, self.z, self.c = seq, seq // 2, seq % 2

    def block(self, g, z, c):
        return self.full.at[g, z, c]

    def source(self, mask, z, first):
        return self.shard if first else self.block(self.g ^ mask, z, self.c)

    def chain(self, z, step, first):
        side = 0 if step < 0 else 1
        return remote(self.source(0, z, first), self.block(self.g, z, self.c),
                      self.chain_send.at[z, side], self.recv.at[self.g, z],
                      {"seq": self.s + 2 * step})

    def cross(self, level, mask, z, first):
        g = self.g ^ mask
        return remote(self.source(mask, z, first), self.block(g, z, self.c),
                      self.level_send.at[level], self.recv.at[g, z],
                      {"grp": self.g ^ self.bits[level]})

    def held(self, level):
        masks = [0]
        for bit in self.bits[:level]:
            masks = masks + [m ^ bit for m in masks]
        return masks

    def here(self, mask, z):
        g = self.g ^ mask
        pltpu.make_async_copy(self.block(g, z, self.c), self.block(g, z, self.c), self.recv.at[g, z]).wait()

    def begin(self):
        self.begin_chain()
        self.begin_cross()

    def begin_chain(self):
        copy = pltpu.make_async_copy(self.shard, self.block(self.g, self.z, self.c), self.own)
        copy.start()

        @pl.when(self.z > 0)
        def _():
            self.chain(self.z, -1, True).start()

        @pl.when(self.z < self.chips - 1)
        def _():
            self.chain(self.z, 1, True).start()

    def begin_cross(self):
        for level in range(len(self.bits)):
            self.cross(level, 0, self.z, True).start()

    def at(self, distance, body):
        if distance == 0:
            body(self.z, 0)
            return

        @pl.when(self.z >= distance)
        def _():
            body(self.z - distance, 1)

        @pl.when(self.z + distance < self.chips)
        def _():
            body(self.z + distance, -1)

    def along(self, distance):
        self.along_chain(distance)
        self.along_cross(distance)

    def along_chain(self, distance):
        def body(z, step):
            self.here(0, z)
            onward = self.z < self.chips - 1 if step > 0 else self.z > 0

            @pl.when(onward)
            def _():
                self.chain(z, step, False).start()

        self.at(distance, body)

    def along_cross(self, distance):
        def body(z, step):
            for level in range(len(self.bits)):
                self.cross(level, 0, z, False).start()

        self.at(distance, body)

    def over(self, level, distance):
        def body(z, step):
            for mask in self.held(level):
                mask = mask ^ self.bits[level]
                self.here(mask, z)
                for later in range(level + 1, len(self.bits)):
                    self.cross(later, mask, z, False).start()

        self.at(distance, body)

    def swap_copy(self):
        mine = self.full.at[:, :, self.c]
        return remote(mine, mine, self.pair.at[0], self.pair.at[1], {"seq": self.s ^ 1})

    def swap(self):
        pltpu.make_async_copy(self.shard, self.shard, self.own).wait()
        self.swap_copy().start()

    def finish(self):
        self.swap_copy().wait_send()
        other = self.full.at[:, :, 1 - self.c]
        pltpu.make_async_copy(other, other, self.pair.at[1]).wait()

        @pl.when(self.z > 0)
        def _():
            self.chain(self.z, -1, True).wait_send()

        @pl.when(self.z < self.chips - 1)
        def _():
            self.chain(self.z, 1, True).wait_send()

        for distance in range(1, self.chips):
            def body(z, step):
                onward = self.z < self.chips - 1 if step > 0 else self.z > 0

                @pl.when(onward)
                def _():
                    self.chain(z, step, False).wait_send()

            self.at(distance, body)
        for level in range(len(self.bits)):
            sent = self.full.at[pl.ds(0, 2 ** level), :, 0]
            pltpu.make_async_copy(sent, sent, self.level_send.at[level]).wait()


def gather_semaphores(count, groups, chips):
    dma = pltpu.SemaphoreType.DMA
    levels = max(len(powers(groups)), 1)
    return [dma((count, chips, 2)), dma((count, levels)), dma((count, groups, chips)), dma((count, 2)), dma((count,))]


def neighbours(groups, n):
    g, s = lax.axis_index("grp"), lax.axis_index("seq")
    out = [{"grp": g ^ bit} for bit in powers(groups)]
    out += [{"seq": s ^ 1}, {"seq": lax.rem(s + 2, n)}, {"seq": lax.rem(s + n - 2, n)}]
    return out


def gather_kernel(groups, chips, orders, *refs):
    count = len(orders)
    shards, fulls, sems = refs[:count], refs[count:2 * count], refs[2 * count:]
    enter(neighbours(groups, 2 * chips))
    gathers = [Gather(groups, chips, orders[i], shards[i], fulls[i], *[s.at[i] for s in sems]) for i in range(count)]
    run_gathers(gathers)


def run_gathers(gathers):
    chips, levels = gathers[0].chips, len(gathers[0].bits)
    for g in gathers:
        g.begin()
    for distance in range(chips + levels):
        for g in gathers:
            if distance + 1 < chips:
                g.along(distance + 1)
            for level in range(levels):
                if 0 <= distance - level < chips:
                    g.over(level, distance - level)
    for g in gathers:
        g.swap()
    for g in gathers:
        g.finish()


def gather_call(groups, chips, shards, orders):
    count = len(shards)
    return pl.pallas_call(
        functools.partial(gather_kernel, groups, chips, orders),
        out_shape=[jax.ShapeDtypeStruct((groups, chips, 2) + x.shape, x.dtype) for x in shards],
        in_specs=[pl.BlockSpec(memory_space=pl.ANY)] * count,
        out_specs=[pl.BlockSpec(memory_space=pl.ANY)] * count,
        scratch_shapes=gather_semaphores(count, groups, chips),
        compiler_params=pltpu.CompilerParams(collective_id=0, has_side_effects=True),
        name="gather_parameters",
    )(*shards)


class Reduce:
    def __init__(self, groups, chips, bits, partial, shard, own, landed, halves, finals, sems):
        self.groups, self.chips, self.bits = groups, chips, bits
        self.partial, self.shard, self.own, self.landed = partial, shard, own, landed
        self.halves, self.finals = halves, finals
        self.load, self.pair, self.level_send, self.level_recv, self.chip_send, self.chip_recv = sems
        self.g = lax.axis_index("grp")
        self.s = lax.axis_index("seq")
        self.z, self.c = self.s // 2, self.s % 2

    def masks(self, level):
        out = [0]
        for bit in self.bits[level:]:
            out = out + [m ^ bit for m in out]
        return out

    def load_copy(self):
        return pltpu.make_async_copy(self.partial.at[:, :, self.c], self.own, self.load.at[0])

    def pair_copy(self):
        return remote(self.partial.at[:, :, 1 - self.c], self.landed, self.pair.at[0], self.pair.at[1],
                      {"seq": self.s ^ 1})

    def begin(self):
        self.pair_copy().start()
        self.load_copy().start()

    def paired(self):
        self.load_copy().wait()
        self.pair_copy().wait_recv()

        @pl.loop(0, self.groups)
        def _(g):
            self.own[g] = self.add(self.own[g], self.landed[g])

        self.cross_start(0)

    def add(self, a, b):
        return a + b

    def cross_copies(self, level):
        bit = self.bits[level]
        out = []
        for where, mask in enumerate(self.masks(level + 1)):
            out.append(remote(self.own.at[self.g ^ bit ^ mask], self.halves[level].at[where],
                              self.level_send.at[level, where], self.level_recv.at[level, where],
                              {"grp": self.g ^ bit}))
        return out

    def cross_start(self, level):
        if level < len(self.bits):
            for copy in self.cross_copies(level):
                copy.start()
        else:
            for copy in self.chip_copies():
                copy.start()

    def crossed(self, level):
        copies = self.cross_copies(level)
        for where, mask in enumerate(self.masks(level + 1)):
            copies[where].wait_recv()
            g = self.g ^ mask
            self.own[g] = self.add(self.own[g], self.halves[level][where])
        self.cross_start(level + 1)

    def chip_copies(self):
        out = []
        for off in range(1, self.chips):
            chip = lax.rem(self.z + off, self.chips)
            out.append(remote(self.own.at[self.g, chip], self.finals.at[off - 1], self.chip_send.at[off - 1],
                              self.chip_recv.at[off - 1], {"seq": 2 * chip + self.c}))
        return out

    def finish(self):
        total = self.own[self.g, self.z].astype(jnp.float32)
        for off, copy in enumerate(self.chip_copies()):
            copy.wait_recv()
            total = total + self.finals[off].astype(jnp.float32)
        self.shard[...] = total

    def drain(self):
        self.pair_copy().wait_send()
        for level in range(len(self.bits)):
            for copy in self.cross_copies(level):
                copy.wait_send()
        for copy in self.chip_copies():
            copy.wait_send()


def reduce_steps(reduces):
    levels = len(reduces[0].bits)
    stages = [lambda r: r.begin(), lambda r: r.paired()]
    for level in range(levels):
        stages.append(lambda r, level=level: r.crossed(level))
    stages += [lambda r: r.finish(), lambda r: r.drain()]
    return [functools.partial(stage, r) for stage in stages for r in reduces]


def reduce_scratch(groups, chips, shapes):
    vmem, dma = pltpu.VMEM, pltpu.SemaphoreType.DMA
    levels = len(powers(groups))
    out = []
    for _, _, _, rows, cols, dtype in shapes:
        out += [vmem((groups, chips, rows, cols), dtype), vmem((groups, chips, rows, cols), dtype)]
        out += [vmem((groups >> (level + 1), chips, rows, cols), dtype) for level in range(levels)]
        out += [vmem((max(chips - 1, 1), rows, cols), dtype)]
        out += [dma((1,)), dma((2,)), dma((max(levels, 1), max(groups // 2, 1))),
                dma((max(levels, 1), max(groups // 2, 1))), dma((max(chips - 1, 1),)),
                dma((max(chips - 1, 1),))]
    return out


def make_reduces(groups, chips, orders, partials, shards, scratch):
    levels = len(powers(groups))
    each = 2 + levels + 1 + 6
    out = []
    for i, (partial, shard) in enumerate(zip(partials, shards)):
        refs = scratch[i * each : (i + 1) * each]
        out.append(Reduce(groups, chips, orders[i], partial, shard, refs[0], refs[1], refs[2 : 2 + levels],
                          refs[2 + levels], refs[3 + levels :]))
    return out


def reduce_kernel(groups, chips, orders, *refs):
    count = len(orders)
    enter(neighbours(groups, 2 * chips))
    for step in reduce_steps(make_reduces(groups, chips, orders, refs[:count], refs[count : 2 * count],
                                          refs[2 * count :])):
        step()


def reduce_call(groups, chips, partials, orders):
    count = len(partials)
    shapes = [p.shape + (p.dtype,) for p in partials]
    return pl.pallas_call(
        functools.partial(reduce_kernel, groups, chips, orders),
        out_shape=[jax.ShapeDtypeStruct(p.shape[3:], jnp.float32) for p in partials],
        in_specs=[pl.BlockSpec(memory_space=pl.ANY)] * count,
        out_specs=[pl.BlockSpec(memory_space=pltpu.VMEM)] * count,
        scratch_shapes=reduce_scratch(groups, chips, shapes),
        compiler_params=pltpu.CompilerParams(collective_id=3, has_side_effects=True, vmem_limit_bytes=64000000),
        name="reduce_gradients",
    )(*partials)


PARTS = 4
NEG = -1e30
EPS = 1e-05


def lanes(shape):
    return lax.broadcasted_iota(jnp.int32, shape, len(shape) - 1)


def swap_lanes(v):
    return pltpu.roll(v, 64, 1)


def fold(v, high):
    half = v.shape[0] // 2
    top, bottom = v[:half], v[half:]
    low = lanes(top.shape) < 64
    if high:
        return jnp.where(low, swap_lanes(top), bottom)
    return jnp.where(low, top, swap_lanes(bottom))


def unfold(v, high):
    low = lanes(v.shape) < 64
    zero = jnp.zeros_like(v)
    if high:
        return jnp.concatenate([jnp.where(low, zero, swap_lanes(v)), jnp.where(low, zero, v)], axis=0)
    return jnp.concatenate([jnp.where(low, v, zero), jnp.where(low, swap_lanes(v), zero)], axis=0)


def product(a, b):
    return lax.dot_general(a, b, (((1,), (0,)), ((), ())), preferred_element_type=jnp.float32)


def product_right(a, b):
    return lax.dot_general(a, b, (((1,), (1,)), ((), ())), preferred_element_type=jnp.float32)


def product_left(a, b):
    return lax.dot_general(a, b, (((0,), (0,)), ((), ())), preferred_element_type=jnp.float32)


def normal_rows(v):
    mean = jnp.mean(v, axis=-1, keepdims=True)
    centred = v - mean
    var = jnp.mean(centred * centred, axis=-1, keepdims=True)
    scale = lax.rsqrt(var + EPS)
    return centred * scale, scale


def pack_heads(v, splits, store):
    size = v.shape[0] // splits
    for tile in range(v.shape[1] // 128):
        for split in range(splits):
            part = v[split * size : (split + 1) * size, tile * 128 : (tile + 1) * 128]
            store(2 * tile, split, fold(part, False))
            store(2 * tile + 1, split, fold(part, True))


def slots_of(table, count):
    out = []
    for piece in range(count):
        slot = jnp.int32(0)
        for place in range(count):
            slot = slot + jnp.where(table[0, place] == piece, place, 0)
        out.append(jnp.minimum(slot, count - 1))
    return out


def pick(values, index):
    out = values[0]
    for i in range(1, len(values)):
        out = jnp.where(index == i, values[i], out)
    return out


class Exchange:
    def __init__(self, n):
        self.n = n
        self.splits = n // PARTS
        self.s = lax.axis_index("seq")
        self.part, self.split = self.s // self.splits, lax.rem(self.s, self.splits)

    def peers(self):
        return [{"seq": lax.rem(self.s + off, self.n)} for off in range(1, self.n)]

    def other(self, off):
        return lax.rem(self.s + off, self.n)

    def scatter(self, j, staged, landed, send, recv):
        out = []
        for off in range(1, self.n):
            t = self.other(off)
            out.append(remote(staged.at[t // self.splits, j, lax.rem(t, self.splits)], landed.at[j, self.s],
                              send.at[j, off - 1], recv.at[j, self.s], {"seq": t}))
        return out

    def own(self, j, staged, landed, recv):
        return pltpu.make_async_copy(staged.at[self.part, j, self.split], landed.at[j, self.s], recv.at[j, self.s])

    def spread(self, j, staged, landed, send, recv):
        out = []
        for off in range(1, PARTS):
            part = lax.rem(self.part + off, PARTS)
            out.append(remote(staged.at[part, j], landed.at[j, self.s], send.at[j, off - 1],
                              recv.at[j, self.s], {"seq": part * self.splits + self.split}))
        return out

    def own_rows(self, j, staged, landed, recv):
        return pltpu.make_async_copy(staged.at[self.part, j], landed.at[j, self.s], recv.at[j, self.s])

    def relay(self, j, off, landed, send, recv):
        slot = lax.rem(self.part + off, PARTS) * self.splits + self.split
        out = []
        for hop in range(1, self.splits):
            split = lax.rem(self.split + hop, self.splits)
            out.append(remote(landed.at[j, slot], landed.at[j, slot], send.at[j, off, hop - 1],
                              recv.at[j, slot], {"seq": self.part * self.splits + split}))
        return slot, out

    def give_back(self, j, heads, staged, landed, send, recv):
        out = []
        row = self.part * heads + j
        for off in range(1, self.n):
            t = self.other(off)
            out.append(remote(staged.at[j, t], landed.at[row, self.split], send.at[j, off - 1],
                              recv.at[j, self.s], {"seq": t}))
        return out

    def keep_own(self, j, heads, staged, landed, recv):
        return pltpu.make_async_copy(staged.at[j, self.s], landed.at[self.part * heads + j, self.split],
                                     recv.at[j, self.s])


def here(ref, sem):
    pltpu.make_async_copy(ref, ref, sem).wait()


def gather_vector(full, row, size):
    count = full.shape[0]
    part = size // count
    rows = full[:, row, :].astype(jnp.bfloat16)
    at = lax.broadcasted_iota(jnp.int32, (128, size), 0)
    to = lax.broadcasted_iota(jnp.int32, (128, size), 1)
    place = jnp.where(lax.rem(to, part) == at, 1.0, 0.0).astype(jnp.bfloat16)
    spread = product(rows, place)
    lane = lax.broadcasted_iota(jnp.int32, (count, size), 1)
    owner = lax.broadcasted_iota(jnp.int32, (count, size), 0)
    mine = (lane >= owner * part) & (lane < owner * part + part)
    return jnp.sum(jnp.where(mine, spread, 0.0), axis=0, keepdims=True)


def forward_kernel(n, groups, heads, orders, sizes, table, x, first, *refs):
    vectors, shards, refs = refs[:9], refs[9:15], refs[15:]
    hidden_out, q_all, kv_all, ol_all, back = refs[:5]
    fulls, vectors_out, refs = refs[5:11], refs[11:20], refs[20:]
    packed, small_full, q_staged, kv_staged, o_staged, q_work, kv_work = refs[:7]
    q_send, kv_send, relay_send, o_send, q_recv, kv_recv, o_recv = refs[7:14]
    sems = refs[14:]
    ex = Exchange(n)
    chips = n // 2
    bits = powers(groups)
    levels = len(bits)
    enter(ex.peers() + [{"grp": lax.axis_index("grp") ^ bit} for bit in bits])
    gathers = [
        Gather(groups, chips, order, shard, full, *[s.at[i] for s in sems])
        for i, (order, shard, full) in enumerate(zip(orders, (packed,) + shards, (small_full,) + fulls))
    ]
    near, far = gathers[:4], gathers[4:]
    packed[...] = jnp.zeros(packed.shape, jnp.float32)
    for row, vector in enumerate(vectors):
        packed[row : row + 1, : vector.shape[1]] = vector[...].astype(jnp.float32)
    for g in (near[1], near[2], near[3], near[0]):
        g.begin()
    splits = ex.splits
    rows, width = x.shape
    share = rows // splits
    half = n // 2
    fresh = width - first.shape[1]
    normed, _ = normal_rows(x[...].astype(jnp.float32))

    def steps(some, along=1):
        out = []
        for distance in range(chips + levels):
            for g in some:
                if along == 1 and distance + 1 < chips:
                    out.append(functools.partial(g.along, distance + 1))
                if along == 2 and 2 <= distance + 1 < chips:
                    out.append(functools.partial(g.along_cross, distance + 1))
                for level in range(levels):
                    if 0 <= distance - level < chips:
                        out.append(functools.partial(g.over, level, distance - level))
        return out

    order = steps(near)
    cut = (min(len(order), len(near) * (1 + levels)), 3 * len(order) // 4)
    for step in order[: cut[0]]:
        step()
    for g in far:
        g.begin_chain()
    for step in order[cut[0] : cut[1]]:
        step()
    if chips > 1:
        for g in far:
            g.along_chain(1)
    for step in order[cut[1] :]:
        step()
    for g in near:
        g.swap()
    for g in far:
        g.begin_cross()
    for distance in range(1, min(2, chips)):
        for g in far:
            g.along_cross(distance)
    for distance in range(2, chips):
        for g in far:
            g.along_chain(distance)
    for g in near:
        g.finish()
    small = small_full[...].reshape((2 * chips * groups,) + packed.shape)
    for row in range(4):
        vectors_out[row][...] = gather_vector(small, row, sizes[row])
    gain, shift, bq, bv = vectors_out[:4]
    wq, wk, wv = [fulls[i][...].reshape(width, -1) for i in range(3)]
    hidden = (normed * gain[...] + shift[...]).astype(jnp.bfloat16)
    hidden_out[...] = hidden
    for step in range(width // 256):
        cols = slice(step * 256, (step + 1) * 256)
        q = product(hidden, wq[:, cols]) + bq[:, cols]

        def store(head, split, v, step=step):
            head = head + 4 * step
            q_staged[head // heads, head % heads, split] = (v * 0.125).astype(jnp.bfloat16)

        pack_heads(q, splits, store)
        k = product(hidden, wk[:, cols])
        for tile in range(2):
            at = step * 256 + tile * 128
            if at < fresh:
                v = product(hidden, wv[:, at : at + 128]) + bv[:, at : at + 128]
            else:
                v = first[:, at - fresh : at - fresh + 128].astype(jnp.float32)
            kt = k[:, tile * 128 : (tile + 1) * 128]
            low = lanes(kt.shape) < 64
            head = at // 64
            kv_staged[head // heads, head % heads] = jnp.where(low, kt, swap_lanes(v)).astype(jnp.bfloat16)
            head = head + 1
            kv_staged[head // heads, head % heads] = jnp.where(low, swap_lanes(kt), v).astype(jnp.bfloat16)

    @pl.loop(0, heads)
    def _(j):
        for copy in ex.spread(j, kv_staged, kv_all, kv_send, kv_recv):
            copy.start()
        for copy in ex.scatter(j, q_staged, q_all, q_send, q_recv):
            copy.start()
        ex.own(j, q_staged, q_all, q_recv).start()
        ex.own_rows(j, kv_staged, kv_all, kv_recv).start()

    slot = slots_of(table, n)
    row = lax.broadcasted_iota(jnp.int32, (share, rows), 0) + ex.split * share
    own_mask = lax.broadcasted_iota(jnp.int32, (share, rows), 1) <= row

    def piece(j, place, at, keys):
        q = unfold(q_work[at].astype(jnp.float32), False).astype(jnp.bfloat16)
        blocks = [kv_work[k] for k in keys] + [kv_work[at]]
        scores = [product_right(q, block) for block in blocks]
        scores[-1] = jnp.where(own_mask, scores[-1], NEG)
        top = scores[0]
        for s in scores[1:]:
            top = jnp.maximum(top, s)
        top = jnp.max(top, axis=1, keepdims=True)
        total = jnp.zeros((share, rows), jnp.float32)
        out = jnp.zeros((share, 128), jnp.float32)
        for s, block in zip(scores, blocks):
            weight = jnp.exp(s - top)
            total = total + weight
            out = out + product(weight.astype(jnp.bfloat16), block)
        denom = jnp.sum(total, axis=1, keepdims=True)
        out = out / denom
        ol_all[j, place] = jnp.where(lanes(out.shape) < 64, top + jnp.log(denom), out)

    later = steps(far, 2)
    cut = (len(later) // 2, 3 * len(later) // 4)
    for step in later[: cut[0]]:
        step()
    for row in range(4, 9):
        vectors_out[row][...] = gather_vector(small, row, sizes[row])

    @pl.loop(0, heads)
    def _(j):
        for off in range(PARTS):
            at, copies = ex.relay(j, off, kv_all, relay_send, kv_recv)
            here(kv_all.at[j, at], kv_recv.at[j, at])
            for copy in copies:
                copy.start()
        for t in range(n):
            here(q_all.at[j, t], q_recv.at[j, t])
        for off in range(PARTS):
            for hop in range(1, splits):
                at = lax.rem(ex.part + off, PARTS) * splits + lax.rem(ex.split + hop, splits)
                here(kv_all.at[j, at], kv_recv.at[j, at])
        for t in range(n):
            q_work[t] = q_all[j, t]
            kv_work[t] = kv_all[j, t]

        @pl.loop(0, half)
        def _(c):
            piece(j, half + c, pick(slot[half:], c), slot[:half])

        for p in range(half):
            piece(j, p, slot[p], slot[:p])
        for t in range(n):
            o_staged[j, t] = fold(ol_all[j, table[0, t]], True).astype(jnp.bfloat16)
        for copy in ex.give_back(j, heads, o_staged, back, o_send, o_recv):
            copy.start()
        ex.keep_own(j, heads, o_staged, back, o_recv).start()

        @pl.when(j == 0)
        def _():
            for step in later[cut[0] : cut[1]]:
                step()

        @pl.when(j == min(1, heads - 1))
        def _():
            for step in later[cut[1] :]:
                step()
            for g in far:
                g.swap()

    @pl.loop(0, heads)
    def _(j):
        for copy in ex.spread(j, kv_staged, kv_all, kv_send, kv_recv):
            copy.wait_send()
        for copy in ex.scatter(j, q_staged, q_all, q_send, q_recv):
            copy.wait_send()
        for off in range(PARTS):
            for copy in ex.relay(j, off, kv_all, relay_send, kv_recv)[1]:
                copy.wait_send()
        for copy in ex.give_back(j, heads, o_staged, back, o_send, o_recv):
            copy.wait_send()
        for t in range(n):
            landed = back.at[t // splits * heads + j, t % splits]
            here(landed, o_recv.at[j, t])
    for g in far:
        g.finish()


def forward_call(n, groups, table, x, first, vectors, shards):
    rows, width = x.shape
    splits = n // PARTS
    chips = n // 2
    heads = width // 64 // PARTS
    share = rows // splits
    low = jnp.bfloat16
    vmem, dma = pltpu.VMEM, pltpu.SemaphoreType.DMA
    inside, outside = pl.BlockSpec(memory_space=vmem), pl.BlockSpec(memory_space=pl.ANY)
    shape = jax.ShapeDtypeStruct
    bits = powers(groups)
    forth, behind = bits, bits[::-1]
    sizes = [v.shape[1] * groups * n for v in vectors]
    block = (groups, chips, 2)
    return pl.pallas_call(
        functools.partial(forward_kernel, n, groups, heads, [forth, forth, behind, forth, behind, forth, behind], sizes),
        out_shape=[
            shape((rows, width), low),
            shape((heads, n, share // 2, 128), low),
            shape((heads, n, rows, 128), low),
            shape((heads, n, share, 128), jnp.float32),
            shape((PARTS * heads, splits, share // 2, 128), low),
        ]
        + [shape(block + w.shape, low) for w in shards]
        + [shape((1, size), jnp.float32) for size in sizes],
        in_specs=[pl.BlockSpec(memory_space=pltpu.SMEM)] + [inside] * 11 + [outside] * 6,
        out_specs=[inside] * 8 + [outside] * 3 + [inside] * 9,
        scratch_shapes=[
            vmem((16, 128), jnp.float32),
            vmem(block + (16, 128), jnp.float32),
            vmem((PARTS, heads, splits, share // 2, 128), low),
            vmem((PARTS, heads, rows, 128), low),
            vmem((heads, n, share // 2, 128), low),
            vmem((n, share // 2, 128), low),
            vmem((n, rows, 128), low),
            dma((heads, n - 1)),
            dma((heads, PARTS - 1)),
            dma((heads, PARTS, max(splits - 1, 1))),
            dma((heads, n - 1)),
            dma((heads, n)),
            dma((heads, n)),
            dma((heads, n)),
        ]
        + gather_semaphores(7, groups, chips),
        compiler_params=pltpu.CompilerParams(
            collective_id=1, has_side_effects=True, vmem_limit_bytes=64000000
        ),
        name="attention_forward",
    )(table, x, first, *vectors, *shards)


def join_tiles(even, odd, high):
    low = lanes(even.shape) < 64
    if high:
        return jnp.where(low, swap_lanes(even), odd)
    return jnp.where(low, even, swap_lanes(odd))


def join_rows(back):
    heads, splits = back.shape[0], back.shape[1]
    tiles = []
    for tile in range(heads // 2):
        parts = []
        for split in range(splits):
            even = back[2 * tile, split].astype(jnp.float32)
            odd = back[2 * tile + 1, split].astype(jnp.float32)
            parts += [join_tiles(even, odd, False), join_tiles(even, odd, True)]
        tiles.append(jnp.concatenate(parts, axis=0))
    return jnp.concatenate(tiles, axis=1)


def spread_vector(vector, count):
    size = vector.shape[1]
    part = size // count
    lane = lax.broadcasted_iota(jnp.int32, (count, size), 1)
    row = lax.broadcasted_iota(jnp.int32, (count, size), 0)
    mine = (lane >= row * part) & (lane < row * part + part)
    spread = jnp.where(mine, vector, 0.0)
    at = lax.broadcasted_iota(jnp.int32, (size, 128), 0)
    to = lax.broadcasted_iota(jnp.int32, (size, 128), 1)
    pick_part = jnp.where(lax.rem(at, part) == to, 1.0, 0.0)
    return lax.dot_general(spread, pick_part, (((1,), (0,)), ((), ())), precision=lax.Precision.HIGHEST,
                           preferred_element_type=jnp.float32)


def backward_kernel(
    n, groups, heads, orders_far, orders_near,
    table, do_in, q_all, kv_all, ol_all, hidden, x, gain, wq, wk, wv, dmid, s_gain2, s_bias2, s_ob, s_eb, s_rb,
    *refs,
):
    count = len(orders_far)
    far_in, refs = refs[:count], refs[count:]
    token_grad, first_grad = refs[:2]
    far_out, refs = refs[2 : 2 + count], refs[2 + count :]
    g_wk, g_wq, g_wv, g_small = refs[:4]
    do_all, do_work, acc, dq_piece, dq_staged, part_staged, part_all, dkv_staged, dq_back, dkv_back = refs[4:14]
    p_wk, p_wq, p_wv, p_small = refs[14:18]
    do_send, do_recv, dq_send, dq_recv, part_send, part_recv, dkv_send, dkv_recv = refs[18:26]
    scratch = refs[26:]
    ex = Exchange(n)
    chips = n // 2
    enter(ex.peers() + [{"grp": ex_g} for ex_g in [lax.axis_index("grp") ^ bit for bit in powers(groups)]])
    each = len(scratch) // (count + 4)
    far = make_reduces(groups, chips, orders_far, far_in, far_out, scratch[: count * each])
    near = make_reduces(groups, chips, orders_near, [p_wk, p_wq, p_wv, p_small], [g_wk, g_wq, g_wv, g_small],
                        scratch[count * each :])
    splits = ex.splits
    rows = kv_all.shape[2]
    share = rows // splits
    half = n // 2
    fresh = wv.shape[1]

    @pl.loop(0, heads)
    def _(j):
        for copy in ex.scatter(j, do_in, do_all, do_send, do_recv):
            copy.start()
        ex.own(j, do_in, do_all, do_recv).start()

    for r in far:
        r.begin()
    slot = slots_of(table, n)
    column = lax.broadcasted_iota(jnp.int32, (rows, share), 1) + ex.split * share
    own_mask = lax.broadcasted_iota(jnp.int32, (rows, share), 0) <= column

    def piece(j, place, at, keys):
        q = unfold(q_all[j, at].astype(jnp.float32), False).astype(jnp.bfloat16)
        grad = unfold(do_work[at].astype(jnp.float32), True)
        ol = ol_all[j, place]
        delta = jnp.sum(jnp.transpose(grad * ol), axis=0, keepdims=True)
        logsum = jnp.transpose(ol)[0:1]
        grad = grad.astype(jnp.bfloat16)
        dq = jnp.zeros((128, share), jnp.float32)
        for where, (key_place, key_slot) in enumerate(keys + [(place, at)]):
            block = kv_all[j, key_slot]
            weight = jnp.exp(product_right(block, q) - logsum)
            if where == len(keys):
                weight = jnp.where(own_mask, weight, 0.0)
            change = (weight * (product_right(block, grad) - delta)).astype(jnp.bfloat16)
            term = product(weight.astype(jnp.bfloat16), grad) + product(change, q)
            acc[key_place] = acc[key_place] + term
            dq = dq + product_left(block, change)
        dq_piece[place] = fold(jnp.transpose(dq) * 0.125, False).astype(jnp.bfloat16)

    def part_copies(j):
        out = []
        for hop in range(1, splits):
            split = lax.rem(ex.split + hop, splits)
            for part in range(PARTS):
                out.append(remote(part_staged.at[j, hop - 1, part], part_all.at[j, hop - 1, part],
                                  part_send.at[j, hop - 1, part], part_recv.at[j, hop - 1, part],
                                  {"seq": ex.part * splits + split}))
        return out

    def back_copies(j):
        out = []
        row = ex.part * heads + j
        for off in range(1, PARTS):
            part = lax.rem(ex.part + off, PARTS)
            out.append(remote(dkv_staged.at[j, part], dkv_back.at[row], dkv_send.at[j, off - 1],
                              dkv_recv.at[j, ex.part], {"seq": part * splits + ex.split}))
        return out

    @pl.loop(0, heads)
    def _(j):
        for t in range(n):
            here(do_all.at[j, t], do_recv.at[j, t])
        for t in range(n):
            do_work[t] = do_all[j, t]
            acc[t] = jnp.zeros((rows, 128), jnp.float32)

        @pl.loop(0, half)
        def _(c):
            piece(j, half + c, pick(slot[half:], c), [(p, slot[p]) for p in range(half)])

        @pl.when(j == 0)
        def _():
            for r in far:
                r.paired()

        for p in range(half):
            piece(j, p, slot[p], [(k, slot[k]) for k in range(p)])
        for hop in range(1, splits):
            split = lax.rem(ex.split + hop, splits)
            for part in range(PARTS):
                part_staged[j, hop - 1, part] = acc[table[0, part * splits + split]].astype(jnp.bfloat16)
        for copy in part_copies(j):
            copy.start()
        for t in range(n):
            dq_staged[j, t] = dq_piece[table[0, t]]
        for hop in range(1, splits):
            for part in range(PARTS):
                here(part_all.at[j, hop - 1, part], part_recv.at[j, hop - 1, part])
        for part in range(PARTS):
            total = acc[table[0, part * splits + ex.split]]
            for hop in range(1, splits):
                total = total + part_all[j, hop - 1, part].astype(jnp.float32)
            dkv_staged[j, part] = total.astype(jnp.bfloat16)
        for copy in back_copies(j):
            copy.start()
        pltpu.make_async_copy(dkv_staged.at[j, ex.part], dkv_back.at[ex.part * heads + j],
                              dkv_recv.at[j, ex.part]).start()
        for copy in ex.give_back(j, heads, dq_staged, dq_back, dq_send, dq_recv):
            copy.start()
        ex.keep_own(j, heads, dq_staged, dq_back, dq_recv).start()

        @pl.when(j == min(1, heads - 1))
        def _():
            for r in far:
                r.crossed(0)

    @pl.loop(0, heads)
    def _(j):
        for t in range(n):
            here(dq_back.at[t // splits * heads + j, t % splits], dq_recv.at[j, t])
        for part in range(PARTS):
            here(dkv_back.at[part * heads + j], dkv_recv.at[j, part])

    for level in range(1, len(powers(groups))):
        for r in far:
            r.crossed(level)
    low = jnp.bfloat16
    h_across = jnp.transpose(hidden[...])

    def keep(partial, value):
        partial[...] = value.reshape(partial.shape).astype(low)

    tiles = range(PARTS * heads // 2)
    pairs = [(dkv_back[2 * t].astype(jnp.float32), dkv_back[2 * t + 1].astype(jnp.float32)) for t in tiles]
    dk = jnp.concatenate([join_tiles(a, b, False) for a, b in pairs], axis=1).astype(low)
    keep(p_wk, product(h_across, dk))
    near[0].begin()
    dq = join_rows(dq_back).astype(low)
    keep(p_wq, product(h_across, dq))
    near[1].begin()
    dv = jnp.concatenate([join_tiles(a, b, True) for a, b in pairs], axis=1)
    first_grad[...] = dv[:, fresh:]
    dvf = dv[:, :fresh].astype(low)
    keep(p_wv, product(h_across, dvf))
    near[2].begin()
    near[0].paired()
    near[1].paired()
    dh = product_right(dq, wq[...]) + product_right(dk, wk[...]) + product_right(dvf, wv[...])
    near[2].paired()
    normed, scale = normal_rows(x[...].astype(jnp.float32))

    def total(v):
        return jnp.sum(v, axis=0, keepdims=True)

    sums = [total(dh * normed), total(dh), total(dq.astype(jnp.float32)), total(dvf.astype(jnp.float32)),
            s_ob[...], s_gain2[...], s_bias2[...], s_eb[...], s_rb[...]]
    devices = groups * n
    spread = [spread_vector(v, devices).reshape(devices, 1, 128) for v in sums]
    spread.append(jnp.zeros((devices, 16 - len(spread), 128), jnp.float32))
    p_small[...] = jnp.concatenate(spread, axis=1).reshape(p_small.shape)
    near[3].begin()
    for level in range(len(powers(groups))):
        for r in near[:3]:
            r.crossed(level)
    scaled = dh * gain[...].astype(jnp.float32)
    inner = jnp.mean(scaled, axis=-1, keepdims=True)
    along = jnp.mean(scaled * normed, axis=-1, keepdims=True)
    token_grad[...] = dmid[...] + scale * (scaled - inner - normed * along)
    near[3].paired()
    for level in range(len(powers(groups))):
        near[3].crossed(level)
    for r in far:
        r.finish()
    for r in near:
        r.finish()
    for r in far + near:
        r.drain()

    @pl.loop(0, heads)
    def _(j):
        for copy in ex.scatter(j, do_in, do_all, do_send, do_recv):
            copy.wait_send()
        for copy in part_copies(j):
            copy.wait_send()
        for copy in back_copies(j):
            copy.wait_send()
        for copy in ex.give_back(j, heads, dq_staged, dq_back, dq_send, dq_recv):
            copy.wait_send()


def backward_call(n, groups, table, do_in, q_all, kv_all, ol_all, hidden, x, gain, wq, wk, wv, dmid, sums, far):
    heads, _, rows, _ = kv_all.shape
    splits = n // PARTS
    chips = n // 2
    share = rows // splits
    width, fresh = wv.shape
    low = jnp.bfloat16
    vmem, dma = pltpu.VMEM, pltpu.SemaphoreType.DMA
    inside = pl.BlockSpec(memory_space=vmem)
    shape = jax.ShapeDtypeStruct
    bits = powers(groups)
    forth, back = bits, bits[::-1]
    block = (groups, chips, 2)
    part = width // (groups * n)
    near = [block + (part, width, low), block + (part, width, low), block + (part, fresh, low),
            block + (16, 128, jnp.float32)]
    shapes = [f.shape + (low,) for f in far] + near
    return pl.pallas_call(
        functools.partial(backward_kernel, n, groups, heads, [forth, back, forth][: len(far)], [back, forth, back, forth]),
        out_shape=[shape((rows, width), jnp.float32), shape((rows, width - fresh), jnp.float32)]
        + [shape(s[3:5], jnp.float32) for s in shapes],
        in_specs=[pl.BlockSpec(memory_space=pltpu.SMEM)] + [inside] * 16 + [pl.BlockSpec(memory_space=pl.ANY)] * len(far),
        out_specs=[inside] * (6 + len(far)),
        scratch_shapes=[
            vmem((heads, n, share // 2, 128), low),
            vmem((n, share // 2, 128), low),
            vmem((n, rows, 128), jnp.float32),
            vmem((n, share // 2, 128), low),
            vmem((heads, n, share // 2, 128), low),
            vmem((heads, max(splits - 1, 1), PARTS, rows, 128), low),
            vmem((heads, max(splits - 1, 1), PARTS, rows, 128), low),
            vmem((heads, PARTS, rows, 128), low),
            vmem((PARTS * heads, splits, share // 2, 128), low),
            vmem((PARTS * heads, rows, 128), low),
        ]
        + [vmem(s[:5], s[5]) for s in near]
        + [
            dma((heads, n - 1)),
            dma((heads, n)),
            dma((heads, n - 1)),
            dma((heads, n)),
            dma((heads, max(splits - 1, 1), PARTS)),
            dma((heads, max(splits - 1, 1), PARTS)),
            dma((heads, PARTS - 1)),
            dma((heads, PARTS)),
        ]
        + reduce_scratch(groups, chips, shapes),
        compiler_params=pltpu.CompilerParams(
            collective_id=2, has_side_effects=True, vmem_limit_bytes=67043328
        ),
        name="attention_backward",
    )(table, do_in, q_all, kv_all, ol_all, hidden, x, gain, wq, wk, wv, dmid, *sums, *far)


def hand_over_kernel(count, sizes, *refs):
    ins, outs = refs[:count], refs[count + 1 : 2 * count + 1]
    held, loads, stores = refs[2 * count + 1 + len(sizes) : -2], refs[-2], refs[-1]
    for i in range(count):
        pltpu.make_async_copy(ins[i], held[i], loads.at[i]).start()
    for row, size in enumerate(sizes):
        refs[2 * count + 1 + row][...] = refs[count][row : row + 1, :size]
    for i in range(count):
        pltpu.make_async_copy(ins[i], held[i], loads.at[i]).wait()
        pltpu.make_async_copy(held[i], outs[i], stores.at[i]).start()
    for i in range(count):
        pltpu.make_async_copy(held[i], outs[i], stores.at[i]).wait()


def hand_over(arrays, small, sizes):
    shape = jax.ShapeDtypeStruct
    count = len(arrays)
    inside, outside = pl.BlockSpec(memory_space=pltpu.VMEM), pl.BlockSpec(memory_space=pl.ANY)
    return pl.pallas_call(
        functools.partial(hand_over_kernel, count, sizes),
        out_shape=[shape(a.shape, a.dtype) for a in arrays] + [shape((1, size), jnp.float32) for size in sizes],
        in_specs=[outside] * count + [inside],
        out_specs=[outside] * count + [inside] * len(sizes),
        scratch_shapes=[pltpu.VMEM(a.shape, a.dtype) for a in arrays]
        + [pltpu.SemaphoreType.DMA((count,)), pltpu.SemaphoreType.DMA((count,))],
        compiler_params=pltpu.CompilerParams(vmem_limit_bytes=60000000),
        name="hand_over",
    )(*arrays, small)


def feed_kernel(
    parts, heads, back, x, dy, bo, gain, shift, be, br, wo_in, we_in, wr_in,
    out, dmid_out, do_staged, s_gain, s_shift, s_ob, s_eb, s_rb, g_we, g_wr, g_wo,
    wo, we, wr, k_we, k_wr, k_wo, dh, load, keep,
):
    low = jnp.bfloat16
    rows, width = x.shape
    step = we.shape[1] // parts
    splits = back.shape[1]

    def total(v):
        return jnp.sum(v, axis=0, keepdims=True)

    def columns(c):
        return pl.ds(pl.multiple_of(c * step, 128), step)

    def fetch(c):
        return (pltpu.make_async_copy(we_in.at[:, columns(c)], we.at[:, columns(c)], load.at[c]),
                pltpu.make_async_copy(wr_in.at[columns(c)], wr.at[columns(c)], load.at[parts + c]))

    def store(c):
        return (pltpu.make_async_copy(k_we.at[:, columns(c)], g_we.at[:, columns(c)], keep.at[c]),
                pltpu.make_async_copy(k_wr.at[columns(c)], g_wr.at[columns(c)], keep.at[parts + c]))

    first = pltpu.make_async_copy(wo_in, wo, load.at[2 * parts])
    first.start()
    for c in range(parts):
        for copy in fetch(c):
            copy.start()
    att = join_rows(back).astype(low)
    first.wait()
    mid = x[...].astype(jnp.float32) + product(att, wo[...]) + bo[...]
    normed, scale = normal_rows(mid)
    second = (normed * gain[...] + shift[...]).astype(low)
    second_across = jnp.transpose(second)
    seed = dy[...]
    seed_full = seed.astype(jnp.float32)
    s_rb[...] = total(seed_full)
    dmid_out[...] = mid + br[...]
    dh[...] = jnp.zeros((rows, width), jnp.float32)

    @pl.loop(0, parts)
    def _(c):
        for copy in fetch(c):
            copy.wait()
        expand, reduce = we[:, columns(c)], wr[columns(c)]
        u = product(second, expand) + be[:, columns(c)]
        square = u * u
        t = jnp.tanh(math.sqrt(2 / math.pi) * (u + 0.044715 * (u * square)))
        z = (0.5 * u * (1.0 + t)).astype(low)
        slope = 0.5 * (1.0 + t) + (0.5 * math.sqrt(2 / math.pi)) * u * (1.0 - t * t) * (1.0 + (3 * 0.044715) * square)
        du_full = (slope * product_right(seed, reduce)).astype(low)
        s_eb[:, columns(c)] = total(du_full.astype(jnp.float32))
        dmid_out[...] += product(z, reduce)
        dh[...] += product_right(du_full, expand)
        k_wr[columns(c)] = product(jnp.transpose(z), seed).astype(low)
        k_we[:, columns(c)] = product(second_across, du_full).astype(low)
        for copy in store(c):
            copy.start()

    out[...] = dmid_out[...].astype(low)
    back_normed = dh[...]
    s_gain[...] = total(back_normed * normed)
    s_shift[...] = total(back_normed)
    scaled = back_normed * gain[...]
    inner = jnp.mean(scaled, axis=-1, keepdims=True)
    along = jnp.mean(scaled * normed, axis=-1, keepdims=True)
    dmid = seed_full + scale * (scaled - inner - normed * along)
    dmid_out[...] = dmid
    branch = dmid.astype(low)
    s_ob[...] = total(branch.astype(jnp.float32))
    k_wo[...] = product(jnp.transpose(att), branch).astype(low)
    last = pltpu.make_async_copy(k_wo, g_wo, keep.at[2 * parts])
    last.start()
    for group in range(width // 256):
        datt = product_right(branch, wo[group * 256 : (group + 1) * 256, :])

        def put(head, split, v, group=group):
            head = head + 4 * group
            do_staged[head // heads, head % heads, split] = v.astype(low)

        pack_heads(datt, splits, put)
    for c in range(parts):
        for copy in store(c):
            copy.wait()
    last.wait()


def feed_call(back, x, dy, bo, gain, shift, be, br, wo, we, wr):
    rows, width = x.shape
    inner = we.shape[1]
    parts = inner // width
    heads = back.shape[0] // PARTS
    splits = back.shape[1]
    low, full = jnp.bfloat16, jnp.float32
    vmem, dma = pltpu.VMEM, pltpu.SemaphoreType.DMA
    inside, outside = pl.BlockSpec(memory_space=vmem), pl.BlockSpec(memory_space=pl.ANY)
    shape = jax.ShapeDtypeStruct
    return pl.pallas_call(
        functools.partial(feed_kernel, parts, heads),
        out_shape=[
            shape((rows, width), low),
            shape((rows, width), full),
            shape((PARTS, heads) + back.shape[1:], low),
            shape((1, width), full),
            shape((1, width), full),
            shape((1, width), full),
            shape((1, inner), full),
            shape((1, width), full),
            shape(we.shape, low),
            shape(wr.shape, low),
            shape(wo.shape, low),
        ],
        in_specs=[inside] * 8 + [outside] * 3,
        out_specs=[inside] * 8 + [outside] * 3,
        scratch_shapes=[
            vmem(wo.shape, low), vmem(we.shape, low), vmem(wr.shape, low),
            vmem(we.shape, low), vmem(wr.shape, low), vmem(wo.shape, low),
            vmem((rows, width), full),
            dma((2 * parts + 1,)), dma((2 * parts + 1,)),
        ],
        compiler_params=pltpu.CompilerParams(vmem_limit_bytes=64000000),
        name="feed_forward",
    )(back, x, dy, bo, gain, shift, be, br, wo, we, wr)


def body(
    tokens,
    first_values,
    placement,
    cotangent,
    *parts,
):
    groups, rows, width = tokens.shape
    n = lax.axis_size("seq")
    small = (0, 1, 3, 6, 8, 9, 10, 12, 14)
    large = (2, 4, 5, 7, 11, 13)
    done = forward_call(n, lax.axis_size("grp"), placement, tokens[0], first_values[0],
                        [parts[i][None] for i in small], [parts[i] for i in large])
    hidden, q_all, kv_all, ol_all, back = done[:5]
    whole = [None] * 15
    for i, v in zip(large, done[5:11]):
        whole[i] = v.reshape(-1, v.shape[-1])
    for i, v in zip(small, done[11:]):
        whole[i] = v[0]
    layer_output, dmid, do_staged, *sums, g_we, g_wr, g_wo = feed_call(
        back, tokens[0], cotangent[0], whole[8][None], whole[9][None], whole[10][None], whole[12][None],
        whole[14][None], whole[7], whole[11], whole[13],
    )
    block = (lax.axis_size("grp"), n // 2, 2)
    far = [v.reshape(block + (-1, v.shape[1])) for v in (g_we, g_wr, g_wo)]
    inside = far if n <= 8 else []
    done = backward_call(
        n, block[0], placement, do_staged, q_all, kv_all, ol_all, hidden, tokens[0],
        whole[0][None], whole[2], whole[4], whole[5], dmid, [sums[0], sums[1], sums[2], sums[3], sums[4]],
        inside,
    )
    token_grad, first_grad = done[:2]
    if not inside:
        forth = powers(block[0])
        done = done[:2] + reduce_call(block[0], block[1], far, [forth, forth[::-1], forth]) + done[2:]
    g_we, g_wr, g_wo, g_wk, g_wq, g_wv, g_small = done[2:]
    sizes = [parts[i].shape[0] for i in small]
    out = hand_over([token_grad, first_grad, g_wq, g_wk, g_wv, g_wo, g_we, g_wr], g_small, sizes)
    owned = [None] * 15
    for i, v in zip((2, 4, 5, 7, 11, 13), out[2:8]):
        owned[i] = v
    for i, v in zip(small, out[8:]):
        owned[i] = v.reshape(-1)
    return (layer_output[None], out[0][None], out[1][None]) + tuple(owned)


def solution(mesh):
    spread = P("grp", "seq", None)
    both = ("grp", "seq")
    vector, matrix = P(both), P(both, None)
    kinds = (vector, vector, matrix, vector, matrix, matrix, vector, matrix, vector, vector, vector,
             matrix, vector, matrix, vector)
    in_specs = (spread, spread, P("grp", None), spread) + kinds
    out_specs = (spread, spread, spread) + kinds
    return jax.shard_map(body, mesh=mesh, in_specs=in_specs, out_specs=out_specs, check_vma=False)
```

```python
import functools
import math

import jax
import jax.numpy as jnp
from jax import lax
from jax.experimental import pallas as pl
from jax.experimental.pallas import tpu as pltpu
from jax.sharding import PartitionSpec as P

MESH = pl.DeviceIdType.MESH


def powers(count):
    out, bit = [], 1
    while bit < count:
        out.append(bit)
        bit *= 2
    return out


def remote(src, dst, send, recv, device):
    return pltpu.make_async_remote_copy(
        src_ref=src, dst_ref=dst, send_sem=send, recv_sem=recv,
        device_id=device, device_id_type=MESH,
    )


def enter(devices):
    barrier = pltpu.get_barrier_semaphore()
    for device in devices:
        pl.semaphore_signal(barrier, inc=1, device_id=device, device_id_type=MESH)
    pl.semaphore_wait(barrier, len(devices))


class Gather:
    def __init__(self, groups, chips, bits, shard, full, chain_send, level_send, recv, pair, own,
                 direct=False):
        self.direct = direct
        self.groups, self.chips, self.bits = groups, chips, bits
        self.shard, self.full = shard, full
        self.chain_send, self.level_send, self.recv, self.pair, self.own = chain_send, level_send, recv, pair, own
        self.g = lax.axis_index("grp")
        seq = lax.axis_index("seq")
        self.s, self.z, self.c = seq, seq // 2, seq % 2

    def block(self, g, z, c):
        return self.full.at[g, z, c]

    def source(self, mask, z, first):
        return self.shard if first else self.block(self.g ^ mask, z, self.c)

    def chain(self, z, step, first):
        side = 0 if step < 0 else 1
        return remote(self.source(0, z, first), self.block(self.g, z, self.c),
                      self.chain_send.at[z, side], self.recv.at[self.g, z],
                      {"seq": self.s + 2 * step})

    def cross(self, level, mask, z, first):
        g = self.g ^ mask
        return remote(self.source(mask, z, first), self.block(g, z, self.c),
                      self.level_send.at[level], self.recv.at[g, z],
                      {"grp": self.g ^ self.bits[level]})

    def held(self, level):
        masks = [0]
        for bit in self.bits[:level]:
            masks = masks + [m ^ bit for m in masks]
        return masks

    def here(self, mask, z):
        g = self.g ^ mask
        pltpu.make_async_copy(self.block(g, z, self.c), self.block(g, z, self.c), self.recv.at[g, z]).wait()

    def begin(self):
        self.begin_chain()
        self.begin_cross()

    def begin_chain(self):
        copy = pltpu.make_async_copy(self.shard, self.block(self.g, self.z, self.c), self.own)
        copy.start()
        if self.direct:
            for out in self.direct_copies():
                out.start()
            return

        @pl.when(self.z > 0)
        def _():
            self.chain(self.z, -1, True).start()

        @pl.when(self.z < self.chips - 1)
        def _():
            self.chain(self.z, 1, True).start()

    def direct_copies(self):
        out = []
        for off in range(1, self.chips):
            chip = lax.rem(self.z + off, self.chips)
            out.append(remote(self.shard, self.block(self.g, self.z, self.c), self.chain_send.at[off, 0],
                              self.recv.at[self.g, self.z], {"seq": 2 * chip + self.c}))
        return out

    def begin_cross(self):
        for level in range(len(self.bits)):
            self.cross(level, 0, self.z, True).start()

    def at(self, distance, body):
        if distance == 0:
            body(self.z, 0)
            return

        @pl.when(self.z >= distance)
        def _():
            body(self.z - distance, 1)

        @pl.when(self.z + distance < self.chips)
        def _():
            body(self.z + distance, -1)

    def along(self, distance):
        self.along_chain(distance)
        self.along_cross(distance)

    def along_chain(self, distance):
        def body(z, step):
            self.here(0, z)
            if self.direct:
                return
            onward = self.z < self.chips - 1 if step > 0 else self.z > 0

            @pl.when(onward)
            def _():
                self.chain(z, step, False).start()

        self.at(distance, body)

    def along_cross(self, distance):
        def body(z, step):
            for level in range(len(self.bits)):
                self.cross(level, 0, z, False).start()

        self.at(distance, body)

    def over(self, level, distance):
        def body(z, step):
            for mask in self.held(level):
                mask = mask ^ self.bits[level]
                self.here(mask, z)
                for later in range(level + 1, len(self.bits)):
                    self.cross(later, mask, z, False).start()

        self.at(distance, body)

    def swap_copy(self):
        mine = self.full.at[:, :, self.c]
        return remote(mine, mine, self.pair.at[0], self.pair.at[1], {"seq": self.s ^ 1})

    def swap(self):
        pltpu.make_async_copy(self.shard, self.shard, self.own).wait()
        self.swap_copy().start()

    def finish(self):
        self.swap_copy().wait_send()
        other = self.full.at[:, :, 1 - self.c]
        pltpu.make_async_copy(other, other, self.pair.at[1]).wait()
        self.sent()

    def sent(self):
        if self.direct:
            for out in self.direct_copies():
                out.wait_send()
        else:
            self.chain_sent()
        for level in range(len(self.bits)):
            sent = self.full.at[pl.ds(0, 2 ** level), :, 0]
            pltpu.make_async_copy(sent, sent, self.level_send.at[level]).wait()

    def chain_sent(self):
        @pl.when(self.z > 0)
        def _():
            self.chain(self.z, -1, True).wait_send()

        @pl.when(self.z < self.chips - 1)
        def _():
            self.chain(self.z, 1, True).wait_send()

        for distance in range(1, self.chips):
            def body(z, step):
                onward = self.z < self.chips - 1 if step > 0 else self.z > 0

                @pl.when(onward)
                def _():
                    self.chain(z, step, False).wait_send()

            self.at(distance, body)


def gather_semaphores(count, groups, chips):
    dma = pltpu.SemaphoreType.DMA
    levels = max(len(powers(groups)), 1)
    return [dma((count, chips, 2)), dma((count, levels)), dma((count, groups, chips)), dma((count, 2)), dma((count,))]


def neighbours(groups, n):
    g, s = lax.axis_index("grp"), lax.axis_index("seq")
    out = [{"grp": g ^ bit} for bit in powers(groups)]
    out += [{"seq": s ^ 1}, {"seq": lax.rem(s + 2, n)}, {"seq": lax.rem(s + n - 2, n)}]
    return out


def gather_kernel(groups, chips, orders, *refs):
    count = len(orders)
    shards, fulls, sems = refs[:count], refs[count:2 * count], refs[2 * count:]
    enter(neighbours(groups, 2 * chips))
    gathers = [Gather(groups, chips, orders[i], shards[i], fulls[i], *[s.at[i] for s in sems]) for i in range(count)]
    run_gathers(gathers)


def run_gathers(gathers):
    chips, levels = gathers[0].chips, len(gathers[0].bits)
    for g in gathers:
        g.begin()
    for distance in range(chips + levels):
        for g in gathers:
            if distance + 1 < chips:
                g.along(distance + 1)
            for level in range(levels):
                if 0 <= distance - level < chips:
                    g.over(level, distance - level)
    for g in gathers:
        g.swap()
    for g in gathers:
        g.finish()


def gather_call(groups, chips, shards, orders):
    count = len(shards)
    return pl.pallas_call(
        functools.partial(gather_kernel, groups, chips, orders),
        out_shape=[jax.ShapeDtypeStruct((groups, chips, 2) + x.shape, x.dtype) for x in shards],
        in_specs=[pl.BlockSpec(memory_space=pl.ANY)] * count,
        out_specs=[pl.BlockSpec(memory_space=pl.ANY)] * count,
        scratch_shapes=gather_semaphores(count, groups, chips),
        compiler_params=pltpu.CompilerParams(collective_id=0, has_side_effects=True),
        name="gather_parameters",
    )(*shards)


class Reduce:
    def __init__(self, groups, chips, bits, partial, shard, own, landed, halves, finals, sems,
                 chain=False):
        self.chain = chain
        self.groups, self.chips, self.bits = groups, chips, bits
        self.partial, self.shard, self.own, self.landed = partial, shard, own, landed
        self.halves, self.finals = halves, finals
        self.load, self.pair, self.level_send, self.level_recv, self.chip_send, self.chip_recv = sems
        self.g = lax.axis_index("grp")
        self.s = lax.axis_index("seq")
        self.z, self.c = self.s // 2, self.s % 2

    def masks(self, level):
        out = [0]
        for bit in self.bits[level:]:
            out = out + [m ^ bit for m in out]
        return out

    def load_copy(self):
        return pltpu.make_async_copy(self.partial.at[:, :, self.c], self.own, self.load.at[0])

    def pair_copy(self):
        return remote(self.partial.at[:, :, 1 - self.c], self.landed, self.pair.at[0], self.pair.at[1],
                      {"seq": self.s ^ 1})

    def begin(self):
        self.pair_copy().start()
        self.load_copy().start()

    def paired(self):
        self.load_copy().wait()
        self.pair_copy().wait_recv()

        @pl.loop(0, self.groups)
        def _(g):
            self.own[g] = self.add(self.own[g], self.landed[g])

        self.cross_start(0)

    def add(self, a, b):
        return a + b

    def cross_copies(self, level):
        bit = self.bits[level]
        out = []
        for where, mask in enumerate(self.masks(level + 1)):
            out.append(remote(self.own.at[self.g ^ bit ^ mask], self.halves[level].at[where],
                              self.level_send.at[level, where], self.level_recv.at[level, where],
                              {"grp": self.g ^ bit}))
        return out

    def cross_start(self, level):
        if level < len(self.bits):
            for copy in self.cross_copies(level):
                copy.start()
        else:
            self.chip_start()

    def chip_start(self):
        if self.chain:
            self.chain_first()
        else:
            for copy in self.chip_copies():
                copy.start()

    def crossed(self, level, onward=True):
        copies = self.cross_copies(level)
        for where, mask in enumerate(self.masks(level + 1)):
            copies[where].wait_recv()
            g = self.g ^ mask
            self.own[g] = self.add(self.own[g], self.halves[level][where])
        if onward:
            self.cross_start(level + 1)

    def chain_copy(self, block, step):
        side = 0 if step > 0 else 1
        return remote(self.own.at[self.g, block], self.finals.at[side, block], self.chip_send.at[side, block],
                      self.chip_recv.at[side, block], {"seq": self.s + 2 * step})

    def chain_add(self, block, side):
        landed = self.finals.at[side, block]
        pltpu.make_async_copy(landed, landed, self.chip_recv.at[side, block]).wait()
        self.own[self.g, block] = self.add(self.own[self.g, block], self.finals[side, block])

    def chain_first(self):
        last = self.chips - 1

        @pl.when(self.z == 0)
        def _():
            for block in range(last, 0, -1):
                self.chain_copy(block, 1).start()

        @pl.when(self.z == last)
        def _():
            for block in range(last):
                self.chain_copy(block, -1).start()

    def chained(self, near_end):
        last = self.chips - 1
        left = self.z < self.chips // 2
        right = jnp.logical_not(left)
        for block in range(last, 0, -1):
            @pl.when((self.z > 0) & (self.z < block) & (left if near_end else right))
            def _():
                self.chain_add(block, 0)
                self.chain_copy(block, 1).start()

        for block in range(last):
            @pl.when((self.z < last) & (self.z > block) & (right if near_end else left))
            def _():
                self.chain_add(block, 1)
                self.chain_copy(block, -1).start()

    def chain_finish(self):
        last = self.chips - 1

        @pl.when(self.z > 0)
        def _():
            self.chain_add(self.z, 0)

        @pl.when(self.z < last)
        def _():
            self.chain_add(self.z, 1)

        self.shard[...] = self.own[self.g, self.z].astype(jnp.float32)

    def chain_drain(self):
        for block in range(self.chips):
            @pl.when(self.z < block)
            def _():
                self.chain_copy(block, 1).wait_send()

            @pl.when(self.z > block)
            def _():
                self.chain_copy(block, -1).wait_send()

    def chip_copies(self):
        out = []
        for off in range(1, self.chips):
            chip = lax.rem(self.z + off, self.chips)
            out.append(remote(self.own.at[self.g, chip], self.finals.at[off - 1], self.chip_send.at[off - 1],
                              self.chip_recv.at[off - 1], {"seq": 2 * chip + self.c}))
        return out

    def finish(self):
        total = self.own[self.g, self.z].astype(jnp.float32)
        for off, copy in enumerate(self.chip_copies()):
            copy.wait_recv()
            total = total + self.finals[off].astype(jnp.float32)
        self.shard[...] = total

    def drain(self):
        self.pair_copy().wait_send()
        for level in range(len(self.bits)):
            for copy in self.cross_copies(level):
                copy.wait_send()
        if self.chain:
            self.chain_drain()
        else:
            for copy in self.chip_copies():
                copy.wait_send()


def reduce_steps(reduces):
    levels = len(reduces[0].bits)
    stages = [lambda r: r.begin(), lambda r: r.paired()]
    for level in range(levels):
        stages.append(lambda r, level=level: r.crossed(level))
    stages += [lambda r: r.finish(), lambda r: r.drain()]
    return [functools.partial(stage, r) for stage in stages for r in reduces]


def reduce_scratch(groups, chips, shapes, chain=False):
    vmem, dma = pltpu.VMEM, pltpu.SemaphoreType.DMA
    levels = len(powers(groups))
    out = []
    for _, _, _, rows, cols, dtype in shapes:
        out += [vmem((groups, chips, rows, cols), dtype), vmem((groups, chips, rows, cols), dtype)]
        out += [vmem((groups >> (level + 1), chips, rows, cols), dtype) for level in range(levels)]
        out += [vmem((2, chips, rows, cols) if chain else (max(chips - 1, 1), rows, cols), dtype)]
        out += [dma((1,)), dma((2,)), dma((max(levels, 1), max(groups // 2, 1))),
                dma((max(levels, 1), max(groups // 2, 1))), dma((2, chips) if chain else (max(chips - 1, 1),)),
                dma((2, chips) if chain else (max(chips - 1, 1),))]
    return out


def make_reduces(groups, chips, orders, partials, shards, scratch, chain=False):
    levels = len(powers(groups))
    each = 2 + levels + 1 + 6
    out = []
    for i, (partial, shard) in enumerate(zip(partials, shards)):
        refs = scratch[i * each : (i + 1) * each]
        out.append(Reduce(groups, chips, orders[i], partial, shard, refs[0], refs[1], refs[2 : 2 + levels],
                          refs[2 + levels], refs[3 + levels :], chain))
    return out


def reduce_kernel(groups, chips, orders, *refs):
    count = len(orders)
    enter(neighbours(groups, 2 * chips))
    for step in reduce_steps(make_reduces(groups, chips, orders, refs[:count], refs[count : 2 * count],
                                          refs[2 * count :])):
        step()


def reduce_call(groups, chips, partials, orders):
    count = len(partials)
    shapes = [p.shape + (p.dtype,) for p in partials]
    return pl.pallas_call(
        functools.partial(reduce_kernel, groups, chips, orders),
        out_shape=[jax.ShapeDtypeStruct(p.shape[3:], jnp.float32) for p in partials],
        in_specs=[pl.BlockSpec(memory_space=pl.ANY)] * count,
        out_specs=[pl.BlockSpec(memory_space=pltpu.VMEM)] * count,
        scratch_shapes=reduce_scratch(groups, chips, shapes),
        compiler_params=pltpu.CompilerParams(collective_id=3, has_side_effects=True, vmem_limit_bytes=64000000),
        name="reduce_gradients",
    )(*partials)


PARTS = 4
NEG = -1e30
EPS = 1e-05


def lanes(shape):
    return lax.broadcasted_iota(jnp.int32, shape, len(shape) - 1)


def swap_lanes(v):
    return pltpu.roll(v, 64, 1)


def fold(v, high):
    half = v.shape[0] // 2
    top, bottom = v[:half], v[half:]
    low = lanes(top.shape) < 64
    if high:
        return jnp.where(low, swap_lanes(top), bottom)
    return jnp.where(low, top, swap_lanes(bottom))


def unfold(v, high):
    low = lanes(v.shape) < 64
    zero = jnp.zeros_like(v)
    if high:
        return jnp.concatenate([jnp.where(low, zero, swap_lanes(v)), jnp.where(low, zero, v)], axis=0)
    return jnp.concatenate([jnp.where(low, v, zero), jnp.where(low, swap_lanes(v), zero)], axis=0)


def product(a, b):
    return lax.dot_general(a, b, (((1,), (0,)), ((), ())), preferred_element_type=jnp.float32)


def product_right(a, b):
    return lax.dot_general(a, b, (((1,), (1,)), ((), ())), preferred_element_type=jnp.float32)


def product_left(a, b):
    return lax.dot_general(a, b, (((0,), (0,)), ((), ())), preferred_element_type=jnp.float32)


def normal_rows(v):
    mean = jnp.mean(v, axis=-1, keepdims=True)
    centred = v - mean
    var = jnp.mean(centred * centred, axis=-1, keepdims=True)
    scale = lax.rsqrt(var + EPS)
    return centred * scale, scale


def pack_heads(v, splits, store):
    size = v.shape[0] // splits
    for tile in range(v.shape[1] // 128):
        for split in range(splits):
            part = v[split * size : (split + 1) * size, tile * 128 : (tile + 1) * 128]
            store(2 * tile, split, fold(part, False))
            store(2 * tile + 1, split, fold(part, True))


def slots_of(table, count):
    out = []
    for piece in range(count):
        slot = jnp.int32(0)
        for place in range(count):
            slot = slot + jnp.where(table[0, place] == piece, place, 0)
        out.append(jnp.minimum(slot, count - 1))
    return out


def pick(values, index):
    out = values[0]
    for i in range(1, len(values)):
        out = jnp.where(index == i, values[i], out)
    return out


class Exchange:
    def __init__(self, n):
        self.n = n
        self.splits = n // PARTS
        self.s = lax.axis_index("seq")
        self.part, self.split = self.s // self.splits, lax.rem(self.s, self.splits)

    def peers(self):
        return [{"seq": lax.rem(self.s + off, self.n)} for off in range(1, self.n)]

    def other(self, off):
        return lax.rem(self.s + off, self.n)

    def scatter(self, j, staged, landed, send, recv):
        out = []
        for off in range(1, self.n):
            t = self.other(off)
            out.append(remote(staged.at[t // self.splits, j, lax.rem(t, self.splits)], landed.at[j, self.s],
                              send.at[j, off - 1], recv.at[j, self.s], {"seq": t}))
        return out

    def own(self, j, staged, landed, recv):
        return pltpu.make_async_copy(staged.at[self.part, j, self.split], landed.at[j, self.s], recv.at[j, self.s])

    def spread(self, j, staged, landed, send, recv):
        out = []
        for off in range(1, PARTS):
            part = lax.rem(self.part + off, PARTS)
            out.append(remote(staged.at[part, j], landed.at[j, self.s], send.at[j, off - 1],
                              recv.at[j, self.s], {"seq": part * self.splits + self.split}))
        return out

    def own_rows(self, j, staged, landed, recv):
        return pltpu.make_async_copy(staged.at[self.part, j], landed.at[j, self.s], recv.at[j, self.s])

    def relay(self, j, off, landed, send, recv):
        slot = lax.rem(self.part + off, PARTS) * self.splits + self.split
        out = []
        for hop in range(1, self.splits):
            split = lax.rem(self.split + hop, self.splits)
            out.append(remote(landed.at[j, slot], landed.at[j, slot], send.at[j, off, hop - 1],
                              recv.at[j, slot], {"seq": self.part * self.splits + split}))
        return slot, out

    def give_back(self, j, heads, staged, landed, send, recv):
        out = []
        row = self.part * heads + j
        for off in range(1, self.n):
            t = self.other(off)
            out.append(remote(staged.at[j, t], landed.at[row, self.split], send.at[j, off - 1],
                              recv.at[j, self.s], {"seq": t}))
        return out

    def keep_own(self, j, heads, staged, landed, recv):
        return pltpu.make_async_copy(staged.at[j, self.s], landed.at[self.part * heads + j, self.split],
                                     recv.at[j, self.s])


def here(ref, sem):
    pltpu.make_async_copy(ref, ref, sem).wait()


def gather_vector(full, row, size):
    count = full.shape[0]
    part = size // count
    rows = full[:, row, :].astype(jnp.bfloat16)
    at = lax.broadcasted_iota(jnp.int32, (128, size), 0)
    to = lax.broadcasted_iota(jnp.int32, (128, size), 1)
    place = jnp.where(lax.rem(to, part) == at, 1.0, 0.0).astype(jnp.bfloat16)
    spread = product(rows, place)
    lane = lax.broadcasted_iota(jnp.int32, (count, size), 1)
    owner = lax.broadcasted_iota(jnp.int32, (count, size), 0)
    mine = (lane >= owner * part) & (lane < owner * part + part)
    return jnp.sum(jnp.where(mine, spread, 0.0), axis=0, keepdims=True)


def forward_kernel(n, groups, heads, orders, sizes, table, x, first, *refs):
    vectors, shards, refs = refs[:9], refs[9:15], refs[15:]
    hidden_out, q_out, kv_out, ol_out, back = refs[:5]
    fulls_out, vectors_out, refs = refs[5:11], refs[11:20], refs[20:]
    hidden_held, q_all, kv_all, ol_all, wq_full, wk_full, wv_full, stores, head_stores = refs[:9]
    fulls, refs = (wq_full, wk_full, wv_full) + fulls_out[3:], refs[9:]
    leaving = [(wq_full, fulls_out[0]), (wk_full, fulls_out[1]), (wv_full, fulls_out[2]), (hidden_held, hidden_out)]

    def leave(i):
        return pltpu.make_async_copy(leaving[i][0], leaving[i][1], stores.at[i])

    def leave_head(j):
        return [pltpu.make_async_copy(held.at[j], out.at[j], head_stores.at[k, j])
                for k, (held, out) in enumerate(((q_all, q_out), (kv_all, kv_out), (ol_all, ol_out)))]

    packed, small_full, q_staged, kv_staged, o_staged, q_work, kv_work = refs[:7]
    q_send, kv_send, relay_send, o_send, q_recv, kv_recv, o_recv = refs[7:14]
    sems = refs[14:]
    ex = Exchange(n)
    chips = n // 2
    bits = powers(groups)
    levels = len(bits)
    enter(ex.peers() + [{"grp": lax.axis_index("grp") ^ bit} for bit in bits])
    gathers = [
        Gather(groups, chips, order, shard, full, *[s.at[i] for s in sems])
        for i, (order, shard, full) in enumerate(zip(orders, (packed,) + shards, (small_full,) + fulls))
    ]
    near, far = gathers[:4], gathers[4:]
    packed[...] = jnp.zeros(packed.shape, jnp.float32)
    for row, vector in enumerate(vectors):
        packed[row : row + 1, : vector.shape[1]] = vector[...].astype(jnp.float32)
    for g in (near[1], near[2], near[3], near[0]):
        g.begin()
    splits = ex.splits
    rows, width = x.shape
    share = rows // splits
    half = n // 2
    fresh = width - first.shape[1]
    normed, _ = normal_rows(x[...].astype(jnp.float32))

    def steps(some, along=1):
        out = []
        for distance in range(chips + levels):
            for g in some:
                if along == 1 and distance + 1 < chips:
                    out.append(functools.partial(g.along, distance + 1))
                if along == 2 and 2 <= distance + 1 < chips:
                    out.append(functools.partial(g.along_cross, distance + 1))
                for level in range(levels):
                    if 0 <= distance - level < chips:
                        out.append(functools.partial(g.over, level, distance - level))
        return out

    order = steps(near)
    cut = (min(len(order), len(near) * (1 + levels)), 3 * len(order) // 4)
    for step in order[: cut[0]]:
        step()
    for g in far:
        g.begin_chain()
    for step in order[cut[0] : cut[1]]:
        step()
    if chips > 1:
        for g in far:
            g.along_chain(1)
    for step in order[cut[1] :]:
        step()
    for g in near:
        g.swap()
    for g in far:
        g.begin_cross()
    for distance in range(1, min(2, chips)):
        for g in far:
            g.along_cross(distance)
    for distance in range(2, chips):
        for g in far:
            g.along_chain(distance)
    for g in near:
        g.finish()
    small = small_full[...].reshape((2 * chips * groups,) + packed.shape)
    for row in range(4):
        vectors_out[row][...] = gather_vector(small, row, sizes[row])
    gain, shift, bq, bv = vectors_out[:4]
    wq, wk, wv = [fulls[i][...].reshape(width, -1) for i in range(3)]
    hidden = (normed * gain[...] + shift[...]).astype(jnp.bfloat16)
    hidden_held[...] = hidden
    for i in range(4):
        leave(i).start()
    for step in range(width // 256):
        cols = slice(step * 256, (step + 1) * 256)
        q = product(hidden, wq[:, cols]) + bq[:, cols]

        def store(head, split, v, step=step):
            head = head + 4 * step
            q_staged[head // heads, head % heads, split] = (v * 0.125).astype(jnp.bfloat16)

        pack_heads(q, splits, store)
        k = product(hidden, wk[:, cols])
        for tile in range(2):
            at = step * 256 + tile * 128
            if at < fresh:
                v = product(hidden, wv[:, at : at + 128]) + bv[:, at : at + 128]
            else:
                v = first[:, at - fresh : at - fresh + 128].astype(jnp.float32)
            kt = k[:, tile * 128 : (tile + 1) * 128]
            low = lanes(kt.shape) < 64
            head = at // 64
            kv_staged[head // heads, head % heads] = jnp.where(low, kt, swap_lanes(v)).astype(jnp.bfloat16)
            head = head + 1
            kv_staged[head // heads, head % heads] = jnp.where(low, swap_lanes(kt), v).astype(jnp.bfloat16)

    @pl.loop(0, heads)
    def _(j):
        for copy in ex.spread(j, kv_staged, kv_all, kv_send, kv_recv):
            copy.start()
        for copy in ex.scatter(j, q_staged, q_all, q_send, q_recv):
            copy.start()
        ex.own(j, q_staged, q_all, q_recv).start()
        ex.own_rows(j, kv_staged, kv_all, kv_recv).start()

    slot = slots_of(table, n)
    row = lax.broadcasted_iota(jnp.int32, (share, rows), 0) + ex.split * share
    own_mask = lax.broadcasted_iota(jnp.int32, (share, rows), 1) <= row

    def piece(j, place, at, keys):
        q = unfold(q_work[at].astype(jnp.float32), False).astype(jnp.bfloat16)
        blocks = [kv_work[k] for k in keys] + [kv_work[at]]
        scores = [product_right(q, block) for block in blocks]
        scores[-1] = jnp.where(own_mask, scores[-1], NEG)
        top = scores[0]
        for s in scores[1:]:
            top = jnp.maximum(top, s)
        top = jnp.max(top, axis=1, keepdims=True)
        total = jnp.zeros((share, rows), jnp.float32)
        out = jnp.zeros((share, 128), jnp.float32)
        for s, block in zip(scores, blocks):
            weight = jnp.exp(s - top)
            total = total + weight
            out = out + product(weight.astype(jnp.bfloat16), block)
        denom = jnp.sum(total, axis=1, keepdims=True)
        out = out / denom
        ol_all[j, place] = jnp.where(lanes(out.shape) < 64, top + jnp.log(denom), out)

    later = steps(far, 2)
    cut = (len(later) // 2, 3 * len(later) // 4)
    for step in later[: cut[0]]:
        step()
    for row in range(4, 9):
        vectors_out[row][...] = gather_vector(small, row, sizes[row])

    @pl.loop(0, heads)
    def _(j):
        for off in range(PARTS):
            at, copies = ex.relay(j, off, kv_all, relay_send, kv_recv)
            here(kv_all.at[j, at], kv_recv.at[j, at])
            for copy in copies:
                copy.start()
        for t in range(n):
            here(q_all.at[j, t], q_recv.at[j, t])
        for off in range(PARTS):
            for hop in range(1, splits):
                at = lax.rem(ex.part + off, PARTS) * splits + lax.rem(ex.split + hop, splits)
                here(kv_all.at[j, at], kv_recv.at[j, at])
        for t in range(n):
            q_work[t] = q_all[j, t]
            kv_work[t] = kv_all[j, t]

        @pl.loop(0, half)
        def _(c):
            piece(j, half + c, pick(slot[half:], c), slot[:half])

        for p in range(half):
            piece(j, p, slot[p], slot[:p])
        for t in range(n):
            o_staged[j, t] = fold(ol_all[j, table[0, t]], True).astype(jnp.bfloat16)
        for copy in ex.give_back(j, heads, o_staged, back, o_send, o_recv):
            copy.start()
        ex.keep_own(j, heads, o_staged, back, o_recv).start()
        for copy in leave_head(j):
            copy.start()

        @pl.when(j == 0)
        def _():
            for step in later[cut[0] : cut[1]]:
                step()

        @pl.when(j == min(1, heads - 1))
        def _():
            for step in later[cut[1] :]:
                step()
            for g in far:
                g.swap()

    @pl.loop(0, heads)
    def _(j):
        for copy in ex.spread(j, kv_staged, kv_all, kv_send, kv_recv):
            copy.wait_send()
        for copy in ex.scatter(j, q_staged, q_all, q_send, q_recv):
            copy.wait_send()
        for off in range(PARTS):
            for copy in ex.relay(j, off, kv_all, relay_send, kv_recv)[1]:
                copy.wait_send()
        for copy in ex.give_back(j, heads, o_staged, back, o_send, o_recv):
            copy.wait_send()
        for t in range(n):
            landed = back.at[t // splits * heads + j, t % splits]
            here(landed, o_recv.at[j, t])
    for g in far:
        g.finish()
    for i in range(4):
        leave(i).wait()

    @pl.loop(0, heads)
    def _(j):
        for copy in leave_head(j):
            copy.wait()


def forward_call(n, groups, table, x, first, vectors, shards):
    rows, width = x.shape
    splits = n // PARTS
    chips = n // 2
    heads = width // 64 // PARTS
    share = rows // splits
    low = jnp.bfloat16
    vmem, dma = pltpu.VMEM, pltpu.SemaphoreType.DMA
    inside, outside = pl.BlockSpec(memory_space=vmem), pl.BlockSpec(memory_space=pl.ANY)
    shape = jax.ShapeDtypeStruct
    bits = powers(groups)
    forth, behind = bits, bits[::-1]
    sizes = [v.shape[1] * groups * n for v in vectors]
    block = (groups, chips, 2)
    return pl.pallas_call(
        functools.partial(forward_kernel, n, groups, heads, [forth, forth, behind, forth, behind, forth, behind], sizes),
        out_shape=[
            shape((rows, width), low),
            shape((heads, n, share // 2, 128), low),
            shape((heads, n, rows, 128), low),
            shape((heads, n, share, 128), jnp.float32),
            shape((PARTS * heads, splits, share // 2, 128), low),
        ]
        + [shape(block + w.shape, low) for w in shards]
        + [shape((1, size), jnp.float32) for size in sizes],
        in_specs=[pl.BlockSpec(memory_space=pltpu.SMEM)] + [inside] * 11 + [outside] * 6,
        out_specs=[outside] * 4 + [inside] + [outside] * 6 + [inside] * 9,
        scratch_shapes=[
            vmem((rows, width), low),
            vmem((heads, n, share // 2, 128), low),
            vmem((heads, n, rows, 128), low),
            vmem((heads, n, share, 128), jnp.float32),
        ]
        + [vmem(block + w.shape, low) for w in shards[:3]]
        + [
            dma((4,)),
            dma((3, heads)),
            vmem((16, 128), jnp.float32),
            vmem(block + (16, 128), jnp.float32),
            vmem((PARTS, heads, splits, share // 2, 128), low),
            vmem((PARTS, heads, rows, 128), low),
            vmem((heads, n, share // 2, 128), low),
            vmem((n, share // 2, 128), low),
            vmem((n, rows, 128), low),
            dma((heads, n - 1)),
            dma((heads, PARTS - 1)),
            dma((heads, PARTS, max(splits - 1, 1))),
            dma((heads, n - 1)),
            dma((heads, n)),
            dma((heads, n)),
            dma((heads, n)),
        ]
        + gather_semaphores(7, groups, chips),
        compiler_params=pltpu.CompilerParams(
            collective_id=1, has_side_effects=True, vmem_limit_bytes=64000000
        ),
        name="attention_forward",
    )(table, x, first, *vectors, *shards)


def join_tiles(even, odd, high):
    low = lanes(even.shape) < 64
    if high:
        return jnp.where(low, swap_lanes(even), odd)
    return jnp.where(low, even, swap_lanes(odd))


def join_rows(back):
    heads, splits = back.shape[0], back.shape[1]
    tiles = []
    for tile in range(heads // 2):
        parts = []
        for split in range(splits):
            even = back[2 * tile, split].astype(jnp.float32)
            odd = back[2 * tile + 1, split].astype(jnp.float32)
            parts += [join_tiles(even, odd, False), join_tiles(even, odd, True)]
        tiles.append(jnp.concatenate(parts, axis=0))
    return jnp.concatenate(tiles, axis=1)


def own_columns(j, heads, wq, wk, wv):
    def column(w, head):
        tile = w[:, head // 2 * 128 : head // 2 * 128 + 128].astype(jnp.float32)
        return tile, head % 2

    tiles = []
    for w in (wq, wk, wv):
        for part in range(0, w.shape[1] // 64 // heads, 2):
            (a, high_a), (b, high_b) = column(w, part * heads + j), column(w, (part + 1) * heads + j)
            a = swap_lanes(a) if high_a else a
            b = b if high_b else swap_lanes(b)
            tiles.append(jnp.where(lanes(a.shape) < 64, a, b).astype(jnp.bfloat16))
    return jnp.concatenate(tiles, axis=1)


def in_order(some, at, parts):
    heads = len(some)
    tiles = []
    for head in range(0, heads * parts, 2):
        def column(h):
            j, part = h % heads, h // heads
            start = at + part // 2 * 128
            return some[j][:, start : start + 128], part % 2

        (a, high_a), (b, high_b) = column(head), column(head + 1)
        a = swap_lanes(a) if high_a else a
        b = b if high_b else swap_lanes(b)
        tiles.append(jnp.where(lanes(a.shape) < 64, a, b))
    return jnp.concatenate(tiles, axis=1)


def own_vectors(sums, parts, fresh_parts):
    sums = [jnp.broadcast_to(s, (8, s.shape[1])) for s in sums]
    return [in_order(sums, 0, parts)[0:1], in_order(sums, parts * 128, fresh_parts)[0:1]]


def spread_vector(vector, count):
    size = vector.shape[1]
    part = size // count
    lane = lax.broadcasted_iota(jnp.int32, (count, size), 1)
    row = lax.broadcasted_iota(jnp.int32, (count, size), 0)
    mine = (lane >= row * part) & (lane < row * part + part)
    spread = jnp.where(mine, vector, 0.0)
    at = lax.broadcasted_iota(jnp.int32, (size, 128), 0)
    to = lax.broadcasted_iota(jnp.int32, (size, 128), 1)
    pick_part = jnp.where(lax.rem(at, part) == to, 1.0, 0.0)
    return lax.dot_general(spread, pick_part, (((1,), (0,)), ((), ())), precision=lax.Precision.HIGHEST,
                           preferred_element_type=jnp.float32)


def backward_kernel(
    n, groups, heads, orders_far, orders_near,
    table, do_in, gain, s_gain2, s_bias2, s_ob, s_eb, s_rb, q_in, kv_in, ol_in, hidden_in, x_in, dmid_in,
    wq_in, wk_in, wv_in, *refs,
):
    count = len(orders_far)
    far_in, refs = refs[:count], refs[count:]
    token_grad, first_grad = refs[:2]
    far_out, refs = refs[2 : 2 + count], refs[2 + count :]
    near_out, refs = refs[: 2 * heads + 1], refs[2 * heads + 1 :]
    do_all, do_work, acc, dq_piece, dq_staged, part_staged, part_all, dkv_staged, dq_back, dkv_back = refs[:10]
    refs = refs[10:]
    near_in, refs = refs[: 2 * heads + 1], refs[2 * heads + 1 :]
    weights, h_across, refs = refs[:heads], refs[heads], refs[heads + 1 :]
    q_all, kv_all, ol_all, hidden, x, dmid, wq, wk, wv, loads = refs[:10]
    refs = refs[10:]
    do_send, do_recv, dq_send, dq_recv, part_send, part_recv, dkv_send, dkv_recv = refs[:8]
    scratch = refs[8:]

    def full_copy(source, held, at):
        pltpu.make_async_copy(source, held, loads.at[at]).wait()
        return held

    entering = [(hidden_in, hidden, 3), (wq_in, wq, 6), (wk_in, wk, 7), (wv_in, wv, 8), (q_in, q_all, 0),
                (kv_in, kv_all, 1), (ol_in, ol_all, 2), (x_in, x, 4), (dmid_in, dmid, 5)]
    ex = Exchange(n)
    chips = n // 2
    enter(ex.peers() + [{"grp": ex_g} for ex_g in [lax.axis_index("grp") ^ bit for bit in powers(groups)]])
    each = len(scratch) // (count + 2 * heads + 1)
    far = make_reduces(groups, chips, orders_far, far_in, far_out, scratch[: count * each], True)
    near = make_reduces(groups, chips, orders_near, near_in, near_out, scratch[count * each :])
    near, small = near[:-1], near[-1]
    near_last = near[-2:]
    near_first = near[:-2]
    splits = ex.splits
    rows = kv_all.shape[2]
    share = rows // splits
    half = n // 2
    fresh = wv.shape[1]

    @pl.loop(0, heads)
    def _(j):
        for copy in ex.scatter(j, do_in, do_all, do_send, do_recv):
            copy.start()
        ex.own(j, do_in, do_all, do_recv).start()

    for source, held, at in entering:
        pltpu.make_async_copy(source, held, loads.at[at]).start()
    for r in far:
        r.begin()
    for source, held, at in entering[:7]:
        full_copy(source, held, at)
    low = jnp.bfloat16
    fresh_parts = PARTS * fresh // x.shape[1]
    h_across[...] = jnp.transpose(hidden[...])
    for j in range(heads):
        weights[j][...] = own_columns(j, heads, wq, wk, wv)
    slot = slots_of(table, n)
    column = lax.broadcasted_iota(jnp.int32, (rows, share), 1) + ex.split * share
    own_mask = lax.broadcasted_iota(jnp.int32, (rows, share), 0) <= column

    def piece(j, place, at, keys):
        q = unfold(q_all[j, at].astype(jnp.float32), False).astype(jnp.bfloat16)
        grad = unfold(do_work[at].astype(jnp.float32), True)
        ol = ol_all[j, place]
        delta = jnp.sum(jnp.transpose(grad * ol), axis=0, keepdims=True)
        logsum = jnp.transpose(ol)[0:1]
        grad = grad.astype(jnp.bfloat16)
        dq = jnp.zeros((128, share), jnp.float32)
        for where, (key_place, key_slot) in enumerate(keys + [(place, at)]):
            block = kv_all[j, key_slot]
            weight = jnp.exp(product_right(block, q) - logsum)
            if where == len(keys):
                weight = jnp.where(own_mask, weight, 0.0)
            change = (weight * (product_right(block, grad) - delta)).astype(jnp.bfloat16)
            term = product(weight.astype(jnp.bfloat16), grad) + product(change, q)
            acc[key_place] = acc[key_place] + term
            dq = dq + product_left(block, change)
        dq_piece[place] = fold(jnp.transpose(dq) * 0.125, False).astype(jnp.bfloat16)

    def part_copies(j):
        out = []
        for hop in range(1, splits):
            split = lax.rem(ex.split + hop, splits)
            for part in range(PARTS):
                out.append(remote(part_staged.at[j, hop - 1, part], part_all.at[j, hop - 1, part],
                                  part_send.at[j, hop - 1, part], part_recv.at[j, hop - 1, part],
                                  {"seq": ex.part * splits + split}))
        return out

    def back_copies(j):
        out = []
        row = ex.part * heads + j
        for off in range(1, PARTS):
            part = lax.rem(ex.part + off, PARTS)
            out.append(remote(dkv_staged.at[j, part], dkv_back.at[row], dkv_send.at[j, off - 1],
                              dkv_recv.at[j, ex.part], {"seq": part * splits + ex.split}))
        return out

    @pl.loop(0, heads)
    def _(j):
        for t in range(n):
            here(do_all.at[j, t], do_recv.at[j, t])
        for t in range(n):
            do_work[t] = do_all[j, t]
            acc[t] = jnp.zeros((rows, 128), jnp.float32)

        @pl.loop(0, half)
        def _(c):
            piece(j, half + c, pick(slot[half:], c), [(p, slot[p]) for p in range(half)])

        @pl.when(j == 0)
        def _():
            for r in far:
                r.paired()

        @pl.when(j == heads - 1)
        def _():
            for r in far:
                r.crossed(0)

        for p in range(half):
            piece(j, p, slot[p], [(k, slot[k]) for k in range(p)])
        for hop in range(1, splits):
            split = lax.rem(ex.split + hop, splits)
            for part in range(PARTS):
                part_staged[j, hop - 1, part] = acc[table[0, part * splits + split]].astype(jnp.bfloat16)
        for copy in part_copies(j):
            copy.start()
        for t in range(n):
            dq_staged[j, t] = dq_piece[table[0, t]]
        for hop in range(1, splits):
            for part in range(PARTS):
                here(part_all.at[j, hop - 1, part], part_recv.at[j, hop - 1, part])
        for part in range(PARTS):
            total = acc[table[0, part * splits + ex.split]]
            for hop in range(1, splits):
                total = total + part_all[j, hop - 1, part].astype(jnp.float32)
            dkv_staged[j, part] = total.astype(jnp.bfloat16)
        for copy in back_copies(j):
            copy.start()
        pltpu.make_async_copy(dkv_staged.at[j, ex.part], dkv_back.at[ex.part * heads + j],
                              dkv_recv.at[j, ex.part]).start()
        for copy in ex.give_back(j, heads, dq_staged, dq_back, dq_send, dq_recv):
            copy.start()
        ex.keep_own(j, heads, dq_staged, dq_back, dq_recv).start()

    levels = len(powers(groups))

    def total(v):
        return jnp.sum(v, axis=0, keepdims=True)

    def project(j):
        for t in range(n):
            here(dq_back.at[t // splits * heads + j, t % splits], dq_recv.at[j, t])
        for part in range(PARTS):
            here(dkv_back.at[part * heads + j], dkv_recv.at[j, part])
        tiles = []
        for part in range(0, PARTS, 2):
            a, b = part * heads + j, part * heads + heads + j
            parts = []
            for split in range(splits):
                even, odd = dq_back[a, split].astype(jnp.float32), dq_back[b, split].astype(jnp.float32)
                parts += [join_tiles(even, odd, False), join_tiles(even, odd, True)]
            tiles.append(jnp.concatenate(parts, axis=0))
        pairs = [(dkv_back[part * heads + j].astype(jnp.float32), dkv_back[(part + 1) * heads + j].astype(jnp.float32))
                 for part in range(0, PARTS, 2)]
        tiles += [join_tiles(a, b, False) for a, b in pairs]
        tiles += [join_tiles(a, b, True) for a, b in pairs[: fresh_parts // 2]]
        grad = jnp.concatenate(tiles, axis=1)
        sums = total(grad)
        grad = grad.astype(low)
        for ref, r, value in ((near_in[2 * j + 1], near[2 * j + 1], grad[:, PARTS * 64 :]),
                              (near_in[2 * j], near[2 * j], grad[:, : PARTS * 64])):
            ref[...] = product(h_across[...], value).reshape(ref.shape).astype(low)
            r.begin()
        return product_right(grad, weights[j][...]), sums

    done = [project(j) for j in range(heads - 1)]
    for r in near_first:
        r.paired()
    for r in far:
        for level in range(1, levels):
            r.crossed(level)
    normed, scale = normal_rows(full_copy(x_in, x, 4)[...].astype(jnp.float32))
    for level in range(levels - 1):
        for r in near_first:
            r.crossed(level)
    done.append(project(heads - 1))
    for r in near_first:
        r.crossed(levels - 1)
    dh = done[0][0]
    for more, _ in done[1:]:
        dh = dh + more
    for r in near_last:
        r.paired()
    sums = [total(dh * normed), total(dh)]
    sums += own_vectors([s for _, s in done], PARTS, fresh_parts)
    sums += [s_ob[...], s_gain2[...], s_bias2[...], s_eb[...], s_rb[...]]
    devices = groups * n
    spread = [spread_vector(v, devices).reshape(devices, 1, 128) for v in sums]
    spread.append(jnp.zeros((devices, 16 - len(spread), 128), jnp.float32))
    near_in[-1][...] = jnp.concatenate(spread, axis=1).reshape(near_in[-1].shape)
    small.begin()
    for level in range(levels):
        for r in near_last:
            r.crossed(level)
        if level == 0:
            small.paired()
        else:
            small.crossed(level - 1)
    for r in far:
        r.chained(True)
    scaled = dh * gain[...].astype(jnp.float32)
    inner = jnp.mean(scaled, axis=-1, keepdims=True)
    along = jnp.mean(scaled * normed, axis=-1, keepdims=True)
    small.crossed(levels - 1)
    token_grad[...] = full_copy(dmid_in, dmid, 5)[...] + scale * (scaled - inner - normed * along)
    for pair in range(fresh // 64, PARTS * heads, 2):
        even, odd = dkv_back[pair].astype(jnp.float32), dkv_back[pair + 1].astype(jnp.float32)
        first_grad[:, pair * 64 - fresh : pair * 64 - fresh + 128] = join_tiles(even, odd, True)
    for r in far:
        r.chained(False)
    for r in far:
        r.chain_finish()
    for r in near + [small]:
        r.finish()
    for r in far + near + [small]:
        r.drain()

    @pl.loop(0, heads)
    def _(j):
        for copy in ex.scatter(j, do_in, do_all, do_send, do_recv):
            copy.wait_send()
        for copy in part_copies(j):
            copy.wait_send()
        for copy in back_copies(j):
            copy.wait_send()
        for copy in ex.give_back(j, heads, dq_staged, dq_back, dq_send, dq_recv):
            copy.wait_send()


def backward_call(n, groups, table, do_in, q_all, kv_all, ol_all, hidden, x, gain, wq, wk, wv, dmid, sums, far):
    heads, _, rows, _ = kv_all.shape
    splits = n // PARTS
    chips = n // 2
    share = rows // splits
    width, fresh = wv.shape
    low = jnp.bfloat16
    vmem, dma = pltpu.VMEM, pltpu.SemaphoreType.DMA
    inside = pl.BlockSpec(memory_space=vmem)
    shape = jax.ShapeDtypeStruct
    bits = powers(groups)
    forth, back = bits, bits[::-1]
    block = (groups, chips, 2)
    part = width // (groups * n)
    wide = 2 * PARTS * 64 + PARTS * 64 * fresh // width
    near = [block + (part, PARTS * 64, low), block + (part, wide - PARTS * 64, low)] * heads
    near += [block + (16, 128, jnp.float32)]
    shapes = [f.shape + (low,) for f in far] + near
    return pl.pallas_call(
        functools.partial(backward_kernel, n, groups, heads, [forth, back, forth][: len(far)],
                          [(forth, back)[j % 2] for j in range(2 * heads + 1)]),
        out_shape=[shape((rows, width), jnp.float32), shape((rows, width - fresh), jnp.float32)]
        + [shape(s[3:5], jnp.float32) for s in shapes],
        in_specs=[pl.BlockSpec(memory_space=pltpu.SMEM)] + [inside] * 7
        + [pl.BlockSpec(memory_space=pl.ANY)] * (9 + len(far)),
        out_specs=[inside] * (3 + 2 * heads + len(far)),
        scratch_shapes=[
            vmem((heads, n, share // 2, 128), low),
            vmem((n, share // 2, 128), low),
            vmem((n, rows, 128), jnp.float32),
            vmem((n, share // 2, 128), low),
            vmem((heads, n, share // 2, 128), low),
            vmem((heads, max(splits - 1, 1), PARTS, rows, 128), low),
            vmem((heads, max(splits - 1, 1), PARTS, rows, 128), low),
            vmem((heads, PARTS, rows, 128), low),
            vmem((PARTS * heads, splits, share // 2, 128), low),
            vmem((PARTS * heads, rows, 128), low),
        ]
        + [vmem(s[:5], s[5]) for s in near]
        + [vmem((width, wide), low)] * heads
        + [vmem((width, rows), low)]
        + [vmem(v.shape, v.dtype) for v in (q_all, kv_all, ol_all, hidden, x, dmid, wq, wk, wv)]
        + [
            dma((9,)),
            dma((heads, n - 1)),
            dma((heads, n)),
            dma((heads, n - 1)),
            dma((heads, n)),
            dma((heads, max(splits - 1, 1), PARTS)),
            dma((heads, max(splits - 1, 1), PARTS)),
            dma((heads, PARTS - 1)),
            dma((heads, PARTS)),
        ]
        + reduce_scratch(groups, chips, shapes[: len(far)], True)
        + reduce_scratch(groups, chips, shapes[len(far) :]),
        compiler_params=pltpu.CompilerParams(
            collective_id=2, has_side_effects=True, vmem_limit_bytes=67043328
        ),
        name="attention_backward",
    )(table, do_in, gain, *sums, q_all, kv_all, ol_all, hidden, x, dmid, wq, wk, wv, *far)


def hand_over_kernel(count, heads, sizes, fresh_parts, *refs):
    ins, refs = refs[:count], refs[count:]
    near, small, refs = refs[: 2 * heads], refs[2 * heads], refs[2 * heads + 1 :]
    outs, refs = refs[:count], refs[count:]
    g_wq, g_wk, g_wv = refs[:3]
    vectors, refs = refs[3 : 3 + len(sizes)], refs[3 + len(sizes) :]
    held, loads, stores = refs[:-2], refs[-2], refs[-1]
    for i in range(count):
        pltpu.make_async_copy(ins[i], held[i], loads.at[i]).start()
    some = [ref[...] for ref in near]
    g_wq[...] = in_order(some[::2], 0, PARTS)
    g_wk[...] = in_order(some[1::2], 0, PARTS)
    g_wv[...] = in_order(some[1::2], PARTS * 64, fresh_parts)
    for row, size in enumerate(sizes):
        vectors[row][...] = small[row : row + 1, :size]
    for i in range(count):
        pltpu.make_async_copy(ins[i], held[i], loads.at[i]).wait()
        pltpu.make_async_copy(held[i], outs[i], stores.at[i]).start()
    for i in range(count):
        pltpu.make_async_copy(held[i], outs[i], stores.at[i]).wait()


def hand_over(arrays, near, small, sizes, width, fresh):
    shape = jax.ShapeDtypeStruct
    count, heads = len(arrays), len(near) // 2
    rows = near[0].shape[0]
    inside, outside = pl.BlockSpec(memory_space=pltpu.VMEM), pl.BlockSpec(memory_space=pl.ANY)
    return pl.pallas_call(
        functools.partial(hand_over_kernel, count, heads, sizes, PARTS * fresh // width),
        out_shape=[shape(a.shape, a.dtype) for a in arrays]
        + [shape((rows, size), jnp.float32) for size in (width, width, fresh)]
        + [shape((1, size), jnp.float32) for size in sizes],
        in_specs=[outside] * count + [inside] * (2 * heads + 1),
        out_specs=[outside] * count + [inside] * (3 + len(sizes)),
        scratch_shapes=[pltpu.VMEM(a.shape, a.dtype) for a in arrays]
        + [pltpu.SemaphoreType.DMA((count,)), pltpu.SemaphoreType.DMA((count,))],
        compiler_params=pltpu.CompilerParams(vmem_limit_bytes=60000000),
        name="hand_over",
    )(*arrays, *near, small)


def feed_kernel(
    parts, heads, back, x, dy, bo, gain, shift, be, br, wo_in, we_in, wr_in,
    out, dmid_out, do_staged, s_gain, s_shift, s_ob, s_eb, s_rb, g_we, g_wr, g_wo,
    wo, we, wr, k_we, k_wr, k_wo, dh, load, keep,
):
    low = jnp.bfloat16
    rows, width = x.shape
    step = we.shape[1] // parts
    splits = back.shape[1]

    def total(v):
        return jnp.sum(v, axis=0, keepdims=True)

    def columns(c):
        return pl.ds(pl.multiple_of(c * step, 128), step)

    def fetch(c):
        return (pltpu.make_async_copy(we_in.at[:, columns(c)], we.at[:, columns(c)], load.at[c]),
                pltpu.make_async_copy(wr_in.at[columns(c)], wr.at[columns(c)], load.at[parts + c]))

    def store(c):
        return (pltpu.make_async_copy(k_we.at[:, columns(c)], g_we.at[:, columns(c)], keep.at[c]),
                pltpu.make_async_copy(k_wr.at[columns(c)], g_wr.at[columns(c)], keep.at[parts + c]))

    first = pltpu.make_async_copy(wo_in, wo, load.at[2 * parts])
    first.start()
    for c in range(parts):
        for copy in fetch(c):
            copy.start()
    att = join_rows(back).astype(low)
    first.wait()
    mid = x[...].astype(jnp.float32) + product(att, wo[...]) + bo[...]
    normed, scale = normal_rows(mid)
    second = (normed * gain[...] + shift[...]).astype(low)
    second_across = jnp.transpose(second)
    seed = dy[...]
    seed_full = seed.astype(jnp.float32)
    s_rb[...] = total(seed_full)
    dmid_out[...] = mid + br[...]
    dh[...] = jnp.zeros((rows, width), jnp.float32)

    @pl.loop(0, parts)
    def _(c):
        for copy in fetch(c):
            copy.wait()
        expand, reduce = we[:, columns(c)], wr[columns(c)]
        u = product(second, expand) + be[:, columns(c)]
        square = u * u
        t = jnp.tanh(math.sqrt(2 / math.pi) * (u + 0.044715 * (u * square)))
        z = (0.5 * u * (1.0 + t)).astype(low)
        slope = 0.5 * (1.0 + t) + (0.5 * math.sqrt(2 / math.pi)) * u * (1.0 - t * t) * (1.0 + (3 * 0.044715) * square)
        du_full = (slope * product_right(seed, reduce)).astype(low)
        s_eb[:, columns(c)] = total(du_full.astype(jnp.float32))
        dmid_out[...] += product(z, reduce)
        dh[...] += product_right(du_full, expand)
        k_wr[columns(c)] = product(jnp.transpose(z), seed).astype(low)
        k_we[:, columns(c)] = product(second_across, du_full).astype(low)
        for copy in store(c):
            copy.start()

    out[...] = dmid_out[...].astype(low)
    back_normed = dh[...]
    s_gain[...] = total(back_normed * normed)
    s_shift[...] = total(back_normed)
    scaled = back_normed * gain[...]
    inner = jnp.mean(scaled, axis=-1, keepdims=True)
    along = jnp.mean(scaled * normed, axis=-1, keepdims=True)
    dmid = seed_full + scale * (scaled - inner - normed * along)
    dmid_out[...] = dmid
    branch = dmid.astype(low)
    s_ob[...] = total(branch.astype(jnp.float32))
    k_wo[...] = product(jnp.transpose(att), branch).astype(low)
    last = pltpu.make_async_copy(k_wo, g_wo, keep.at[2 * parts])
    last.start()
    for group in range(width // 256):
        datt = product_right(branch, wo[group * 256 : (group + 1) * 256, :])

        def put(head, split, v, group=group):
            head = head + 4 * group
            do_staged[head // heads, head % heads, split] = v.astype(low)

        pack_heads(datt, splits, put)
    for c in range(parts):
        for copy in store(c):
            copy.wait()
    last.wait()


def feed_call(back, x, dy, bo, gain, shift, be, br, wo, we, wr):
    rows, width = x.shape
    inner = we.shape[1]
    parts = inner // width
    heads = back.shape[0] // PARTS
    splits = back.shape[1]
    low, full = jnp.bfloat16, jnp.float32
    vmem, dma = pltpu.VMEM, pltpu.SemaphoreType.DMA
    inside, outside = pl.BlockSpec(memory_space=vmem), pl.BlockSpec(memory_space=pl.ANY)
    shape = jax.ShapeDtypeStruct
    return pl.pallas_call(
        functools.partial(feed_kernel, parts, heads),
        out_shape=[
            shape((rows, width), low),
            shape((rows, width), full),
            shape((PARTS, heads) + back.shape[1:], low),
            shape((1, width), full),
            shape((1, width), full),
            shape((1, width), full),
            shape((1, inner), full),
            shape((1, width), full),
            shape(we.shape, low),
            shape(wr.shape, low),
            shape(wo.shape, low),
        ],
        in_specs=[inside] * 8 + [outside] * 3,
        out_specs=[inside] * 8 + [outside] * 3,
        scratch_shapes=[
            vmem(wo.shape, low), vmem(we.shape, low), vmem(wr.shape, low),
            vmem(we.shape, low), vmem(wr.shape, low), vmem(wo.shape, low),
            vmem((rows, width), full),
            dma((2 * parts + 1,)), dma((2 * parts + 1,)),
        ],
        compiler_params=pltpu.CompilerParams(vmem_limit_bytes=64000000),
        name="feed_forward",
    )(back, x, dy, bo, gain, shift, be, br, wo, we, wr)


def body(
    tokens,
    first_values,
    placement,
    cotangent,
    *parts,
):
    groups, rows, width = tokens.shape
    n = lax.axis_size("seq")
    small = (0, 1, 3, 6, 8, 9, 10, 12, 14)
    large = (2, 4, 5, 7, 11, 13)
    done = forward_call(n, lax.axis_size("grp"), placement, tokens[0], first_values[0],
                        [parts[i][None] for i in small], [parts[i] for i in large])
    hidden, q_all, kv_all, ol_all, back = done[:5]
    whole = [None] * 15
    for i, v in zip(large, done[5:11]):
        whole[i] = v.reshape(-1, v.shape[-1])
    for i, v in zip(small, done[11:]):
        whole[i] = v[0]
    layer_output, dmid, do_staged, *sums, g_we, g_wr, g_wo = feed_call(
        back, tokens[0], cotangent[0], whole[8][None], whole[9][None], whole[10][None], whole[12][None],
        whole[14][None], whole[7], whole[11], whole[13],
    )
    block = (lax.axis_size("grp"), n // 2, 2)
    far = [v.reshape(block + (-1, v.shape[1])) for v in (g_we, g_wr, g_wo)]
    inside = far if n <= 8 else []
    done = backward_call(
        n, block[0], placement, do_staged, q_all, kv_all, ol_all, hidden, tokens[0],
        whole[0][None], whole[2], whole[4], whole[5], dmid, [sums[0], sums[1], sums[2], sums[3], sums[4]],
        inside,
    )
    token_grad, first_grad = done[:2]
    if not inside:
        forth = powers(block[0])
        done = done[:2] + reduce_call(block[0], block[1], far, [forth, forth[::-1], forth]) + done[2:]
    g_we, g_wr, g_wo = done[2:5]
    near, g_small = done[5:-1], done[-1]
    sizes = [parts[i].shape[0] for i in small]
    out = hand_over([token_grad, first_grad, g_wo, g_we, g_wr], near, g_small, sizes, whole[2].shape[1], whole[5].shape[1])
    owned = [None] * 15
    for i, v in zip((7, 11, 13, 2, 4, 5), out[2:8]):
        owned[i] = v
    for i, v in zip(small, out[8:]):
        owned[i] = v.reshape(-1)
    return (layer_output[None], out[0][None], out[1][None]) + tuple(owned)


def solution(mesh):
    spread = P("grp", "seq", None)
    both = ("grp", "seq")
    vector, matrix = P(both), P(both, None)
    kinds = (vector, vector, matrix, vector, matrix, matrix, vector, matrix, vector, vector, vector,
             matrix, vector, matrix, vector)
    in_specs = (spread, spread, P("grp", None), spread) + kinds
    out_specs = (spread, spread, spread) + kinds
    return jax.shard_map(body, mesh=mesh, in_specs=in_specs, out_specs=out_specs, check_vma=False)
```

```python
import functools
import math

import jax
import jax.numpy as jnp
from jax import lax
from jax.experimental import pallas as pl
from jax.experimental.pallas import tpu as pltpu
from jax.sharding import PartitionSpec as P

MESH = pl.DeviceIdType.MESH


def powers(count):
    out, bit = [], 1
    while bit < count:
        out.append(bit)
        bit *= 2
    return out


def remote(src, dst, send, recv, device):
    return pltpu.make_async_remote_copy(
        src_ref=src, dst_ref=dst, send_sem=send, recv_sem=recv,
        device_id=device, device_id_type=MESH,
    )


def enter(devices):
    barrier = pltpu.get_barrier_semaphore()
    for device in devices:
        pl.semaphore_signal(barrier, inc=1, device_id=device, device_id_type=MESH)
    pl.semaphore_wait(barrier, len(devices))


class Gather:
    def __init__(self, groups, chips, bits, shard, full, chain_send, level_send, recv, pair, own,
                 direct=False):
        self.direct = direct
        self.groups, self.chips, self.bits = groups, chips, bits
        self.shard, self.full = shard, full
        self.chain_send, self.level_send, self.recv, self.pair, self.own = chain_send, level_send, recv, pair, own
        self.g = lax.axis_index("grp")
        seq = lax.axis_index("seq")
        self.s, self.z, self.c = seq, seq // 2, seq % 2

    def block(self, g, z, c):
        return self.full.at[g, z, c]

    def source(self, mask, z, first):
        return self.shard if first else self.block(self.g ^ mask, z, self.c)

    def chain(self, z, step, first):
        side = 0 if step < 0 else 1
        return remote(self.source(0, z, first), self.block(self.g, z, self.c),
                      self.chain_send.at[z, side], self.recv.at[self.g, z],
                      {"seq": self.s + 2 * step})

    def cross(self, level, mask, z, first):
        g = self.g ^ mask
        return remote(self.source(mask, z, first), self.block(g, z, self.c),
                      self.level_send.at[level], self.recv.at[g, z],
                      {"grp": self.g ^ self.bits[level]})

    def held(self, level):
        masks = [0]
        for bit in self.bits[:level]:
            masks = masks + [m ^ bit for m in masks]
        return masks

    def here(self, mask, z):
        g = self.g ^ mask
        pltpu.make_async_copy(self.block(g, z, self.c), self.block(g, z, self.c), self.recv.at[g, z]).wait()

    def begin(self):
        self.begin_chain()
        self.begin_cross()

    def begin_chain(self):
        copy = pltpu.make_async_copy(self.shard, self.block(self.g, self.z, self.c), self.own)
        copy.start()
        if self.direct:
            for out in self.direct_copies():
                out.start()
            return

        @pl.when(self.z > 0)
        def _():
            self.chain(self.z, -1, True).start()

        @pl.when(self.z < self.chips - 1)
        def _():
            self.chain(self.z, 1, True).start()

    def direct_copies(self):
        out = []
        for off in range(1, self.chips):
            chip = lax.rem(self.z + off, self.chips)
            out.append(remote(self.shard, self.block(self.g, self.z, self.c), self.chain_send.at[off, 0],
                              self.recv.at[self.g, self.z], {"seq": 2 * chip + self.c}))
        return out

    def begin_cross(self):
        for level in range(len(self.bits)):
            self.cross(level, 0, self.z, True).start()

    def at(self, distance, body):
        if distance == 0:
            body(self.z, 0)
            return

        @pl.when(self.z >= distance)
        def _():
            body(self.z - distance, 1)

        @pl.when(self.z + distance < self.chips)
        def _():
            body(self.z + distance, -1)

    def along(self, distance):
        self.along_chain(distance)
        self.along_cross(distance)

    def along_chain(self, distance):
        def body(z, step):
            self.here(0, z)
            if self.direct:
                return
            onward = self.z < self.chips - 1 if step > 0 else self.z > 0

            @pl.when(onward)
            def _():
                self.chain(z, step, False).start()

        self.at(distance, body)

    def along_cross(self, distance):
        def body(z, step):
            for level in range(len(self.bits)):
                self.cross(level, 0, z, False).start()

        self.at(distance, body)

    def over(self, level, distance):
        def body(z, step):
            for mask in self.held(level):
                mask = mask ^ self.bits[level]
                self.here(mask, z)
                for later in range(level + 1, len(self.bits)):
                    self.cross(later, mask, z, False).start()

        self.at(distance, body)

    def swap_copy(self):
        mine = self.full.at[:, :, self.c]
        return remote(mine, mine, self.pair.at[0], self.pair.at[1], {"seq": self.s ^ 1})

    def swap(self):
        pltpu.make_async_copy(self.shard, self.shard, self.own).wait()
        self.swap_copy().start()

    def finish(self):
        self.swap_copy().wait_send()
        other = self.full.at[:, :, 1 - self.c]
        pltpu.make_async_copy(other, other, self.pair.at[1]).wait()
        self.sent()

    def sent(self):
        if self.direct:
            for out in self.direct_copies():
                out.wait_send()
        else:
            self.chain_sent()
        for level in range(len(self.bits)):
            sent = self.full.at[pl.ds(0, 2 ** level), :, 0]
            pltpu.make_async_copy(sent, sent, self.level_send.at[level]).wait()

    def chain_sent(self):
        @pl.when(self.z > 0)
        def _():
            self.chain(self.z, -1, True).wait_send()

        @pl.when(self.z < self.chips - 1)
        def _():
            self.chain(self.z, 1, True).wait_send()

        for distance in range(1, self.chips):
            def body(z, step):
                onward = self.z < self.chips - 1 if step > 0 else self.z > 0

                @pl.when(onward)
                def _():
                    self.chain(z, step, False).wait_send()

            self.at(distance, body)


def gather_semaphores(count, groups, chips):
    dma = pltpu.SemaphoreType.DMA
    levels = max(len(powers(groups)), 1)
    return [dma((count, chips, 2)), dma((count, levels)), dma((count, groups, chips)), dma((count, 2)), dma((count,))]


def neighbours(groups, n):
    g, s = lax.axis_index("grp"), lax.axis_index("seq")
    out = [{"grp": g ^ bit} for bit in powers(groups)]
    out += [{"seq": s ^ 1}, {"seq": lax.rem(s + 2, n)}, {"seq": lax.rem(s + n - 2, n)}]
    return out


def gather_kernel(groups, chips, orders, *refs):
    count = len(orders)
    shards, fulls, sems = refs[:count], refs[count:2 * count], refs[2 * count:]
    enter(neighbours(groups, 2 * chips))
    gathers = [Gather(groups, chips, orders[i], shards[i], fulls[i], *[s.at[i] for s in sems]) for i in range(count)]
    run_gathers(gathers)


def run_gathers(gathers):
    chips, levels = gathers[0].chips, len(gathers[0].bits)
    for g in gathers:
        g.begin()
    for distance in range(chips + levels):
        for g in gathers:
            if distance + 1 < chips:
                g.along(distance + 1)
            for level in range(levels):
                if 0 <= distance - level < chips:
                    g.over(level, distance - level)
    for g in gathers:
        g.swap()
    for g in gathers:
        g.finish()


def gather_call(groups, chips, shards, orders):
    count = len(shards)
    return pl.pallas_call(
        functools.partial(gather_kernel, groups, chips, orders),
        out_shape=[jax.ShapeDtypeStruct((groups, chips, 2) + x.shape, x.dtype) for x in shards],
        in_specs=[pl.BlockSpec(memory_space=pl.ANY)] * count,
        out_specs=[pl.BlockSpec(memory_space=pl.ANY)] * count,
        scratch_shapes=gather_semaphores(count, groups, chips),
        compiler_params=pltpu.CompilerParams(collective_id=0, has_side_effects=True),
        name="gather_parameters",
    )(*shards)


class Reduce:
    def __init__(self, groups, chips, bits, partial, shard, own, landed, halves, finals, sems,
                 chain=False, direct=False):
        self.chain, self.direct = chain, direct
        self.groups, self.chips, self.bits = groups, chips, bits
        self.partial, self.shard, self.own, self.landed = partial, shard, own, landed
        self.halves, self.finals, self.mail = halves, finals, halves[0] if direct else None
        self.load, self.pair, self.level_send, self.level_recv, self.chip_send, self.chip_recv = sems
        self.g = lax.axis_index("grp")
        self.s = lax.axis_index("seq")
        self.z, self.c = self.s // 2, self.s % 2

    def masks(self, level):
        out = [0]
        for bit in self.bits[level:]:
            out = out + [m ^ bit for m in out]
        return out

    def load_copy(self):
        return pltpu.make_async_copy(self.partial.at[:, :, self.c], self.own, self.load.at[0])

    def pair_copy(self):
        return remote(self.partial.at[:, :, 1 - self.c], self.landed, self.pair.at[0], self.pair.at[1],
                      {"seq": self.s ^ 1})

    def begin(self):
        self.pair_copy().start()
        self.load_copy().start()

    def paired(self):
        self.load_copy().wait()
        self.pair_copy().wait_recv()

        @pl.loop(0, self.groups)
        def _(g):
            @pl.loop(0, self.chips)
            def _(z):
                self.own[g, z] = self.add(self.own[g, z], self.landed[g, z])

        self.cross_start(0)

    def add(self, a, b):
        return a + b

    def cross_copies(self, level):
        bit = self.bits[level]
        out = []
        for where, mask in enumerate(self.masks(level + 1)):
            out.append(remote(self.own.at[self.g ^ bit ^ mask], self.halves[level].at[where],
                              self.level_send.at[level, where], self.level_recv.at[level, where],
                              {"grp": self.g ^ bit}))
        return out

    def cross_start(self, level):
        if self.direct:
            for copy in self.direct_copies():
                copy.start()
        elif level < len(self.bits):
            for copy in self.cross_copies(level):
                copy.start()
        else:
            self.chip_start()

    def chip_start(self):
        if self.chain:
            self.chain_first()
        else:
            for copy in self.chip_copies():
                copy.start()

    def crossed(self, level, onward=True):
        copies = self.cross_copies(level)
        for where, mask in enumerate(self.masks(level + 1)):
            copies[where].wait_recv()
            g = self.g ^ mask

            @pl.loop(0, self.chips)
            def _(z):
                self.own[g, z] = self.add(self.own[g, z], self.halves[level][where, z])

        if onward:
            self.cross_start(level + 1)

    def chain_copy(self, block, step):
        side = 0 if step > 0 else 1
        return remote(self.own.at[self.g, block], self.finals.at[side, block], self.chip_send.at[side, block],
                      self.chip_recv.at[side, block], {"seq": self.s + 2 * step})

    def chain_add(self, block, side):
        landed = self.finals.at[side, block]
        pltpu.make_async_copy(landed, landed, self.chip_recv.at[side, block]).wait()
        self.own[self.g, block] = self.add(self.own[self.g, block], self.finals[side, block])

    def chain_first(self):
        last = self.chips - 1

        @pl.when(self.z == 0)
        def _():
            for block in range(last, 0, -1):
                self.chain_copy(block, 1).start()

        @pl.when(self.z == last)
        def _():
            for block in range(last):
                self.chain_copy(block, -1).start()

    def chained(self, near_end):
        last = self.chips - 1
        left = self.z < self.chips // 2
        right = jnp.logical_not(left)
        for block in range(last, 0, -1):
            @pl.when((self.z > 0) & (self.z < block) & (left if near_end else right))
            def _():
                self.chain_add(block, 0)
                self.chain_copy(block, 1).start()

        for block in range(last):
            @pl.when((self.z < last) & (self.z > block) & (right if near_end else left))
            def _():
                self.chain_add(block, 1)
                self.chain_copy(block, -1).start()

    def chain_finish(self):
        last = self.chips - 1

        @pl.when(self.z > 0)
        def _():
            self.chain_add(self.z, 0)

        @pl.when(self.z < last)
        def _():
            self.chain_add(self.z, 1)

        self.shard[...] = self.own[self.g, self.z].astype(jnp.float32)

    def chain_drain(self):
        for block in range(self.chips):
            @pl.when(self.z < block)
            def _():
                self.chain_copy(block, 1).wait_send()

            @pl.when(self.z > block)
            def _():
                self.chain_copy(block, -1).wait_send()

    def chip_copies(self):
        out = []
        for off in range(1, self.chips):
            chip = lax.rem(self.z + off, self.chips)
            out.append(remote(self.own.at[self.g, chip], self.finals.at[off - 1], self.chip_send.at[off - 1],
                              self.chip_recv.at[off - 1], {"seq": 2 * chip + self.c}))
        return out

    def direct_copies(self):
        out = []
        for off in range(1, self.groups * self.chips):
            g = lax.rem(self.g + off // self.chips, self.groups)
            z = lax.rem(self.z + off % self.chips, self.chips)
            out.append(remote(self.own.at[g, z], self.mail.at[off // self.chips, off % self.chips],
                              self.level_send.at[off], self.level_recv.at[off], {"grp": g, "seq": 2 * z + self.c}))
        return out

    def direct_finish(self):
        total = self.own[self.g, self.z]
        for off, copy in enumerate(self.direct_copies()):
            copy.wait_recv()
            total = total + self.mail[(off + 1) // self.chips, (off + 1) % self.chips]
        self.shard[...] = total

    def finish(self):
        total = self.own[self.g, self.z].astype(jnp.float32)
        for off, copy in enumerate(self.chip_copies()):
            copy.wait_recv()
            total = total + self.finals[off].astype(jnp.float32)
        self.shard[...] = total

    def drain(self):
        self.pair_copy().wait_send()
        if self.direct:
            for copy in self.direct_copies():
                copy.wait_send()
            return
        for level in range(len(self.bits)):
            for copy in self.cross_copies(level):
                copy.wait_send()
        if self.chain:
            self.chain_drain()
        else:
            for copy in self.chip_copies():
                copy.wait_send()


def reduce_steps(reduces):
    levels = len(reduces[0].bits)
    stages = [lambda r: r.begin(), lambda r: r.paired()]
    for level in range(levels):
        stages.append(lambda r, level=level: r.crossed(level))
    stages += [lambda r: r.finish(), lambda r: r.drain()]
    return [functools.partial(stage, r) for stage in stages for r in reduces]


def direct_scratch(groups, chips, shape):
    vmem, dma = pltpu.VMEM, pltpu.SemaphoreType.DMA
    whole = vmem((groups, chips) + shape[3:5], shape[5])
    count = groups * chips
    return [whole, whole, whole, dma((1,)), dma((2,)), dma((count,)), dma((count,))]


def make_direct(groups, chips, partial, shard, scratch):
    own, landed, mail, load, pair, send, recv = scratch
    return Reduce(groups, chips, powers(groups), partial, shard, own, landed, [mail], None,
                  (load, pair, send, recv, None, None), direct=True)


def reduce_scratch(groups, chips, shapes, chain=False):
    vmem, dma = pltpu.VMEM, pltpu.SemaphoreType.DMA
    levels = len(powers(groups))
    out = []
    for _, _, _, rows, cols, dtype in shapes:
        out += [vmem((groups, chips, rows, cols), dtype), vmem((groups, chips, rows, cols), dtype)]
        out += [vmem((groups >> (level + 1), chips, rows, cols), dtype) for level in range(levels)]
        out += [vmem((2, chips, rows, cols) if chain else (max(chips - 1, 1), rows, cols), dtype)]
        out += [dma((1,)), dma((2,)), dma((max(levels, 1), max(groups // 2, 1))),
                dma((max(levels, 1), max(groups // 2, 1))), dma((2, chips) if chain else (max(chips - 1, 1),)),
                dma((2, chips) if chain else (max(chips - 1, 1),))]
    return out


def make_reduces(groups, chips, orders, partials, shards, scratch, chain=False):
    levels = len(powers(groups))
    each = 2 + levels + 1 + 6
    out = []
    for i, (partial, shard) in enumerate(zip(partials, shards)):
        refs = scratch[i * each : (i + 1) * each]
        out.append(Reduce(groups, chips, orders[i], partial, shard, refs[0], refs[1], refs[2 : 2 + levels],
                          refs[2 + levels], refs[3 + levels :], chain))
    return out


def reduce_kernel(groups, chips, orders, *refs):
    count = len(orders)
    enter(neighbours(groups, 2 * chips))
    for step in reduce_steps(make_reduces(groups, chips, orders, refs[:count], refs[count : 2 * count],
                                          refs[2 * count :])):
        step()


def reduce_call(groups, chips, partials, orders):
    count = len(partials)
    shapes = [p.shape + (p.dtype,) for p in partials]
    return pl.pallas_call(
        functools.partial(reduce_kernel, groups, chips, orders),
        out_shape=[jax.ShapeDtypeStruct(p.shape[3:], jnp.float32) for p in partials],
        in_specs=[pl.BlockSpec(memory_space=pl.ANY)] * count,
        out_specs=[pl.BlockSpec(memory_space=pltpu.VMEM)] * count,
        scratch_shapes=reduce_scratch(groups, chips, shapes),
        compiler_params=pltpu.CompilerParams(collective_id=3, has_side_effects=True, vmem_limit_bytes=64000000),
        name="reduce_gradients",
    )(*partials)


PARTS = 4
NEG = -1e30
EPS = 1e-05


def lanes(shape):
    return lax.broadcasted_iota(jnp.int32, shape, len(shape) - 1)


def swap_lanes(v):
    return pltpu.roll(v, 64, 1)


def fold(v, high):
    half = v.shape[0] // 2
    top, bottom = v[:half], v[half:]
    low = lanes(top.shape) < 64
    if high:
        return jnp.where(low, swap_lanes(top), bottom)
    return jnp.where(low, top, swap_lanes(bottom))


def unfold(v, high):
    low = lanes(v.shape) < 64
    zero = jnp.zeros_like(v)
    if high:
        return jnp.concatenate([jnp.where(low, zero, swap_lanes(v)), jnp.where(low, zero, v)], axis=0)
    return jnp.concatenate([jnp.where(low, v, zero), jnp.where(low, swap_lanes(v), zero)], axis=0)


def product(a, b):
    return lax.dot_general(a, b, (((1,), (0,)), ((), ())), preferred_element_type=jnp.float32)


def product_right(a, b):
    return lax.dot_general(a, b, (((1,), (1,)), ((), ())), preferred_element_type=jnp.float32)


def product_left(a, b):
    return lax.dot_general(a, b, (((0,), (0,)), ((), ())), preferred_element_type=jnp.float32)


def normal_rows(v):
    mean = jnp.mean(v, axis=-1, keepdims=True)
    centred = v - mean
    var = jnp.mean(centred * centred, axis=-1, keepdims=True)
    scale = lax.rsqrt(var + EPS)
    return centred * scale, scale


def pack_heads(v, splits, store):
    size = v.shape[0] // splits
    for tile in range(v.shape[1] // 128):
        for split in range(splits):
            part = v[split * size : (split + 1) * size, tile * 128 : (tile + 1) * 128]
            store(2 * tile, split, fold(part, False))
            store(2 * tile + 1, split, fold(part, True))


def slots_of(table, count):
    out = []
    for piece in range(count):
        slot = jnp.int32(0)
        for place in range(count):
            slot = slot + jnp.where(table[0, place] == piece, place, 0)
        out.append(jnp.minimum(slot, count - 1))
    return out


def pick(values, index):
    out = values[0]
    for i in range(1, len(values)):
        out = jnp.where(index == i, values[i], out)
    return out


class Exchange:
    def __init__(self, n):
        self.n = n
        self.splits = n // PARTS
        self.s = lax.axis_index("seq")
        self.part, self.split = self.s // self.splits, lax.rem(self.s, self.splits)

    def peers(self):
        return [{"seq": lax.rem(self.s + off, self.n)} for off in range(1, self.n)]

    def other(self, off):
        return lax.rem(self.s + off, self.n)

    def scatter(self, j, staged, landed, send, recv):
        out = []
        for off in range(1, self.n):
            t = self.other(off)
            out.append(remote(staged.at[t // self.splits, j, lax.rem(t, self.splits)], landed.at[j, self.s],
                              send.at[j, off - 1], recv.at[j, self.s], {"seq": t}))
        return out

    def own(self, j, staged, landed, recv):
        return pltpu.make_async_copy(staged.at[self.part, j, self.split], landed.at[j, self.s], recv.at[j, self.s])

    def spread(self, j, staged, landed, send, recv):
        out = []
        for off in range(1, PARTS):
            part = lax.rem(self.part + off, PARTS)
            out.append(remote(staged.at[part, j], landed.at[j, self.s], send.at[j, off - 1],
                              recv.at[j, self.s], {"seq": part * self.splits + self.split}))
        return out

    def own_rows(self, j, staged, landed, recv):
        return pltpu.make_async_copy(staged.at[self.part, j], landed.at[j, self.s], recv.at[j, self.s])

    def relay(self, j, off, landed, send, recv):
        slot = lax.rem(self.part + off, PARTS) * self.splits + self.split
        out = []
        for hop in range(1, self.splits):
            split = lax.rem(self.split + hop, self.splits)
            out.append(remote(landed.at[j, slot], landed.at[j, slot], send.at[j, off, hop - 1],
                              recv.at[j, slot], {"seq": self.part * self.splits + split}))
        return slot, out

    def give_back(self, j, heads, staged, landed, send, recv):
        out = []
        row = self.part * heads + j
        for off in range(1, self.n):
            t = self.other(off)
            out.append(remote(staged.at[j, t], landed.at[row, self.split], send.at[j, off - 1],
                              recv.at[j, self.s], {"seq": t}))
        return out

    def keep_own(self, j, heads, staged, landed, recv):
        return pltpu.make_async_copy(staged.at[j, self.s], landed.at[self.part * heads + j, self.split],
                                     recv.at[j, self.s])


def here(ref, sem):
    pltpu.make_async_copy(ref, ref, sem).wait()


def gather_vectors(full, rows, size):
    count = full.shape[0]
    at = lax.broadcasted_iota(jnp.int32, (128, size), 0)
    to = lax.broadcasted_iota(jnp.int32, (128, size), 1)
    place = jnp.where(lax.rem(to, size // count) == at, 1.0, 0.0).astype(jnp.bfloat16)
    some = jnp.concatenate([full[:, row, :].astype(jnp.bfloat16) for row in rows], axis=0)
    spread = product(some, place)
    mine = part_of_lane(count, size)
    return [jnp.sum(jnp.where(mine, spread[i * count : (i + 1) * count], 0.0), axis=0, keepdims=True)
            for i in range(len(rows))]


def forward_kernel(n, groups, heads, orders, sizes, table, x, first, *refs):
    vectors, shards, refs = refs[:9], refs[9:15], refs[15:]
    hidden_out, q_out, kv_out, ol_out, back = refs[:5]
    fulls_out, vectors_out, refs = refs[5:11], refs[11:20], refs[20:]
    hidden_held, q_all, kv_all, ol_all, wq_full, wk_full, wv_full, stores, head_stores = refs[:9]
    fulls, refs = (wq_full, wk_full, wv_full) + fulls_out[3:], refs[9:]
    leaving = [(wq_full, fulls_out[0]), (wk_full, fulls_out[1]), (wv_full, fulls_out[2]), (hidden_held, hidden_out)]

    def leave(i):
        return pltpu.make_async_copy(leaving[i][0], leaving[i][1], stores.at[i])

    def leave_head(j):
        return [pltpu.make_async_copy(held.at[j], out.at[j], head_stores.at[k, j])
                for k, (held, out) in enumerate(((q_all, q_out), (kv_all, kv_out), (ol_all, ol_out)))]

    packed, small_full, q_staged, kv_staged, o_staged, q_work, kv_work = refs[:7]
    q_send, kv_send, relay_send, o_send, q_recv, kv_recv, o_recv = refs[7:14]
    sems = refs[14:]
    ex = Exchange(n)
    chips = n // 2
    bits = powers(groups)
    levels = len(bits)
    enter(ex.peers() + [{"grp": lax.axis_index("grp") ^ bit} for bit in bits])
    gathers = [
        Gather(groups, chips, order, shard, full, *[s.at[i] for s in sems])
        for i, (order, shard, full) in enumerate(zip(orders, (packed,) + shards, (small_full,) + fulls))
    ]
    near, far = gathers[:4], gathers[4:]
    packed[...] = jnp.zeros(packed.shape, jnp.float32)
    for row, vector in enumerate(vectors):
        packed[row : row + 1, : vector.shape[1]] = vector[...].astype(jnp.float32)
    for g in (near[1], near[2], near[3], near[0]):
        g.begin()
    splits = ex.splits
    rows, width = x.shape
    share = rows // splits
    half = n // 2
    fresh = width - first.shape[1]
    normed, _ = normal_rows(x[...].astype(jnp.float32))

    def steps(some, along=1):
        out = []
        for distance in range(chips + levels):
            for g in some:
                if along == 1 and distance + 1 < chips:
                    out.append(functools.partial(g.along, distance + 1))
                if along == 2 and 2 <= distance + 1 < chips:
                    out.append(functools.partial(g.along_cross, distance + 1))
                for level in range(levels):
                    if 0 <= distance - level < chips:
                        out.append(functools.partial(g.over, level, distance - level))
        return out

    order = steps(near)
    cut = (min(len(order), len(near) * (1 + levels)), 3 * len(order) // 4)
    for step in order[: cut[0]]:
        step()
    for g in far:
        g.begin_chain()
    for step in order[cut[0] : cut[1]]:
        step()
    if chips > 1:
        for g in far:
            g.along_chain(1)
    for step in order[cut[1] :]:
        step()
    for g in near:
        g.swap()
    for g in far:
        g.begin_cross()
    for distance in range(1, min(2, chips)):
        for g in far:
            g.along_cross(distance)
    for distance in range(2, chips):
        for g in far:
            g.along_chain(distance)
    for g in near:
        g.finish()
    small = small_full[...].reshape((2 * chips * groups,) + packed.shape)

    def open_vectors(some):
        for size in sorted({sizes[row] for row in some}):
            same = [row for row in some if sizes[row] == size]
            for row, value in zip(same, gather_vectors(small, same, size)):
                vectors_out[row][...] = value

    open_vectors(range(4))
    gain, shift, bq, bv = vectors_out[:4]
    wq, wk, wv = [fulls[i][...].reshape(width, -1) for i in range(3)]
    hidden = (normed * gain[...] + shift[...]).astype(jnp.bfloat16)
    hidden_held[...] = hidden
    for i in range(4):
        leave(i).start()
    for step in range(width // 256):
        cols = slice(step * 256, (step + 1) * 256)
        q = product(hidden, wq[:, cols]) + bq[:, cols]

        def store(head, split, v, step=step):
            head = head + 4 * step
            q_staged[head // heads, head % heads, split] = (v * 0.125).astype(jnp.bfloat16)

        pack_heads(q, splits, store)
        k = product(hidden, wk[:, cols])
        for tile in range(2):
            at = step * 256 + tile * 128
            if at < fresh:
                v = product(hidden, wv[:, at : at + 128]) + bv[:, at : at + 128]
            else:
                v = first[:, at - fresh : at - fresh + 128].astype(jnp.float32)
            kt = k[:, tile * 128 : (tile + 1) * 128]
            low = lanes(kt.shape) < 64
            head = at // 64
            kv_staged[head // heads, head % heads] = jnp.where(low, kt, swap_lanes(v)).astype(jnp.bfloat16)
            head = head + 1
            kv_staged[head // heads, head % heads] = jnp.where(low, swap_lanes(kt), v).astype(jnp.bfloat16)

    @pl.loop(0, heads)
    def _(j):
        for copy in ex.spread(j, kv_staged, kv_all, kv_send, kv_recv):
            copy.start()
        for copy in ex.scatter(j, q_staged, q_all, q_send, q_recv):
            copy.start()
        ex.own(j, q_staged, q_all, q_recv).start()
        ex.own_rows(j, kv_staged, kv_all, kv_recv).start()

    slot = slots_of(table, n)
    row = lax.broadcasted_iota(jnp.int32, (share, rows), 0) + ex.split * share
    own_mask = lax.broadcasted_iota(jnp.int32, (share, rows), 1) <= row

    def piece(j, place, at, keys):
        q = unfold(q_work[at].astype(jnp.float32), False).astype(jnp.bfloat16)
        blocks = [kv_work[k] for k in keys] + [kv_work[at]]
        scores = [product_right(q, block) for block in blocks]
        scores[-1] = jnp.where(own_mask, scores[-1], NEG)
        top = scores[0]
        for s in scores[1:]:
            top = jnp.maximum(top, s)
        top = jnp.max(top, axis=1, keepdims=True)
        total = jnp.zeros((share, rows), jnp.float32)
        out = jnp.zeros((share, 128), jnp.float32)
        for s, block in zip(scores, blocks):
            weight = jnp.exp(s - top)
            total = total + weight
            out = out + product(weight.astype(jnp.bfloat16), block)
        denom = jnp.sum(total, axis=1, keepdims=True)
        out = out / denom
        ol_all[j, place] = jnp.where(lanes(out.shape) < 64, top + jnp.log(denom), out)

    later = steps(far, 2)
    cut = (len(later) // 2, 3 * len(later) // 4)
    for step in later[: cut[0]]:
        step()
    open_vectors(range(4, 9))

    @pl.loop(0, heads)
    def _(j):
        for off in range(PARTS):
            at, copies = ex.relay(j, off, kv_all, relay_send, kv_recv)
            here(kv_all.at[j, at], kv_recv.at[j, at])
            for copy in copies:
                copy.start()
        for t in range(n):
            here(q_all.at[j, t], q_recv.at[j, t])
        for off in range(PARTS):
            for hop in range(1, splits):
                at = lax.rem(ex.part + off, PARTS) * splits + lax.rem(ex.split + hop, splits)
                here(kv_all.at[j, at], kv_recv.at[j, at])
        for t in range(n):
            q_work[t] = q_all[j, t]
            kv_work[t] = kv_all[j, t]

        @pl.loop(0, half)
        def _(c):
            piece(j, half + c, pick(slot[half:], c), slot[:half])

        for p in range(half):
            piece(j, p, slot[p], slot[:p])
        for t in range(n):
            o_staged[j, t] = fold(ol_all[j, table[0, t]], True).astype(jnp.bfloat16)
        for copy in ex.give_back(j, heads, o_staged, back, o_send, o_recv):
            copy.start()
        ex.keep_own(j, heads, o_staged, back, o_recv).start()
        for copy in leave_head(j):
            copy.start()

        @pl.when(j == 0)
        def _():
            for step in later[cut[0] : cut[1]]:
                step()

        @pl.when(j == min(1, heads - 1))
        def _():
            for step in later[cut[1] :]:
                step()
            for g in far:
                g.swap()

    @pl.loop(0, heads)
    def _(j):
        for copy in ex.spread(j, kv_staged, kv_all, kv_send, kv_recv):
            copy.wait_send()
        for copy in ex.scatter(j, q_staged, q_all, q_send, q_recv):
            copy.wait_send()
        for off in range(PARTS):
            for copy in ex.relay(j, off, kv_all, relay_send, kv_recv)[1]:
                copy.wait_send()
        for copy in ex.give_back(j, heads, o_staged, back, o_send, o_recv):
            copy.wait_send()
        for t in range(n):
            landed = back.at[t // splits * heads + j, t % splits]
            here(landed, o_recv.at[j, t])
    for g in far:
        g.finish()
    for i in range(4):
        leave(i).wait()

    @pl.loop(0, heads)
    def _(j):
        for copy in leave_head(j):
            copy.wait()


def forward_call(n, groups, table, x, first, vectors, shards):
    rows, width = x.shape
    splits = n // PARTS
    chips = n // 2
    heads = width // 64 // PARTS
    share = rows // splits
    low = jnp.bfloat16
    vmem, dma = pltpu.VMEM, pltpu.SemaphoreType.DMA
    inside, outside = pl.BlockSpec(memory_space=vmem), pl.BlockSpec(memory_space=pl.ANY)
    shape = jax.ShapeDtypeStruct
    bits = powers(groups)
    forth, behind = bits, bits[::-1]
    sizes = [v.shape[1] * groups * n for v in vectors]
    block = (groups, chips, 2)
    return pl.pallas_call(
        functools.partial(forward_kernel, n, groups, heads, [forth, forth, behind, forth, behind, forth, behind], sizes),
        out_shape=[
            shape((rows, width), low),
            shape((heads, n, share // 2, 128), low),
            shape((heads, n, rows, 128), low),
            shape((heads, n, share, 128), jnp.float32),
            shape((PARTS * heads, splits, share // 2, 128), low),
        ]
        + [shape(block + w.shape, low) for w in shards]
        + [shape((1, size), jnp.float32) for size in sizes],
        in_specs=[pl.BlockSpec(memory_space=pltpu.SMEM)] + [inside] * 11 + [outside] * 6,
        out_specs=[outside] * 4 + [inside] + [outside] * 6 + [inside] * 9,
        scratch_shapes=[
            vmem((rows, width), low),
            vmem((heads, n, share // 2, 128), low),
            vmem((heads, n, rows, 128), low),
            vmem((heads, n, share, 128), jnp.float32),
        ]
        + [vmem(block + w.shape, low) for w in shards[:3]]
        + [
            dma((4,)),
            dma((3, heads)),
            vmem((16, 128), jnp.float32),
            vmem(block + (16, 128), jnp.float32),
            vmem((PARTS, heads, splits, share // 2, 128), low),
            vmem((PARTS, heads, rows, 128), low),
            vmem((heads, n, share // 2, 128), low),
            vmem((n, share // 2, 128), low),
            vmem((n, rows, 128), low),
            dma((heads, n - 1)),
            dma((heads, PARTS - 1)),
            dma((heads, PARTS, max(splits - 1, 1))),
            dma((heads, n - 1)),
            dma((heads, n)),
            dma((heads, n)),
            dma((heads, n)),
        ]
        + gather_semaphores(7, groups, chips),
        compiler_params=pltpu.CompilerParams(
            collective_id=1, has_side_effects=True, vmem_limit_bytes=64000000
        ),
        name="attention_forward",
    )(table, x, first, *vectors, *shards)


def join_tiles(even, odd, high):
    low = lanes(even.shape) < 64
    if high:
        return jnp.where(low, swap_lanes(even), odd)
    return jnp.where(low, even, swap_lanes(odd))


def join_rows(back):
    heads, splits = back.shape[0], back.shape[1]
    tiles = []
    for tile in range(heads // 2):
        parts = []
        for split in range(splits):
            even = back[2 * tile, split].astype(jnp.float32)
            odd = back[2 * tile + 1, split].astype(jnp.float32)
            parts += [join_tiles(even, odd, False), join_tiles(even, odd, True)]
        tiles.append(jnp.concatenate(parts, axis=0))
    return jnp.concatenate(tiles, axis=1)


def own_columns(j, heads, wq, wk, wv):
    def column(w, head):
        tile = w[:, head // 2 * 128 : head // 2 * 128 + 128].astype(jnp.float32)
        return tile, head % 2

    tiles = []
    for w in (wq, wk, wv):
        for part in range(0, w.shape[1] // 64 // heads, 2):
            (a, high_a), (b, high_b) = column(w, part * heads + j), column(w, (part + 1) * heads + j)
            a = swap_lanes(a) if high_a else a
            b = b if high_b else swap_lanes(b)
            tiles.append(jnp.where(lanes(a.shape) < 64, a, b).astype(jnp.bfloat16))
    return jnp.concatenate(tiles, axis=1)


def in_order(some, at, parts):
    heads = len(some)
    tiles = []
    for head in range(0, heads * parts, 2):
        def column(h):
            j, part = h % heads, h // heads
            start = at + part // 2 * 128
            return some[j][:, start : start + 128], part % 2

        (a, high_a), (b, high_b) = column(head), column(head + 1)
        a = swap_lanes(a) if high_a else a
        b = b if high_b else swap_lanes(b)
        tiles.append(jnp.where(lanes(a.shape) < 64, a, b))
    return jnp.concatenate(tiles, axis=1)


def own_vectors(sums, parts, fresh_parts):
    sums = [jnp.broadcast_to(s, (8, s.shape[1])) for s in sums]
    return [in_order(sums, 0, parts)[0:1], in_order(sums, parts * 128, fresh_parts)[0:1]]


def part_of_lane(count, size):
    part = size // count
    lane = lax.broadcasted_iota(jnp.int32, (count, size), 1)
    row = lax.broadcasted_iota(jnp.int32, (count, size), 0)
    return (lane >= row * part) & (lane < row * part + part)


def spread_vectors(vectors, count):
    size = vectors[0].shape[1]
    mine = part_of_lane(count, size)
    at = lax.broadcasted_iota(jnp.int32, (size, 128), 0)
    to = lax.broadcasted_iota(jnp.int32, (size, 128), 1)
    pick_part = jnp.where(lax.rem(at, size // count) == to, 1.0, 0.0).astype(jnp.bfloat16)
    rows = []
    for vector in vectors:
        value = jnp.where(mine, vector, 0.0)
        for _ in range(3):
            high = value.astype(jnp.bfloat16)
            rows.append(high)
            value = value - high.astype(jnp.float32)
    out = product(jnp.concatenate(rows, axis=0), pick_part)
    parts = [out[i * count : (i + 1) * count] for i in range(len(rows))]
    return [(parts[3 * i] + parts[3 * i + 1] + parts[3 * i + 2]).reshape(count, 1, 128) for i in range(len(vectors))]


def backward_kernel(
    n, groups, heads, orders_far, orders_near,
    table, do_in, gain, s_gain2, s_bias2, s_ob, s_eb, s_rb, q_in, kv_in, ol_in, hidden_in, x_in, dmid_in,
    wq_in, wk_in, wv_in, *refs,
):
    count = len(orders_far)
    far_in, refs = refs[:count], refs[count:]
    token_grad, first_grad = refs[:2]
    far_out, refs = refs[2 : 2 + count], refs[2 + count :]
    near_out, refs = refs[: 2 * heads + 1], refs[2 * heads + 1 :]
    do_all, do_work, acc, dq_piece, dq_staged, part_staged, part_all, dkv_staged, dq_back, dkv_back = refs[:10]
    refs = refs[10:]
    near_in, refs = refs[: 2 * heads + 1], refs[2 * heads + 1 :]
    weights, h_across, refs = refs[:heads], refs[heads], refs[heads + 1 :]
    q_all, kv_all, ol_all, hidden, x, dmid, wq, wk, wv, loads = refs[:10]
    refs = refs[10:]
    do_send, do_recv, dq_send, dq_recv, part_send, part_recv, dkv_send, dkv_recv = refs[:8]
    scratch = refs[8:]

    def full_copy(source, held, at):
        pltpu.make_async_copy(source, held, loads.at[at]).wait()
        return held

    entering = [(hidden_in, hidden, 3), (wq_in, wq, 6), (wk_in, wk, 7), (wv_in, wv, 8), (q_in, q_all, 0),
                (kv_in, kv_all, 1), (ol_in, ol_all, 2), (x_in, x, 4), (dmid_in, dmid, 5)]
    ex = Exchange(n)
    chips = n // 2
    g, z, c = lax.axis_index("grp"), ex.s // 2, lax.rem(ex.s, 2)
    enter(ex.peers() + [
        {"grp": lax.rem(g + off // chips, groups), "seq": 2 * lax.rem(z + off % chips, chips) + c}
        for off in range(chips, groups * chips)
    ])
    small = make_direct(groups, chips, near_in[-1], near_out[-1], scratch[-7:])
    scratch = scratch[:-7]
    each = len(scratch) // (count + 2 * heads)
    far = make_reduces(groups, chips, orders_far, far_in, far_out, scratch[: count * each], True)
    near = make_reduces(groups, chips, orders_near, near_in[:-1], near_out[:-1], scratch[count * each :])
    near_last = near[-2:]
    near_first = near[:-2]
    splits = ex.splits
    rows = kv_all.shape[2]
    share = rows // splits
    half = n // 2
    fresh = wv.shape[1]

    @pl.loop(0, heads)
    def _(j):
        for copy in ex.scatter(j, do_in, do_all, do_send, do_recv):
            copy.start()
        ex.own(j, do_in, do_all, do_recv).start()

    for source, held, at in entering:
        pltpu.make_async_copy(source, held, loads.at[at]).start()
    for r in far:
        r.begin()
    for source, held, at in entering[:7]:
        full_copy(source, held, at)
    low = jnp.bfloat16
    fresh_parts = PARTS * fresh // x.shape[1]
    h_across[...] = jnp.transpose(hidden[...])
    for j in range(heads):
        weights[j][...] = own_columns(j, heads, wq, wk, wv)
    slot = slots_of(table, n)
    column = lax.broadcasted_iota(jnp.int32, (rows, share), 1) + ex.split * share
    own_mask = lax.broadcasted_iota(jnp.int32, (rows, share), 0) <= column

    def piece(j, place, at, keys):
        q = unfold(q_all[j, at].astype(jnp.float32), False).astype(jnp.bfloat16)
        grad = unfold(do_work[at].astype(jnp.float32), True)
        ol = ol_all[j, place]
        delta = jnp.sum(jnp.transpose(grad * ol), axis=0, keepdims=True)
        logsum = jnp.transpose(ol)[0:1]
        grad = grad.astype(jnp.bfloat16)

        def block_terms(key_place, key_slot, mask):
            block = kv_all[j, key_slot]
            weight = jnp.exp(product_right(block, q) - logsum)
            if mask:
                weight = jnp.where(own_mask, weight, 0.0)
            change = (weight * (product_right(block, grad) - delta)).astype(jnp.bfloat16)
            term = product(weight.astype(jnp.bfloat16), grad) + product(change, q)
            acc[key_place] = acc[key_place] + term
            return product_left(block, change)

        dq = block_terms(place, at, True)
        if len(keys) in (2, 3):
            slots = [s for _, s in keys]
            dq = lax.fori_loop(0, len(keys), lambda k, v: v + block_terms(k, pick(slots, k), False), dq)
        else:
            for key_place, key_slot in keys:
                dq = dq + block_terms(key_place, key_slot, False)
        dq_piece[place] = fold(jnp.transpose(dq) * 0.125, False).astype(jnp.bfloat16)

    def part_copies(j):
        out = []
        for hop in range(1, splits):
            split = lax.rem(ex.split + hop, splits)
            for part in range(PARTS):
                out.append(remote(part_staged.at[j, hop - 1, part], part_all.at[j, hop - 1, part],
                                  part_send.at[j, hop - 1, part], part_recv.at[j, hop - 1, part],
                                  {"seq": ex.part * splits + split}))
        return out

    def back_copies(j):
        out = []
        row = ex.part * heads + j
        for off in range(1, PARTS):
            part = lax.rem(ex.part + off, PARTS)
            out.append(remote(dkv_staged.at[j, part], dkv_back.at[row], dkv_send.at[j, off - 1],
                              dkv_recv.at[j, ex.part], {"seq": part * splits + ex.split}))
        return out

    @pl.loop(0, heads)
    def _(j):
        for t in range(n):
            here(do_all.at[j, t], do_recv.at[j, t])
        for t in range(n):
            do_work[t] = do_all[j, t]
            acc[t] = jnp.zeros((rows, 128), jnp.float32)

        @pl.loop(0, half)
        def _(c):
            piece(j, half + c, pick(slot[half:], c), [(p, slot[p]) for p in range(half)])

            @pl.when((j == 0) & (c == 1))
            def _():
                for r in far:
                    r.paired()

            @pl.when((j == heads - 1) & (c == 1))
            def _():
                for r in far:
                    r.crossed(0)

        for p in range(half):
            piece(j, p, slot[p], [(k, slot[k]) for k in range(p)])
        for hop in range(1, splits):
            split = lax.rem(ex.split + hop, splits)
            for part in range(PARTS):
                part_staged[j, hop - 1, part] = acc[table[0, part * splits + split]].astype(jnp.bfloat16)
        for copy in part_copies(j):
            copy.start()
        for t in range(n):
            dq_staged[j, t] = dq_piece[table[0, t]]
        for hop in range(1, splits):
            for part in range(PARTS):
                here(part_all.at[j, hop - 1, part], part_recv.at[j, hop - 1, part])
        for part in range(PARTS):
            total = acc[table[0, part * splits + ex.split]]
            for hop in range(1, splits):
                total = total + part_all[j, hop - 1, part].astype(jnp.float32)
            dkv_staged[j, part] = total.astype(jnp.bfloat16)
        for copy in back_copies(j):
            copy.start()
        pltpu.make_async_copy(dkv_staged.at[j, ex.part], dkv_back.at[ex.part * heads + j],
                              dkv_recv.at[j, ex.part]).start()
        for copy in ex.give_back(j, heads, dq_staged, dq_back, dq_send, dq_recv):
            copy.start()
        ex.keep_own(j, heads, dq_staged, dq_back, dq_recv).start()

    levels = len(powers(groups))

    def total(v):
        return jnp.sum(v, axis=0, keepdims=True)

    def project(j):
        for t in range(n):
            here(dq_back.at[t // splits * heads + j, t % splits], dq_recv.at[j, t])
        for part in range(PARTS):
            here(dkv_back.at[part * heads + j], dkv_recv.at[j, part])
        tiles = []
        for part in range(0, PARTS, 2):
            a, b = part * heads + j, part * heads + heads + j
            parts = []
            for split in range(splits):
                even, odd = dq_back[a, split].astype(jnp.float32), dq_back[b, split].astype(jnp.float32)
                parts += [join_tiles(even, odd, False), join_tiles(even, odd, True)]
            tiles.append(jnp.concatenate(parts, axis=0))
        pairs = [(dkv_back[part * heads + j].astype(jnp.float32), dkv_back[(part + 1) * heads + j].astype(jnp.float32))
                 for part in range(0, PARTS, 2)]
        tiles += [join_tiles(a, b, False) for a, b in pairs]
        tiles += [join_tiles(a, b, True) for a, b in pairs[: fresh_parts // 2]]
        grad = jnp.concatenate(tiles, axis=1)
        sums = total(grad)
        grad = grad.astype(low)
        for ref, r, value in ((near_in[2 * j + 1], near[2 * j + 1], grad[:, PARTS * 64 :]),
                              (near_in[2 * j], near[2 * j], grad[:, : PARTS * 64])):
            ref[...] = product(h_across[...], value).reshape(ref.shape).astype(low)
            r.begin()
        return product_right(grad, weights[j][...]), sums

    devices = groups * n
    ob, gain2, bias2, rb = spread_vectors([s_ob[...], s_gain2[...], s_bias2[...], s_rb[...]], devices)
    later_rows = [ob, gain2, bias2] + spread_vectors([s_eb[...]], devices) + [rb]
    later_rows.append(jnp.zeros((devices, 16 - 9, 128), jnp.float32))
    done = [project(0)]
    for r in far:
        for level in range(1, levels):
            r.crossed(level)
    done += [project(j) for j in range(1, heads - 1)]
    for r in near_first:
        r.paired()
    normed, scale = normal_rows(full_copy(x_in, x, 4)[...].astype(jnp.float32))
    for level in range(levels - 1):
        for r in near_first:
            r.crossed(level)
    done.append(project(heads - 1))
    for r in far:
        r.chained(True)
    for r in near_first:
        r.crossed(levels - 1)
    dh = done[0][0]
    for more, _ in done[1:]:
        dh = dh + more
    for r in near_last:
        r.paired()
    sums = [total(dh * normed), total(dh)]
    sum_q, sum_v = own_vectors([s for _, s in done], PARTS, fresh_parts)
    first_rows = spread_vectors(sums + [sum_q], devices) + spread_vectors([sum_v], devices)
    spread = jnp.concatenate(first_rows + later_rows, axis=1)
    near_in[-1][...] = spread.reshape(near_in[-1].shape)
    small.begin()
    for level in range(levels):
        for r in near_last:
            r.crossed(level)
        if level == 0:
            small.paired()
    scaled = dh * gain[...].astype(jnp.float32)
    inner = jnp.mean(scaled, axis=-1, keepdims=True)
    along = jnp.mean(scaled * normed, axis=-1, keepdims=True)
    token_grad[...] = full_copy(dmid_in, dmid, 5)[...] + scale * (scaled - inner - normed * along)
    for pair in range(fresh // 64, PARTS * heads, 2):
        even, odd = dkv_back[pair].astype(jnp.float32), dkv_back[pair + 1].astype(jnp.float32)
        first_grad[:, pair * 64 - fresh : pair * 64 - fresh + 128] = join_tiles(even, odd, True)
    for r in far:
        r.chained(False)
    for r in far:
        r.chain_finish()
    for r in near:
        r.finish()
    small.direct_finish()
    for r in far + near + [small]:
        r.drain()

    @pl.loop(0, heads)
    def _(j):
        for copy in ex.scatter(j, do_in, do_all, do_send, do_recv):
            copy.wait_send()
        for copy in part_copies(j):
            copy.wait_send()
        for copy in back_copies(j):
            copy.wait_send()
        for copy in ex.give_back(j, heads, dq_staged, dq_back, dq_send, dq_recv):
            copy.wait_send()


def backward_call(n, groups, table, do_in, q_all, kv_all, ol_all, hidden, x, gain, wq, wk, wv, dmid, sums, far):
    heads, _, rows, _ = kv_all.shape
    splits = n // PARTS
    chips = n // 2
    share = rows // splits
    width, fresh = wv.shape
    low = jnp.bfloat16
    vmem, dma = pltpu.VMEM, pltpu.SemaphoreType.DMA
    inside = pl.BlockSpec(memory_space=vmem)
    shape = jax.ShapeDtypeStruct
    bits = powers(groups)
    forth, back = bits, bits[::-1]
    block = (groups, chips, 2)
    part = width // (groups * n)
    wide = 2 * PARTS * 64 + PARTS * 64 * fresh // width
    near = [block + (part, PARTS * 64, low), block + (part, wide - PARTS * 64, low)] * heads
    near += [block + (16, 128, jnp.float32)]
    shapes = [f.shape + (low,) for f in far] + near
    return pl.pallas_call(
        functools.partial(backward_kernel, n, groups, heads, [forth, back, forth][: len(far)],
                          [(forth, back)[j % 2] for j in range(2 * heads)]),
        out_shape=[shape((rows, width), jnp.float32), shape((rows, width - fresh), jnp.float32)]
        + [shape(s[3:5], jnp.float32) for s in shapes],
        in_specs=[pl.BlockSpec(memory_space=pltpu.SMEM)] + [inside] * 7
        + [pl.BlockSpec(memory_space=pl.ANY)] * (9 + len(far)),
        out_specs=[inside] * (3 + 2 * heads + len(far)),
        scratch_shapes=[
            vmem((heads, n, share // 2, 128), low),
            vmem((n, share // 2, 128), low),
            vmem((n, rows, 128), jnp.float32),
            vmem((n, share // 2, 128), low),
            vmem((heads, n, share // 2, 128), low),
            vmem((heads, max(splits - 1, 1), PARTS, rows, 128), low),
            vmem((heads, max(splits - 1, 1), PARTS, rows, 128), low),
            vmem((heads, PARTS, rows, 128), low),
            vmem((PARTS * heads, splits, share // 2, 128), low),
            vmem((PARTS * heads, rows, 128), low),
        ]
        + [vmem(s[:5], s[5]) for s in near]
        + [vmem((width, wide), low)] * heads
        + [vmem((width, rows), low)]
        + [vmem(v.shape, v.dtype) for v in (q_all, kv_all, ol_all, hidden, x, dmid, wq, wk, wv)]
        + [
            dma((9,)),
            dma((heads, n - 1)),
            dma((heads, n)),
            dma((heads, n - 1)),
            dma((heads, n)),
            dma((heads, max(splits - 1, 1), PARTS)),
            dma((heads, max(splits - 1, 1), PARTS)),
            dma((heads, PARTS - 1)),
            dma((heads, PARTS)),
        ]
        + reduce_scratch(groups, chips, shapes[: len(far)], True)
        + reduce_scratch(groups, chips, shapes[len(far) : -1])
        + direct_scratch(groups, chips, shapes[-1]),
        compiler_params=pltpu.CompilerParams(
            collective_id=2, has_side_effects=True, vmem_limit_bytes=67043328
        ),
        name="attention_backward",
    )(table, do_in, gain, *sums, q_all, kv_all, ol_all, hidden, x, dmid, wq, wk, wv, *far)


def hand_over_kernel(count, heads, sizes, fresh_parts, *refs):
    ins, refs = refs[:count], refs[count:]
    near, small, refs = refs[: 2 * heads], refs[2 * heads], refs[2 * heads + 1 :]
    outs, refs = refs[:count], refs[count:]
    g_wq, g_wk, g_wv = refs[:3]
    vectors, refs = refs[3 : 3 + len(sizes)], refs[3 + len(sizes) :]
    held, loads, stores = refs[:-2], refs[-2], refs[-1]
    for i in range(count):
        pltpu.make_async_copy(ins[i], held[i], loads.at[i]).start()
    some = [ref[...] for ref in near]
    g_wq[...] = in_order(some[::2], 0, PARTS)
    g_wk[...] = in_order(some[1::2], 0, PARTS)
    g_wv[...] = in_order(some[1::2], PARTS * 64, fresh_parts)
    for row, size in enumerate(sizes):
        vectors[row][...] = small[row : row + 1, :size]
    for i in range(count):
        pltpu.make_async_copy(ins[i], held[i], loads.at[i]).wait()
        pltpu.make_async_copy(held[i], outs[i], stores.at[i]).start()
    for i in range(count):
        pltpu.make_async_copy(held[i], outs[i], stores.at[i]).wait()


def hand_over(arrays, near, small, sizes, width, fresh):
    shape = jax.ShapeDtypeStruct
    count, heads = len(arrays), len(near) // 2
    rows = near[0].shape[0]
    inside, outside = pl.BlockSpec(memory_space=pltpu.VMEM), pl.BlockSpec(memory_space=pl.ANY)
    return pl.pallas_call(
        functools.partial(hand_over_kernel, count, heads, sizes, PARTS * fresh // width),
        out_shape=[shape(a.shape, a.dtype) for a in arrays]
        + [shape((rows, size), jnp.float32) for size in (width, width, fresh)]
        + [shape((1, size), jnp.float32) for size in sizes],
        in_specs=[outside] * count + [inside] * (2 * heads + 1),
        out_specs=[outside] * count + [inside] * (3 + len(sizes)),
        scratch_shapes=[pltpu.VMEM(a.shape, a.dtype) for a in arrays]
        + [pltpu.SemaphoreType.DMA((count,)), pltpu.SemaphoreType.DMA((count,))],
        compiler_params=pltpu.CompilerParams(vmem_limit_bytes=60000000),
        name="hand_over",
    )(*arrays, *near, small)


def feed_kernel(
    parts, heads, back, x, dy, bo, gain, shift, be, br, wo_in, we_in, wr_in,
    out, dmid_out, do_staged, s_gain, s_shift, s_ob, s_eb, s_rb, g_we, g_wr, g_wo,
    wo, we, wr, k_we, k_wr, k_wo, dh, load, keep,
):
    low = jnp.bfloat16
    rows, width = x.shape
    step = we.shape[1] // parts
    splits = back.shape[1]

    def total(v):
        return jnp.sum(v, axis=0, keepdims=True)

    def columns(c):
        return pl.ds(pl.multiple_of(c * step, 128), step)

    def fetch(c):
        return (pltpu.make_async_copy(we_in.at[:, columns(c)], we.at[:, columns(c)], load.at[c]),
                pltpu.make_async_copy(wr_in.at[columns(c)], wr.at[columns(c)], load.at[parts + c]))

    def store(c):
        return (pltpu.make_async_copy(k_we.at[:, columns(c)], g_we.at[:, columns(c)], keep.at[c]),
                pltpu.make_async_copy(k_wr.at[columns(c)], g_wr.at[columns(c)], keep.at[parts + c]))

    first = pltpu.make_async_copy(wo_in, wo, load.at[2 * parts])
    first.start()
    for c in range(parts):
        for copy in fetch(c):
            copy.start()
    att = join_rows(back).astype(low)
    first.wait()
    mid = x[...].astype(jnp.float32) + product(att, wo[...]) + bo[...]
    normed, scale = normal_rows(mid)
    second = (normed * gain[...] + shift[...]).astype(low)
    second_across = jnp.transpose(second)
    seed = dy[...]
    seed_full = seed.astype(jnp.float32)
    s_rb[...] = total(seed_full)
    dmid_out[...] = mid + br[...]
    dh[...] = jnp.zeros((rows, width), jnp.float32)

    @pl.loop(0, parts)
    def _(c):
        for copy in fetch(c):
            copy.wait()
        expand, reduce = we[:, columns(c)], wr[columns(c)]
        u = product(second, expand) + be[:, columns(c)]
        square = u * u
        t = jnp.tanh(math.sqrt(2 / math.pi) * (u + 0.044715 * (u * square)))
        z = (0.5 * u * (1.0 + t)).astype(low)
        slope = 0.5 * (1.0 + t) + (0.5 * math.sqrt(2 / math.pi)) * u * (1.0 - t * t) * (1.0 + (3 * 0.044715) * square)
        du_full = (slope * product_right(seed, reduce)).astype(low)
        s_eb[:, columns(c)] = total(du_full.astype(jnp.float32))
        dmid_out[...] += product(z, reduce)
        dh[...] += product_right(du_full, expand)
        k_wr[columns(c)] = product(jnp.transpose(z), seed).astype(low)
        k_we[:, columns(c)] = product(second_across, du_full).astype(low)
        for copy in store(c):
            copy.start()

    out[...] = dmid_out[...].astype(low)
    back_normed = dh[...]
    s_gain[...] = total(back_normed * normed)
    s_shift[...] = total(back_normed)
    scaled = back_normed * gain[...]
    inner = jnp.mean(scaled, axis=-1, keepdims=True)
    along = jnp.mean(scaled * normed, axis=-1, keepdims=True)
    dmid = seed_full + scale * (scaled - inner - normed * along)
    dmid_out[...] = dmid
    branch = dmid.astype(low)
    s_ob[...] = total(branch.astype(jnp.float32))
    k_wo[...] = product(jnp.transpose(att), branch).astype(low)
    last = pltpu.make_async_copy(k_wo, g_wo, keep.at[2 * parts])
    last.start()
    for group in range(width // 256):
        datt = product_right(branch, wo[group * 256 : (group + 1) * 256, :])

        def put(head, split, v, group=group):
            head = head + 4 * group
            do_staged[head // heads, head % heads, split] = v.astype(low)

        pack_heads(datt, splits, put)
    for c in range(parts):
        for copy in store(c):
            copy.wait()
    last.wait()


def feed_call(back, x, dy, bo, gain, shift, be, br, wo, we, wr):
    rows, width = x.shape
    inner = we.shape[1]
    parts = inner // width
    heads = back.shape[0] // PARTS
    splits = back.shape[1]
    low, full = jnp.bfloat16, jnp.float32
    vmem, dma = pltpu.VMEM, pltpu.SemaphoreType.DMA
    inside, outside = pl.BlockSpec(memory_space=vmem), pl.BlockSpec(memory_space=pl.ANY)
    shape = jax.ShapeDtypeStruct
    return pl.pallas_call(
        functools.partial(feed_kernel, parts, heads),
        out_shape=[
            shape((rows, width), low),
            shape((rows, width), full),
            shape((PARTS, heads) + back.shape[1:], low),
            shape((1, width), full),
            shape((1, width), full),
            shape((1, width), full),
            shape((1, inner), full),
            shape((1, width), full),
            shape(we.shape, low),
            shape(wr.shape, low),
            shape(wo.shape, low),
        ],
        in_specs=[inside] * 8 + [outside] * 3,
        out_specs=[inside] * 8 + [outside] * 3,
        scratch_shapes=[
            vmem(wo.shape, low), vmem(we.shape, low), vmem(wr.shape, low),
            vmem(we.shape, low), vmem(wr.shape, low), vmem(wo.shape, low),
            vmem((rows, width), full),
            dma((2 * parts + 1,)), dma((2 * parts + 1,)),
        ],
        compiler_params=pltpu.CompilerParams(vmem_limit_bytes=64000000),
        name="feed_forward",
    )(back, x, dy, bo, gain, shift, be, br, wo, we, wr)


def body(
    tokens,
    first_values,
    placement,
    cotangent,
    *parts,
):
    groups, rows, width = tokens.shape
    n = lax.axis_size("seq")
    small = (0, 1, 3, 6, 8, 9, 10, 12, 14)
    large = (2, 4, 5, 7, 11, 13)
    done = forward_call(n, lax.axis_size("grp"), placement, tokens[0], first_values[0],
                        [parts[i][None] for i in small], [parts[i] for i in large])
    hidden, q_all, kv_all, ol_all, back = done[:5]
    whole = [None] * 15
    for i, v in zip(large, done[5:11]):
        whole[i] = v.reshape(-1, v.shape[-1])
    for i, v in zip(small, done[11:]):
        whole[i] = v[0]
    layer_output, dmid, do_staged, *sums, g_we, g_wr, g_wo = feed_call(
        back, tokens[0], cotangent[0], whole[8][None], whole[9][None], whole[10][None], whole[12][None],
        whole[14][None], whole[7], whole[11], whole[13],
    )
    block = (lax.axis_size("grp"), n // 2, 2)
    far = [v.reshape(block + (-1, v.shape[1])) for v in (g_we, g_wr, g_wo)]
    inside = far if n <= 8 else []
    done = backward_call(
        n, block[0], placement, do_staged, q_all, kv_all, ol_all, hidden, tokens[0],
        whole[0][None], whole[2], whole[4], whole[5], dmid, [sums[0], sums[1], sums[2], sums[3], sums[4]],
        inside,
    )
    token_grad, first_grad = done[:2]
    if not inside:
        forth = powers(block[0])
        done = done[:2] + reduce_call(block[0], block[1], far, [forth, forth[::-1], forth]) + done[2:]
    g_we, g_wr, g_wo = done[2:5]
    near, g_small = done[5:-1], done[-1]
    sizes = [parts[i].shape[0] for i in small]
    out = hand_over([token_grad, first_grad, g_wo, g_we, g_wr], near, g_small, sizes, whole[2].shape[1], whole[5].shape[1])
    owned = [None] * 15
    for i, v in zip((7, 11, 13, 2, 4, 5), out[2:8]):
        owned[i] = v
    for i, v in zip(small, out[8:]):
        owned[i] = v.reshape(-1)
    return (layer_output[None], out[0][None], out[1][None]) + tuple(owned)


def solution(mesh):
    spread = P("grp", "seq", None)
    both = ("grp", "seq")
    vector, matrix = P(both), P(both, None)
    kinds = (vector, vector, matrix, vector, matrix, matrix, vector, matrix, vector, vector, vector,
             matrix, vector, matrix, vector)
    in_specs = (spread, spread, P("grp", None), spread) + kinds
    out_specs = (spread, spread, spread) + kinds
    return jax.shard_map(body, mesh=mesh, in_specs=in_specs, out_specs=out_specs, check_vma=False)
```

```python
import functools
import math

import jax
import jax.numpy as jnp
from jax import lax
from jax.experimental import pallas as pl
from jax.experimental.pallas import tpu as pltpu
from jax.sharding import PartitionSpec as P

MESH = pl.DeviceIdType.MESH


def powers(count):
    out, bit = [], 1
    while bit < count:
        out.append(bit)
        bit *= 2
    return out


def remote(src, dst, send, recv, device):
    return pltpu.make_async_remote_copy(
        src_ref=src, dst_ref=dst, send_sem=send, recv_sem=recv,
        device_id=device, device_id_type=MESH,
    )


def enter(devices):
    barrier = pltpu.get_barrier_semaphore()
    for device in devices:
        pl.semaphore_signal(barrier, inc=1, device_id=device, device_id_type=MESH)
    pl.semaphore_wait(barrier, len(devices))


class Gather:
    def __init__(self, groups, chips, bits, shard, full, chain_send, level_send, recv, pair, own,
                 direct=False):
        self.direct = direct
        self.groups, self.chips, self.bits = groups, chips, bits
        self.shard, self.full = shard, full
        self.chain_send, self.level_send, self.recv, self.pair, self.own = chain_send, level_send, recv, pair, own
        self.g = lax.axis_index("grp")
        seq = lax.axis_index("seq")
        self.s, self.z, self.c = seq, seq // 2, seq % 2

    def block(self, g, z, c):
        return self.full.at[g, z, c]

    def source(self, mask, z, first):
        return self.shard if first else self.block(self.g ^ mask, z, self.c)

    def chain(self, z, step, first):
        side = 0 if step < 0 else 1
        return remote(self.source(0, z, first), self.block(self.g, z, self.c),
                      self.chain_send.at[z, side], self.recv.at[self.g, z],
                      {"seq": self.s + 2 * step})

    def cross(self, level, mask, z, first):
        g = self.g ^ mask
        return remote(self.source(mask, z, first), self.block(g, z, self.c),
                      self.level_send.at[level], self.recv.at[g, z],
                      {"grp": self.g ^ self.bits[level]})

    def held(self, level):
        masks = [0]
        for bit in self.bits[:level]:
            masks = masks + [m ^ bit for m in masks]
        return masks

    def here(self, mask, z):
        g = self.g ^ mask
        pltpu.make_async_copy(self.block(g, z, self.c), self.block(g, z, self.c), self.recv.at[g, z]).wait()

    def begin(self):
        self.begin_chain()
        self.begin_cross()

    def begin_chain(self):
        copy = pltpu.make_async_copy(self.shard, self.block(self.g, self.z, self.c), self.own)
        copy.start()
        if self.direct:
            for out in self.direct_copies():
                out.start()
            return

        @pl.when(self.z > 0)
        def _():
            self.chain(self.z, -1, True).start()

        @pl.when(self.z < self.chips - 1)
        def _():
            self.chain(self.z, 1, True).start()

    def direct_copies(self):
        out = []
        for off in range(1, self.chips):
            chip = lax.rem(self.z + off, self.chips)
            out.append(remote(self.shard, self.block(self.g, self.z, self.c), self.chain_send.at[off, 0],
                              self.recv.at[self.g, self.z], {"seq": 2 * chip + self.c}))
        return out

    def begin_cross(self):
        for level in range(len(self.bits)):
            self.cross(level, 0, self.z, True).start()

    def at(self, distance, body):
        if distance == 0:
            body(self.z, 0)
            return

        @pl.when(self.z >= distance)
        def _():
            body(self.z - distance, 1)

        @pl.when(self.z + distance < self.chips)
        def _():
            body(self.z + distance, -1)

    def along(self, distance):
        self.along_chain(distance)
        self.along_cross(distance)

    def along_chain(self, distance):
        def body(z, step):
            self.here(0, z)
            if self.direct:
                return
            onward = self.z < self.chips - 1 if step > 0 else self.z > 0

            @pl.when(onward)
            def _():
                self.chain(z, step, False).start()

        self.at(distance, body)

    def along_cross(self, distance):
        def body(z, step):
            for level in range(len(self.bits)):
                self.cross(level, 0, z, False).start()

        self.at(distance, body)

    def over(self, level, distance):
        def body(z, step):
            for mask in self.held(level):
                mask = mask ^ self.bits[level]
                self.here(mask, z)
                for later in range(level + 1, len(self.bits)):
                    self.cross(later, mask, z, False).start()

        self.at(distance, body)

    def swap_copy(self):
        mine = self.full.at[:, :, self.c]
        return remote(mine, mine, self.pair.at[0], self.pair.at[1], {"seq": self.s ^ 1})

    def swap(self):
        pltpu.make_async_copy(self.shard, self.shard, self.own).wait()
        self.swap_copy().start()

    def finish(self):
        self.swap_copy().wait_send()
        other = self.full.at[:, :, 1 - self.c]
        pltpu.make_async_copy(other, other, self.pair.at[1]).wait()
        self.sent()

    def sent(self):
        if self.direct:
            for out in self.direct_copies():
                out.wait_send()
        else:
            self.chain_sent()
        for level in range(len(self.bits)):
            sent = self.full.at[pl.ds(0, 2 ** level), :, 0]
            pltpu.make_async_copy(sent, sent, self.level_send.at[level]).wait()

    def chain_sent(self):
        @pl.when(self.z > 0)
        def _():
            self.chain(self.z, -1, True).wait_send()

        @pl.when(self.z < self.chips - 1)
        def _():
            self.chain(self.z, 1, True).wait_send()

        for distance in range(1, self.chips):
            def body(z, step):
                onward = self.z < self.chips - 1 if step > 0 else self.z > 0

                @pl.when(onward)
                def _():
                    self.chain(z, step, False).wait_send()

            self.at(distance, body)


def gather_semaphores(count, groups, chips):
    dma = pltpu.SemaphoreType.DMA
    levels = max(len(powers(groups)), 1)
    return [dma((count, chips, 2)), dma((count, levels)), dma((count, groups, chips)), dma((count, 2)), dma((count,))]


def neighbours(groups, n):
    g, s = lax.axis_index("grp"), lax.axis_index("seq")
    out = [{"grp": g ^ bit} for bit in powers(groups)]
    out += [{"seq": s ^ 1}, {"seq": lax.rem(s + 2, n)}, {"seq": lax.rem(s + n - 2, n)}]
    return out


def gather_kernel(groups, chips, orders, *refs):
    count = len(orders)
    shards, fulls, sems = refs[:count], refs[count:2 * count], refs[2 * count:]
    enter(neighbours(groups, 2 * chips))
    gathers = [Gather(groups, chips, orders[i], shards[i], fulls[i], *[s.at[i] for s in sems]) for i in range(count)]
    run_gathers(gathers)


def run_gathers(gathers):
    chips, levels = gathers[0].chips, len(gathers[0].bits)
    for g in gathers:
        g.begin()
    for distance in range(chips + levels):
        for g in gathers:
            if distance + 1 < chips:
                g.along(distance + 1)
            for level in range(levels):
                if 0 <= distance - level < chips:
                    g.over(level, distance - level)
    for g in gathers:
        g.swap()
    for g in gathers:
        g.finish()


def gather_call(groups, chips, shards, orders):
    count = len(shards)
    return pl.pallas_call(
        functools.partial(gather_kernel, groups, chips, orders),
        out_shape=[jax.ShapeDtypeStruct((groups, chips, 2) + x.shape, x.dtype) for x in shards],
        in_specs=[pl.BlockSpec(memory_space=pl.ANY)] * count,
        out_specs=[pl.BlockSpec(memory_space=pl.ANY)] * count,
        scratch_shapes=gather_semaphores(count, groups, chips),
        compiler_params=pltpu.CompilerParams(collective_id=0, has_side_effects=True),
        name="gather_parameters",
    )(*shards)


class Reduce:
    def __init__(self, groups, chips, bits, partial, shard, own, landed, halves, finals, sems,
                 chain=False, direct=False):
        self.chain, self.direct = chain, direct
        self.groups, self.chips, self.bits = groups, chips, bits
        self.partial, self.shard, self.own, self.landed = partial, shard, own, landed
        self.halves, self.finals, self.mail = halves, finals, halves[0] if direct else None
        self.load, self.pair, self.level_send, self.level_recv, self.chip_send, self.chip_recv = sems
        self.g = lax.axis_index("grp")
        self.s = lax.axis_index("seq")
        self.z, self.c = self.s // 2, self.s % 2

    def masks(self, level):
        out = [0]
        for bit in self.bits[level:]:
            out = out + [m ^ bit for m in out]
        return out

    def load_copy(self):
        return pltpu.make_async_copy(self.partial.at[:, :, self.c], self.own, self.load.at[0])

    def pair_copy(self):
        return remote(self.partial.at[:, :, 1 - self.c], self.landed, self.pair.at[0], self.pair.at[1],
                      {"seq": self.s ^ 1})

    def begin(self):
        self.pair_copy().start()
        self.load_copy().start()

    def paired(self):
        self.load_copy().wait()
        self.pair_copy().wait_recv()

        @pl.loop(0, self.groups)
        def _(g):
            @pl.loop(0, self.chips)
            def _(z):
                self.own[g, z] = self.add(self.own[g, z], self.landed[g, z])

        self.cross_start(0)

    def add(self, a, b):
        return a + b

    def cross_copies(self, level):
        bit = self.bits[level]
        out = []
        for where, mask in enumerate(self.masks(level + 1)):
            out.append(remote(self.own.at[self.g ^ bit ^ mask], self.halves[level].at[where],
                              self.level_send.at[level, where], self.level_recv.at[level, where],
                              {"grp": self.g ^ bit}))
        return out

    def cross_start(self, level):
        if self.direct:
            for copy in self.direct_copies():
                copy.start()
        elif level < len(self.bits):
            for copy in self.cross_copies(level):
                copy.start()
        else:
            self.chip_start()

    def chip_start(self):
        if self.chain:
            self.chain_first()
        else:
            for copy in self.chip_copies():
                copy.start()

    def crossed(self, level, onward=True):
        copies = self.cross_copies(level)
        for where, mask in enumerate(self.masks(level + 1)):
            copies[where].wait_recv()
            g = self.g ^ mask

            @pl.loop(0, self.chips)
            def _(z):
                self.own[g, z] = self.add(self.own[g, z], self.halves[level][where, z])

        if onward:
            self.cross_start(level + 1)

    def chain_copy(self, block, step):
        side = 0 if step > 0 else 1
        return remote(self.own.at[self.g, block], self.finals.at[side, block], self.chip_send.at[side, block],
                      self.chip_recv.at[side, block], {"seq": self.s + 2 * step})

    def chain_add(self, block, side):
        landed = self.finals.at[side, block]
        pltpu.make_async_copy(landed, landed, self.chip_recv.at[side, block]).wait()
        self.own[self.g, block] = self.add(self.own[self.g, block], self.finals[side, block])

    def chain_first(self):
        last = self.chips - 1

        @pl.when(self.z == 0)
        def _():
            for block in range(last, 0, -1):
                self.chain_copy(block, 1).start()

        @pl.when(self.z == last)
        def _():
            for block in range(last):
                self.chain_copy(block, -1).start()

    def chained(self, near_end):
        last = self.chips - 1
        left = self.z < self.chips // 2
        right = jnp.logical_not(left)
        for block in range(last, 0, -1):
            @pl.when((self.z > 0) & (self.z < block) & (left if near_end else right))
            def _():
                self.chain_add(block, 0)
                self.chain_copy(block, 1).start()

        for block in range(last):
            @pl.when((self.z < last) & (self.z > block) & (right if near_end else left))
            def _():
                self.chain_add(block, 1)
                self.chain_copy(block, -1).start()

    def chain_finish(self):
        last = self.chips - 1

        @pl.when(self.z > 0)
        def _():
            self.chain_add(self.z, 0)

        @pl.when(self.z < last)
        def _():
            self.chain_add(self.z, 1)

        self.shard[...] = self.own[self.g, self.z].astype(jnp.float32)

    def chain_drain(self):
        for block in range(self.chips):
            @pl.when(self.z < block)
            def _():
                self.chain_copy(block, 1).wait_send()

            @pl.when(self.z > block)
            def _():
                self.chain_copy(block, -1).wait_send()

    def chip_copies(self):
        out = []
        for off in range(1, self.chips):
            chip = lax.rem(self.z + off, self.chips)
            out.append(remote(self.own.at[self.g, chip], self.finals.at[off - 1], self.chip_send.at[off - 1],
                              self.chip_recv.at[off - 1], {"seq": 2 * chip + self.c}))
        return out

    def direct_copies(self):
        out = []
        for off in range(1, self.groups * self.chips):
            g = lax.rem(self.g + off // self.chips, self.groups)
            z = lax.rem(self.z + off % self.chips, self.chips)
            out.append(remote(self.own.at[g, z], self.mail.at[off // self.chips, off % self.chips],
                              self.level_send.at[off], self.level_recv.at[off], {"grp": g, "seq": 2 * z + self.c}))
        return out

    def direct_finish(self):
        total = self.own[self.g, self.z]
        for off, copy in enumerate(self.direct_copies()):
            copy.wait_recv()
            total = total + self.mail[(off + 1) // self.chips, (off + 1) % self.chips]
        self.shard[...] = total

    def finish(self):
        total = self.own[self.g, self.z].astype(jnp.float32)
        for off, copy in enumerate(self.chip_copies()):
            copy.wait_recv()
            total = total + self.finals[off].astype(jnp.float32)
        self.shard[...] = total

    def drain(self):
        self.pair_copy().wait_send()
        if self.direct:
            for copy in self.direct_copies():
                copy.wait_send()
            return
        for level in range(len(self.bits)):
            for copy in self.cross_copies(level):
                copy.wait_send()
        if self.chain:
            self.chain_drain()
        else:
            for copy in self.chip_copies():
                copy.wait_send()


def reduce_steps(reduces):
    levels = len(reduces[0].bits)
    stages = [lambda r: r.begin(), lambda r: r.paired()]
    for level in range(levels):
        stages.append(lambda r, level=level: r.crossed(level))
    stages += [lambda r: r.finish(), lambda r: r.drain()]
    return [functools.partial(stage, r) for stage in stages for r in reduces]


def direct_scratch(groups, chips, shape):
    vmem, dma = pltpu.VMEM, pltpu.SemaphoreType.DMA
    whole = vmem((groups, chips) + shape[3:5], shape[5])
    count = groups * chips
    return [whole, whole, whole, dma((1,)), dma((2,)), dma((count,)), dma((count,))]


def make_direct(groups, chips, partial, shard, scratch):
    own, landed, mail, load, pair, send, recv = scratch
    return Reduce(groups, chips, powers(groups), partial, shard, own, landed, [mail], None,
                  (load, pair, send, recv, None, None), direct=True)


def reduce_scratch(groups, chips, shapes, chain=False):
    vmem, dma = pltpu.VMEM, pltpu.SemaphoreType.DMA
    levels = len(powers(groups))
    out = []
    for _, _, _, rows, cols, dtype in shapes:
        out += [vmem((groups, chips, rows, cols), dtype), vmem((groups, chips, rows, cols), dtype)]
        out += [vmem((groups >> (level + 1), chips, rows, cols), dtype) for level in range(levels)]
        out += [vmem((2, chips, rows, cols) if chain else (max(chips - 1, 1), rows, cols), dtype)]
        out += [dma((1,)), dma((2,)), dma((max(levels, 1), max(groups // 2, 1))),
                dma((max(levels, 1), max(groups // 2, 1))), dma((2, chips) if chain else (max(chips - 1, 1),)),
                dma((2, chips) if chain else (max(chips - 1, 1),))]
    return out


def make_reduces(groups, chips, orders, partials, shards, scratch, chain=False):
    levels = len(powers(groups))
    each = 2 + levels + 1 + 6
    out = []
    for i, (partial, shard) in enumerate(zip(partials, shards)):
        refs = scratch[i * each : (i + 1) * each]
        out.append(Reduce(groups, chips, orders[i], partial, shard, refs[0], refs[1], refs[2 : 2 + levels],
                          refs[2 + levels], refs[3 + levels :], chain))
    return out


def reduce_kernel(groups, chips, orders, *refs):
    count = len(orders)
    enter(neighbours(groups, 2 * chips))
    for step in reduce_steps(make_reduces(groups, chips, orders, refs[:count], refs[count : 2 * count],
                                          refs[2 * count :])):
        step()


def reduce_call(groups, chips, partials, orders):
    count = len(partials)
    shapes = [p.shape + (p.dtype,) for p in partials]
    return pl.pallas_call(
        functools.partial(reduce_kernel, groups, chips, orders),
        out_shape=[jax.ShapeDtypeStruct(p.shape[3:], jnp.float32) for p in partials],
        in_specs=[pl.BlockSpec(memory_space=pl.ANY)] * count,
        out_specs=[pl.BlockSpec(memory_space=pltpu.VMEM)] * count,
        scratch_shapes=reduce_scratch(groups, chips, shapes),
        compiler_params=pltpu.CompilerParams(collective_id=3, has_side_effects=True, vmem_limit_bytes=64000000),
        name="reduce_gradients",
    )(*partials)


PARTS = 4
NEG = -1e30
EPS = 1e-05


def lanes(shape):
    return lax.broadcasted_iota(jnp.int32, shape, len(shape) - 1)


def swap_lanes(v):
    return pltpu.roll(v, 64, 1)


def fold(v, high):
    half = v.shape[0] // 2
    top, bottom = v[:half], v[half:]
    low = lanes(top.shape) < 64
    if high:
        return jnp.where(low, swap_lanes(top), bottom)
    return jnp.where(low, top, swap_lanes(bottom))


def unfold(v, high):
    low = lanes(v.shape) < 64
    zero = jnp.zeros_like(v)
    if high:
        return jnp.concatenate([jnp.where(low, zero, swap_lanes(v)), jnp.where(low, zero, v)], axis=0)
    return jnp.concatenate([jnp.where(low, v, zero), jnp.where(low, swap_lanes(v), zero)], axis=0)


def product(a, b):
    return lax.dot_general(a, b, (((1,), (0,)), ((), ())), preferred_element_type=jnp.float32)


def product_right(a, b):
    return lax.dot_general(a, b, (((1,), (1,)), ((), ())), preferred_element_type=jnp.float32)


def product_left(a, b):
    return lax.dot_general(a, b, (((0,), (0,)), ((), ())), preferred_element_type=jnp.float32)


def normal_rows(v):
    mean = jnp.mean(v, axis=-1, keepdims=True)
    centred = v - mean
    var = jnp.mean(centred * centred, axis=-1, keepdims=True)
    scale = lax.rsqrt(var + EPS)
    return centred * scale, scale


def pack_heads(v, splits, store):
    size = v.shape[0] // splits
    for tile in range(v.shape[1] // 128):
        for split in range(splits):
            part = v[split * size : (split + 1) * size, tile * 128 : (tile + 1) * 128]
            store(2 * tile, split, fold(part, False))
            store(2 * tile + 1, split, fold(part, True))


def slots_of(table, count):
    out = []
    for piece in range(count):
        slot = jnp.int32(0)
        for place in range(count):
            slot = slot + jnp.where(table[0, place] == piece, place, 0)
        out.append(jnp.minimum(slot, count - 1))
    return out


def pick(values, index):
    out = values[0]
    for i in range(1, len(values)):
        out = jnp.where(index == i, values[i], out)
    return out


class Exchange:
    def __init__(self, n):
        self.n = n
        self.splits = n // PARTS
        self.s = lax.axis_index("seq")
        self.part, self.split = self.s // self.splits, lax.rem(self.s, self.splits)

    def peers(self):
        return [{"seq": lax.rem(self.s + off, self.n)} for off in range(1, self.n)]

    def other(self, off):
        return lax.rem(self.s + off, self.n)

    def scatter(self, j, staged, landed, send, recv):
        out = []
        for off in range(1, self.n):
            t = self.other(off)
            out.append(remote(staged.at[t // self.splits, j, lax.rem(t, self.splits)], landed.at[j, self.s],
                              send.at[j, off - 1], recv.at[j, self.s], {"seq": t}))
        return out

    def own(self, j, staged, landed, recv):
        return pltpu.make_async_copy(staged.at[self.part, j, self.split], landed.at[j, self.s], recv.at[j, self.s])

    def spread(self, j, staged, landed, send, recv):
        out = []
        for off in range(1, PARTS):
            part = lax.rem(self.part + off, PARTS)
            out.append(remote(staged.at[part, j], landed.at[j, self.s], send.at[j, off - 1],
                              recv.at[j, self.s], {"seq": part * self.splits + self.split}))
        return out

    def own_rows(self, j, staged, landed, recv):
        return pltpu.make_async_copy(staged.at[self.part, j], landed.at[j, self.s], recv.at[j, self.s])

    def relay(self, j, off, landed, send, recv):
        slot = lax.rem(self.part + off, PARTS) * self.splits + self.split
        out = []
        for hop in range(1, self.splits):
            split = lax.rem(self.split + hop, self.splits)
            out.append(remote(landed.at[j, slot], landed.at[j, slot], send.at[j, off, hop - 1],
                              recv.at[j, slot], {"seq": self.part * self.splits + split}))
        return slot, out

    def give_back(self, j, heads, staged, landed, send, recv):
        out = []
        row = self.part * heads + j
        for off in range(1, self.n):
            t = self.other(off)
            out.append(remote(staged.at[j, t], landed.at[row, self.split], send.at[j, off - 1],
                              recv.at[j, self.s], {"seq": t}))
        return out

    def keep_own(self, j, heads, staged, landed, recv):
        return pltpu.make_async_copy(staged.at[j, self.s], landed.at[self.part * heads + j, self.split],
                                     recv.at[j, self.s])


def here(ref, sem):
    pltpu.make_async_copy(ref, ref, sem).wait()


def gather_vectors(full, rows, size):
    count = full.shape[0]
    at = lax.broadcasted_iota(jnp.int32, (128, size), 0)
    to = lax.broadcasted_iota(jnp.int32, (128, size), 1)
    place = jnp.where(lax.rem(to, size // count) == at, 1.0, 0.0).astype(jnp.bfloat16)
    some = jnp.concatenate([full[:, row, :].astype(jnp.bfloat16) for row in rows], axis=0)
    spread = product(some, place)
    mine = part_of_lane(count, size)
    return [jnp.sum(jnp.where(mine, spread[i * count : (i + 1) * count], 0.0), axis=0, keepdims=True)
            for i in range(len(rows))]


def forward_kernel(n, groups, heads, orders, sizes, table, x, first, *refs):
    vectors, shards, refs = refs[:9], refs[9:15], refs[15:]
    hidden_out, q_out, kv_out, ol_out, back = refs[:5]
    fulls_out, vectors_out, refs = refs[5:11], refs[11:20], refs[20:]
    hidden_held, q_all, kv_all, ol_all, wq_full, wk_full, wv_full, stores, head_stores = refs[:9]
    fulls, refs = (wq_full, wk_full, wv_full) + fulls_out[3:], refs[9:]
    leaving = [(wq_full, fulls_out[0]), (wk_full, fulls_out[1]), (wv_full, fulls_out[2]), (hidden_held, hidden_out)]

    def leave(i):
        return pltpu.make_async_copy(leaving[i][0], leaving[i][1], stores.at[i])

    def leave_head(j):
        return [pltpu.make_async_copy(held.at[j], out.at[j], head_stores.at[k, j])
                for k, (held, out) in enumerate(((q_all, q_out), (kv_all, kv_out), (ol_all, ol_out)))]

    packed, small_full, q_staged, kv_staged, o_staged, q_work, kv_work = refs[:7]
    q_send, kv_send, relay_send, o_send, q_recv, kv_recv, o_recv = refs[7:14]
    sems = refs[14:]
    ex = Exchange(n)
    chips = n // 2
    bits = powers(groups)
    levels = len(bits)
    enter(ex.peers() + [{"grp": lax.axis_index("grp") ^ bit} for bit in bits])
    gathers = [
        Gather(groups, chips, order, shard, full, *[s.at[i] for s in sems])
        for i, (order, shard, full) in enumerate(zip(orders, (packed,) + shards, (small_full,) + fulls))
    ]
    near, far = gathers[:4], gathers[4:]
    packed[...] = jnp.zeros(packed.shape, jnp.float32)
    for row, vector in enumerate(vectors):
        packed[row : row + 1, : vector.shape[1]] = vector[...].astype(jnp.float32)
    for g in (near[1], near[2], near[3], near[0]):
        g.begin()
    splits = ex.splits
    rows, width = x.shape
    share = rows // splits
    half = n // 2
    fresh = width - first.shape[1]
    normed, _ = normal_rows(x[...].astype(jnp.float32))

    def steps(some, along=1):
        out = []
        for distance in range(chips + levels):
            for g in some:
                if along == 1 and distance + 1 < chips:
                    out.append(functools.partial(g.along, distance + 1))
                if along == 2 and 2 <= distance + 1 < chips:
                    out.append(functools.partial(g.along_cross, distance + 1))
                for level in range(levels):
                    if 0 <= distance - level < chips:
                        out.append(functools.partial(g.over, level, distance - level))
        return out

    order = steps(near)
    cut = (min(len(order), len(near) * (1 + levels)), 3 * len(order) // 4)
    for step in order[: cut[0]]:
        step()
    for g in far:
        g.begin_chain()
    for step in order[cut[0] : cut[1]]:
        step()
    if chips > 1:
        for g in far:
            g.along_chain(1)
    for step in order[cut[1] :]:
        step()
    for g in near:
        g.swap()
    for g in far:
        g.begin_cross()
    for distance in range(1, min(2, chips)):
        for g in far:
            g.along_cross(distance)
    for distance in range(2, chips):
        for g in far:
            g.along_chain(distance)
    for g in near:
        g.finish()
    small = small_full[...].reshape((2 * chips * groups,) + packed.shape)

    def open_vectors(some):
        for size in sorted({sizes[row] for row in some}):
            same = [row for row in some if sizes[row] == size]
            for row, value in zip(same, gather_vectors(small, same, size)):
                vectors_out[row][...] = value

    open_vectors(range(4))
    gain, shift, bq, bv = vectors_out[:4]
    wq, wk, wv = [fulls[i][...].reshape(width, -1) for i in range(3)]
    hidden = (normed * gain[...] + shift[...]).astype(jnp.bfloat16)
    hidden_held[...] = hidden
    for i in range(4):
        leave(i).start()
    for step in range(width // 256):
        cols = slice(step * 256, (step + 1) * 256)
        q = product(hidden, wq[:, cols]) + bq[:, cols]

        def store(head, split, v, step=step):
            head = head + 4 * step
            q_staged[head // heads, head % heads, split] = (v * 0.125).astype(jnp.bfloat16)

        pack_heads(q, splits, store)
        k = product(hidden, wk[:, cols])
        for tile in range(2):
            at = step * 256 + tile * 128
            if at < fresh:
                v = product(hidden, wv[:, at : at + 128]) + bv[:, at : at + 128]
            else:
                v = first[:, at - fresh : at - fresh + 128].astype(jnp.float32)
            kt = k[:, tile * 128 : (tile + 1) * 128]
            low = lanes(kt.shape) < 64
            head = at // 64
            kv_staged[head // heads, head % heads] = jnp.where(low, kt, swap_lanes(v)).astype(jnp.bfloat16)
            head = head + 1
            kv_staged[head // heads, head % heads] = jnp.where(low, swap_lanes(kt), v).astype(jnp.bfloat16)

    @pl.loop(0, heads)
    def _(j):
        for copy in ex.spread(j, kv_staged, kv_all, kv_send, kv_recv):
            copy.start()
        for copy in ex.scatter(j, q_staged, q_all, q_send, q_recv):
            copy.start()
        ex.own(j, q_staged, q_all, q_recv).start()
        ex.own_rows(j, kv_staged, kv_all, kv_recv).start()

    slot = slots_of(table, n)
    row = lax.broadcasted_iota(jnp.int32, (share, rows), 0) + ex.split * share
    own_mask = lax.broadcasted_iota(jnp.int32, (share, rows), 1) <= row

    def piece(j, place, at, keys):
        q = unfold(q_work[at].astype(jnp.float32), False).astype(jnp.bfloat16)
        blocks = [kv_work[k] for k in keys] + [kv_work[at]]
        scores = [product_right(q, block) for block in blocks]
        scores[-1] = jnp.where(own_mask, scores[-1], NEG)
        top = scores[0]
        for s in scores[1:]:
            top = jnp.maximum(top, s)
        top = jnp.max(top, axis=1, keepdims=True)
        total = jnp.zeros((share, rows), jnp.float32)
        out = jnp.zeros((share, 128), jnp.float32)
        for s, block in zip(scores, blocks):
            weight = jnp.exp(s - top)
            total = total + weight
            out = out + product(weight.astype(jnp.bfloat16), block)
        denom = jnp.sum(total, axis=1, keepdims=True)
        out = out / denom
        ol_all[j, place] = jnp.where(lanes(out.shape) < 64, top + jnp.log(denom), out)

    later = steps(far, 2)
    cut = (3 * len(later) // 4, 7 * len(later) // 8)
    for step in later[: cut[0]]:
        step()
    open_vectors(range(4, 9))

    @pl.loop(0, heads)
    def _(j):
        for off in range(PARTS):
            at, copies = ex.relay(j, off, kv_all, relay_send, kv_recv)
            here(kv_all.at[j, at], kv_recv.at[j, at])
            for copy in copies:
                copy.start()
        for t in range(n):
            here(q_all.at[j, t], q_recv.at[j, t])
        for off in range(PARTS):
            for hop in range(1, splits):
                at = lax.rem(ex.part + off, PARTS) * splits + lax.rem(ex.split + hop, splits)
                here(kv_all.at[j, at], kv_recv.at[j, at])
        for t in range(n):
            q_work[t] = q_all[j, t]
            kv_work[t] = kv_all[j, t]

        @pl.loop(0, half)
        def _(c):
            piece(j, half + c, pick(slot[half:], c), slot[:half])

        for p in range(half):
            piece(j, p, slot[p], slot[:p])
        for t in range(n):
            o_staged[j, t] = fold(ol_all[j, table[0, t]], True).astype(jnp.bfloat16)
        for copy in ex.give_back(j, heads, o_staged, back, o_send, o_recv):
            copy.start()
        ex.keep_own(j, heads, o_staged, back, o_recv).start()
        for copy in leave_head(j):
            copy.start()

        @pl.when(j == 0)
        def _():
            for step in later[cut[0] : cut[1]]:
                step()

        @pl.when(j == min(1, heads - 1))
        def _():
            for step in later[cut[1] :]:
                step()
            for g in far:
                g.swap()

    @pl.loop(0, heads)
    def _(j):
        for copy in ex.spread(j, kv_staged, kv_all, kv_send, kv_recv):
            copy.wait_send()
        for copy in ex.scatter(j, q_staged, q_all, q_send, q_recv):
            copy.wait_send()
        for off in range(PARTS):
            for copy in ex.relay(j, off, kv_all, relay_send, kv_recv)[1]:
                copy.wait_send()
        for copy in ex.give_back(j, heads, o_staged, back, o_send, o_recv):
            copy.wait_send()
        for t in range(n):
            landed = back.at[t // splits * heads + j, t % splits]
            here(landed, o_recv.at[j, t])
    for g in far:
        g.finish()
    for i in range(4):
        leave(i).wait()

    @pl.loop(0, heads)
    def _(j):
        for copy in leave_head(j):
            copy.wait()


def forward_call(n, groups, table, x, first, vectors, shards):
    rows, width = x.shape
    splits = n // PARTS
    chips = n // 2
    heads = width // 64 // PARTS
    share = rows // splits
    low = jnp.bfloat16
    vmem, dma = pltpu.VMEM, pltpu.SemaphoreType.DMA
    inside, outside = pl.BlockSpec(memory_space=vmem), pl.BlockSpec(memory_space=pl.ANY)
    shape = jax.ShapeDtypeStruct
    bits = powers(groups)
    forth, behind = bits, bits[::-1]
    sizes = [v.shape[1] * groups * n for v in vectors]
    block = (groups, chips, 2)
    return pl.pallas_call(
        functools.partial(forward_kernel, n, groups, heads, [forth, forth, behind, forth, behind, forth, behind], sizes),
        out_shape=[
            shape((rows, width), low),
            shape((heads, n, share // 2, 128), low),
            shape((heads, n, rows, 128), low),
            shape((heads, n, share, 128), jnp.float32),
            shape((PARTS * heads, splits, share // 2, 128), low),
        ]
        + [shape(block + w.shape, low) for w in shards]
        + [shape((1, size), jnp.float32) for size in sizes],
        in_specs=[pl.BlockSpec(memory_space=pltpu.SMEM)] + [inside] * 11 + [outside] * 6,
        out_specs=[outside] * 4 + [inside] + [outside] * 6 + [inside] * 9,
        scratch_shapes=[
            vmem((rows, width), low),
            vmem((heads, n, share // 2, 128), low),
            vmem((heads, n, rows, 128), low),
            vmem((heads, n, share, 128), jnp.float32),
        ]
        + [vmem(block + w.shape, low) for w in shards[:3]]
        + [
            dma((4,)),
            dma((3, heads)),
            vmem((16, 128), jnp.float32),
            vmem(block + (16, 128), jnp.float32),
            vmem((PARTS, heads, splits, share // 2, 128), low),
            vmem((PARTS, heads, rows, 128), low),
            vmem((heads, n, share // 2, 128), low),
            vmem((n, share // 2, 128), low),
            vmem((n, rows, 128), low),
            dma((heads, n - 1)),
            dma((heads, PARTS - 1)),
            dma((heads, PARTS, max(splits - 1, 1))),
            dma((heads, n - 1)),
            dma((heads, n)),
            dma((heads, n)),
            dma((heads, n)),
        ]
        + gather_semaphores(7, groups, chips),
        compiler_params=pltpu.CompilerParams(
            collective_id=1, has_side_effects=True, vmem_limit_bytes=64000000
        ),
        name="attention_forward",
    )(table, x, first, *vectors, *shards)


def join_tiles(even, odd, high):
    low = lanes(even.shape) < 64
    if high:
        return jnp.where(low, swap_lanes(even), odd)
    return jnp.where(low, even, swap_lanes(odd))


def join_rows(back):
    heads, splits = back.shape[0], back.shape[1]
    tiles = []
    for tile in range(heads // 2):
        parts = []
        for split in range(splits):
            even = back[2 * tile, split].astype(jnp.float32)
            odd = back[2 * tile + 1, split].astype(jnp.float32)
            parts += [join_tiles(even, odd, False), join_tiles(even, odd, True)]
        tiles.append(jnp.concatenate(parts, axis=0))
    return jnp.concatenate(tiles, axis=1)


def own_columns(j, heads, wq, wk, wv):
    def column(w, head):
        tile = w[:, head // 2 * 128 : head // 2 * 128 + 128].astype(jnp.float32)
        return tile, head % 2

    tiles = []
    for w in (wq, wk, wv):
        for part in range(0, w.shape[1] // 64 // heads, 2):
            (a, high_a), (b, high_b) = column(w, part * heads + j), column(w, (part + 1) * heads + j)
            a = swap_lanes(a) if high_a else a
            b = b if high_b else swap_lanes(b)
            tiles.append(jnp.where(lanes(a.shape) < 64, a, b).astype(jnp.bfloat16))
    return jnp.concatenate(tiles, axis=1)


def in_order(some, at, parts):
    heads = len(some)
    tiles = []
    for head in range(0, heads * parts, 2):
        def column(h):
            j, part = h % heads, h // heads
            start = at + part // 2 * 128
            return some[j][:, start : start + 128], part % 2

        (a, high_a), (b, high_b) = column(head), column(head + 1)
        a = swap_lanes(a) if high_a else a
        b = b if high_b else swap_lanes(b)
        tiles.append(jnp.where(lanes(a.shape) < 64, a, b))
    return jnp.concatenate(tiles, axis=1)


def own_vectors(sums, parts, fresh_parts):
    sums = [jnp.broadcast_to(s, (8, s.shape[1])) for s in sums]
    return [in_order(sums, 0, parts)[0:1], in_order(sums, parts * 128, fresh_parts)[0:1]]


def part_of_lane(count, size):
    part = size // count
    lane = lax.broadcasted_iota(jnp.int32, (count, size), 1)
    row = lax.broadcasted_iota(jnp.int32, (count, size), 0)
    return (lane >= row * part) & (lane < row * part + part)


def spread_vectors(vectors, count):
    size = vectors[0].shape[1]
    mine = part_of_lane(count, size)
    at = lax.broadcasted_iota(jnp.int32, (size, 128), 0)
    to = lax.broadcasted_iota(jnp.int32, (size, 128), 1)
    pick_part = jnp.where(lax.rem(at, size // count) == to, 1.0, 0.0).astype(jnp.bfloat16)
    rows = []
    for vector in vectors:
        value = jnp.where(mine, vector, 0.0)
        for _ in range(3):
            high = value.astype(jnp.bfloat16)
            rows.append(high)
            value = value - high.astype(jnp.float32)
    out = product(jnp.concatenate(rows, axis=0), pick_part)
    parts = [out[i * count : (i + 1) * count] for i in range(len(rows))]
    return [(parts[3 * i] + parts[3 * i + 1] + parts[3 * i + 2]).reshape(count, 1, 128) for i in range(len(vectors))]


def backward_kernel(
    n, groups, heads, orders_far, orders_near,
    table, do_in, gain, s_gain2, s_bias2, s_ob, s_eb, s_rb, q_in, kv_in, ol_in, hidden_in, x_in, dmid_in,
    wq_in, wk_in, wv_in, *refs,
):
    count = len(orders_far)
    far_in, refs = refs[:count], refs[count:]
    token_grad, first_grad = refs[:2]
    far_out, refs = refs[2 : 2 + count], refs[2 + count :]
    near_out, refs = refs[: 2 * heads + 1], refs[2 * heads + 1 :]
    do_all, do_work, acc, dq_piece, dq_staged, part_staged, part_all, dkv_staged, dq_back, dkv_back = refs[:10]
    refs = refs[10:]
    near_in, refs = refs[: 2 * heads + 1], refs[2 * heads + 1 :]
    weights, h_across, refs = refs[:heads], refs[heads], refs[heads + 1 :]
    q_all, kv_all, ol_all, hidden, x, dmid, wq, wk, wv, loads = refs[:10]
    refs = refs[10:]
    do_send, do_recv, dq_send, dq_recv, part_send, part_recv, dkv_send, dkv_recv = refs[:8]
    scratch = refs[8:]

    def full_copy(source, held, at):
        pltpu.make_async_copy(source, held, loads.at[at]).wait()
        return held

    entering = [(hidden_in, hidden, 3), (wq_in, wq, 6), (wk_in, wk, 7), (wv_in, wv, 8), (q_in, q_all, 0),
                (kv_in, kv_all, 1), (ol_in, ol_all, 2), (x_in, x, 4), (dmid_in, dmid, 5)]
    ex = Exchange(n)
    chips = n // 2
    g, z, c = lax.axis_index("grp"), ex.s // 2, lax.rem(ex.s, 2)
    enter(ex.peers() + [
        {"grp": lax.rem(g + off // chips, groups), "seq": 2 * lax.rem(z + off % chips, chips) + c}
        for off in range(chips, groups * chips)
    ])
    small = make_direct(groups, chips, near_in[-1], near_out[-1], scratch[-7:])
    scratch = scratch[:-7]
    each = len(scratch) // (count + 2 * heads)
    far = make_reduces(groups, chips, orders_far, far_in, far_out, scratch[: count * each], True)
    near = make_reduces(groups, chips, orders_near, near_in[:-1], near_out[:-1], scratch[count * each :])
    near_last = near[-2:]
    near_first = near[:-2]
    splits = ex.splits
    rows = kv_all.shape[2]
    share = rows // splits
    half = n // 2
    fresh = wv.shape[1]

    @pl.loop(0, heads)
    def _(j):
        for copy in ex.scatter(j, do_in, do_all, do_send, do_recv):
            copy.start()
        ex.own(j, do_in, do_all, do_recv).start()

    for source, held, at in entering:
        pltpu.make_async_copy(source, held, loads.at[at]).start()
    for r in far:
        r.begin()
    for source, held, at in entering[:7]:
        full_copy(source, held, at)
    low = jnp.bfloat16
    fresh_parts = PARTS * fresh // x.shape[1]
    h_across[...] = jnp.transpose(hidden[...])
    for j in range(heads):
        weights[j][...] = own_columns(j, heads, wq, wk, wv)
    slot = slots_of(table, n)
    column = lax.broadcasted_iota(jnp.int32, (rows, share), 1) + ex.split * share
    own_mask = lax.broadcasted_iota(jnp.int32, (rows, share), 0) <= column

    def piece(j, place, at, keys):
        q = unfold(q_all[j, at].astype(jnp.float32), False).astype(jnp.bfloat16)
        grad = unfold(do_work[at].astype(jnp.float32), True)
        ol = ol_all[j, place]
        delta = jnp.sum(jnp.transpose(grad * ol), axis=0, keepdims=True)
        logsum = jnp.transpose(ol)[0:1]
        grad = grad.astype(jnp.bfloat16)

        def block_terms(key_place, key_slot, mask):
            block = kv_all[j, key_slot]
            weight = jnp.exp(product_right(block, q) - logsum)
            if mask:
                weight = jnp.where(own_mask, weight, 0.0)
            change = (weight * (product_right(block, grad) - delta)).astype(jnp.bfloat16)
            term = product(weight.astype(jnp.bfloat16), grad) + product(change, q)
            acc[key_place] = acc[key_place] + term
            return product_left(block, change)

        dq = block_terms(place, at, True)
        if len(keys) in (2, 3):
            slots = [s for _, s in keys]
            dq = lax.fori_loop(0, len(keys), lambda k, v: v + block_terms(k, pick(slots, k), False), dq)
        else:
            for key_place, key_slot in keys:
                dq = dq + block_terms(key_place, key_slot, False)
        dq_piece[place] = fold(jnp.transpose(dq) * 0.125, False).astype(jnp.bfloat16)

    def part_copies(j):
        out = []
        for hop in range(1, splits):
            split = lax.rem(ex.split + hop, splits)
            for part in range(PARTS):
                out.append(remote(part_staged.at[j, hop - 1, part], part_all.at[j, hop - 1, part],
                                  part_send.at[j, hop - 1, part], part_recv.at[j, hop - 1, part],
                                  {"seq": ex.part * splits + split}))
        return out

    def back_copies(j):
        out = []
        row = ex.part * heads + j
        for off in range(1, PARTS):
            part = lax.rem(ex.part + off, PARTS)
            out.append(remote(dkv_staged.at[j, part], dkv_back.at[row], dkv_send.at[j, off - 1],
                              dkv_recv.at[j, ex.part], {"seq": part * splits + ex.split}))
        return out

    @pl.loop(0, heads)
    def _(j):
        for t in range(n):
            here(do_all.at[j, t], do_recv.at[j, t])
        for t in range(n):
            do_work[t] = do_all[j, t]
            acc[t] = jnp.zeros((rows, 128), jnp.float32)

        @pl.loop(0, half)
        def _(c):
            piece(j, half + c, pick(slot[half:], c), [(p, slot[p]) for p in range(half)])

            @pl.when((j == 0) & (c == 1))
            def _():
                for r in far:
                    r.paired()

            @pl.when((j == heads - 1) & (c == 1))
            def _():
                for r in far:
                    r.crossed(0)

        for p in range(half):
            piece(j, p, slot[p], [(k, slot[k]) for k in range(p)])
        for hop in range(1, splits):
            split = lax.rem(ex.split + hop, splits)
            for part in range(PARTS):
                part_staged[j, hop - 1, part] = acc[table[0, part * splits + split]].astype(jnp.bfloat16)
        for copy in part_copies(j):
            copy.start()
        for t in range(n):
            dq_staged[j, t] = dq_piece[table[0, t]]
        for hop in range(1, splits):
            for part in range(PARTS):
                here(part_all.at[j, hop - 1, part], part_recv.at[j, hop - 1, part])
        for part in range(PARTS):
            total = acc[table[0, part * splits + ex.split]]
            for hop in range(1, splits):
                total = total + part_all[j, hop - 1, part].astype(jnp.float32)
            dkv_staged[j, part] = total.astype(jnp.bfloat16)
        for copy in back_copies(j):
            copy.start()
        pltpu.make_async_copy(dkv_staged.at[j, ex.part], dkv_back.at[ex.part * heads + j],
                              dkv_recv.at[j, ex.part]).start()
        for copy in ex.give_back(j, heads, dq_staged, dq_back, dq_send, dq_recv):
            copy.start()
        ex.keep_own(j, heads, dq_staged, dq_back, dq_recv).start()

    levels = len(powers(groups))

    def total(v):
        return jnp.sum(v, axis=0, keepdims=True)

    def project(j):
        for t in range(n):
            here(dq_back.at[t // splits * heads + j, t % splits], dq_recv.at[j, t])
        for part in range(PARTS):
            here(dkv_back.at[part * heads + j], dkv_recv.at[j, part])
        tiles = []
        for part in range(0, PARTS, 2):
            a, b = part * heads + j, part * heads + heads + j
            parts = []
            for split in range(splits):
                even, odd = dq_back[a, split].astype(jnp.float32), dq_back[b, split].astype(jnp.float32)
                parts += [join_tiles(even, odd, False), join_tiles(even, odd, True)]
            tiles.append(jnp.concatenate(parts, axis=0))
        pairs = [(dkv_back[part * heads + j].astype(jnp.float32), dkv_back[(part + 1) * heads + j].astype(jnp.float32))
                 for part in range(0, PARTS, 2)]
        tiles += [join_tiles(a, b, False) for a, b in pairs]
        tiles += [join_tiles(a, b, True) for a, b in pairs[: fresh_parts // 2]]
        grad = jnp.concatenate(tiles, axis=1)
        sums = total(grad)
        grad = grad.astype(low)
        for ref, r, value in ((near_in[2 * j + 1], near[2 * j + 1], grad[:, PARTS * 64 :]),
                              (near_in[2 * j], near[2 * j], grad[:, : PARTS * 64])):
            ref[...] = product(h_across[...], value).reshape(ref.shape).astype(low)
            r.begin()
        return product_right(grad, weights[j][...]), sums

    devices = groups * n
    ob, gain2, bias2, rb = spread_vectors([s_ob[...], s_gain2[...], s_bias2[...], s_rb[...]], devices)
    later_rows = [ob, gain2, bias2] + spread_vectors([s_eb[...]], devices) + [rb]
    later_rows.append(jnp.zeros((devices, 16 - 9, 128), jnp.float32))
    done = [project(0)]
    for r in far:
        for level in range(1, levels):
            r.crossed(level)
    done += [project(j) for j in range(1, heads - 1)]
    for r in near_first:
        r.paired()
    normed, scale = normal_rows(full_copy(x_in, x, 4)[...].astype(jnp.float32))
    for level in range(levels - 1):
        for r in near_first:
            r.crossed(level)
    done.append(project(heads - 1))
    for r in far:
        r.chained(True)
    for r in near_first:
        r.crossed(levels - 1)
    dh = done[0][0]
    for more, _ in done[1:]:
        dh = dh + more
    for r in near_last:
        r.paired()
    sums = [total(dh * normed), total(dh)]
    sum_q, sum_v = own_vectors([s for _, s in done], PARTS, fresh_parts)
    first_rows = spread_vectors(sums + [sum_q], devices) + spread_vectors([sum_v], devices)
    spread = jnp.concatenate(first_rows + later_rows, axis=1)
    near_in[-1][...] = spread.reshape(near_in[-1].shape)
    small.begin()
    for level in range(levels):
        for r in near_last:
            r.crossed(level)
        if level == 0:
            small.paired()
    scaled = dh * gain[...].astype(jnp.float32)
    inner = jnp.mean(scaled, axis=-1, keepdims=True)
    along = jnp.mean(scaled * normed, axis=-1, keepdims=True)
    token_grad[...] = full_copy(dmid_in, dmid, 5)[...] + scale * (scaled - inner - normed * along)
    for pair in range(fresh // 64, PARTS * heads, 2):
        even, odd = dkv_back[pair].astype(jnp.float32), dkv_back[pair + 1].astype(jnp.float32)
        first_grad[:, pair * 64 - fresh : pair * 64 - fresh + 128] = join_tiles(even, odd, True)
    for r in far:
        r.chained(False)
    for r in far:
        r.chain_finish()
    for r in near:
        r.finish()
    small.direct_finish()
    for r in far + near + [small]:
        r.drain()

    @pl.loop(0, heads)
    def _(j):
        for copy in ex.scatter(j, do_in, do_all, do_send, do_recv):
            copy.wait_send()
        for copy in part_copies(j):
            copy.wait_send()
        for copy in back_copies(j):
            copy.wait_send()
        for copy in ex.give_back(j, heads, dq_staged, dq_back, dq_send, dq_recv):
            copy.wait_send()


def backward_call(n, groups, table, do_in, q_all, kv_all, ol_all, hidden, x, gain, wq, wk, wv, dmid, sums, far):
    heads, _, rows, _ = kv_all.shape
    splits = n // PARTS
    chips = n // 2
    share = rows // splits
    width, fresh = wv.shape
    low = jnp.bfloat16
    vmem, dma = pltpu.VMEM, pltpu.SemaphoreType.DMA
    inside = pl.BlockSpec(memory_space=vmem)
    shape = jax.ShapeDtypeStruct
    bits = powers(groups)
    forth, back = bits, bits[::-1]
    block = (groups, chips, 2)
    part = width // (groups * n)
    wide = 2 * PARTS * 64 + PARTS * 64 * fresh // width
    near = [block + (part, PARTS * 64, low), block + (part, wide - PARTS * 64, low)] * heads
    near += [block + (16, 128, jnp.float32)]
    shapes = [f.shape + (low,) for f in far] + near
    return pl.pallas_call(
        functools.partial(backward_kernel, n, groups, heads, [forth, back, forth][: len(far)],
                          [(forth, back)[j % 2] for j in range(2 * heads)]),
        out_shape=[shape((rows, width), jnp.float32), shape((rows, width - fresh), jnp.float32)]
        + [shape(s[3:5], jnp.float32) for s in shapes],
        in_specs=[pl.BlockSpec(memory_space=pltpu.SMEM)] + [inside] * 7
        + [pl.BlockSpec(memory_space=pl.ANY)] * (9 + len(far)),
        out_specs=[inside] * (3 + 2 * heads + len(far)),
        scratch_shapes=[
            vmem((heads, n, share // 2, 128), low),
            vmem((n, share // 2, 128), low),
            vmem((n, rows, 128), jnp.float32),
            vmem((n, share // 2, 128), low),
            vmem((heads, n, share // 2, 128), low),
            vmem((heads, max(splits - 1, 1), PARTS, rows, 128), low),
            vmem((heads, max(splits - 1, 1), PARTS, rows, 128), low),
            vmem((heads, PARTS, rows, 128), low),
            vmem((PARTS * heads, splits, share // 2, 128), low),
            vmem((PARTS * heads, rows, 128), low),
        ]
        + [vmem(s[:5], s[5]) for s in near]
        + [vmem((width, wide), low)] * heads
        + [vmem((width, rows), low)]
        + [vmem(v.shape, v.dtype) for v in (q_all, kv_all, ol_all, hidden, x, dmid, wq, wk, wv)]
        + [
            dma((9,)),
            dma((heads, n - 1)),
            dma((heads, n)),
            dma((heads, n - 1)),
            dma((heads, n)),
            dma((heads, max(splits - 1, 1), PARTS)),
            dma((heads, max(splits - 1, 1), PARTS)),
            dma((heads, PARTS - 1)),
            dma((heads, PARTS)),
        ]
        + reduce_scratch(groups, chips, shapes[: len(far)], True)
        + reduce_scratch(groups, chips, shapes[len(far) : -1])
        + direct_scratch(groups, chips, shapes[-1]),
        compiler_params=pltpu.CompilerParams(
            collective_id=2, has_side_effects=True, vmem_limit_bytes=67043328
        ),
        name="attention_backward",
    )(table, do_in, gain, *sums, q_all, kv_all, ol_all, hidden, x, dmid, wq, wk, wv, *far)


def hand_over_kernel(count, heads, sizes, fresh_parts, *refs):
    ins, refs = refs[:count], refs[count:]
    near, small, refs = refs[: 2 * heads], refs[2 * heads], refs[2 * heads + 1 :]
    outs, refs = refs[:count], refs[count:]
    g_wq, g_wk, g_wv = refs[:3]
    vectors, refs = refs[3 : 3 + len(sizes)], refs[3 + len(sizes) :]
    held, loads, stores = refs[:-2], refs[-2], refs[-1]
    for i in range(count):
        pltpu.make_async_copy(ins[i], held[i], loads.at[i]).start()
    some = [ref[...] for ref in near]
    g_wq[...] = in_order(some[::2], 0, PARTS)
    g_wk[...] = in_order(some[1::2], 0, PARTS)
    g_wv[...] = in_order(some[1::2], PARTS * 64, fresh_parts)
    for row, size in enumerate(sizes):
        vectors[row][...] = small[row : row + 1, :size]
    for i in range(count):
        pltpu.make_async_copy(ins[i], held[i], loads.at[i]).wait()
        pltpu.make_async_copy(held[i], outs[i], stores.at[i]).start()
    for i in range(count):
        pltpu.make_async_copy(held[i], outs[i], stores.at[i]).wait()


def hand_over(arrays, near, small, sizes, width, fresh):
    shape = jax.ShapeDtypeStruct
    count, heads = len(arrays), len(near) // 2
    rows = near[0].shape[0]
    inside, outside = pl.BlockSpec(memory_space=pltpu.VMEM), pl.BlockSpec(memory_space=pl.ANY)
    return pl.pallas_call(
        functools.partial(hand_over_kernel, count, heads, sizes, PARTS * fresh // width),
        out_shape=[shape(a.shape, a.dtype) for a in arrays]
        + [shape((rows, size), jnp.float32) for size in (width, width, fresh)]
        + [shape((1, size), jnp.float32) for size in sizes],
        in_specs=[outside] * count + [inside] * (2 * heads + 1),
        out_specs=[outside] * count + [inside] * (3 + len(sizes)),
        scratch_shapes=[pltpu.VMEM(a.shape, a.dtype) for a in arrays]
        + [pltpu.SemaphoreType.DMA((count,)), pltpu.SemaphoreType.DMA((count,))],
        compiler_params=pltpu.CompilerParams(vmem_limit_bytes=60000000),
        name="hand_over",
    )(*arrays, *near, small)


def feed_kernel(
    parts, heads, back, x, dy, bo, gain, shift, be, br, wo_in, we_in, wr_in,
    out, dmid_out, do_staged, s_gain, s_shift, s_ob, s_eb, s_rb, g_we, g_wr, g_wo,
    wo, we, wr, k_we, k_wr, k_wo, dh, load, keep,
):
    low = jnp.bfloat16
    rows, width = x.shape
    step = we.shape[1] // parts
    splits = back.shape[1]

    def total(v):
        return jnp.sum(v, axis=0, keepdims=True)

    def columns(c):
        return pl.ds(pl.multiple_of(c * step, 128), step)

    def fetch(c):
        return (pltpu.make_async_copy(we_in.at[:, columns(c)], we.at[:, columns(c)], load.at[c]),
                pltpu.make_async_copy(wr_in.at[columns(c)], wr.at[columns(c)], load.at[parts + c]))

    def store(c):
        return (pltpu.make_async_copy(k_we.at[:, columns(c)], g_we.at[:, columns(c)], keep.at[c]),
                pltpu.make_async_copy(k_wr.at[columns(c)], g_wr.at[columns(c)], keep.at[parts + c]))

    first = pltpu.make_async_copy(wo_in, wo, load.at[2 * parts])
    first.start()
    for c in range(parts):
        for copy in fetch(c):
            copy.start()
    att = join_rows(back).astype(low)
    first.wait()
    mid = x[...].astype(jnp.float32) + product(att, wo[...]) + bo[...]
    normed, scale = normal_rows(mid)
    second = (normed * gain[...] + shift[...]).astype(low)
    second_across = jnp.transpose(second)
    seed = dy[...]
    seed_full = seed.astype(jnp.float32)
    s_rb[...] = total(seed_full)
    dmid_out[...] = mid + br[...]
    dh[...] = jnp.zeros((rows, width), jnp.float32)

    @pl.loop(0, parts)
    def _(c):
        for copy in fetch(c):
            copy.wait()
        expand, reduce = we[:, columns(c)], wr[columns(c)]
        u = product(second, expand) + be[:, columns(c)]
        square = u * u
        t = jnp.tanh(math.sqrt(2 / math.pi) * (u + 0.044715 * (u * square)))
        z = (0.5 * u * (1.0 + t)).astype(low)
        slope = 0.5 * (1.0 + t) + (0.5 * math.sqrt(2 / math.pi)) * u * (1.0 - t * t) * (1.0 + (3 * 0.044715) * square)
        du_full = (slope * product_right(seed, reduce)).astype(low)
        s_eb[:, columns(c)] = total(du_full.astype(jnp.float32))
        dmid_out[...] += product(z, reduce)
        dh[...] += product_right(du_full, expand)
        k_wr[columns(c)] = product(jnp.transpose(z), seed).astype(low)
        k_we[:, columns(c)] = product(second_across, du_full).astype(low)
        for copy in store(c):
            copy.start()

    out[...] = dmid_out[...].astype(low)
    back_normed = dh[...]
    s_gain[...] = total(back_normed * normed)
    s_shift[...] = total(back_normed)
    scaled = back_normed * gain[...]
    inner = jnp.mean(scaled, axis=-1, keepdims=True)
    along = jnp.mean(scaled * normed, axis=-1, keepdims=True)
    dmid = seed_full + scale * (scaled - inner - normed * along)
    dmid_out[...] = dmid
    branch = dmid.astype(low)
    s_ob[...] = total(branch.astype(jnp.float32))
    k_wo[...] = product(jnp.transpose(att), branch).astype(low)
    last = pltpu.make_async_copy(k_wo, g_wo, keep.at[2 * parts])
    last.start()
    for group in range(width // 256):
        datt = product_right(branch, wo[group * 256 : (group + 1) * 256, :])

        def put(head, split, v, group=group):
            head = head + 4 * group
            do_staged[head // heads, head % heads, split] = v.astype(low)

        pack_heads(datt, splits, put)
    for c in range(parts):
        for copy in store(c):
            copy.wait()
    last.wait()


def feed_call(back, x, dy, bo, gain, shift, be, br, wo, we, wr):
    rows, width = x.shape
    inner = we.shape[1]
    parts = inner // width
    heads = back.shape[0] // PARTS
    splits = back.shape[1]
    low, full = jnp.bfloat16, jnp.float32
    vmem, dma = pltpu.VMEM, pltpu.SemaphoreType.DMA
    inside, outside = pl.BlockSpec(memory_space=vmem), pl.BlockSpec(memory_space=pl.ANY)
    shape = jax.ShapeDtypeStruct
    return pl.pallas_call(
        functools.partial(feed_kernel, parts, heads),
        out_shape=[
            shape((rows, width), low),
            shape((rows, width), full),
            shape((PARTS, heads) + back.shape[1:], low),
            shape((1, width), full),
            shape((1, width), full),
            shape((1, width), full),
            shape((1, inner), full),
            shape((1, width), full),
            shape(we.shape, low),
            shape(wr.shape, low),
            shape(wo.shape, low),
        ],
        in_specs=[inside] * 8 + [outside] * 3,
        out_specs=[inside] * 8 + [outside] * 3,
        scratch_shapes=[
            vmem(wo.shape, low), vmem(we.shape, low), vmem(wr.shape, low),
            vmem(we.shape, low), vmem(wr.shape, low), vmem(wo.shape, low),
            vmem((rows, width), full),
            dma((2 * parts + 1,)), dma((2 * parts + 1,)),
        ],
        compiler_params=pltpu.CompilerParams(vmem_limit_bytes=64000000),
        name="feed_forward",
    )(back, x, dy, bo, gain, shift, be, br, wo, we, wr)


def body(
    tokens,
    first_values,
    placement,
    cotangent,
    *parts,
):
    groups, rows, width = tokens.shape
    n = lax.axis_size("seq")
    small = (0, 1, 3, 6, 8, 9, 10, 12, 14)
    large = (2, 4, 5, 7, 11, 13)
    done = forward_call(n, lax.axis_size("grp"), placement, tokens[0], first_values[0],
                        [parts[i][None] for i in small], [parts[i] for i in large])
    hidden, q_all, kv_all, ol_all, back = done[:5]
    whole = [None] * 15
    for i, v in zip(large, done[5:11]):
        whole[i] = v.reshape(-1, v.shape[-1])
    for i, v in zip(small, done[11:]):
        whole[i] = v[0]
    layer_output, dmid, do_staged, *sums, g_we, g_wr, g_wo = feed_call(
        back, tokens[0], cotangent[0], whole[8][None], whole[9][None], whole[10][None], whole[12][None],
        whole[14][None], whole[7], whole[11], whole[13],
    )
    block = (lax.axis_size("grp"), n // 2, 2)
    far = [v.reshape(block + (-1, v.shape[1])) for v in (g_we, g_wr, g_wo)]
    inside = far if n <= 8 else []
    done = backward_call(
        n, block[0], placement, do_staged, q_all, kv_all, ol_all, hidden, tokens[0],
        whole[0][None], whole[2], whole[4], whole[5], dmid, [sums[0], sums[1], sums[2], sums[3], sums[4]],
        inside,
    )
    token_grad, first_grad = done[:2]
    if not inside:
        forth = powers(block[0])
        done = done[:2] + reduce_call(block[0], block[1], far, [forth, forth[::-1], forth]) + done[2:]
    g_we, g_wr, g_wo = done[2:5]
    near, g_small = done[5:-1], done[-1]
    sizes = [parts[i].shape[0] for i in small]
    out = hand_over([token_grad, first_grad, g_wo, g_we, g_wr], near, g_small, sizes, whole[2].shape[1], whole[5].shape[1])
    owned = [None] * 15
    for i, v in zip((7, 11, 13, 2, 4, 5), out[2:8]):
        owned[i] = v
    for i, v in zip(small, out[8:]):
        owned[i] = v.reshape(-1)
    return (layer_output[None], out[0][None], out[1][None]) + tuple(owned)


def solution(mesh):
    spread = P("grp", "seq", None)
    both = ("grp", "seq")
    vector, matrix = P(both), P(both, None)
    kinds = (vector, vector, matrix, vector, matrix, matrix, vector, matrix, vector, vector, vector,
             matrix, vector, matrix, vector)
    in_specs = (spread, spread, P("grp", None), spread) + kinds
    out_specs = (spread, spread, spread) + kinds
    return jax.shard_map(body, mesh=mesh, in_specs=in_specs, out_specs=out_specs, check_vma=False)
```

```python
import functools
import math

import jax
import jax.numpy as jnp
from jax import lax
from jax.experimental import pallas as pl
from jax.experimental.pallas import tpu as pltpu
from jax.sharding import PartitionSpec as P

MESH = pl.DeviceIdType.MESH


def powers(count):
    out, bit = [], 1
    while bit < count:
        out.append(bit)
        bit *= 2
    return out


def remote(src, dst, send, recv, device):
    return pltpu.make_async_remote_copy(
        src_ref=src, dst_ref=dst, send_sem=send, recv_sem=recv,
        device_id=device, device_id_type=MESH,
    )


def enter(devices):
    barrier = pltpu.get_barrier_semaphore()
    for device in devices:
        pl.semaphore_signal(barrier, inc=1, device_id=device, device_id_type=MESH)
    pl.semaphore_wait(barrier, len(devices))


class Gather:
    def __init__(self, groups, chips, bits, shard, full, chain_send, level_send, recv, pair, own,
                 direct=False):
        self.direct = direct
        self.groups, self.chips, self.bits = groups, chips, bits
        self.shard, self.full = shard, full
        self.chain_send, self.level_send, self.recv, self.pair, self.own = chain_send, level_send, recv, pair, own
        self.g = lax.axis_index("grp")
        seq = lax.axis_index("seq")
        self.s, self.z, self.c = seq, seq // 2, seq % 2

    def block(self, g, z, c):
        return self.full.at[g, z, c]

    def source(self, mask, z, first):
        return self.shard if first else self.block(self.g ^ mask, z, self.c)

    def chain(self, z, step, first):
        side = 0 if step < 0 else 1
        return remote(self.source(0, z, first), self.block(self.g, z, self.c),
                      self.chain_send.at[z, side], self.recv.at[self.g, z],
                      {"seq": self.s + 2 * step})

    def cross(self, level, mask, z, first):
        g = self.g ^ mask
        return remote(self.source(mask, z, first), self.block(g, z, self.c),
                      self.level_send.at[level], self.recv.at[g, z],
                      {"grp": self.g ^ self.bits[level]})

    def held(self, level):
        masks = [0]
        for bit in self.bits[:level]:
            masks = masks + [m ^ bit for m in masks]
        return masks

    def here(self, mask, z):
        g = self.g ^ mask
        pltpu.make_async_copy(self.block(g, z, self.c), self.block(g, z, self.c), self.recv.at[g, z]).wait()

    def begin(self):
        self.begin_chain()
        self.begin_cross()

    def begin_chain(self):
        copy = pltpu.make_async_copy(self.shard, self.block(self.g, self.z, self.c), self.own)
        copy.start()
        if self.direct:
            for out in self.direct_copies():
                out.start()
            return

        @pl.when(self.z > 0)
        def _():
            self.chain(self.z, -1, True).start()

        @pl.when(self.z < self.chips - 1)
        def _():
            self.chain(self.z, 1, True).start()

    def direct_copies(self):
        out = []
        for off in range(1, self.chips):
            chip = lax.rem(self.z + off, self.chips)
            out.append(remote(self.shard, self.block(self.g, self.z, self.c), self.chain_send.at[off, 0],
                              self.recv.at[self.g, self.z], {"seq": 2 * chip + self.c}))
        return out

    def begin_cross(self):
        for level in range(len(self.bits)):
            self.cross(level, 0, self.z, True).start()

    def at(self, distance, body):
        if distance == 0:
            body(self.z, 0)
            return

        @pl.when(self.z >= distance)
        def _():
            body(self.z - distance, 1)

        @pl.when(self.z + distance < self.chips)
        def _():
            body(self.z + distance, -1)

    def along(self, distance):
        self.along_chain(distance)
        self.along_cross(distance)

    def along_chain(self, distance):
        def body(z, step):
            self.here(0, z)
            if self.direct:
                return
            onward = self.z < self.chips - 1 if step > 0 else self.z > 0

            @pl.when(onward)
            def _():
                self.chain(z, step, False).start()

        self.at(distance, body)

    def along_cross(self, distance):
        def body(z, step):
            for level in range(len(self.bits)):
                self.cross(level, 0, z, False).start()

        self.at(distance, body)

    def over(self, level, distance):
        def body(z, step):
            for mask in self.held(level):
                mask = mask ^ self.bits[level]
                self.here(mask, z)
                for later in range(level + 1, len(self.bits)):
                    self.cross(later, mask, z, False).start()

        self.at(distance, body)

    def swap_copy(self):
        mine = self.full.at[:, :, self.c]
        return remote(mine, mine, self.pair.at[0], self.pair.at[1], {"seq": self.s ^ 1})

    def swap(self):
        pltpu.make_async_copy(self.shard, self.shard, self.own).wait()
        self.swap_copy().start()

    def finish(self):
        self.swap_copy().wait_send()
        other = self.full.at[:, :, 1 - self.c]
        pltpu.make_async_copy(other, other, self.pair.at[1]).wait()
        self.sent()

    def sent(self):
        if self.direct:
            for out in self.direct_copies():
                out.wait_send()
        else:
            self.chain_sent()
        for level in range(len(self.bits)):
            sent = self.full.at[pl.ds(0, 2 ** level), :, 0]
            pltpu.make_async_copy(sent, sent, self.level_send.at[level]).wait()

    def chain_sent(self):
        @pl.when(self.z > 0)
        def _():
            self.chain(self.z, -1, True).wait_send()

        @pl.when(self.z < self.chips - 1)
        def _():
            self.chain(self.z, 1, True).wait_send()

        for distance in range(1, self.chips):
            def body(z, step):
                onward = self.z < self.chips - 1 if step > 0 else self.z > 0

                @pl.when(onward)
                def _():
                    self.chain(z, step, False).wait_send()

            self.at(distance, body)


def gather_semaphores(count, groups, chips):
    dma = pltpu.SemaphoreType.DMA
    levels = max(len(powers(groups)), 1)
    return [dma((count, chips, 2)), dma((count, levels)), dma((count, groups, chips)), dma((count, 2)), dma((count,))]


def neighbours(groups, n):
    g, s = lax.axis_index("grp"), lax.axis_index("seq")
    out = [{"grp": g ^ bit} for bit in powers(groups)]
    out += [{"seq": s ^ 1}, {"seq": lax.rem(s + 2, n)}, {"seq": lax.rem(s + n - 2, n)}]
    return out


def gather_kernel(groups, chips, orders, *refs):
    count = len(orders)
    shards, fulls, sems = refs[:count], refs[count:2 * count], refs[2 * count:]
    enter(neighbours(groups, 2 * chips))
    gathers = [Gather(groups, chips, orders[i], shards[i], fulls[i], *[s.at[i] for s in sems]) for i in range(count)]
    run_gathers(gathers)


def run_gathers(gathers):
    chips, levels = gathers[0].chips, len(gathers[0].bits)
    for g in gathers:
        g.begin()
    for distance in range(chips + levels):
        for g in gathers:
            if distance + 1 < chips:
                g.along(distance + 1)
            for level in range(levels):
                if 0 <= distance - level < chips:
                    g.over(level, distance - level)
    for g in gathers:
        g.swap()
    for g in gathers:
        g.finish()


def gather_call(groups, chips, shards, orders):
    count = len(shards)
    return pl.pallas_call(
        functools.partial(gather_kernel, groups, chips, orders),
        out_shape=[jax.ShapeDtypeStruct((groups, chips, 2) + x.shape, x.dtype) for x in shards],
        in_specs=[pl.BlockSpec(memory_space=pl.ANY)] * count,
        out_specs=[pl.BlockSpec(memory_space=pl.ANY)] * count,
        scratch_shapes=gather_semaphores(count, groups, chips),
        compiler_params=pltpu.CompilerParams(collective_id=0, has_side_effects=True),
        name="gather_parameters",
    )(*shards)


class Reduce:
    def __init__(self, groups, chips, bits, partial, shard, own, landed, halves, finals, sems,
                 chain=False, direct=False):
        self.chain, self.direct = chain, direct
        self.groups, self.chips, self.bits = groups, chips, bits
        self.partial, self.shard, self.own, self.landed = partial, shard, own, landed
        self.halves, self.finals, self.mail = halves, finals, halves[0] if direct else None
        self.load, self.pair, self.level_send, self.level_recv, self.chip_send, self.chip_recv = sems
        self.g = lax.axis_index("grp")
        self.s = lax.axis_index("seq")
        self.z, self.c = self.s // 2, self.s % 2

    def masks(self, level):
        out = [0]
        for bit in self.bits[level:]:
            out = out + [m ^ bit for m in out]
        return out

    def load_copy(self):
        return pltpu.make_async_copy(self.partial.at[:, :, self.c], self.own, self.load.at[0])

    def pair_copy(self):
        return remote(self.partial.at[:, :, 1 - self.c], self.landed, self.pair.at[0], self.pair.at[1],
                      {"seq": self.s ^ 1})

    def begin(self):
        self.pair_copy().start()
        self.load_copy().start()

    def paired(self):
        self.load_copy().wait()
        self.pair_copy().wait_recv()

        @pl.loop(0, self.groups)
        def _(g):
            @pl.loop(0, self.chips)
            def _(z):
                self.own[g, z] = self.add(self.own[g, z], self.landed[g, z])

        self.cross_start(0)

    def add(self, a, b):
        return a + b

    def cross_copies(self, level):
        bit = self.bits[level]
        out = []
        for where, mask in enumerate(self.masks(level + 1)):
            out.append(remote(self.own.at[self.g ^ bit ^ mask], self.halves[level].at[where],
                              self.level_send.at[level, where], self.level_recv.at[level, where],
                              {"grp": self.g ^ bit}))
        return out

    def cross_start(self, level):
        if self.direct:
            for copy in self.direct_copies():
                copy.start()
        elif level < len(self.bits):
            for copy in self.cross_copies(level):
                copy.start()
        else:
            self.chip_start()

    def chip_start(self):
        if self.chain:
            self.chain_first()
        else:
            for copy in self.chip_copies():
                copy.start()

    def crossed(self, level, onward=True):
        copies = self.cross_copies(level)
        for where, mask in enumerate(self.masks(level + 1)):
            copies[where].wait_recv()
            g = self.g ^ mask

            @pl.loop(0, self.chips)
            def _(z):
                self.own[g, z] = self.add(self.own[g, z], self.halves[level][where, z])

        if onward:
            self.cross_start(level + 1)

    def chain_copy(self, block, step):
        side = 0 if step > 0 else 1
        return remote(self.own.at[self.g, block], self.finals.at[side, block], self.chip_send.at[side, block],
                      self.chip_recv.at[side, block], {"seq": self.s + 2 * step})

    def chain_add(self, block, side):
        landed = self.finals.at[side, block]
        pltpu.make_async_copy(landed, landed, self.chip_recv.at[side, block]).wait()
        self.own[self.g, block] = self.add(self.own[self.g, block], self.finals[side, block])

    def chain_first(self):
        last = self.chips - 1

        @pl.when(self.z == 0)
        def _():
            for block in range(last, 0, -1):
                self.chain_copy(block, 1).start()

        @pl.when(self.z == last)
        def _():
            for block in range(last):
                self.chain_copy(block, -1).start()

    def chained(self, near_end):
        last = self.chips - 1
        left = self.z < self.chips // 2
        right = jnp.logical_not(left)
        for block in range(last, 0, -1):
            @pl.when((self.z > 0) & (self.z < block) & (left if near_end else right))
            def _():
                self.chain_add(block, 0)
                self.chain_copy(block, 1).start()

        for block in range(last):
            @pl.when((self.z < last) & (self.z > block) & (right if near_end else left))
            def _():
                self.chain_add(block, 1)
                self.chain_copy(block, -1).start()

    def chain_finish(self):
        last = self.chips - 1

        @pl.when(self.z > 0)
        def _():
            self.chain_add(self.z, 0)

        @pl.when(self.z < last)
        def _():
            self.chain_add(self.z, 1)

        self.shard[...] = self.own[self.g, self.z].astype(jnp.float32)

    def chain_drain(self):
        for block in range(self.chips):
            @pl.when(self.z < block)
            def _():
                self.chain_copy(block, 1).wait_send()

            @pl.when(self.z > block)
            def _():
                self.chain_copy(block, -1).wait_send()

    def chip_copies(self):
        out = []
        for off in range(1, self.chips):
            chip = lax.rem(self.z + off, self.chips)
            out.append(remote(self.own.at[self.g, chip], self.finals.at[off - 1], self.chip_send.at[off - 1],
                              self.chip_recv.at[off - 1], {"seq": 2 * chip + self.c}))
        return out

    def direct_copies(self):
        out = []
        for off in range(1, self.groups * self.chips):
            g = lax.rem(self.g + off // self.chips, self.groups)
            z = lax.rem(self.z + off % self.chips, self.chips)
            out.append(remote(self.own.at[g, z], self.mail.at[off // self.chips, off % self.chips],
                              self.level_send.at[off], self.level_recv.at[off], {"grp": g, "seq": 2 * z + self.c}))
        return out

    def direct_finish(self):
        total = self.own[self.g, self.z]
        for off, copy in enumerate(self.direct_copies()):
            copy.wait_recv()
            total = total + self.mail[(off + 1) // self.chips, (off + 1) % self.chips]
        self.shard[...] = total

    def finish(self):
        total = self.own[self.g, self.z].astype(jnp.float32)
        for off, copy in enumerate(self.chip_copies()):
            copy.wait_recv()
            total = total + self.finals[off].astype(jnp.float32)
        self.shard[...] = total

    def drain(self):
        self.pair_copy().wait_send()
        if self.direct:
            for copy in self.direct_copies():
                copy.wait_send()
            return
        for level in range(len(self.bits)):
            for copy in self.cross_copies(level):
                copy.wait_send()
        if self.chain:
            self.chain_drain()
        else:
            for copy in self.chip_copies():
                copy.wait_send()


def reduce_steps(reduces):
    levels = len(reduces[0].bits)
    stages = [lambda r: r.begin(), lambda r: r.paired()]
    for level in range(levels):
        stages.append(lambda r, level=level: r.crossed(level))
    stages += [lambda r: r.finish(), lambda r: r.drain()]
    return [functools.partial(stage, r) for stage in stages for r in reduces]


def direct_scratch(groups, chips, shape):
    vmem, dma = pltpu.VMEM, pltpu.SemaphoreType.DMA
    whole = vmem((groups, chips) + shape[3:5], shape[5])
    count = groups * chips
    return [whole, whole, whole, dma((1,)), dma((2,)), dma((count,)), dma((count,))]


def make_direct(groups, chips, partial, shard, scratch):
    own, landed, mail, load, pair, send, recv = scratch
    return Reduce(groups, chips, powers(groups), partial, shard, own, landed, [mail], None,
                  (load, pair, send, recv, None, None), direct=True)


def reduce_scratch(groups, chips, shapes, chain=False):
    vmem, dma = pltpu.VMEM, pltpu.SemaphoreType.DMA
    levels = len(powers(groups))
    out = []
    for _, _, _, rows, cols, dtype in shapes:
        out += [vmem((groups, chips, rows, cols), dtype), vmem((groups, chips, rows, cols), dtype)]
        out += [vmem((groups >> (level + 1), chips, rows, cols), dtype) for level in range(levels)]
        out += [vmem((2, chips, rows, cols) if chain else (max(chips - 1, 1), rows, cols), dtype)]
        out += [dma((1,)), dma((2,)), dma((max(levels, 1), max(groups // 2, 1))),
                dma((max(levels, 1), max(groups // 2, 1))), dma((2, chips) if chain else (max(chips - 1, 1),)),
                dma((2, chips) if chain else (max(chips - 1, 1),))]
    return out


def make_reduces(groups, chips, orders, partials, shards, scratch, chain=False):
    levels = len(powers(groups))
    each = 2 + levels + 1 + 6
    out = []
    for i, (partial, shard) in enumerate(zip(partials, shards)):
        refs = scratch[i * each : (i + 1) * each]
        out.append(Reduce(groups, chips, orders[i], partial, shard, refs[0], refs[1], refs[2 : 2 + levels],
                          refs[2 + levels], refs[3 + levels :], chain))
    return out


def reduce_kernel(groups, chips, orders, *refs):
    count = len(orders)
    enter(neighbours(groups, 2 * chips))
    for step in reduce_steps(make_reduces(groups, chips, orders, refs[:count], refs[count : 2 * count],
                                          refs[2 * count :])):
        step()


def reduce_call(groups, chips, partials, orders):
    count = len(partials)
    shapes = [p.shape + (p.dtype,) for p in partials]
    return pl.pallas_call(
        functools.partial(reduce_kernel, groups, chips, orders),
        out_shape=[jax.ShapeDtypeStruct(p.shape[3:], jnp.float32) for p in partials],
        in_specs=[pl.BlockSpec(memory_space=pl.ANY)] * count,
        out_specs=[pl.BlockSpec(memory_space=pltpu.VMEM)] * count,
        scratch_shapes=reduce_scratch(groups, chips, shapes),
        compiler_params=pltpu.CompilerParams(collective_id=3, has_side_effects=True, vmem_limit_bytes=64000000),
        name="reduce_gradients",
    )(*partials)


PARTS = 4
NEG = -1e30
EPS = 1e-05


def lanes(shape):
    return lax.broadcasted_iota(jnp.int32, shape, len(shape) - 1)


def swap_lanes(v):
    return pltpu.roll(v, 64, 1)


def fold(v, high):
    half = v.shape[0] // 2
    top, bottom = v[:half], v[half:]
    low = lanes(top.shape) < 64
    if high:
        return jnp.where(low, swap_lanes(top), bottom)
    return jnp.where(low, top, swap_lanes(bottom))


def unfold(v, high):
    low = lanes(v.shape) < 64
    zero = jnp.zeros_like(v)
    if high:
        return jnp.concatenate([jnp.where(low, zero, swap_lanes(v)), jnp.where(low, zero, v)], axis=0)
    return jnp.concatenate([jnp.where(low, v, zero), jnp.where(low, swap_lanes(v), zero)], axis=0)


def product(a, b):
    return lax.dot_general(a, b, (((1,), (0,)), ((), ())), preferred_element_type=jnp.float32)


def product_right(a, b):
    return lax.dot_general(a, b, (((1,), (1,)), ((), ())), preferred_element_type=jnp.float32)


def product_left(a, b):
    return lax.dot_general(a, b, (((0,), (0,)), ((), ())), preferred_element_type=jnp.float32)


def normal_rows(v):
    mean = jnp.mean(v, axis=-1, keepdims=True)
    centred = v - mean
    var = jnp.mean(centred * centred, axis=-1, keepdims=True)
    scale = lax.rsqrt(var + EPS)
    return centred * scale, scale


def pack_heads(v, splits, store):
    size = v.shape[0] // splits
    for tile in range(v.shape[1] // 128):
        for split in range(splits):
            part = v[split * size : (split + 1) * size, tile * 128 : (tile + 1) * 128]
            store(2 * tile, split, fold(part, False))
            store(2 * tile + 1, split, fold(part, True))


def slots_of(table, count):
    out = []
    for piece in range(count):
        slot = jnp.int32(0)
        for place in range(count):
            slot = slot + jnp.where(table[0, place] == piece, place, 0)
        out.append(jnp.minimum(slot, count - 1))
    return out


def pick(values, index):
    out = values[0]
    for i in range(1, len(values)):
        out = jnp.where(index == i, values[i], out)
    return out


class Exchange:
    def __init__(self, n):
        self.n = n
        self.splits = n // PARTS
        self.s = lax.axis_index("seq")
        self.part, self.split = self.s // self.splits, lax.rem(self.s, self.splits)

    def peers(self):
        return [{"seq": lax.rem(self.s + off, self.n)} for off in range(1, self.n)]

    def other(self, off):
        return lax.rem(self.s + off, self.n)

    def scatter(self, j, staged, landed, send, recv):
        out = []
        for off in sorted(range(1, self.n), key=lambda o: abs(o - self.n // 2)):
            t = self.other(off)
            out.append(remote(staged.at[t // self.splits, j, lax.rem(t, self.splits)], landed.at[j, self.s],
                              send.at[j, off - 1], recv.at[j, self.s], {"seq": t}))
        return out

    def own(self, j, staged, landed, recv):
        return pltpu.make_async_copy(staged.at[self.part, j, self.split], landed.at[j, self.s], recv.at[j, self.s])

    def spread(self, j, staged, landed, send, recv):
        out = []
        for off in sorted(range(1, PARTS), key=lambda o: abs(o - PARTS // 2)):
            part = lax.rem(self.part + off, PARTS)
            out.append(remote(staged.at[part, j], landed.at[j, self.s], send.at[j, off - 1],
                              recv.at[j, self.s], {"seq": part * self.splits + self.split}))
        return out

    def own_rows(self, j, staged, landed, recv):
        return pltpu.make_async_copy(staged.at[self.part, j], landed.at[j, self.s], recv.at[j, self.s])

    def relay(self, j, off, landed, send, recv):
        slot = lax.rem(self.part + off, PARTS) * self.splits + self.split
        out = []
        for hop in range(1, self.splits):
            split = lax.rem(self.split + hop, self.splits)
            out.append(remote(landed.at[j, slot], landed.at[j, slot], send.at[j, off, hop - 1],
                              recv.at[j, slot], {"seq": self.part * self.splits + split}))
        return slot, out

    def give_back(self, j, heads, staged, landed, send, recv):
        out = []
        row = self.part * heads + j
        for off in sorted(range(1, self.n), key=lambda o: abs(o - self.n // 2)):
            t = self.other(off)
            out.append(remote(staged.at[j, t], landed.at[row, self.split], send.at[j, off - 1],
                              recv.at[j, self.s], {"seq": t}))
        return out

    def keep_own(self, j, heads, staged, landed, recv):
        return pltpu.make_async_copy(staged.at[j, self.s], landed.at[self.part * heads + j, self.split],
                                     recv.at[j, self.s])


def here(ref, sem):
    pltpu.make_async_copy(ref, ref, sem).wait()


def gather_vectors(full, rows, size):
    count = full.shape[0]
    at = lax.broadcasted_iota(jnp.int32, (128, size), 0)
    to = lax.broadcasted_iota(jnp.int32, (128, size), 1)
    place = jnp.where(lax.rem(to, size // count) == at, 1.0, 0.0).astype(jnp.bfloat16)
    some = jnp.concatenate([full[:, row, :].astype(jnp.bfloat16) for row in rows], axis=0)
    spread = product(some, place)
    mine = part_of_lane(count, size)
    return [jnp.sum(jnp.where(mine, spread[i * count : (i + 1) * count], 0.0), axis=0, keepdims=True)
            for i in range(len(rows))]


def forward_kernel(n, groups, heads, orders, sizes, table, x, first, *refs):
    vectors, shards, refs = refs[:9], refs[9:15], refs[15:]
    hidden_out, q_out, kv_out, ol_out, back = refs[:5]
    fulls_out, vectors_out, refs = refs[5:11], refs[11:20], refs[20:]
    hidden_held, q_all, kv_all, ol_all, wq_full, wk_full, wv_full, stores, head_stores = refs[:9]
    fulls, refs = (wq_full, wk_full, wv_full) + fulls_out[3:], refs[9:]
    leaving = [(wq_full, fulls_out[0]), (wk_full, fulls_out[1]), (wv_full, fulls_out[2]), (hidden_held, hidden_out)]

    def leave(i):
        return pltpu.make_async_copy(leaving[i][0], leaving[i][1], stores.at[i])

    def leave_head(j):
        return [pltpu.make_async_copy(held.at[j], out.at[j], head_stores.at[k, j])
                for k, (held, out) in enumerate(((q_all, q_out), (kv_all, kv_out), (ol_all, ol_out)))]

    packed, small_full, q_staged, kv_staged, o_staged, q_work, kv_work = refs[:7]
    q_send, kv_send, relay_send, o_send, q_recv, kv_recv, o_recv = refs[7:14]
    sems = refs[14:]
    ex = Exchange(n)
    chips = n // 2
    bits = powers(groups)
    levels = len(bits)
    enter(ex.peers() + [{"grp": lax.axis_index("grp") ^ bit} for bit in bits])
    gathers = [
        Gather(groups, chips, order, shard, full, *[s.at[i] for s in sems])
        for i, (order, shard, full) in enumerate(zip(orders, (packed,) + shards, (small_full,) + fulls))
    ]
    near, far = gathers[:4], gathers[4:]
    packed[...] = jnp.zeros(packed.shape, jnp.float32)
    for row, vector in enumerate(vectors):
        packed[row : row + 1, : vector.shape[1]] = vector[...].astype(jnp.float32)
    for g in (near[1], near[2], near[3], near[0]):
        g.begin()
    splits = ex.splits
    rows, width = x.shape
    share = rows // splits
    half = n // 2
    fresh = width - first.shape[1]
    normed, _ = normal_rows(x[...].astype(jnp.float32))

    def steps(some, along=1):
        out = []
        for distance in range(chips + levels):
            for g in some:
                if along == 1 and distance + 1 < chips:
                    out.append(functools.partial(g.along, distance + 1))
                if along == 2 and 2 <= distance + 1 < chips:
                    out.append(functools.partial(g.along_cross, distance + 1))
                for level in range(levels):
                    if 0 <= distance - level < chips:
                        out.append(functools.partial(g.over, level, distance - level))
        return out

    order = steps(near)
    cut = (min(len(order), len(near) * (1 + levels)), 3 * len(order) // 4)
    for step in order[: cut[0]]:
        step()
    for g in far:
        g.begin_chain()
    for step in order[cut[0] : cut[1]]:
        step()
    if chips > 1:
        for g in far:
            g.along_chain(1)
    for step in order[cut[1] :]:
        step()
    for g in near:
        g.swap()
    for g in far:
        g.begin_cross()
    for distance in range(1, min(2, chips)):
        for g in far:
            g.along_cross(distance)
    for distance in range(2, chips):
        for g in far:
            g.along_chain(distance)
    for g in near:
        g.finish()
    small = small_full[...].reshape((2 * chips * groups,) + packed.shape)

    def open_vectors(some):
        for size in sorted({sizes[row] for row in some}):
            same = [row for row in some if sizes[row] == size]
            for row, value in zip(same, gather_vectors(small, same, size)):
                vectors_out[row][...] = value

    open_vectors(range(4))
    gain, shift, bq, bv = vectors_out[:4]
    wq, wk, wv = [fulls[i][...].reshape(width, -1) for i in range(3)]
    hidden = (normed * gain[...] + shift[...]).astype(jnp.bfloat16)
    hidden_held[...] = hidden
    for i in range(4):
        leave(i).start()
    for step in range(width // 256):
        cols = slice(step * 256, (step + 1) * 256)
        q = product(hidden, wq[:, cols]) + bq[:, cols]

        def store(head, split, v, step=step):
            head = head + 4 * step
            q_staged[head // heads, head % heads, split] = (v * 0.125).astype(jnp.bfloat16)

        pack_heads(q, splits, store)
        k = product(hidden, wk[:, cols])
        for tile in range(2):
            at = step * 256 + tile * 128
            if at < fresh:
                v = product(hidden, wv[:, at : at + 128]) + bv[:, at : at + 128]
            else:
                v = first[:, at - fresh : at - fresh + 128].astype(jnp.float32)
            kt = k[:, tile * 128 : (tile + 1) * 128]
            low = lanes(kt.shape) < 64
            head = at // 64
            kv_staged[head // heads, head % heads] = jnp.where(low, kt, swap_lanes(v)).astype(jnp.bfloat16)
            head = head + 1
            kv_staged[head // heads, head % heads] = jnp.where(low, swap_lanes(kt), v).astype(jnp.bfloat16)

    @pl.loop(0, heads)
    def _(j):
        for copy in ex.spread(j, kv_staged, kv_all, kv_send, kv_recv):
            copy.start()
        for copy in ex.scatter(j, q_staged, q_all, q_send, q_recv):
            copy.start()
        ex.own(j, q_staged, q_all, q_recv).start()
        ex.own_rows(j, kv_staged, kv_all, kv_recv).start()

    slot = slots_of(table, n)
    row = lax.broadcasted_iota(jnp.int32, (share, rows), 0) + ex.split * share
    own_mask = lax.broadcasted_iota(jnp.int32, (share, rows), 1) <= row

    def piece(j, place, at, keys):
        q = unfold(q_work[at].astype(jnp.float32), False).astype(jnp.bfloat16)
        blocks = [kv_work[k] for k in keys] + [kv_work[at]]
        scores = [product_right(q, block) for block in blocks]
        scores[-1] = jnp.where(own_mask, scores[-1], NEG)
        top = scores[0]
        for s in scores[1:]:
            top = jnp.maximum(top, s)
        top = jnp.max(top, axis=1, keepdims=True)
        total = jnp.zeros((share, rows), jnp.float32)
        out = jnp.zeros((share, 128), jnp.float32)
        for s, block in zip(scores, blocks):
            weight = jnp.exp(s - top)
            total = total + weight
            out = out + product(weight.astype(jnp.bfloat16), block)
        denom = jnp.sum(total, axis=1, keepdims=True)
        out = out / denom
        ol_all[j, place] = jnp.where(lanes(out.shape) < 64, top + jnp.log(denom), out)

    later = steps(far, 2)
    cut = (3 * len(later) // 4, 7 * len(later) // 8)
    for step in later[: cut[0]]:
        step()
    open_vectors(range(4, 9))

    @pl.loop(0, heads)
    def _(j):
        for off in range(PARTS):
            at, copies = ex.relay(j, off, kv_all, relay_send, kv_recv)
            here(kv_all.at[j, at], kv_recv.at[j, at])
            for copy in copies:
                copy.start()
        for t in range(n):
            here(q_all.at[j, t], q_recv.at[j, t])
        for off in range(PARTS):
            for hop in range(1, splits):
                at = lax.rem(ex.part + off, PARTS) * splits + lax.rem(ex.split + hop, splits)
                here(kv_all.at[j, at], kv_recv.at[j, at])
        for t in range(n):
            q_work[t] = q_all[j, t]
            kv_work[t] = kv_all[j, t]

        @pl.loop(0, half)
        def _(c):
            piece(j, half + c, pick(slot[half:], c), slot[:half])

        for p in range(half):
            piece(j, p, slot[p], slot[:p])
        for t in range(n):
            o_staged[j, t] = fold(ol_all[j, table[0, t]], True).astype(jnp.bfloat16)
        for copy in ex.give_back(j, heads, o_staged, back, o_send, o_recv):
            copy.start()
        ex.keep_own(j, heads, o_staged, back, o_recv).start()
        for copy in leave_head(j):
            copy.start()

        @pl.when(j == 0)
        def _():
            for step in later[cut[0] : cut[1]]:
                step()

        @pl.when(j == min(1, heads - 1))
        def _():
            for step in later[cut[1] :]:
                step()
            for g in far:
                g.swap()

    @pl.loop(0, heads)
    def _(j):
        for copy in ex.spread(j, kv_staged, kv_all, kv_send, kv_recv):
            copy.wait_send()
        for copy in ex.scatter(j, q_staged, q_all, q_send, q_recv):
            copy.wait_send()
        for off in range(PARTS):
            for copy in ex.relay(j, off, kv_all, relay_send, kv_recv)[1]:
                copy.wait_send()
        for copy in ex.give_back(j, heads, o_staged, back, o_send, o_recv):
            copy.wait_send()
        for t in range(n):
            landed = back.at[t // splits * heads + j, t % splits]
            here(landed, o_recv.at[j, t])
    for g in far:
        g.finish()
    for i in range(4):
        leave(i).wait()

    @pl.loop(0, heads)
    def _(j):
        for copy in leave_head(j):
            copy.wait()


def forward_call(n, groups, table, x, first, vectors, shards):
    rows, width = x.shape
    splits = n // PARTS
    chips = n // 2
    heads = width // 64 // PARTS
    share = rows // splits
    low = jnp.bfloat16
    vmem, dma = pltpu.VMEM, pltpu.SemaphoreType.DMA
    inside, outside = pl.BlockSpec(memory_space=vmem), pl.BlockSpec(memory_space=pl.ANY)
    shape = jax.ShapeDtypeStruct
    bits = powers(groups)
    forth, behind = bits, bits[::-1]
    sizes = [v.shape[1] * groups * n for v in vectors]
    block = (groups, chips, 2)
    return pl.pallas_call(
        functools.partial(forward_kernel, n, groups, heads, [forth, forth, behind, forth, behind, forth, behind], sizes),
        out_shape=[
            shape((rows, width), low),
            shape((heads, n, share // 2, 128), low),
            shape((heads, n, rows, 128), low),
            shape((heads, n, share, 128), jnp.float32),
            shape((PARTS * heads, splits, share // 2, 128), low),
        ]
        + [shape(block + w.shape, low) for w in shards]
        + [shape((1, size), jnp.float32) for size in sizes],
        in_specs=[pl.BlockSpec(memory_space=pltpu.SMEM)] + [inside] * 11 + [outside] * 6,
        out_specs=[outside] * 4 + [inside] + [outside] * 6 + [inside] * 9,
        scratch_shapes=[
            vmem((rows, width), low),
            vmem((heads, n, share // 2, 128), low),
            vmem((heads, n, rows, 128), low),
            vmem((heads, n, share, 128), jnp.float32),
        ]
        + [vmem(block + w.shape, low) for w in shards[:3]]
        + [
            dma((4,)),
            dma((3, heads)),
            vmem((16, 128), jnp.float32),
            vmem(block + (16, 128), jnp.float32),
            vmem((PARTS, heads, splits, share // 2, 128), low),
            vmem((PARTS, heads, rows, 128), low),
            vmem((heads, n, share // 2, 128), low),
            vmem((n, share // 2, 128), low),
            vmem((n, rows, 128), low),
            dma((heads, n - 1)),
            dma((heads, PARTS - 1)),
            dma((heads, PARTS, max(splits - 1, 1))),
            dma((heads, n - 1)),
            dma((heads, n)),
            dma((heads, n)),
            dma((heads, n)),
        ]
        + gather_semaphores(7, groups, chips),
        compiler_params=pltpu.CompilerParams(
            collective_id=1, has_side_effects=True, vmem_limit_bytes=64000000
        ),
        name="attention_forward",
    )(table, x, first, *vectors, *shards)


def join_tiles(even, odd, high):
    low = lanes(even.shape) < 64
    if high:
        return jnp.where(low, swap_lanes(even), odd)
    return jnp.where(low, even, swap_lanes(odd))


def join_rows(back):
    heads, splits = back.shape[0], back.shape[1]
    tiles = []
    for tile in range(heads // 2):
        parts = []
        for split in range(splits):
            even = back[2 * tile, split].astype(jnp.float32)
            odd = back[2 * tile + 1, split].astype(jnp.float32)
            parts += [join_tiles(even, odd, False), join_tiles(even, odd, True)]
        tiles.append(jnp.concatenate(parts, axis=0))
    return jnp.concatenate(tiles, axis=1)


def own_columns(j, heads, wq, wk, wv):
    def column(w, head):
        tile = w[:, head // 2 * 128 : head // 2 * 128 + 128].astype(jnp.float32)
        return tile, head % 2

    tiles = []
    for w in (wq, wk, wv):
        for part in range(0, w.shape[1] // 64 // heads, 2):
            (a, high_a), (b, high_b) = column(w, part * heads + j), column(w, (part + 1) * heads + j)
            a = swap_lanes(a) if high_a else a
            b = b if high_b else swap_lanes(b)
            tiles.append(jnp.where(lanes(a.shape) < 64, a, b).astype(jnp.bfloat16))
    return jnp.concatenate(tiles, axis=1)


def in_order(some, at, parts):
    heads = len(some)
    tiles = []
    for head in range(0, heads * parts, 2):
        def column(h):
            j, part = h % heads, h // heads
            start = at + part // 2 * 128
            return some[j][:, start : start + 128], part % 2

        (a, high_a), (b, high_b) = column(head), column(head + 1)
        a = swap_lanes(a) if high_a else a
        b = b if high_b else swap_lanes(b)
        tiles.append(jnp.where(lanes(a.shape) < 64, a, b))
    return jnp.concatenate(tiles, axis=1)


def own_vectors(sums, parts, fresh_parts):
    sums = [jnp.broadcast_to(s, (8, s.shape[1])) for s in sums]
    return [in_order(sums, 0, parts)[0:1], in_order(sums, parts * 128, fresh_parts)[0:1]]


def part_of_lane(count, size):
    part = size // count
    lane = lax.broadcasted_iota(jnp.int32, (count, size), 1)
    row = lax.broadcasted_iota(jnp.int32, (count, size), 0)
    return (lane >= row * part) & (lane < row * part + part)


def spread_vectors(vectors, count):
    size = vectors[0].shape[1]
    mine = part_of_lane(count, size)
    at = lax.broadcasted_iota(jnp.int32, (size, 128), 0)
    to = lax.broadcasted_iota(jnp.int32, (size, 128), 1)
    pick_part = jnp.where(lax.rem(at, size // count) == to, 1.0, 0.0).astype(jnp.bfloat16)
    rows = []
    for vector in vectors:
        value = jnp.where(mine, vector, 0.0)
        for _ in range(3):
            high = value.astype(jnp.bfloat16)
            rows.append(high)
            value = value - high.astype(jnp.float32)
    out = product(jnp.concatenate(rows, axis=0), pick_part)
    parts = [out[i * count : (i + 1) * count] for i in range(len(rows))]
    return [(parts[3 * i] + parts[3 * i + 1] + parts[3 * i + 2]).reshape(count, 1, 128) for i in range(len(vectors))]


def backward_kernel(
    n, groups, heads, orders_far, orders_near,
    table, do_in, gain, s_gain2, s_bias2, s_ob, s_eb, s_rb, q_in, kv_in, ol_in, hidden_in, x_in, dmid_in,
    wq_in, wk_in, wv_in, *refs,
):
    count = len(orders_far)
    far_in, refs = refs[:count], refs[count:]
    token_grad, first_grad = refs[:2]
    far_out, refs = refs[2 : 2 + count], refs[2 + count :]
    near_out, refs = refs[: 2 * heads + 1], refs[2 * heads + 1 :]
    do_all, do_work, acc, dq_piece, dq_staged, part_staged, part_all, dkv_staged, dq_back, dkv_back = refs[:10]
    refs = refs[10:]
    near_in, refs = refs[: 2 * heads + 1], refs[2 * heads + 1 :]
    weights, h_across, refs = refs[:heads], refs[heads], refs[heads + 1 :]
    q_all, kv_all, ol_all, hidden, x, dmid, wq, wk, wv, loads = refs[:10]
    refs = refs[10:]
    do_send, do_recv, dq_send, dq_recv, part_send, part_recv, dkv_send, dkv_recv = refs[:8]
    scratch = refs[8:]

    def full_copy(source, held, at):
        pltpu.make_async_copy(source, held, loads.at[at]).wait()
        return held

    entering = [(hidden_in, hidden, 3), (wq_in, wq, 6), (wk_in, wk, 7), (wv_in, wv, 8), (q_in, q_all, 0),
                (kv_in, kv_all, 1), (ol_in, ol_all, 2), (x_in, x, 4), (dmid_in, dmid, 5)]
    ex = Exchange(n)
    chips = n // 2
    g, z, c = lax.axis_index("grp"), ex.s // 2, lax.rem(ex.s, 2)
    enter(ex.peers() + [
        {"grp": lax.rem(g + off // chips, groups), "seq": 2 * lax.rem(z + off % chips, chips) + c}
        for off in range(chips, groups * chips)
    ])
    small = make_direct(groups, chips, near_in[-1], near_out[-1], scratch[-7:])
    scratch = scratch[:-7]
    each = len(scratch) // (count + 2 * heads)
    far = make_reduces(groups, chips, orders_far, far_in, far_out, scratch[: count * each], True)
    near = make_reduces(groups, chips, orders_near, near_in[:-1], near_out[:-1], scratch[count * each :])
    near_last = near[-2:]
    near_first = near[:-2]
    splits = ex.splits
    rows = kv_all.shape[2]
    share = rows // splits
    half = n // 2
    fresh = wv.shape[1]

    @pl.loop(0, heads)
    def _(j):
        for copy in ex.scatter(j, do_in, do_all, do_send, do_recv):
            copy.start()
        ex.own(j, do_in, do_all, do_recv).start()

    for source, held, at in entering:
        pltpu.make_async_copy(source, held, loads.at[at]).start()
    for r in far:
        r.begin()
    for source, held, at in entering[:7]:
        full_copy(source, held, at)
    low = jnp.bfloat16
    fresh_parts = PARTS * fresh // x.shape[1]
    h_across[...] = jnp.transpose(hidden[...])
    for j in range(heads):
        weights[j][...] = own_columns(j, heads, wq, wk, wv)
    slot = slots_of(table, n)
    column = lax.broadcasted_iota(jnp.int32, (rows, share), 1) + ex.split * share
    own_mask = lax.broadcasted_iota(jnp.int32, (rows, share), 0) <= column

    def piece(j, place, at, keys):
        q = unfold(q_all[j, at].astype(jnp.float32), False).astype(jnp.bfloat16)
        grad = unfold(do_work[at].astype(jnp.float32), True)
        ol = ol_all[j, place]
        delta = jnp.sum(jnp.transpose(grad * ol), axis=0, keepdims=True)
        logsum = jnp.transpose(ol)[0:1]
        grad = grad.astype(jnp.bfloat16)

        def block_terms(key_place, key_slot, mask):
            block = kv_all[j, key_slot]
            weight = jnp.exp(product_right(block, q) - logsum)
            if mask:
                weight = jnp.where(own_mask, weight, 0.0)
            change = (weight * (product_right(block, grad) - delta)).astype(jnp.bfloat16)
            term = product(weight.astype(jnp.bfloat16), grad) + product(change, q)
            acc[key_place] = acc[key_place] + term
            return product_left(block, change)

        dq = block_terms(place, at, True)
        if len(keys) in (2, 3):
            slots = [s for _, s in keys]
            dq = lax.fori_loop(0, len(keys), lambda k, v: v + block_terms(k, pick(slots, k), False), dq)
        else:
            for key_place, key_slot in keys:
                dq = dq + block_terms(key_place, key_slot, False)
        dq_piece[place] = fold(jnp.transpose(dq) * 0.125, False).astype(jnp.bfloat16)

    def part_copies(j):
        out = []
        for hop in range(1, splits):
            split = lax.rem(ex.split + hop, splits)
            for part in range(PARTS):
                out.append(remote(part_staged.at[j, hop - 1, part], part_all.at[j, hop - 1, part],
                                  part_send.at[j, hop - 1, part], part_recv.at[j, hop - 1, part],
                                  {"seq": ex.part * splits + split}))
        return out

    def back_copies(j):
        out = []
        row = ex.part * heads + j
        for off in range(1, PARTS):
            part = lax.rem(ex.part + off, PARTS)
            out.append(remote(dkv_staged.at[j, part], dkv_back.at[row], dkv_send.at[j, off - 1],
                              dkv_recv.at[j, ex.part], {"seq": part * splits + ex.split}))
        return out

    @pl.loop(0, heads)
    def _(j):
        for t in range(n):
            here(do_all.at[j, t], do_recv.at[j, t])
        for t in range(n):
            do_work[t] = do_all[j, t]
            acc[t] = jnp.zeros((rows, 128), jnp.float32)

        @pl.loop(0, half)
        def _(c):
            piece(j, half + c, pick(slot[half:], c), [(p, slot[p]) for p in range(half)])

            @pl.when((j == 0) & (c == 1))
            def _():
                for r in far:
                    r.paired()

            @pl.when((j == heads - 1) & (c == 1))
            def _():
                for r in far:
                    r.crossed(0)

        for p in range(half):
            piece(j, p, slot[p], [(k, slot[k]) for k in range(p)])
        for hop in range(1, splits):
            split = lax.rem(ex.split + hop, splits)
            for part in range(PARTS):
                part_staged[j, hop - 1, part] = acc[table[0, part * splits + split]].astype(jnp.bfloat16)
        for copy in part_copies(j):
            copy.start()
        for t in range(n):
            dq_staged[j, t] = dq_piece[table[0, t]]
        for hop in range(1, splits):
            for part in range(PARTS):
                here(part_all.at[j, hop - 1, part], part_recv.at[j, hop - 1, part])
        for part in range(PARTS):
            total = acc[table[0, part * splits + ex.split]]
            for hop in range(1, splits):
                total = total + part_all[j, hop - 1, part].astype(jnp.float32)
            dkv_staged[j, part] = total.astype(jnp.bfloat16)
        for copy in back_copies(j):
            copy.start()
        pltpu.make_async_copy(dkv_staged.at[j, ex.part], dkv_back.at[ex.part * heads + j],
                              dkv_recv.at[j, ex.part]).start()
        for copy in ex.give_back(j, heads, dq_staged, dq_back, dq_send, dq_recv):
            copy.start()
        ex.keep_own(j, heads, dq_staged, dq_back, dq_recv).start()

    levels = len(powers(groups))

    def total(v):
        return jnp.sum(v, axis=0, keepdims=True)

    def project(j):
        for t in range(n):
            here(dq_back.at[t // splits * heads + j, t % splits], dq_recv.at[j, t])
        for part in range(PARTS):
            here(dkv_back.at[part * heads + j], dkv_recv.at[j, part])
        tiles = []
        for part in range(0, PARTS, 2):
            a, b = part * heads + j, part * heads + heads + j
            parts = []
            for split in range(splits):
                even, odd = dq_back[a, split].astype(jnp.float32), dq_back[b, split].astype(jnp.float32)
                parts += [join_tiles(even, odd, False), join_tiles(even, odd, True)]
            tiles.append(jnp.concatenate(parts, axis=0))
        pairs = [(dkv_back[part * heads + j].astype(jnp.float32), dkv_back[(part + 1) * heads + j].astype(jnp.float32))
                 for part in range(0, PARTS, 2)]
        tiles += [join_tiles(a, b, False) for a, b in pairs]
        tiles += [join_tiles(a, b, True) for a, b in pairs[: fresh_parts // 2]]
        grad = jnp.concatenate(tiles, axis=1)
        sums = total(grad)
        grad = grad.astype(low)
        for ref, r, value in ((near_in[2 * j + 1], near[2 * j + 1], grad[:, PARTS * 64 :]),
                              (near_in[2 * j], near[2 * j], grad[:, : PARTS * 64])):
            ref[...] = product(h_across[...], value).reshape(ref.shape).astype(low)
            r.begin()
        return product_right(grad, weights[j][...]), sums

    devices = groups * n
    ob, gain2, bias2, rb = spread_vectors([s_ob[...], s_gain2[...], s_bias2[...], s_rb[...]], devices)
    later_rows = [ob, gain2, bias2] + spread_vectors([s_eb[...]], devices) + [rb]
    later_rows.append(jnp.zeros((devices, 16 - 9, 128), jnp.float32))
    done = [project(0)]
    for r in far:
        for level in range(1, levels):
            r.crossed(level)
    done += [project(j) for j in range(1, heads - 1)]
    for r in near_first:
        r.paired()
    normed, scale = normal_rows(full_copy(x_in, x, 4)[...].astype(jnp.float32))
    for level in range(levels - 1):
        for r in near_first:
            r.crossed(level)
    done.append(project(heads - 1))
    for r in far:
        r.chained(True)
    for r in near_first:
        r.crossed(levels - 1)
    dh = done[0][0]
    for more, _ in done[1:]:
        dh = dh + more
    for r in near_last:
        r.paired()
    sums = [total(dh * normed), total(dh)]
    sum_q, sum_v = own_vectors([s for _, s in done], PARTS, fresh_parts)
    first_rows = spread_vectors(sums + [sum_q], devices) + spread_vectors([sum_v], devices)
    spread = jnp.concatenate(first_rows + later_rows, axis=1)
    near_in[-1][...] = spread.reshape(near_in[-1].shape)
    small.begin()
    for level in range(levels):
        for r in near_last:
            r.crossed(level)
        if level == 0:
            small.paired()
    scaled = dh * gain[...].astype(jnp.float32)
    inner = jnp.mean(scaled, axis=-1, keepdims=True)
    along = jnp.mean(scaled * normed, axis=-1, keepdims=True)
    token_grad[...] = full_copy(dmid_in, dmid, 5)[...] + scale * (scaled - inner - normed * along)
    for pair in range(fresh // 64, PARTS * heads, 2):
        even, odd = dkv_back[pair].astype(jnp.float32), dkv_back[pair + 1].astype(jnp.float32)
        first_grad[:, pair * 64 - fresh : pair * 64 - fresh + 128] = join_tiles(even, odd, True)
    for r in far:
        r.chained(False)
    for r in far:
        r.chain_finish()
    for r in near:
        r.finish()
    small.direct_finish()
    for r in far + near + [small]:
        r.drain()

    @pl.loop(0, heads)
    def _(j):
        for copy in ex.scatter(j, do_in, do_all, do_send, do_recv):
            copy.wait_send()
        for copy in part_copies(j):
            copy.wait_send()
        for copy in back_copies(j):
            copy.wait_send()
        for copy in ex.give_back(j, heads, dq_staged, dq_back, dq_send, dq_recv):
            copy.wait_send()


def backward_call(n, groups, table, do_in, q_all, kv_all, ol_all, hidden, x, gain, wq, wk, wv, dmid, sums, far):
    heads, _, rows, _ = kv_all.shape
    splits = n // PARTS
    chips = n // 2
    share = rows // splits
    width, fresh = wv.shape
    low = jnp.bfloat16
    vmem, dma = pltpu.VMEM, pltpu.SemaphoreType.DMA
    inside = pl.BlockSpec(memory_space=vmem)
    shape = jax.ShapeDtypeStruct
    bits = powers(groups)
    forth, back = bits, bits[::-1]
    block = (groups, chips, 2)
    part = width // (groups * n)
    wide = 2 * PARTS * 64 + PARTS * 64 * fresh // width
    near = [block + (part, PARTS * 64, low), block + (part, wide - PARTS * 64, low)] * heads
    near += [block + (16, 128, jnp.float32)]
    shapes = [f.shape + (low,) for f in far] + near
    return pl.pallas_call(
        functools.partial(backward_kernel, n, groups, heads, [forth, back, forth][: len(far)],
                          [(forth, back)[j % 2] for j in range(2 * heads)]),
        out_shape=[shape((rows, width), jnp.float32), shape((rows, width - fresh), jnp.float32)]
        + [shape(s[3:5], jnp.float32) for s in shapes],
        in_specs=[pl.BlockSpec(memory_space=pltpu.SMEM)] + [inside] * 7
        + [pl.BlockSpec(memory_space=pl.ANY)] * (9 + len(far)),
        out_specs=[inside] * (3 + 2 * heads + len(far)),
        scratch_shapes=[
            vmem((heads, n, share // 2, 128), low),
            vmem((n, share // 2, 128), low),
            vmem((n, rows, 128), jnp.float32),
            vmem((n, share // 2, 128), low),
            vmem((heads, n, share // 2, 128), low),
            vmem((heads, max(splits - 1, 1), PARTS, rows, 128), low),
            vmem((heads, max(splits - 1, 1), PARTS, rows, 128), low),
            vmem((heads, PARTS, rows, 128), low),
            vmem((PARTS * heads, splits, share // 2, 128), low),
            vmem((PARTS * heads, rows, 128), low),
        ]
        + [vmem(s[:5], s[5]) for s in near]
        + [vmem((width, wide), low)] * heads
        + [vmem((width, rows), low)]
        + [vmem(v.shape, v.dtype) for v in (q_all, kv_all, ol_all, hidden, x, dmid, wq, wk, wv)]
        + [
            dma((9,)),
            dma((heads, n - 1)),
            dma((heads, n)),
            dma((heads, n - 1)),
            dma((heads, n)),
            dma((heads, max(splits - 1, 1), PARTS)),
            dma((heads, max(splits - 1, 1), PARTS)),
            dma((heads, PARTS - 1)),
            dma((heads, PARTS)),
        ]
        + reduce_scratch(groups, chips, shapes[: len(far)], True)
        + reduce_scratch(groups, chips, shapes[len(far) : -1])
        + direct_scratch(groups, chips, shapes[-1]),
        compiler_params=pltpu.CompilerParams(
            collective_id=2, has_side_effects=True, vmem_limit_bytes=67043328
        ),
        name="attention_backward",
    )(table, do_in, gain, *sums, q_all, kv_all, ol_all, hidden, x, dmid, wq, wk, wv, *far)


def hand_over_kernel(count, heads, sizes, fresh_parts, *refs):
    ins, refs = refs[:count], refs[count:]
    near, small, refs = refs[: 2 * heads], refs[2 * heads], refs[2 * heads + 1 :]
    outs, refs = refs[:count], refs[count:]
    g_wq, g_wk, g_wv = refs[:3]
    vectors, refs = refs[3 : 3 + len(sizes)], refs[3 + len(sizes) :]
    held, loads, stores = refs[:-2], refs[-2], refs[-1]
    for i in range(count):
        pltpu.make_async_copy(ins[i], held[i], loads.at[i]).start()
    some = [ref[...] for ref in near]
    g_wq[...] = in_order(some[::2], 0, PARTS)
    g_wk[...] = in_order(some[1::2], 0, PARTS)
    g_wv[...] = in_order(some[1::2], PARTS * 64, fresh_parts)
    for row, size in enumerate(sizes):
        vectors[row][...] = small[row : row + 1, :size]
    for i in range(count):
        pltpu.make_async_copy(ins[i], held[i], loads.at[i]).wait()
        pltpu.make_async_copy(held[i], outs[i], stores.at[i]).start()
    for i in range(count):
        pltpu.make_async_copy(held[i], outs[i], stores.at[i]).wait()


def hand_over(arrays, near, small, sizes, width, fresh):
    shape = jax.ShapeDtypeStruct
    count, heads = len(arrays), len(near) // 2
    rows = near[0].shape[0]
    inside, outside = pl.BlockSpec(memory_space=pltpu.VMEM), pl.BlockSpec(memory_space=pl.ANY)
    return pl.pallas_call(
        functools.partial(hand_over_kernel, count, heads, sizes, PARTS * fresh // width),
        out_shape=[shape(a.shape, a.dtype) for a in arrays]
        + [shape((rows, size), jnp.float32) for size in (width, width, fresh)]
        + [shape((1, size), jnp.float32) for size in sizes],
        in_specs=[outside] * count + [inside] * (2 * heads + 1),
        out_specs=[outside] * count + [inside] * (3 + len(sizes)),
        scratch_shapes=[pltpu.VMEM(a.shape, a.dtype) for a in arrays]
        + [pltpu.SemaphoreType.DMA((count,)), pltpu.SemaphoreType.DMA((count,))],
        compiler_params=pltpu.CompilerParams(vmem_limit_bytes=60000000),
        name="hand_over",
    )(*arrays, *near, small)


def feed_kernel(
    parts, heads, back, x, dy, bo, gain, shift, be, br, wo_in, we_in, wr_in,
    out, dmid_out, do_staged, s_gain, s_shift, s_ob, s_eb, s_rb, g_we, g_wr, g_wo,
    wo, we, wr, k_we, k_wr, k_wo, dh, load, keep,
):
    low = jnp.bfloat16
    rows, width = x.shape
    step = we.shape[1] // parts
    splits = back.shape[1]

    def total(v):
        return jnp.sum(v, axis=0, keepdims=True)

    def columns(c):
        return pl.ds(pl.multiple_of(c * step, 128), step)

    def fetch(c):
        return (pltpu.make_async_copy(we_in.at[:, columns(c)], we.at[:, columns(c)], load.at[c]),
                pltpu.make_async_copy(wr_in.at[columns(c)], wr.at[columns(c)], load.at[parts + c]))

    def store(c):
        return (pltpu.make_async_copy(k_we.at[:, columns(c)], g_we.at[:, columns(c)], keep.at[c]),
                pltpu.make_async_copy(k_wr.at[columns(c)], g_wr.at[columns(c)], keep.at[parts + c]))

    first = pltpu.make_async_copy(wo_in, wo, load.at[2 * parts])
    first.start()
    for c in range(parts):
        for copy in fetch(c):
            copy.start()
    att = join_rows(back).astype(low)
    first.wait()
    mid = x[...].astype(jnp.float32) + product(att, wo[...]) + bo[...]
    normed, scale = normal_rows(mid)
    second = (normed * gain[...] + shift[...]).astype(low)
    second_across = jnp.transpose(second)
    seed = dy[...]
    seed_full = seed.astype(jnp.float32)
    s_rb[...] = total(seed_full)
    dmid_out[...] = mid + br[...]
    dh[...] = jnp.zeros((rows, width), jnp.float32)

    @pl.loop(0, parts)
    def _(c):
        for copy in fetch(c):
            copy.wait()
        expand, reduce = we[:, columns(c)], wr[columns(c)]
        u = product(second, expand) + be[:, columns(c)]
        square = u * u
        t = jnp.tanh(math.sqrt(2 / math.pi) * (u + 0.044715 * (u * square)))
        z = (0.5 * u * (1.0 + t)).astype(low)
        slope = 0.5 * (1.0 + t) + (0.5 * math.sqrt(2 / math.pi)) * u * (1.0 - t * t) * (1.0 + (3 * 0.044715) * square)
        du_full = (slope * product_right(seed, reduce)).astype(low)
        s_eb[:, columns(c)] = total(du_full.astype(jnp.float32))
        dmid_out[...] += product(z, reduce)
        dh[...] += product_right(du_full, expand)
        k_wr[columns(c)] = product(jnp.transpose(z), seed).astype(low)
        k_we[:, columns(c)] = product(second_across, du_full).astype(low)
        for copy in store(c):
            copy.start()

    out[...] = dmid_out[...].astype(low)
    back_normed = dh[...]
    s_gain[...] = total(back_normed * normed)
    s_shift[...] = total(back_normed)
    scaled = back_normed * gain[...]
    inner = jnp.mean(scaled, axis=-1, keepdims=True)
    along = jnp.mean(scaled * normed, axis=-1, keepdims=True)
    dmid = seed_full + scale * (scaled - inner - normed * along)
    dmid_out[...] = dmid
    branch = dmid.astype(low)
    s_ob[...] = total(branch.astype(jnp.float32))
    k_wo[...] = product(jnp.transpose(att), branch).astype(low)
    last = pltpu.make_async_copy(k_wo, g_wo, keep.at[2 * parts])
    last.start()
    for group in range(width // 256):
        datt = product_right(branch, wo[group * 256 : (group + 1) * 256, :])

        def put(head, split, v, group=group):
            head = head + 4 * group
            do_staged[head // heads, head % heads, split] = v.astype(low)

        pack_heads(datt, splits, put)
    for c in range(parts):
        for copy in store(c):
            copy.wait()
    last.wait()


def feed_call(back, x, dy, bo, gain, shift, be, br, wo, we, wr):
    rows, width = x.shape
    inner = we.shape[1]
    parts = inner // width
    heads = back.shape[0] // PARTS
    splits = back.shape[1]
    low, full = jnp.bfloat16, jnp.float32
    vmem, dma = pltpu.VMEM, pltpu.SemaphoreType.DMA
    inside, outside = pl.BlockSpec(memory_space=vmem), pl.BlockSpec(memory_space=pl.ANY)
    shape = jax.ShapeDtypeStruct
    return pl.pallas_call(
        functools.partial(feed_kernel, parts, heads),
        out_shape=[
            shape((rows, width), low),
            shape((rows, width), full),
            shape((PARTS, heads) + back.shape[1:], low),
            shape((1, width), full),
            shape((1, width), full),
            shape((1, width), full),
            shape((1, inner), full),
            shape((1, width), full),
            shape(we.shape, low),
            shape(wr.shape, low),
            shape(wo.shape, low),
        ],
        in_specs=[inside] * 8 + [outside] * 3,
        out_specs=[inside] * 8 + [outside] * 3,
        scratch_shapes=[
            vmem(wo.shape, low), vmem(we.shape, low), vmem(wr.shape, low),
            vmem(we.shape, low), vmem(wr.shape, low), vmem(wo.shape, low),
            vmem((rows, width), full),
            dma((2 * parts + 1,)), dma((2 * parts + 1,)),
        ],
        compiler_params=pltpu.CompilerParams(vmem_limit_bytes=64000000),
        name="feed_forward",
    )(back, x, dy, bo, gain, shift, be, br, wo, we, wr)


def body(
    tokens,
    first_values,
    placement,
    cotangent,
    *parts,
):
    groups, rows, width = tokens.shape
    n = lax.axis_size("seq")
    small = (0, 1, 3, 6, 8, 9, 10, 12, 14)
    large = (2, 4, 5, 7, 11, 13)
    done = forward_call(n, lax.axis_size("grp"), placement, tokens[0], first_values[0],
                        [parts[i][None] for i in small], [parts[i] for i in large])
    hidden, q_all, kv_all, ol_all, back = done[:5]
    whole = [None] * 15
    for i, v in zip(large, done[5:11]):
        whole[i] = v.reshape(-1, v.shape[-1])
    for i, v in zip(small, done[11:]):
        whole[i] = v[0]
    layer_output, dmid, do_staged, *sums, g_we, g_wr, g_wo = feed_call(
        back, tokens[0], cotangent[0], whole[8][None], whole[9][None], whole[10][None], whole[12][None],
        whole[14][None], whole[7], whole[11], whole[13],
    )
    block = (lax.axis_size("grp"), n // 2, 2)
    far = [v.reshape(block + (-1, v.shape[1])) for v in (g_we, g_wr, g_wo)]
    inside = far if n <= 8 else []
    done = backward_call(
        n, block[0], placement, do_staged, q_all, kv_all, ol_all, hidden, tokens[0],
        whole[0][None], whole[2], whole[4], whole[5], dmid, [sums[0], sums[1], sums[2], sums[3], sums[4]],
        inside,
    )
    token_grad, first_grad = done[:2]
    if not inside:
        forth = powers(block[0])
        done = done[:2] + reduce_call(block[0], block[1], far, [forth, forth[::-1], forth]) + done[2:]
    g_we, g_wr, g_wo = done[2:5]
    near, g_small = done[5:-1], done[-1]
    sizes = [parts[i].shape[0] for i in small]
    out = hand_over([token_grad, first_grad, g_wo, g_we, g_wr], near, g_small, sizes, whole[2].shape[1], whole[5].shape[1])
    owned = [None] * 15
    for i, v in zip((7, 11, 13, 2, 4, 5), out[2:8]):
        owned[i] = v
    for i, v in zip(small, out[8:]):
        owned[i] = v.reshape(-1)
    return (layer_output[None], out[0][None], out[1][None]) + tuple(owned)


def solution(mesh):
    spread = P("grp", "seq", None)
    both = ("grp", "seq")
    vector, matrix = P(both), P(both, None)
    kinds = (vector, vector, matrix, vector, matrix, matrix, vector, matrix, vector, vector, vector,
             matrix, vector, matrix, vector)
    in_specs = (spread, spread, P("grp", None), spread) + kinds
    out_specs = (spread, spread, spread) + kinds
    return jax.shard_map(body, mesh=mesh, in_specs=in_specs, out_specs=out_specs, check_vma=False)
```
